32 devices in a mesh: dp: 8 (over y, x, core), mp: 4 (over z).
Axes of the slice: x: 2, y: 2, z: 4, core: 2. Of those that a mesh axis runs over, the one named last changes fastest.
Arguments:
- tokens: bfloat16 [8192, 768], P('dp'), may hold values from -6 to 6
- lengths: int32 [8], P('dp'), may hold values from 128 to 1024, as said below
- w_query: bfloat16 [1, 768, 768], P(None, None, 'mp'), may hold values from -0.21875 to 0.21875
- w_key: bfloat16 [1, 768, 768], P(None, None, 'mp'), may hold values from -0.21875 to 0.21875
- w_value: bfloat16 [1, 768, 768], P(None, None, 'mp'), may hold values from -0.21875 to 0.21875
- b_query: float32 [1, 768], P(None, 'mp'), may hold values from -3 to 3
- b_value: float32 [1, 768], P(None, 'mp'), may hold values from -3 to 3
- conv_key: float32 [1, 5, 768], P(None, None, 'mp'), may hold values from -2.5 to 2.5
- conv_value: float32 [1, 5, 768], P(None, None, 'mp'), may hold values from -2.5 to 2.5
- w_out: bfloat16 [1, 768, 768], P(None, 'mp'), may hold values from -1.5 to 1.5
- b_out: float32 [1, 768], replicated, may hold values from -3 to 3
- attn_gain: float32 [1, 768], replicated, may hold values from 0.1 to 1.9
- attn_shift: float32 [1, 768], replicated, may hold values from -2 to 2
- w_up: bfloat16 [1, 768, 3072], P(None, None, 'mp'), may hold values from -0.21875 to 0.21875
- b_up: float32 [1, 3072], P(None, 'mp'), may hold values from -3 to 3
- w_down: bfloat16 [1, 3072, 768], P(None, 'mp'), may hold values from -0.15625 to 0.15625
- b_down: float32 [1, 768], replicated, may hold values from -3 to 3
- ffn_gain: float32 [1, 768], replicated, may hold values from 0.1 to 1.9
- ffn_shift: float32 [1, 768], replicated, may hold values from -2 to 2
- cotangent: bfloat16 [8192, 768], P(('dp', 'mp')), may hold values from -6 to 6
Outputs:
- activations: bfloat16 [8192, 768], P(('dp', 'mp'))
- grad_tokens: float32 [8192, 768], P(('dp', 'mp'))
- grad_w_query: float32 [1, 768, 768], P(None, 'dp', 'mp')
- grad_w_key: float32 [1, 768, 768], P(None, 'dp', 'mp')
- grad_w_value: float32 [1, 768, 768], P(None, 'dp', 'mp')
- grad_b_query: float32 [1, 768], replicated
- grad_b_value: float32 [1, 768], replicated
- grad_conv_key: float32 [1, 5, 768], replicated
- grad_conv_value: float32 [1, 5, 768], replicated
- grad_w_out: float32 [1, 768, 768], P(None, 'mp', 'dp')
- grad_b_out: float32 [1, 768], replicated
- grad_attn_gain: float32 [1, 768], replicated
- grad_attn_shift: float32 [1, 768], replicated
- grad_w_up: float32 [1, 768, 3072], P(None, 'dp', 'mp')
- grad_b_up: float32 [1, 3072], replicated
- grad_w_down: float32 [1, 3072, 768], P(None, 'mp', 'dp')
- grad_b_down: float32 [1, 768], replicated
- grad_ffn_gain: float32 [1, 768], replicated
- grad_ffn_shift: float32 [1, 768], replicated
The draws below stay inside these ranges and needn't reach their ends.
Inputs may be any that keep to these rules, and one draw needn't show every extreme that they name: Positions from lengths[b] on are padding; some sequence has all 1024 slots live and some has 128.
All inputs are finite; a program needn't handle non-finite values.
Results may differ from the reference program's by a relative error of at most 0.015.
The reference program's roundings to bfloat16 on the way count: a program that leaves them out, or rounds other values in their place, can miss the bound.
Values may be sent and summed in bfloat16 or wider, within the bound.
A program may use at most 128 MiB of HBM per device.

```python
import math
import jax
import jax.numpy as jnp
from jax import lax

D = 768
HEADS = 12
HEAD_DIM = 64
FF = 3072
WINDOW = 128
POOL_WINDOW = 512
KERNEL = 5
STRIDE = 4
LAYERS = 1
SEQ_LEN = 1024
BATCH = 8
TOKENS = 8192


def draw_lengths(key, part):
    drawn = jax.random.randint(key, (BATCH,), SEQ_LEN // 8, SEQ_LEN + 1, dtype=jnp.int32)
    return drawn.at[0].set(SEQ_LEN).at[1].set(SEQ_LEN // 8)


def block_scale(key, dims, split, smallest, top_value):
    factor_of = 1.0
    for position, shards_of in split:
        heights = jax.random.uniform(jax.random.fold_in(jax.random.fold_in(key, 6), position), (shards_of,), jnp.float32, smallest / len(split), top_value / len(split))
        factor_of = factor_of * jnp.repeat(jnp.exp(heights), dims[position] // shards_of).reshape((-1,) + (1,) * (len(dims) - 1 - position))
    return factor_of


def scatter_about(own_key, dims, scale, most, cuts=(), kind=jnp.bfloat16):
    level = block_scale(own_key, dims, cuts, -0.22, 0.18) if cuts else 1.0
    values = jax.random.normal(own_key, dims, jnp.float32) * scale * level
    return jnp.minimum(jnp.maximum(values, -most), most).astype(kind)


def setup_inputs(seed: int = 0) -> dict:
    seeds = jax.random.split(jax.random.key(seed), 21)
    return {
        "tokens": scatter_about(seeds[0], (TOKENS, D), 1.0, 6.0, ((0, 8),)),
        "lengths": draw_lengths(jax.random.fold_in(seeds[20], 71), 0),
        "w_query": scatter_about(seeds[2], (LAYERS, D, D), D ** -0.5, 0.21875, ((2, 4),)),
        "w_key": scatter_about(seeds[3], (LAYERS, D, D), D ** -0.5, 0.21875, ((2, 4),)),
        "w_value": scatter_about(seeds[4], (LAYERS, D, D), D ** -0.5, 0.21875, ((2, 4),)),
        "b_query": scatter_about(seeds[5], (LAYERS, D), 0.5, 3.0, ((1, 4),), jnp.float32),
        "b_value": scatter_about(seeds[6], (LAYERS, D), 0.5, 3.0, ((1, 4),), jnp.float32),
        "conv_key": scatter_about(seeds[7], (LAYERS, KERNEL, D), 0.45, 2.5, ((2, 4),), jnp.float32),
        "conv_value": scatter_about(seeds[8], (LAYERS, KERNEL, D), 0.45, 2.5, ((2, 4),), jnp.float32),
        "w_out": scatter_about(seeds[9], (LAYERS, D, D), (D // 48) ** -0.5, 1.5, ((1, 4),)),
        "b_out": scatter_about(seeds[10], (LAYERS, D), 0.5, 3.0, (), jnp.float32),
        "attn_gain": jnp.clip(1.0 + 0.18 * jax.random.normal(seeds[11], (LAYERS, D), jnp.float32), 0.1, 1.9),
        "attn_shift": scatter_about(seeds[12], (LAYERS, D), 0.3, 2.0, (), jnp.float32),
        "w_up": scatter_about(seeds[13], (LAYERS, D, FF), D ** -0.5, 0.21875, ((2, 4),)),
        "b_up": scatter_about(seeds[14], (LAYERS, FF), 0.5, 3.0, ((1, 4),), jnp.float32),
        "w_down": scatter_about(seeds[15], (LAYERS, FF, D), (FF // 2) ** -0.5, 0.15625, ((1, 4),)),
        "b_down": scatter_about(seeds[16], (LAYERS, D), 0.5, 3.0, (), jnp.float32),
        "ffn_gain": jnp.clip(1.0 + 0.18 * jax.random.normal(seeds[17], (LAYERS, D), jnp.float32), 0.1, 1.9),
        "ffn_shift": scatter_about(seeds[18], (LAYERS, D), 0.3, 2.0, (), jnp.float32),
        "cotangent": scatter_about(seeds[19], (TOKENS, D), 1.0, 6.0, ((0, 32),)),
    }


@jax.custom_vjp
def low(v):
    return lax.optimization_barrier(v.astype(jnp.bfloat16)).astype(jnp.float32)

@jax.custom_vjp
def low_back(v):
    return v

def low_keep(v):
    return (low(v), None)

def low_pass(kept, grad):
    return (grad,)

def back_keep(v):
    return (v, None)

def back_low(kept, grad):
    return (low(grad),)
low.defvjp(low_keep, low_pass)
low_back.defvjp(back_keep, back_low)
block_rows = 512
mask_fill = -1000000000.0
epsilon = 1e-05

def matmul_high(left, right):
    return jnp.matmul(left, right, precision=lax.Precision.HIGHEST)

def norm_rows(hidden, gain, shift):
    center = hidden - lax.optimization_barrier(jnp.mean(hidden, axis=-1, keepdims=True))
    spread = lax.optimization_barrier(jnp.mean(center * center, axis=-1, keepdims=True))
    return center * lax.rsqrt(spread + epsilon) * gain + shift

def pool_rows(values, kernel):
    seqs, length, chans = values.shape
    width = kernel.shape[0]
    half = width // 2
    pooled_len = length // STRIDE
    padded = jnp.pad(values, ((0, 0), (half, width), (0, 0)))
    total = jnp.zeros((seqs, pooled_len, chans), jnp.float32)
    for offset in range(width):
        total = total + kernel[offset] * padded[:, offset:offset + STRIDE * pooled_len:STRIDE]
    return total

def block_mask(start, lengths):
    reach = WINDOW // 2
    pool_reach = POOL_WINDOW // 2 // STRIDE
    span = block_rows // STRIDE + 2 * pool_reach
    rows = start + jnp.arange(block_rows, dtype=jnp.int32)
    near_pos = start - reach + jnp.arange(block_rows + 2 * reach, dtype=jnp.int32)
    far_pos = (start // STRIDE - pool_reach + jnp.arange(span, dtype=jnp.int32)) * STRIDE
    limit = lengths[:, None, None]
    near_ok = (jnp.abs(rows[:, None] - near_pos[None, :]) <= reach)[None] & (near_pos >= 0)[None, None] & (near_pos[None, None] < limit)
    far_ok = (jnp.abs(rows[:, None] - far_pos[None, :]) <= POOL_WINDOW // 2)[None] & (far_pos >= 0)[None, None] & (far_pos[None, None] < limit)
    return jnp.concatenate([near_ok, far_ok], axis=-1)

def attend(queries, keys_loc, vals_loc, far_keys, far_vals, lengths):
    seqs, length, heads, size = queries.shape
    reach = WINDOW // 2
    pool_reach = POOL_WINDOW // 2 // STRIDE
    span = block_rows // STRIDE + 2 * pool_reach
    near_len = block_rows + 2 * reach
    pad_near = ((0, 0), (reach, reach), (0, 0), (0, 0))
    pad_far = ((0, 0), (pool_reach, pool_reach), (0, 0), (0, 0))
    near_k = jnp.pad(keys_loc, pad_near)
    near_v = jnp.pad(vals_loc, pad_near)
    far_k = jnp.pad(far_keys, pad_far)
    far_v = jnp.pad(far_vals, pad_far)
    scale = size ** (-0.5)

    def one_block(block):
        start = (block * block_rows).astype(jnp.int32)
        pool_start = (block * (block_rows // STRIDE)).astype(jnp.int32)
        q_rows = lax.dynamic_slice_in_dim(queries, start, block_rows, 1)
        keys_b = jnp.concatenate([lax.dynamic_slice_in_dim(near_k, start, near_len, 1), lax.dynamic_slice_in_dim(far_k, pool_start, span, 1)], axis=1)
        vals_b = jnp.concatenate([lax.dynamic_slice_in_dim(near_v, start, near_len, 1), lax.dynamic_slice_in_dim(far_v, pool_start, span, 1)], axis=1)
        mask = block_mask(start, lengths)
        scores = jnp.einsum('sqhe,skhe->shqk', q_rows, keys_b, precision=lax.Precision.HIGHEST) * scale
        scores = low_back(jnp.where(mask[:, None], scores, mask_fill))
        peak = lax.optimization_barrier(jnp.max(scores, axis=-1, keepdims=True))
        expo = jnp.exp(scores - peak)
        weights = low(expo / lax.optimization_barrier(jnp.sum(expo, axis=-1, keepdims=True)))
        result = jnp.einsum('shqk,skhe->sqhe', weights, vals_b, precision=lax.Precision.HIGHEST)
        live = start + jnp.arange(block_rows, dtype=jnp.int32)[None, :] < lengths[:, None]
        return jnp.where(live[:, :, None, None], result, 0.0)
    blocks = lax.map(jax.checkpoint(one_block), jnp.arange(length // block_rows, dtype=jnp.int32))
    return jnp.moveaxis(blocks, 0, 1).reshape(seqs, length, heads, size)

def layer_forward(values, lens_group, weights):
    w_query, w_key, w_value, b_query, b_value, conv_key, conv_value, w_out, b_out, attn_gain, attn_shift, w_up, b_up, w_down, b_down, ffn_gain, ffn_shift = weights
    seqs, length, width = values.shape
    inputs_low = low(values)
    queries = low(low_back(matmul_high(inputs_low, w_query) + b_query))
    keys_loc = low(low_back(matmul_high(inputs_low, w_key)))
    vals_loc = low(low_back(matmul_high(inputs_low, w_value) + b_value))
    valid = (jnp.arange(length, dtype=jnp.int32)[None, :] < lens_group[:, None]).astype(jnp.float32)[:, :, None]
    far_keys = low(pool_rows(keys_loc * valid, conv_key))
    far_vals = low(pool_rows(vals_loc * valid, conv_value))

    def split_heads(array):
        return array.reshape(array.shape[0], array.shape[1], HEADS, HEAD_DIM)
    context = attend(split_heads(queries), split_heads(keys_loc), split_heads(vals_loc), split_heads(far_keys), split_heads(far_vals), lens_group)
    context = low(low_back(context.reshape(seqs, length, width)))
    attn = low_back(matmul_high(context, w_out) + b_out)
    normed = norm_rows(values + attn, attn_gain, attn_shift)
    upper = low_back(matmul_high(low(normed), w_up) + b_up)
    active = low(jax.nn.gelu(upper, approximate=False))
    ffn = low_back(matmul_high(active, w_down) + b_down)
    return norm_rows(normed + ffn, ffn_gain, ffn_shift)

def reference(tokens, lengths, w_query, w_key, w_value, b_query, b_value, conv_key, conv_value, w_out, b_out, attn_gain, attn_shift, w_up, b_up, w_down, b_down, ffn_gain, ffn_shift, cotangent):
    params = tuple((item.astype(jnp.float32) for item in (w_query, w_key, w_value, b_query, b_value, conv_key, conv_value, w_out, b_out, attn_gain, attn_shift, w_up, b_up, w_down, b_down, ffn_gain, ffn_shift)))
    group = math.gcd(max(1, 4096 // SEQ_LEN), BATCH)
    count = BATCH // group
    inputs = tokens.astype(jnp.float32).reshape(count, group, SEQ_LEN, D)
    cots = cotangent.astype(jnp.float32).reshape(count, group, SEQ_LEN, D)
    lens = lengths.reshape(count, group)

    def forward(values, lens_group, weights):
        for layer in range(LAYERS):
            values = layer_forward(values, lens_group, tuple((item[layer] for item in weights)))
        return values

    def step(totals, item):
        values, lens_group, cot_group = item
        result, pull = jax.vjp(lambda values_in, weights_in: forward(values_in, lens_group, weights_in), values, params)
        grad_in, grad_weights = pull(cot_group)
        totals = tuple((total + grad for total, grad in zip(totals, grad_weights)))
        return (totals, (result.astype(jnp.bfloat16), grad_in))
    zeros = tuple((jnp.zeros_like(item) for item in params))
    totals, (results, grads_in) = lax.scan(step, zeros, (inputs, lens, cots))
    return (results.reshape(TOKENS, D), grads_in.reshape(TOKENS, D), totals[0], totals[1], totals[2], totals[3], totals[4], totals[5], totals[6], totals[7], totals[8], totals[9], totals[10], totals[11], totals[12], totals[13], totals[14], totals[15], totals[16])
```

```python
import jax
import jax.numpy as jnp
from jax import lax
from jax.experimental import pallas as pl
from jax.experimental.pallas import tpu as pltpu
from jax.sharding import PartitionSpec as P

D = 768
HEAD_DIM = 64
FF = 3072
WINDOW = 128
POOL_WINDOW = 512
STRIDE = 4
LAYERS = 1


block_rows = 512
mask_fill = -1000000000.0
epsilon = 1e-05


def norm_rows(hidden, gain, shift):
    center = hidden - jnp.mean(hidden, axis=-1, keepdims=True)
    spread = jnp.mean(center * center, axis=-1, keepdims=True)
    return center * lax.rsqrt(spread + epsilon) * gain + shift


def gelu_exact(values):
    return jax.nn.gelu(values, approximate=False)


def pool_rows(values, kernel):
    seqs, length, chans = values.shape
    width = kernel.shape[0]
    half = width // 2
    pooled_len = length // STRIDE
    padded = jnp.pad(values, ((0, 0), (half, width), (0, 0)))
    total = jnp.zeros((seqs, pooled_len, chans), jnp.float32)
    for offset in range(width):
        total = total + kernel[offset] * padded[:, offset : offset + STRIDE * pooled_len : STRIDE]
    return total


def block_mask(start, lengths):
    reach = WINDOW // 2
    pool_reach = POOL_WINDOW // 2 // STRIDE
    span = block_rows // STRIDE + 2 * pool_reach
    rows = start + jnp.arange(block_rows, dtype=jnp.int32)
    near_pos = start - reach + jnp.arange(block_rows + 2 * reach, dtype=jnp.int32)
    far_pos = (start // STRIDE - pool_reach + jnp.arange(span, dtype=jnp.int32)) * STRIDE
    limit = lengths[:, None, None]
    near_ok = (
        (jnp.abs(rows[:, None] - near_pos[None, :]) <= reach)[None]
        & (near_pos >= 0)[None, None]
        & (near_pos[None, None] < limit)
    )
    far_ok = (
        (jnp.abs(rows[:, None] - far_pos[None, :]) <= POOL_WINDOW // 2)[None]
        & (far_pos >= 0)[None, None]
        & (far_pos[None, None] < limit)
    )
    return jnp.concatenate([near_ok, far_ok], axis=-1)


def padded_keys(keys_loc, vals_loc, far_keys, far_vals):
    reach = WINDOW // 2
    pool_reach = POOL_WINDOW // 2 // STRIDE
    pad_near = ((0, 0), (reach, reach), (0, 0), (0, 0))
    pad_far = ((0, 0), (pool_reach, pool_reach), (0, 0), (0, 0))
    return (
        jnp.pad(keys_loc, pad_near),
        jnp.pad(vals_loc, pad_near),
        jnp.pad(far_keys, pad_far),
        jnp.pad(far_vals, pad_far),
    )


def block_inputs(start, queries, padded):
    near_k, near_v, far_k, far_v = padded
    near_len = block_rows + 2 * (WINDOW // 2)
    span = block_rows // STRIDE + 2 * (POOL_WINDOW // 2 // STRIDE)
    pool_start = start // STRIDE
    q_rows = queries[:, start : start + block_rows]
    keys_b = jnp.concatenate(
        [near_k[:, start : start + near_len], far_k[:, pool_start : pool_start + span]], axis=1
    )
    vals_b = jnp.concatenate(
        [near_v[:, start : start + near_len], far_v[:, pool_start : pool_start + span]], axis=1
    )
    return (q_rows, keys_b, vals_b)


def forward_block(q_rows, keys_b, vals_b, mask, live):
    scale = q_rows.shape[-1] ** (-0.5)
    scores = (
        jnp.einsum("sqhe,skhe->shqk", q_rows, keys_b, preferred_element_type=jnp.float32) * scale
    )
    scores = jnp.where(mask[:, None], scores, mask_fill)
    peak = jnp.max(scores, axis=-1, keepdims=True)
    expo = jnp.exp(scores - peak)
    total = jnp.sum(expo, axis=-1, keepdims=True)
    weights = (expo / total).astype(jnp.bfloat16)
    result = jnp.einsum("shqk,skhe->sqhe", weights, vals_b, preferred_element_type=jnp.float32)
    result = jnp.where(live[:, :, None, None], result, 0.0)
    return (result, peak + jnp.log(total))


def forward_skip(q_rows, keys_b, vals_b, mask, live):
    seqs, rows, heads, size = q_rows.shape
    return (
        jnp.zeros((seqs, rows, heads, size), jnp.float32),
        jnp.zeros((seqs, heads, rows, 1), jnp.float32),
    )


def backward_block(q_rows, keys_b, vals_b, mask, logsum, grad_rows):
    scale = q_rows.shape[-1] ** (-0.5)
    scores = (
        jnp.einsum("sqhe,skhe->shqk", q_rows, keys_b, preferred_element_type=jnp.float32) * scale
    )
    scores = jnp.where(mask[:, None], scores, mask_fill)
    probs = jnp.exp(scores - logsum)
    grad_probs = jnp.einsum(
        "sqhe,skhe->shqk", grad_rows, vals_b, preferred_element_type=jnp.float32
    )
    delta = jnp.sum(probs * grad_probs, axis=-1, keepdims=True)
    grad_scores = (probs * (grad_probs - delta)).astype(jnp.bfloat16)
    grad_q = (
        jnp.einsum("shqk,skhe->sqhe", grad_scores, keys_b, preferred_element_type=jnp.float32)
        * scale
    )
    grad_keys = (
        jnp.einsum("shqk,sqhe->skhe", grad_scores, q_rows, preferred_element_type=jnp.float32)
        * scale
    )
    grad_vals = jnp.einsum(
        "shqk,sqhe->skhe", probs.astype(jnp.bfloat16), grad_rows, preferred_element_type=jnp.float32
    )
    return (grad_q, grad_keys, grad_vals)


def backward_skip(q_rows, keys_b, vals_b, mask, logsum, grad_rows):
    return (
        jnp.zeros(q_rows.shape, jnp.float32),
        jnp.zeros(keys_b.shape, jnp.float32),
        jnp.zeros(vals_b.shape, jnp.float32),
    )


def attend_forward(queries, keys_loc, vals_loc, far_keys, far_vals, lengths):
    length = queries.shape[1]
    padded = padded_keys(keys_loc, vals_loc, far_keys, far_vals)
    longest = jnp.max(lengths)
    results, logsums = ([], [])
    for block in range(length // block_rows):
        start = block * block_rows
        q_rows, keys_b, vals_b = block_inputs(start, queries, padded)
        mask = block_mask(start, lengths)
        live = start + jnp.arange(block_rows, dtype=jnp.int32)[None, :] < lengths[:, None]
        result, logsum = lax.cond(
            start < longest, forward_block, forward_skip, q_rows, keys_b, vals_b, mask, live
        )
        results.append(result)
        logsums.append(logsum)
    return (jnp.concatenate(results, axis=1), logsums)


def attend_backward(
    queries, keys_loc, vals_loc, far_keys, far_vals, lengths, logsums, grad_context
):
    seqs, length, heads, size = queries.shape
    pooled_len = far_keys.shape[1]
    reach = WINDOW // 2
    pool_reach = POOL_WINDOW // 2 // STRIDE
    near_len = block_rows + 2 * reach
    span = block_rows // STRIDE + 2 * pool_reach
    padded = padded_keys(keys_loc, vals_loc, far_keys, far_vals)
    longest = jnp.max(lengths)
    grad_near_k = jnp.zeros((seqs, length + 2 * reach, heads, size), jnp.float32)
    grad_near_v = jnp.zeros((seqs, length + 2 * reach, heads, size), jnp.float32)
    grad_far_k = jnp.zeros((seqs, pooled_len + 2 * pool_reach, heads, size), jnp.float32)
    grad_far_v = jnp.zeros((seqs, pooled_len + 2 * pool_reach, heads, size), jnp.float32)
    grad_queries = []
    for block in range(length // block_rows):
        start = block * block_rows
        pool_start = start // STRIDE
        q_rows, keys_b, vals_b = block_inputs(start, queries, padded)
        mask = block_mask(start, lengths)
        grad_rows = grad_context[:, start : start + block_rows]
        grad_q, grad_keys, grad_vals = lax.cond(
            start < longest,
            backward_block,
            backward_skip,
            q_rows,
            keys_b,
            vals_b,
            mask,
            logsums[block],
            grad_rows,
        )
        grad_queries.append(grad_q)
        grad_near_k = grad_near_k.at[:, start : start + near_len].add(grad_keys[:, :near_len])
        grad_near_v = grad_near_v.at[:, start : start + near_len].add(grad_vals[:, :near_len])
        grad_far_k = grad_far_k.at[:, pool_start : pool_start + span].add(grad_keys[:, near_len:])
        grad_far_v = grad_far_v.at[:, pool_start : pool_start + span].add(grad_vals[:, near_len:])
    return (
        jnp.concatenate(grad_queries, axis=1),
        grad_near_k[:, reach : reach + length],
        grad_near_v[:, reach : reach + length],
        grad_far_k[:, pool_reach : pool_reach + pooled_len],
        grad_far_v[:, pool_reach : pool_reach + pooled_len],
    )


def row_sum(left, right, share):

    def term(start, count):
        return jnp.dot(left, right, preferred_element_type=jnp.float32)

    return lax.psum_scatter(
        term(jnp.int32(0), share * lax.axis_size("mp")), "mp", scatter_dimension=0, tiled=True
    )


def share_rows(values):
    return lax.all_gather(values, "mp", axis=0, tiled=True)


def share_back(values):
    return lax.all_gather(values, "mp", axis=0, tiled=True)


def back_sum(term, share):
    return lax.psum_scatter(
        term(jnp.int32(0), share * lax.axis_size("mp")), "mp", scatter_dimension=0, tiled=True
    )


def spread(values, width):
    whole = jnp.zeros(values.shape[:-1] + (width,), jnp.float32)
    start = lax.axis_index("mp") * values.shape[-1]
    return lax.dynamic_update_slice_in_dim(whole, values, start, values.ndim - 1)


def layer_forward(full_in, resid, lengths, params, share):
    (
        w_query,
        w_key,
        w_value,
        b_query,
        b_value,
        conv_key,
        conv_value,
        w_out,
        b_out,
        attn_gain,
        attn_shift,
        w_up,
        b_up,
        w_down,
        b_down,
        ffn_gain,
        ffn_shift,
    ) = params
    seqs = lengths.shape[0]
    total_rows = full_in.shape[0]
    length = total_rows // seqs
    chans = w_query.shape[1]
    heads = chans // HEAD_DIM
    pooled_len = length // STRIDE
    queries = (jnp.dot(full_in, w_query, preferred_element_type=jnp.float32) + b_query).astype(
        jnp.bfloat16
    )
    keys_loc = jnp.dot(full_in, w_key, preferred_element_type=jnp.float32).astype(jnp.bfloat16)
    vals_loc = (jnp.dot(full_in, w_value, preferred_element_type=jnp.float32) + b_value).astype(
        jnp.bfloat16
    )
    valid = (jnp.arange(length, dtype=jnp.int32)[None, :] < lengths[:, None]).astype(jnp.float32)[
        :, :, None
    ]
    far_keys = pool_rows(
        keys_loc.reshape(seqs, length, chans).astype(jnp.float32) * valid, conv_key
    ).astype(jnp.bfloat16)
    far_vals = pool_rows(
        vals_loc.reshape(seqs, length, chans).astype(jnp.float32) * valid, conv_value
    ).astype(jnp.bfloat16)
    context, logsums = attend_forward(
        queries.reshape(seqs, length, heads, HEAD_DIM),
        keys_loc.reshape(seqs, length, heads, HEAD_DIM),
        vals_loc.reshape(seqs, length, heads, HEAD_DIM),
        far_keys.reshape(seqs, pooled_len, heads, HEAD_DIM),
        far_vals.reshape(seqs, pooled_len, heads, HEAD_DIM),
        lengths,
    )
    context = context.reshape(total_rows, chans).astype(jnp.bfloat16)
    hidden_one = resid + (row_sum(context, w_out, share) + b_out)
    normed = norm_rows(hidden_one, attn_gain, attn_shift)
    full_normed = share_rows(normed.astype(jnp.bfloat16))
    upper = jnp.dot(full_normed, w_up, preferred_element_type=jnp.float32) + b_up
    active = gelu_exact(upper).astype(jnp.bfloat16)
    hidden_two = normed + (row_sum(active, w_down, share) + b_down)
    result = norm_rows(hidden_two, ffn_gain, ffn_shift)
    kept = (
        full_in,
        queries,
        keys_loc,
        vals_loc,
        far_keys,
        far_vals,
        logsums,
        context,
        hidden_one,
        full_normed,
        upper,
        active,
        hidden_two,
    )
    return (result, kept)


def layer_backward(grad_out, kept, params, lengths, share):
    (
        w_query,
        w_key,
        w_value,
        b_query,
        b_value,
        conv_key,
        conv_value,
        w_out,
        b_out,
        attn_gain,
        attn_shift,
        w_up,
        b_up,
        w_down,
        b_down,
        ffn_gain,
        ffn_shift,
    ) = params
    (
        full_in,
        queries,
        keys_loc,
        vals_loc,
        far_keys,
        far_vals,
        logsums,
        context,
        hidden_one,
        full_normed,
        saved_upper,
        active,
        hidden_two,
    ) = kept
    seqs = lengths.shape[0]
    total_rows = full_in.shape[0]
    length = total_rows // seqs
    chans = w_query.shape[1]
    heads = chans // HEAD_DIM
    pooled_len = length // STRIDE
    unused_two, pull_two = jax.vjp(norm_rows, hidden_two, ffn_gain, ffn_shift)
    grad_h2, grad_fgain, grad_fshift = pull_two(grad_out)
    grad_ffn = grad_h2.astype(jnp.bfloat16)
    grad_bdown = jnp.sum(grad_ffn.astype(jnp.float32), axis=0)
    full_gffn = share_back(grad_ffn)
    grad_wdown = jnp.einsum("tf,td->fd", active, full_gffn, preferred_element_type=jnp.float32)
    grad_active = jnp.einsum("td,fd->tf", full_gffn, w_down, preferred_element_type=jnp.float32)
    unused_gelu, pull_gelu = jax.vjp(gelu_exact, saved_upper)
    grad_upper = pull_gelu(grad_active)[0].astype(jnp.bfloat16)
    grad_bup = jnp.sum(grad_upper.astype(jnp.float32), axis=0)
    grad_wup = jnp.einsum("td,tf->df", full_normed, grad_upper, preferred_element_type=jnp.float32)

    def up_term(start, count):
        return jnp.einsum("tf,df->td", grad_upper, w_up, preferred_element_type=jnp.float32)

    grad_y1 = grad_h2 + back_sum(up_term, share)
    unused_one, pull_one = jax.vjp(norm_rows, hidden_one, attn_gain, attn_shift)
    grad_h1, grad_again, grad_ashift = pull_one(grad_y1)
    grad_attn = grad_h1.astype(jnp.bfloat16)
    grad_bout = jnp.sum(grad_attn.astype(jnp.float32), axis=0)
    full_gattn = share_back(grad_attn)
    grad_wout = jnp.einsum("tc,td->cd", context, full_gattn, preferred_element_type=jnp.float32)
    grad_context = jnp.einsum("td,cd->tc", full_gattn, w_out, preferred_element_type=jnp.float32)
    valid = (jnp.arange(length, dtype=jnp.int32)[None, :] < lengths[:, None]).astype(jnp.float32)[
        :, :, None
    ]
    grad_context = (grad_context.reshape(seqs, length, chans) * valid).astype(jnp.bfloat16)
    grad_q, grad_near_k, grad_near_v, grad_far_k, grad_far_v = attend_backward(
        queries.reshape(seqs, length, heads, HEAD_DIM),
        keys_loc.reshape(seqs, length, heads, HEAD_DIM),
        vals_loc.reshape(seqs, length, heads, HEAD_DIM),
        far_keys.reshape(seqs, pooled_len, heads, HEAD_DIM),
        far_vals.reshape(seqs, pooled_len, heads, HEAD_DIM),
        lengths,
        logsums,
        grad_context.reshape(seqs, length, heads, HEAD_DIM),
    )
    masked_keys = keys_loc.reshape(seqs, length, chans).astype(jnp.float32) * valid
    masked_vals = vals_loc.reshape(seqs, length, chans).astype(jnp.float32) * valid
    unused_pk, pull_key = jax.vjp(pool_rows, masked_keys, conv_key)
    grad_kpool, grad_ckey = pull_key(grad_far_k.reshape(seqs, pooled_len, chans))
    unused_pv, pull_val = jax.vjp(pool_rows, masked_vals, conv_value)
    grad_vpool, grad_cval = pull_val(grad_far_v.reshape(seqs, pooled_len, chans))
    grad_queries = grad_q.reshape(total_rows, chans).astype(jnp.bfloat16)
    grad_keys = (
        (grad_near_k.reshape(seqs, length, chans) + grad_kpool * valid)
        .reshape(total_rows, chans)
        .astype(jnp.bfloat16)
    )
    grad_vals = (
        (grad_near_v.reshape(seqs, length, chans) + grad_vpool * valid)
        .reshape(total_rows, chans)
        .astype(jnp.bfloat16)
    )
    grad_wquery = jnp.einsum("td,tc->dc", full_in, grad_queries, preferred_element_type=jnp.float32)
    grad_wkey = jnp.einsum("td,tc->dc", full_in, grad_keys, preferred_element_type=jnp.float32)
    grad_wvalue = jnp.einsum("td,tc->dc", full_in, grad_vals, preferred_element_type=jnp.float32)
    grad_bquery = jnp.sum(grad_queries.astype(jnp.float32), axis=0)
    grad_bvalue = jnp.sum(grad_vals.astype(jnp.float32), axis=0)

    def input_term(start, count):
        total = jnp.einsum("tc,dc->td", grad_queries, w_query, preferred_element_type=jnp.float32)
        total = total + jnp.einsum(
            "tc,dc->td", grad_keys, w_key, preferred_element_type=jnp.float32
        )
        return total + jnp.einsum(
            "tc,dc->td", grad_vals, w_value, preferred_element_type=jnp.float32
        )

    grad_input = grad_h1 + back_sum(input_term, share)
    matrices = (
        grad_wquery[None],
        grad_wkey[None],
        grad_wvalue[None],
        grad_wout[None],
        grad_wup[None],
        grad_wdown[None],
    )
    vectors = (
        spread(grad_bquery, D)[None],
        spread(grad_bvalue, D)[None],
        spread(grad_ckey, D)[None],
        spread(grad_cval, D)[None],
        grad_bout[None],
        grad_again[None],
        grad_ashift[None],
        spread(grad_bup, FF)[None],
        grad_bdown[None],
        grad_fgain[None],
        grad_fshift[None],
    )
    return (grad_input, matrices, vectors)


def on_device(
    tokens,
    lengths,
    w_query,
    w_key,
    w_value,
    b_query,
    b_value,
    conv_key,
    conv_value,
    w_out,
    b_out,
    attn_gain,
    attn_shift,
    w_up,
    b_up,
    w_down,
    b_down,
    ffn_gain,
    ffn_shift,
    cotangent,
):
    stacks = (
        w_query,
        w_key,
        w_value,
        b_query,
        b_value,
        conv_key,
        conv_value,
        w_out,
        b_out,
        attn_gain,
        attn_shift,
        w_up,
        b_up,
        w_down,
        b_down,
        ffn_gain,
        ffn_shift,
    )
    total_rows = tokens.shape[0]
    share = total_rows // lax.axis_size("mp")
    place = lax.axis_index("mp") * share
    resid = lax.dynamic_slice_in_dim(tokens, place, share, 0).astype(jnp.float32)
    layer = 0
    params = tuple((stack[layer] for stack in stacks))
    result, kept = layer_forward(tokens, resid, lengths, params, share)
    kept_all = [kept]
    activations = result.astype(jnp.bfloat16)
    grad_out = cotangent.astype(jnp.float32)
    matrix_list = [None] * LAYERS
    vector_list = [None] * LAYERS
    for layer in reversed(range(LAYERS)):
        params = tuple((stack[layer] for stack in stacks))
        grad_out, matrices, vectors = layer_backward(
            grad_out, kept_all[layer], params, lengths, share
        )
        matrix_list[layer] = matrices
        vector_list[layer] = vectors
    grad_wquery, grad_wkey, grad_wvalue, grad_wout, grad_wup, grad_wdown = tuple(
        (jnp.concatenate([entry[index] for entry in matrix_list], axis=0) for index in range(6))
    )
    (
        grad_bquery,
        grad_bvalue,
        grad_ckey,
        grad_cval,
        grad_bout,
        grad_again,
        grad_ashift,
        grad_bup,
        grad_bdown,
        grad_fgain,
        grad_fshift,
    ) = tuple(
        (jnp.concatenate([entry[index] for entry in vector_list], axis=0) for index in range(11))
    )
    grad_wquery, grad_wkey, grad_wvalue, grad_wout, grad_wup, grad_wdown = (
        lax.psum_scatter(grad_wquery, "dp", scatter_dimension=1, tiled=True),
        lax.psum_scatter(grad_wkey, "dp", scatter_dimension=1, tiled=True),
        lax.psum_scatter(grad_wvalue, "dp", scatter_dimension=1, tiled=True),
        lax.psum_scatter(grad_wout, "dp", scatter_dimension=2, tiled=True),
        lax.psum_scatter(grad_wup, "dp", scatter_dimension=1, tiled=True),
        lax.psum_scatter(grad_wdown, "dp", scatter_dimension=2, tiled=True),
    )
    (
        grad_bquery,
        grad_bvalue,
        grad_ckey,
        grad_cval,
        grad_bout,
        grad_again,
        grad_ashift,
        grad_bup,
        grad_bdown,
        grad_fgain,
        grad_fshift,
    ) = lax.psum(
        (
            grad_bquery,
            grad_bvalue,
            grad_ckey,
            grad_cval,
            grad_bout,
            grad_again,
            grad_ashift,
            grad_bup,
            grad_bdown,
            grad_fgain,
            grad_fshift,
        ),
        ("dp", "mp"),
    )
    return (
        activations,
        grad_out,
        grad_wquery,
        grad_wkey,
        grad_wvalue,
        grad_bquery,
        grad_bvalue,
        grad_ckey,
        grad_cval,
        grad_wout,
        grad_bout,
        grad_again,
        grad_ashift,
        grad_wup,
        grad_bup,
        grad_wdown,
        grad_bdown,
        grad_fgain,
        grad_fshift,
    )


BF = jnp.bfloat16
F32 = jnp.float32
MESH = pl.DeviceIdType.MESH
ROWS = 256
QUARTERS = 4
CHANS = D // QUARTERS
QHEADS = CHANS // HEAD_DIM
SEQ = QUARTERS * ROWS
REACH = WINDOW // 2
PREACH = POOL_WINDOW // 2 // STRIDE
OWNP = ROWS // STRIDE
KW = ROWS + 2 * REACH
KP = OWNP + 2 * PREACH
KEYS = KW + KP
QB = 128
NEAR = QB + 2 * REACH
FAR = QB // STRIDE + 2 * PREACH
COMP = 800
HALFC = COMP // 2
FRONT = 256
KVROWS = 1408
BASE = 288
PIECE = D // 8
BIG_NEG = -1e30
SCALE = HEAD_DIM ** -0.5
VROWS = 40
TILES = 2 * CHANS // 128


def nn(a, b):
    return jnp.dot(a, b, preferred_element_type=F32)


def nt(a, b):
    return lax.dot_general(a, b, (((1,), (1,)), ((), ())), preferred_element_type=F32)


def tn(a, b):
    return lax.dot_general(a, b, (((0,), (0,)), ((), ())), preferred_element_type=F32)


def rows_iota(rows, cols):
    return lax.broadcasted_iota(jnp.int32, (rows, cols), 0)


def cols_iota(rows, cols):
    return lax.broadcasted_iota(jnp.int32, (rows, cols), 1)


def mean_row(v):
    return jnp.mean(v, axis=-1, keepdims=True)


def sum_col(v):
    return jnp.sum(v, axis=0, keepdims=True)


def kernel(
    len_ref, tok, wattn, wup, wdown, vec, bvec, cot,
    act_out, gtok, gmats, gvec,
    W, VEC, kvf, KV, KVS, Q, CTX, P, maskn, maskf, n1, r1, y1, y1b, dg, av,
    yT, fT, gab, GKV, pt, GQ, VG,
    CR, S1, S2, ZR, HL, HR, HLL, SL, SR, GVR, GVZ,
    lsem, asend, arecv, vsend, vrecv, hsend, hrecv, rsend, rrecv, gsend, grecv,
):
    acc, n2, xT = gtok, y1, yT
    dp = lax.axis_index("dp")
    z = lax.axis_index("mp")
    c = lax.rem(dp, 2)
    x = lax.rem(lax.div(dp, 2), 2)
    y = lax.div(dp, 4)
    core = (dp + 1 - 2 * c, z)
    xdev = (dp + 2 - 4 * x, z)
    ydev = (dp + 4 - 8 * y, z)
    yx = 2 * y + x
    length = len_ref[0]

    def zdev(step):
        return (dp, lax.rem(z + step, QUARTERS))

    def rcopy(src, dst, ssem, rsem, dev):
        return pltpu.make_async_remote_copy(
            src_ref=src, dst_ref=dst, send_sem=ssem, recv_sem=rsem,
            device_id=dev, device_id_type=MESH,
        )

    own = [
        pltpu.make_async_copy(src, W.at[i, z], lsem.at[i])
        for i, src in enumerate((wattn, wup, wdown))
    ]
    for cp in own:
        cp.start()
    HL[...] = jnp.zeros_like(HL)
    HR[...] = jnp.zeros_like(HR)
    HLL[...] = jnp.zeros_like(HLL)
    barrier = pltpu.get_barrier_semaphore()
    for dev in (core, xdev, ydev, zdev(1), zdev(2), zdev(3)):
        pl.semaphore_signal(barrier, inc=1, device_id=dev, device_id_type=MESH)
    pl.semaphore_wait(barrier, 6)

    def block(j):
        return pl.ds(pl.multiple_of(j * PIECE, PIECE), PIECE)

    piece_me = c * 4 + yx
    piece_x = c * 4 + 2 * y + 1 - x
    piece_y = c * 4 + 2 * (1 - y) + x
    piece_d = c * 4 + 2 * (1 - y) + 1 - x
    LO, HI = pl.ds(0, D // 2), pl.ds(D // 2, D // 2)

    def wz(m, s):
        zz = lax.rem(z + s, QUARTERS)
        src = W.at[m, z, block(piece_me), :]
        return rcopy(src, src, asend.at[m, s - 1, 0], arecv.at[m, s - 1, 0], (dp, zz))

    def got(m, s):
        return lax.rem(z + QUARTERS - s, QUARTERS)

    def wz_in(m, s):
        dst = W.at[m, got(m, s), block(piece_me), :]
        return rcopy(dst, dst, asend.at[m, s - 1, 0], arecv.at[m, s - 1, 0], core)

    def plane(m, s, which, piece, cols, dev):
        ref = W.at[m, got(m, s), block(piece), cols]
        return rcopy(ref, ref, asend.at[m, s - 1, which], arecv.at[m, s - 1, which], dev)

    ALL = pl.ds(0, D)

    def first(m, s):
        wz_in(m, s).wait_recv()
        plane(m, s, 1, piece_me, ALL, xdev).start()
        plane(m, s, 2, piece_me, ALL, ydev).start()

    def second(m, s):
        plane(m, s, 1, piece_x, ALL, xdev).wait_recv()
        plane(m, s, 3, piece_x, LO, ydev).start()
        plane(m, s, 2, piece_y, ALL, ydev).wait_recv()
        plane(m, s, 4, piece_y, HI, xdev).start()

    def half(j):
        return pl.ds(pl.multiple_of(j * (D // 2), D // 2), D // 2)

    def cross(m, s, j):
        ref = W.at[m, got(m, s), half(j), :]
        return rcopy(ref, ref, asend.at[m, s - 1, 5], arecv.at[m, s - 1, 5], core)

    def third(m, s):
        plane(m, s, 3, piece_d, LO, ydev).wait_recv()
        plane(m, s, 4, piece_d, HI, xdev).wait_recv()
        cross(m, s, c).start()

    def fourth(m, s):
        cross(m, s, 1 - c).wait_recv()

    def gather_done(m, s):
        wz(m, s).wait_send()
        plane(m, s, 1, piece_me, ALL, xdev).wait_send()
        plane(m, s, 2, piece_me, ALL, ydev).wait_send()
        plane(m, s, 3, piece_x, LO, ydev).wait_send()
        plane(m, s, 4, piece_y, HI, xdev).wait_send()
        cross(m, s, c).wait_send()

    def vz(s):
        return rcopy(vec, VEC.at[z], vsend.at[s - 1], vrecv.at[s - 1], zdev(s))

    def vz_in(s):
        dst = VEC.at[got(0, s)]
        return rcopy(vec, dst, vsend.at[s - 1], vrecv.at[s - 1], core)

    for cp in own:
        cp.wait()
    for s in (1, 2, 3):
        vz(s).start()
    for m in (0, 1, 2):
        for s in (1, 2, 3):
            wz(m, s).start()
    VEC[z] = vec[...]
    for s in (1, 2, 3):
        vz_in(s).wait_recv()
    chunks = [(m, s) for m in (0, 1, 2) for s in (1, 2, 3)]
    for stage in (first, second, third, fourth):
        for m, s in chunks:
            stage(m, s)

    base = z * ROWS
    start = lax.select(z < 2, jnp.int32(0), jnp.int32(SEQ - COMP))
    place = pl.multiple_of(start - base + BASE + FRONT, 32)
    start = pl.multiple_of(start, 32)
    kvf[...] = jnp.zeros_like(kvf)
    for b in range(2):
        i = base + b * QB + cols_iota(1, QB)
        j = base - REACH + b * QB + rows_iota(NEAR, 1)
        ok = (jnp.abs(i - j) <= REACH) & (j >= 0) & (j < length)
        maskn[b] = jnp.where(ok, 0.0, BIG_NEG)
        j = (OWNP * z - PREACH + b * (QB // STRIDE) + rows_iota(FAR, 1)) * STRIDE
        ok = (jnp.abs(i - j) <= POOL_WINDOW // 2) & (j >= 0) & (j < length)
        maskf[b] = jnp.where(ok, 0.0, BIG_NEG)
    own_rows = pl.ds(pl.multiple_of(base, ROWS), ROWS)
    xb = tok[own_rows, :]
    acc[...] = jnp.zeros_like(acc)

    def taps(zq, t):
        return VEC[zq, 2 + t : 3 + t, 0 : 2 * CHANS]

    def strided(t):
        at = pl.ds(FRONT + BASE - POOL_WINDOW // 2 - 2 + t, KP, stride=STRIDE)
        return jnp.concatenate([kvf[i, at, :] for i in range(TILES)], axis=1)

    def tile(i):
        return slice(i * 128, (i + 1) * 128)

    def window(lo, rows):
        return jnp.concatenate([kvf[i, lo : lo + rows, :] for i in range(TILES)], axis=1)

    def attend(s, carry):
        zq = lax.rem(z + QUARTERS - s, QUARTERS)
        for blk in range(2):
            xr = tok[pl.ds(pl.multiple_of(start + blk * HALFC, 16), HALFC), :]
            kv = nn(xr, W[0, zq, :, 0 : 2 * CHANS]) + VEC[zq, 1:2, 0 : 2 * CHANS]
            pos = start + blk * HALFC + rows_iota(HALFC, 1)
            kvb = jnp.where(pos < length, kv.astype(BF).astype(F32), 0.0)
            for i in range(TILES):
                kvf[i, pl.ds(pl.multiple_of(place + blk * HALFC, 8), HALFC), :] = kvb[:, tile(i)]
        KVS[zq] = window(FRONT, COMP).astype(BF)
        KV[zq, 0:KW, :] = window(FRONT + BASE - REACH, KW).astype(BF)
        pooled = jnp.zeros((KP, 2 * CHANS), F32)
        for t in range(5):
            pooled = pooled + taps(zq, t) * strided(t)
        KV[zq, KW:KEYS, :] = pooled.astype(BF)
        qz = nn(xb, W[0, zq, :, 2 * CHANS : 3 * CHANS]) + VEC[zq, 1:2, 2 * CHANS : 3 * CHANS]
        Q[zq] = qz.astype(BF)
        for b in range(2):
            live = base + b * QB + cols_iota(1, QB) < length
            n0, f0 = b * QB, KW + b * (QB // STRIDE)
            for h in range(QHEADS):
                kl = slice(h * HEAD_DIM, (h + 1) * HEAD_DIM)
                vl = slice(CHANS + h * HEAD_DIM, CHANS + (h + 1) * HEAD_DIM)
                qh = Q[zq, b * QB : (b + 1) * QB, kl]
                sn = nt(KV[zq, n0 : n0 + NEAR, kl], qh) * SCALE + maskn[b]
                sf = nt(KV[zq, f0 : f0 + FAR, kl], qh) * SCALE + maskf[b]
                peak = jnp.maximum(
                    jnp.max(sn, axis=0, keepdims=True), jnp.max(sf, axis=0, keepdims=True)
                )
                en, ef = jnp.exp(sn - peak), jnp.exp(sf - peak)
                inv = 1.0 / (sum_col(en) + sum_col(ef))
                pn, pf = en * inv, ef * inv
                P[zq, h, b, 0:NEAR, :] = pn
                P[zq, h, b, NEAR : NEAR + FAR, :] = pf
                ct = tn(KV[zq, n0 : n0 + NEAR, vl], pn.astype(BF))
                ct = ct + tn(KV[zq, f0 : f0 + FAR, vl], pf.astype(BF))
                ct = jnp.where(live, ct, 0.0)
                CTX[zq, b * QB : (b + 1) * QB, kl] = ct.T.astype(BF)
        acc[...] += nt(CTX[zq], W[0, zq, :, 3 * CHANS : D])
        return carry

    lax.fori_loop(0, QUARTERS, attend, 0)

    hid = xb.astype(F32) + (acc[...] + bvec[0:1, :])
    cen = hid - mean_row(hid)
    r = lax.rsqrt(mean_row(cen * cen) + epsilon)
    n1[...] = cen * r
    r1[...] = r
    y1[...] = n1[...] * bvec[1:2, :] + bvec[2:3, :]
    y1b[...] = y1[...].astype(BF)
    acc[...] = jnp.zeros_like(acc)

    def feed(s, carry):
        zq = lax.rem(z + QUARTERS - s, QUARTERS)
        u = nn(y1b[...], W[1, zq]) + VEC[zq, 0:1, :]
        cdf = 0.5 * (1.0 + lax.erf(u * (0.5 ** 0.5)))
        dg[zq] = cdf + u * jnp.exp(-0.5 * u * u) * ((2.0 * 3.141592653589793) ** -0.5)
        av[zq] = (u * cdf).astype(BF)
        acc[...] += nn(av[zq], W[2, zq])
        return carry

    lax.fori_loop(0, QUARTERS, feed, 0)
    hid = y1[...] + (acc[...] + bvec[3:4, :])
    cen = hid - mean_row(hid)
    r = lax.rsqrt(mean_row(cen * cen) + epsilon)
    n2[...] = cen * r
    act_out[...] = (n2[...] * bvec[4:5, :] + bvec[5:6, :]).astype(BF)

    VG[...] = jnp.zeros_like(VG)
    GEN = 8 * QUARTERS

    def place_T(dst, v):
        for j in range(8):
            to = (j % 2) * 4 + j // 2
            dst[to * PIECE : (to + 1) * PIECE, :] = v[:, j * PIECE : (j + 1) * PIECE].T.astype(BF)

    g = cot[...].astype(F32)
    VG[GEN + 4 : GEN + 5, :] = sum_col(g * n2[...])
    VG[GEN + 5 : GEN + 6, :] = sum_col(g)
    e = g * bvec[4:5, :]
    gh2 = r * (e - mean_row(e) - n2[...] * mean_row(e * n2[...]))
    gf = gh2.astype(BF)
    gab[...] = gf
    gff = gf.astype(F32)
    VG[GEN + 3 : GEN + 4, :] = sum_col(gff)
    acc[...] = gh2
    place_T(fT, gff)
    place_T(yT, y1b[...].astype(F32))

    def feed_back(s, carry):
        zq = lax.rem(z + 1 + s, QUARTERS)
        gact = nt(gab[...], W[2, zq])
        gu = (gact * dg[zq]).astype(BF)
        vrow = pl.multiple_of(8 * zq, 8)
        VG[pl.ds(vrow, 1), :] = sum_col(gu.astype(F32))
        acc[...] += nt(gu, W[1, zq])
        W[1, zq] = nn(yT[...], gu).astype(BF)
        W[2, zq] = nn(fT[...], av[zq]).astype(BF)
        return carry

    for m, s in chunks:
        gather_done(m, s)
    for s in (1, 2, 3):
        vz(s).wait_send()
    lax.fori_loop(0, QUARTERS, feed_back, 0)

    gy = acc[...]
    VG[GEN + 1 : GEN + 2, :] = sum_col(gy * n1[...])
    VG[GEN + 2 : GEN + 3, :] = sum_col(gy)
    e = gy * bvec[1:2, :]
    gh1 = r1[...] * (e - mean_row(e) - n1[...] * mean_row(e * n1[...]))
    ga = gh1.astype(BF)
    gab[...] = ga
    gaf = ga.astype(F32)
    VG[GEN : GEN + 1, :] = sum_col(gaf)
    acc[...] = gh1
    place_T(fT, gaf)
    place_T(xT, xb.astype(F32))

    def hl(zq):
        return rcopy(SL.at[zq], HL.at[zq], hsend.at[0, zq], hrecv.at[0, zq], zdev(3))

    def hr(zq):
        return rcopy(SR.at[zq], HR.at[zq], hsend.at[1, zq], hrecv.at[1, zq], zdev(1))

    def hll(zq):
        return rcopy(
            SL.at[zq, REACH : REACH + 16, :], HLL.at[zq], hsend.at[2, zq], hrecv.at[2, zq], zdev(2)
        )

    def attend_back(s, carry):
        zq = lax.rem(z + 1 + s, QUARTERS)
        gc = nn(gab[...], W[0, zq, :, 3 * CHANS : D])
        alive = base + rows_iota(ROWS, 1) < length
        gcb = jnp.where(alive, gc, 0.0).astype(BF)
        GKV[zq] = jnp.zeros((KEYS, 2 * CHANS), F32)
        for b in range(2):
            n0, f0 = b * QB, KW + b * (QB // STRIDE)
            for h in range(QHEADS):
                kl = slice(h * HEAD_DIM, (h + 1) * HEAD_DIM)
                vl = slice(CHANS + h * HEAD_DIM, CHANS + (h + 1) * HEAD_DIM)
                gch = gcb[b * QB : (b + 1) * QB, kl]
                qh = Q[zq, b * QB : (b + 1) * QB, kl]
                pn = P[zq, h, b, 0:NEAR, :]
                pf = P[zq, h, b, NEAR : NEAR + FAR, :]
                gpn = nt(KV[zq, n0 : n0 + NEAR, vl], gch)
                gpf = nt(KV[zq, f0 : f0 + FAR, vl], gch)
                delta = sum_col(pn * gpn) + sum_col(pf * gpf)
                gsn = (pn * (gpn - delta)).astype(BF)
                gsf = (pf * (gpf - delta)).astype(BF)
                qt = tn(KV[zq, n0 : n0 + NEAR, kl], gsn) + tn(KV[zq, f0 : f0 + FAR, kl], gsf)
                GQ[zq, b * QB : (b + 1) * QB, 2 * CHANS + h * HEAD_DIM : 2 * CHANS + (h + 1) * HEAD_DIM] = (
                    (qt * SCALE).T.astype(BF)
                )
                GKV[zq, n0 : n0 + NEAR, kl] += nn(gsn, qh) * SCALE
                GKV[zq, f0 : f0 + FAR, kl] += nn(gsf, qh) * SCALE
                GKV[zq, n0 : n0 + NEAR, vl] += nn(pn.astype(BF), gch)
                GKV[zq, f0 : f0 + FAR, vl] += nn(pf.astype(BF), gch)
        vrow = pl.multiple_of(8 * zq, 8)
        for i in range(TILES):
            kvf[i, FRONT : FRONT + COMP, :] = KVS[zq, :, tile(i)].astype(F32)
        gp = GKV[zq, KW:KEYS, :]
        for t in range(5):
            VG[pl.ds(vrow + 2 + t, 1), 0 : 2 * CHANS] = sum_col(gp * strided(t))
        SL[zq, 0:REACH, :] = GKV[zq, 0:REACH, :].astype(BF)
        SL[zq, REACH : REACH + 80, :] = GKV[zq, KW : KW + 80, :].astype(BF)
        SR[zq, 0:REACH, :] = GKV[zq, KW - REACH : KW, :].astype(BF)
        SR[zq, REACH : REACH + OWNP, :] = GKV[zq, KEYS - OWNP : KEYS, :].astype(BF)
        pl.when(z > 0)(lambda: hl(zq).start())
        pl.when(z < QUARTERS - 1)(lambda: hr(zq).start())
        pl.when(z > 1)(lambda: hll(zq).start())
        return carry

    lax.fori_loop(0, QUARTERS, attend_back, 0)

    def project_back(s, carry):
        zq = lax.rem(z + 1 + s, QUARTERS)
        pl.when(z < QUARTERS - 1)(lambda: hl(zq).wait_recv())
        pl.when(z > 0)(lambda: hr(zq).wait_recv())
        pl.when(z < QUARTERS - 2)(lambda: hll(zq).wait_recv())
        near = GKV.at[zq]
        near[REACH : 2 * REACH, :] += HR[zq, 0:REACH, :].astype(F32)
        near[ROWS : ROWS + REACH, :] += HL[zq, 0:REACH, :].astype(F32)
        gp = GKV[zq, KW + OWNP : KW + 2 * OWNP, :] + HR[zq, REACH : REACH + OWNP, :].astype(F32)
        gp = gp + HL[zq, REACH : REACH + OWNP, :].astype(F32)
        nxt = GKV[zq, KW + 2 * OWNP : KW + 2 * OWNP + 1, :]
        nxt = nxt + HL[zq, REACH + OWNP : REACH + OWNP + 16, :].astype(F32)[0:1, :]
        nxt = nxt + HLL[zq].astype(F32)[0:1, :]
        gp1 = jnp.concatenate([gp[1:, :], nxt], axis=0)
        fills = (
            taps(zq, 2) * gp,
            taps(zq, 3) * gp,
            taps(zq, 4) * gp + taps(zq, 0) * gp1,
            taps(zq, 1) * gp1,
        )
        for k, fill in enumerate(fills):
            for i in range(TILES):
                pt[i, pl.ds(k, OWNP, stride=STRIDE), :] = fill[:, tile(i)]
        back = jnp.concatenate([pt[i] for i in range(TILES)], axis=1)
        alive = base + rows_iota(ROWS, 1) < length
        gkv = GKV[zq, REACH : REACH + ROWS, :] + jnp.where(alive, back, 0.0)
        GQ[zq, :, 0 : 2 * CHANS] = gkv.astype(BF)
        vrow = pl.multiple_of(8 * zq, 8)
        VG[pl.ds(vrow + 1, 1), 0 : 3 * CHANS] = sum_col(GQ[zq].astype(F32))
        acc[...] += nt(GQ[zq], W[0, zq, :, 0 : 3 * CHANS])
        W[0, zq, :, 0 : 3 * CHANS] = nn(xT[...], GQ[zq]).astype(BF)
        W[0, zq, :, 3 * CHANS : D] = nn(fT[...], CTX[zq]).astype(BF)
        return carry

    lax.fori_loop(0, QUARTERS, project_back, 0)
    for zq in range(QUARTERS):
        pl.when(z > 0)(lambda: hl(zq).wait_send())
        pl.when(z < QUARTERS - 1)(lambda: hr(zq).wait_send())
        pl.when(z > 1)(lambda: hll(zq).wait_send())

    pieces = [(m, t) for m in (1, 2, 0) for t in range(QUARTERS)]

    def zq_of(t):
        return lax.rem(z + 1 + t, QUARTERS)

    def r_core(m, t):
        src = W.at[m, zq_of(t), half(1 - c), :]
        return rcopy(src, CR.at[m, t], rsend.at[m, t, 0], rrecv.at[m, t, 0], core)

    def blk4(m, t, yy, xx, cols):
        return CR.at[m, t, block(2 * yy + xx), cols]

    def r_stage1(m, t, i):
        if i < 2:
            src = blk4(m, t, i, 1 - x, LO)
            dev = xdev
        else:
            src = blk4(m, t, 1 - y, i - 2, HI)
            dev = ydev
        return rcopy(src, S1.at[m, t, i], rsend.at[m, t, 1 + i], rrecv.at[m, t, 1 + i], dev)

    def r_stage2(m, t, i):
        if i == 0:
            src, dev = blk4(m, t, 1 - y, x, LO), ydev
        else:
            src, dev = blk4(m, t, y, 1 - x, HI), xdev
        return rcopy(src, S2.at[m, t, i], rsend.at[m, t, 5 + i], rrecv.at[m, t, 5 + i], dev)

    def r_z(m, t):
        src = CR.at[m, t, block(yx), :]
        return rcopy(src, ZR.at[m, t], rsend.at[m, t, 7], rrecv.at[m, t, 7], zdev(1 + t))

    def reduce1(m, t):
        r_core(m, t).wait_recv()
        mine = W[m, zq_of(t), half(c), :].astype(F32)
        CR[m, t] = (CR[m, t].astype(F32) + mine).astype(BF)
        for i in range(4):
            r_stage1(m, t, i).start()

    def reduce2(m, t):
        for i in range(4):
            r_stage1(m, t, i).wait_recv()
        for i in range(2):
            a = blk4(m, t, i, x, LO)
            a[...] = (a[...].astype(F32) + S1[m, t, i].astype(F32)).astype(BF)
            a = blk4(m, t, y, i, HI)
            a[...] = (a[...].astype(F32) + S1[m, t, 2 + i].astype(F32)).astype(BF)
        for i in range(2):
            r_stage2(m, t, i).start()

    def reduce3(m, t):
        for i in range(2):
            r_stage2(m, t, i).wait_recv()
        for i, cols in enumerate((LO, HI)):
            a = blk4(m, t, y, x, cols)
            a[...] = (a[...].astype(F32) + S2[m, t, i].astype(F32)).astype(BF)
        if t < QUARTERS - 1:
            r_z(m, t).start()

    for m, t in pieces:
        r_core(m, t).start()

    def g_step(i, dev):
        return rcopy(VG, GVR.at[i], gsend.at[i], grecv.at[i], dev)

    def g_z(s):
        return rcopy(VG, GVZ.at[z], gsend.at[2 + s], grecv.at[2 + s], zdev(s))

    def g_z_in(s):
        return rcopy(VG, GVZ.at[got(0, s)], gsend.at[2 + s], grecv.at[2 + s], core)

    for m, t in pieces:
        reduce1(m, t)
    for i, dev in enumerate((core, xdev, ydev)):
        g_step(i, dev).start()
        g_step(i, dev).wait()
        VG[...] = VG[...] + GVR[i]
    for s in (1, 2, 3):
        g_z(s).start()
    GVZ[z] = VG[...]
    for stage in (reduce2, reduce3):
        for m, t in pieces:
            stage(m, t)
    for s in (1, 2, 3):
        g_z_in(s).wait_recv()
    gvec[...] = GVZ[0] + GVZ[1] + GVZ[2] + GVZ[3]
    for m in range(3):
        total = CR[m, QUARTERS - 1, block(yx), :].astype(F32)
        for t in range(QUARTERS - 1):
            r_z(m, t).wait_recv()
            total = total + ZR[m, t].astype(F32)
        gmats[m] = total
    for s in (1, 2, 3):
        g_z(s).wait_send()
    for m, t in pieces:
        r_core(m, t).wait_send()
        for i in range(4):
            r_stage1(m, t, i).wait_send()
        for i in range(2):
            r_stage2(m, t, i).wait_send()
        if t < QUARTERS - 1:
            r_z(m, t).wait_send()


def fused_layer(
    tokens, lengths, w_query, w_key, w_value, b_query, b_value, conv_key, conv_value, w_out,
    b_out, attn_gain, attn_shift, w_up, b_up, w_down, b_down, ffn_gain, ffn_shift, cotangent,
):
    wattn = jnp.concatenate([w_key[0], w_value[0], w_query[0], w_out[0].T], axis=1)
    zero = jnp.zeros((1, CHANS), F32)
    vec = jnp.concatenate(
        [
            b_up,
            jnp.concatenate([zero, b_value, b_query, zero], axis=1),
            jnp.pad(jnp.concatenate([conv_key[0], conv_value[0]], axis=1), ((0, 9), (0, D - 2 * CHANS))),
        ],
        axis=0,
    )
    bvec = jnp.concatenate(
        [b_out, attn_gain, attn_shift, b_down, ffn_gain, ffn_shift, jnp.zeros((2, D), F32)], axis=0
    )
    Q4 = QUARTERS
    vm = pltpu.VMEM
    scratch = [
        vm((3, Q4, D, D), BF),
        vm((Q4, 16, D), F32),
        vm((TILES, KVROWS, 128), F32),
        vm((Q4, KEYS, 2 * CHANS), BF),
        vm((Q4, COMP, 2 * CHANS), BF),
        vm((Q4, ROWS, CHANS), BF),
        vm((Q4, ROWS, CHANS), BF),
        vm((Q4, QHEADS, 2, NEAR + FAR, QB), F32),
        vm((2, NEAR, QB), F32),
        vm((2, FAR, QB), F32),
        vm((ROWS, D), F32),
        vm((ROWS, 1), F32),
        vm((ROWS, D), F32),
        vm((ROWS, D), BF),
        vm((Q4, ROWS, D), F32),
        vm((Q4, ROWS, D), BF),
        vm((D, ROWS), BF),
        vm((D, ROWS), BF),
        vm((ROWS, D), BF),
        vm((Q4, KEYS, 2 * CHANS), F32),
        vm((TILES, ROWS, 128), F32),
        vm((Q4, ROWS, 3 * CHANS), BF),
        vm((VROWS, D), F32),
        vm((3, Q4, D // 2, D), BF),
        vm((3, Q4, 4, PIECE, D // 2), BF),
        vm((3, Q4, 2, PIECE, D // 2), BF),
        vm((3, Q4 - 1, PIECE, D), BF),
        vm((Q4, REACH + 80, 2 * CHANS), BF),
        vm((Q4, REACH + OWNP, 2 * CHANS), BF),
        vm((Q4, 16, 2 * CHANS), BF),
        vm((Q4, REACH + 80, 2 * CHANS), BF),
        vm((Q4, REACH + OWNP, 2 * CHANS), BF),
        vm((3, VROWS, D), F32),
        vm((Q4, VROWS, D), F32),
        pltpu.SemaphoreType.DMA((3,)),
        pltpu.SemaphoreType.DMA((3, 3, 6)),
        pltpu.SemaphoreType.DMA((3, 3, 6)),
        pltpu.SemaphoreType.DMA((3,)),
        pltpu.SemaphoreType.DMA((3,)),
        pltpu.SemaphoreType.DMA((3, Q4)),
        pltpu.SemaphoreType.DMA((3, Q4)),
        pltpu.SemaphoreType.DMA((3, Q4, 8)),
        pltpu.SemaphoreType.DMA((3, Q4, 8)),
        pltpu.SemaphoreType.DMA((6,)),
        pltpu.SemaphoreType.DMA((6,)),
    ]
    vspec = pl.BlockSpec(memory_space=pltpu.VMEM)
    hspec = pl.BlockSpec(memory_space=pl.ANY)
    act, gtok, gm, gv = pl.pallas_call(
        kernel,
        out_shape=(
            jax.ShapeDtypeStruct((ROWS, D), BF),
            jax.ShapeDtypeStruct((ROWS, D), F32),
            jax.ShapeDtypeStruct((3, PIECE, D), F32),
            jax.ShapeDtypeStruct((VROWS, D), F32),
        ),
        in_specs=[pl.BlockSpec(memory_space=pltpu.SMEM), vspec, hspec, hspec, hspec, vspec, vspec, vspec],
        out_specs=(vspec, vspec, vspec, vspec),
        scratch_shapes=scratch,
        compiler_params=pltpu.CompilerParams(
            collective_id=0, has_side_effects=True, vmem_limit_bytes=67043328
        ),
        name="layer",
    )(lengths, tokens, wattn, w_up[0], w_down[0], vec, bvec, cotangent)
    per = gv[: 8 * Q4].reshape(Q4, 8, D)

    def channels(lo, hi, r0, r1):
        return per[:, r0:r1, lo:hi].transpose(1, 0, 2).reshape(r1 - r0, D)[None]

    g8 = gv[8 * Q4 :]
    return (
        act,
        gtok,
        gm[0:1, :, 2 * CHANS : 3 * CHANS],
        gm[0:1, :, 0:CHANS],
        gm[0:1, :, CHANS : 2 * CHANS],
        channels(2 * CHANS, 3 * CHANS, 1, 2)[0],
        channels(CHANS, 2 * CHANS, 1, 2)[0],
        channels(0, CHANS, 2, 7),
        channels(CHANS, 2 * CHANS, 2, 7),
        gm[0, :, 3 * CHANS :].T[None],
        g8[0:1],
        g8[1:2],
        g8[2:3],
        gm[1:2],
        per[:, 0, :].reshape(1, FF),
        gm[2].T[None],
        g8[3:4],
        g8[4:5],
        g8[5:6],
    )


def solution(mesh):
    small = mesh.shape["dp"] == 8 and mesh.shape["mp"] == QUARTERS
    return jax.shard_map(
        fused_layer if small else on_device,
        mesh=mesh,
        in_specs=(
            P("dp", None),
            P("dp"),
            P(None, None, "mp"),
            P(None, None, "mp"),
            P(None, None, "mp"),
            P(None, "mp"),
            P(None, "mp"),
            P(None, None, "mp"),
            P(None, None, "mp"),
            P(None, "mp", None),
            P(),
            P(),
            P(),
            P(None, None, "mp"),
            P(None, "mp"),
            P(None, "mp", None),
            P(),
            P(),
            P(),
            P(("dp", "mp"), None),
        ),
        out_specs=(
            P(("dp", "mp"), None),
            P(("dp", "mp"), None),
            P(None, "dp", "mp"),
            P(None, "dp", "mp"),
            P(None, "dp", "mp"),
            P(),
            P(),
            P(),
            P(),
            P(None, "mp", "dp"),
            P(),
            P(),
            P(),
            P(None, "dp", "mp"),
            P(),
            P(None, "mp", "dp"),
            P(),
            P(),
            P(),
        ),
        check_vma=False,
    )
```

```python
import jax
import jax.numpy as jnp
from jax import lax
from jax.experimental import pallas as pl
from jax.experimental.pallas import tpu as pltpu
from jax.sharding import PartitionSpec as P

D = 768
HEAD_DIM = 64
FF = 3072
WINDOW = 128
POOL_WINDOW = 512
STRIDE = 4
LAYERS = 1


block_rows = 512
mask_fill = -1000000000.0
epsilon = 1e-05


def norm_rows(hidden, gain, shift):
    center = hidden - jnp.mean(hidden, axis=-1, keepdims=True)
    spread = jnp.mean(center * center, axis=-1, keepdims=True)
    return center * lax.rsqrt(spread + epsilon) * gain + shift


def gelu_exact(values):
    return jax.nn.gelu(values, approximate=False)


def pool_rows(values, kernel):
    seqs, length, chans = values.shape
    width = kernel.shape[0]
    half = width // 2
    pooled_len = length // STRIDE
    padded = jnp.pad(values, ((0, 0), (half, width), (0, 0)))
    total = jnp.zeros((seqs, pooled_len, chans), jnp.float32)
    for offset in range(width):
        total = total + kernel[offset] * padded[:, offset : offset + STRIDE * pooled_len : STRIDE]
    return total


def block_mask(start, lengths):
    reach = WINDOW // 2
    pool_reach = POOL_WINDOW // 2 // STRIDE
    span = block_rows // STRIDE + 2 * pool_reach
    rows = start + jnp.arange(block_rows, dtype=jnp.int32)
    near_pos = start - reach + jnp.arange(block_rows + 2 * reach, dtype=jnp.int32)
    far_pos = (start // STRIDE - pool_reach + jnp.arange(span, dtype=jnp.int32)) * STRIDE
    limit = lengths[:, None, None]
    near_ok = (
        (jnp.abs(rows[:, None] - near_pos[None, :]) <= reach)[None]
        & (near_pos >= 0)[None, None]
        & (near_pos[None, None] < limit)
    )
    far_ok = (
        (jnp.abs(rows[:, None] - far_pos[None, :]) <= POOL_WINDOW // 2)[None]
        & (far_pos >= 0)[None, None]
        & (far_pos[None, None] < limit)
    )
    return jnp.concatenate([near_ok, far_ok], axis=-1)


def padded_keys(keys_loc, vals_loc, far_keys, far_vals):
    reach = WINDOW // 2
    pool_reach = POOL_WINDOW // 2 // STRIDE
    pad_near = ((0, 0), (reach, reach), (0, 0), (0, 0))
    pad_far = ((0, 0), (pool_reach, pool_reach), (0, 0), (0, 0))
    return (
        jnp.pad(keys_loc, pad_near),
        jnp.pad(vals_loc, pad_near),
        jnp.pad(far_keys, pad_far),
        jnp.pad(far_vals, pad_far),
    )


def block_inputs(start, queries, padded):
    near_k, near_v, far_k, far_v = padded
    near_len = block_rows + 2 * (WINDOW // 2)
    span = block_rows // STRIDE + 2 * (POOL_WINDOW // 2 // STRIDE)
    pool_start = start // STRIDE
    q_rows = queries[:, start : start + block_rows]
    keys_b = jnp.concatenate(
        [near_k[:, start : start + near_len], far_k[:, pool_start : pool_start + span]], axis=1
    )
    vals_b = jnp.concatenate(
        [near_v[:, start : start + near_len], far_v[:, pool_start : pool_start + span]], axis=1
    )
    return (q_rows, keys_b, vals_b)


def forward_block(q_rows, keys_b, vals_b, mask, live):
    scale = q_rows.shape[-1] ** (-0.5)
    scores = (
        jnp.einsum("sqhe,skhe->shqk", q_rows, keys_b, preferred_element_type=jnp.float32) * scale
    )
    scores = jnp.where(mask[:, None], scores, mask_fill)
    peak = jnp.max(scores, axis=-1, keepdims=True)
    expo = jnp.exp(scores - peak)
    total = jnp.sum(expo, axis=-1, keepdims=True)
    weights = (expo / total).astype(jnp.bfloat16)
    result = jnp.einsum("shqk,skhe->sqhe", weights, vals_b, preferred_element_type=jnp.float32)
    result = jnp.where(live[:, :, None, None], result, 0.0)
    return (result, peak + jnp.log(total))


def forward_skip(q_rows, keys_b, vals_b, mask, live):
    seqs, rows, heads, size = q_rows.shape
    return (
        jnp.zeros((seqs, rows, heads, size), jnp.float32),
        jnp.zeros((seqs, heads, rows, 1), jnp.float32),
    )


def backward_block(q_rows, keys_b, vals_b, mask, logsum, grad_rows):
    scale = q_rows.shape[-1] ** (-0.5)
    scores = (
        jnp.einsum("sqhe,skhe->shqk", q_rows, keys_b, preferred_element_type=jnp.float32) * scale
    )
    scores = jnp.where(mask[:, None], scores, mask_fill)
    probs = jnp.exp(scores - logsum)
    grad_probs = jnp.einsum(
        "sqhe,skhe->shqk", grad_rows, vals_b, preferred_element_type=jnp.float32
    )
    delta = jnp.sum(probs * grad_probs, axis=-1, keepdims=True)
    grad_scores = (probs * (grad_probs - delta)).astype(jnp.bfloat16)
    grad_q = (
        jnp.einsum("shqk,skhe->sqhe", grad_scores, keys_b, preferred_element_type=jnp.float32)
        * scale
    )
    grad_keys = (
        jnp.einsum("shqk,sqhe->skhe", grad_scores, q_rows, preferred_element_type=jnp.float32)
        * scale
    )
    grad_vals = jnp.einsum(
        "shqk,sqhe->skhe", probs.astype(jnp.bfloat16), grad_rows, preferred_element_type=jnp.float32
    )
    return (grad_q, grad_keys, grad_vals)


def backward_skip(q_rows, keys_b, vals_b, mask, logsum, grad_rows):
    return (
        jnp.zeros(q_rows.shape, jnp.float32),
        jnp.zeros(keys_b.shape, jnp.float32),
        jnp.zeros(vals_b.shape, jnp.float32),
    )


def attend_forward(queries, keys_loc, vals_loc, far_keys, far_vals, lengths):
    length = queries.shape[1]
    padded = padded_keys(keys_loc, vals_loc, far_keys, far_vals)
    longest = jnp.max(lengths)
    results, logsums = ([], [])
    for block in range(length // block_rows):
        start = block * block_rows
        q_rows, keys_b, vals_b = block_inputs(start, queries, padded)
        mask = block_mask(start, lengths)
        live = start + jnp.arange(block_rows, dtype=jnp.int32)[None, :] < lengths[:, None]
        result, logsum = lax.cond(
            start < longest, forward_block, forward_skip, q_rows, keys_b, vals_b, mask, live
        )
        results.append(result)
        logsums.append(logsum)
    return (jnp.concatenate(results, axis=1), logsums)


def attend_backward(
    queries, keys_loc, vals_loc, far_keys, far_vals, lengths, logsums, grad_context
):
    seqs, length, heads, size = queries.shape
    pooled_len = far_keys.shape[1]
    reach = WINDOW // 2
    pool_reach = POOL_WINDOW // 2 // STRIDE
    near_len = block_rows + 2 * reach
    span = block_rows // STRIDE + 2 * pool_reach
    padded = padded_keys(keys_loc, vals_loc, far_keys, far_vals)
    longest = jnp.max(lengths)
    grad_near_k = jnp.zeros((seqs, length + 2 * reach, heads, size), jnp.float32)
    grad_near_v = jnp.zeros((seqs, length + 2 * reach, heads, size), jnp.float32)
    grad_far_k = jnp.zeros((seqs, pooled_len + 2 * pool_reach, heads, size), jnp.float32)
    grad_far_v = jnp.zeros((seqs, pooled_len + 2 * pool_reach, heads, size), jnp.float32)
    grad_queries = []
    for block in range(length // block_rows):
        start = block * block_rows
        pool_start = start // STRIDE
        q_rows, keys_b, vals_b = block_inputs(start, queries, padded)
        mask = block_mask(start, lengths)
        grad_rows = grad_context[:, start : start + block_rows]
        grad_q, grad_keys, grad_vals = lax.cond(
            start < longest,
            backward_block,
            backward_skip,
            q_rows,
            keys_b,
            vals_b,
            mask,
            logsums[block],
            grad_rows,
        )
        grad_queries.append(grad_q)
        grad_near_k = grad_near_k.at[:, start : start + near_len].add(grad_keys[:, :near_len])
        grad_near_v = grad_near_v.at[:, start : start + near_len].add(grad_vals[:, :near_len])
        grad_far_k = grad_far_k.at[:, pool_start : pool_start + span].add(grad_keys[:, near_len:])
        grad_far_v = grad_far_v.at[:, pool_start : pool_start + span].add(grad_vals[:, near_len:])
    return (
        jnp.concatenate(grad_queries, axis=1),
        grad_near_k[:, reach : reach + length],
        grad_near_v[:, reach : reach + length],
        grad_far_k[:, pool_reach : pool_reach + pooled_len],
        grad_far_v[:, pool_reach : pool_reach + pooled_len],
    )


def row_sum(left, right, share):

    def term(start, count):
        return jnp.dot(left, right, preferred_element_type=jnp.float32)

    return lax.psum_scatter(
        term(jnp.int32(0), share * lax.axis_size("mp")), "mp", scatter_dimension=0, tiled=True
    )


def share_rows(values):
    return lax.all_gather(values, "mp", axis=0, tiled=True)


def share_back(values):
    return lax.all_gather(values, "mp", axis=0, tiled=True)


def back_sum(term, share):
    return lax.psum_scatter(
        term(jnp.int32(0), share * lax.axis_size("mp")), "mp", scatter_dimension=0, tiled=True
    )


def spread(values, width):
    whole = jnp.zeros(values.shape[:-1] + (width,), jnp.float32)
    start = lax.axis_index("mp") * values.shape[-1]
    return lax.dynamic_update_slice_in_dim(whole, values, start, values.ndim - 1)


def layer_forward(full_in, resid, lengths, params, share):
    (
        w_query,
        w_key,
        w_value,
        b_query,
        b_value,
        conv_key,
        conv_value,
        w_out,
        b_out,
        attn_gain,
        attn_shift,
        w_up,
        b_up,
        w_down,
        b_down,
        ffn_gain,
        ffn_shift,
    ) = params
    seqs = lengths.shape[0]
    total_rows = full_in.shape[0]
    length = total_rows // seqs
    chans = w_query.shape[1]
    heads = chans // HEAD_DIM
    pooled_len = length // STRIDE
    queries = (jnp.dot(full_in, w_query, preferred_element_type=jnp.float32) + b_query).astype(
        jnp.bfloat16
    )
    keys_loc = jnp.dot(full_in, w_key, preferred_element_type=jnp.float32).astype(jnp.bfloat16)
    vals_loc = (jnp.dot(full_in, w_value, preferred_element_type=jnp.float32) + b_value).astype(
        jnp.bfloat16
    )
    valid = (jnp.arange(length, dtype=jnp.int32)[None, :] < lengths[:, None]).astype(jnp.float32)[
        :, :, None
    ]
    far_keys = pool_rows(
        keys_loc.reshape(seqs, length, chans).astype(jnp.float32) * valid, conv_key
    ).astype(jnp.bfloat16)
    far_vals = pool_rows(
        vals_loc.reshape(seqs, length, chans).astype(jnp.float32) * valid, conv_value
    ).astype(jnp.bfloat16)
    context, logsums = attend_forward(
        queries.reshape(seqs, length, heads, HEAD_DIM),
        keys_loc.reshape(seqs, length, heads, HEAD_DIM),
        vals_loc.reshape(seqs, length, heads, HEAD_DIM),
        far_keys.reshape(seqs, pooled_len, heads, HEAD_DIM),
        far_vals.reshape(seqs, pooled_len, heads, HEAD_DIM),
        lengths,
    )
    context = context.reshape(total_rows, chans).astype(jnp.bfloat16)
    hidden_one = resid + (row_sum(context, w_out, share) + b_out)
    normed = norm_rows(hidden_one, attn_gain, attn_shift)
    full_normed = share_rows(normed.astype(jnp.bfloat16))
    upper = jnp.dot(full_normed, w_up, preferred_element_type=jnp.float32) + b_up
    active = gelu_exact(upper).astype(jnp.bfloat16)
    hidden_two = normed + (row_sum(active, w_down, share) + b_down)
    result = norm_rows(hidden_two, ffn_gain, ffn_shift)
    kept = (
        full_in,
        queries,
        keys_loc,
        vals_loc,
        far_keys,
        far_vals,
        logsums,
        context,
        hidden_one,
        full_normed,
        upper,
        active,
        hidden_two,
    )
    return (result, kept)


def layer_backward(grad_out, kept, params, lengths, share):
    (
        w_query,
        w_key,
        w_value,
        b_query,
        b_value,
        conv_key,
        conv_value,
        w_out,
        b_out,
        attn_gain,
        attn_shift,
        w_up,
        b_up,
        w_down,
        b_down,
        ffn_gain,
        ffn_shift,
    ) = params
    (
        full_in,
        queries,
        keys_loc,
        vals_loc,
        far_keys,
        far_vals,
        logsums,
        context,
        hidden_one,
        full_normed,
        saved_upper,
        active,
        hidden_two,
    ) = kept
    seqs = lengths.shape[0]
    total_rows = full_in.shape[0]
    length = total_rows // seqs
    chans = w_query.shape[1]
    heads = chans // HEAD_DIM
    pooled_len = length // STRIDE
    unused_two, pull_two = jax.vjp(norm_rows, hidden_two, ffn_gain, ffn_shift)
    grad_h2, grad_fgain, grad_fshift = pull_two(grad_out)
    grad_ffn = grad_h2.astype(jnp.bfloat16)
    grad_bdown = jnp.sum(grad_ffn.astype(jnp.float32), axis=0)
    full_gffn = share_back(grad_ffn)
    grad_wdown = jnp.einsum("tf,td->fd", active, full_gffn, preferred_element_type=jnp.float32)
    grad_active = jnp.einsum("td,fd->tf", full_gffn, w_down, preferred_element_type=jnp.float32)
    unused_gelu, pull_gelu = jax.vjp(gelu_exact, saved_upper)
    grad_upper = pull_gelu(grad_active)[0].astype(jnp.bfloat16)
    grad_bup = jnp.sum(grad_upper.astype(jnp.float32), axis=0)
    grad_wup = jnp.einsum("td,tf->df", full_normed, grad_upper, preferred_element_type=jnp.float32)

    def up_term(start, count):
        return jnp.einsum("tf,df->td", grad_upper, w_up, preferred_element_type=jnp.float32)

    grad_y1 = grad_h2 + back_sum(up_term, share)
    unused_one, pull_one = jax.vjp(norm_rows, hidden_one, attn_gain, attn_shift)
    grad_h1, grad_again, grad_ashift = pull_one(grad_y1)
    grad_attn = grad_h1.astype(jnp.bfloat16)
    grad_bout = jnp.sum(grad_attn.astype(jnp.float32), axis=0)
    full_gattn = share_back(grad_attn)
    grad_wout = jnp.einsum("tc,td->cd", context, full_gattn, preferred_element_type=jnp.float32)
    grad_context = jnp.einsum("td,cd->tc", full_gattn, w_out, preferred_element_type=jnp.float32)
    valid = (jnp.arange(length, dtype=jnp.int32)[None, :] < lengths[:, None]).astype(jnp.float32)[
        :, :, None
    ]
    grad_context = (grad_context.reshape(seqs, length, chans) * valid).astype(jnp.bfloat16)
    grad_q, grad_near_k, grad_near_v, grad_far_k, grad_far_v = attend_backward(
        queries.reshape(seqs, length, heads, HEAD_DIM),
        keys_loc.reshape(seqs, length, heads, HEAD_DIM),
        vals_loc.reshape(seqs, length, heads, HEAD_DIM),
        far_keys.reshape(seqs, pooled_len, heads, HEAD_DIM),
        far_vals.reshape(seqs, pooled_len, heads, HEAD_DIM),
        lengths,
        logsums,
        grad_context.reshape(seqs, length, heads, HEAD_DIM),
    )
    masked_keys = keys_loc.reshape(seqs, length, chans).astype(jnp.float32) * valid
    masked_vals = vals_loc.reshape(seqs, length, chans).astype(jnp.float32) * valid
    unused_pk, pull_key = jax.vjp(pool_rows, masked_keys, conv_key)
    grad_kpool, grad_ckey = pull_key(grad_far_k.reshape(seqs, pooled_len, chans))
    unused_pv, pull_val = jax.vjp(pool_rows, masked_vals, conv_value)
    grad_vpool, grad_cval = pull_val(grad_far_v.reshape(seqs, pooled_len, chans))
    grad_queries = grad_q.reshape(total_rows, chans).astype(jnp.bfloat16)
    grad_keys = (
        (grad_near_k.reshape(seqs, length, chans) + grad_kpool * valid)
        .reshape(total_rows, chans)
        .astype(jnp.bfloat16)
    )
    grad_vals = (
        (grad_near_v.reshape(seqs, length, chans) + grad_vpool * valid)
        .reshape(total_rows, chans)
        .astype(jnp.bfloat16)
    )
    grad_wquery = jnp.einsum("td,tc->dc", full_in, grad_queries, preferred_element_type=jnp.float32)
    grad_wkey = jnp.einsum("td,tc->dc", full_in, grad_keys, preferred_element_type=jnp.float32)
    grad_wvalue = jnp.einsum("td,tc->dc", full_in, grad_vals, preferred_element_type=jnp.float32)
    grad_bquery = jnp.sum(grad_queries.astype(jnp.float32), axis=0)
    grad_bvalue = jnp.sum(grad_vals.astype(jnp.float32), axis=0)

    def input_term(start, count):
        total = jnp.einsum("tc,dc->td", grad_queries, w_query, preferred_element_type=jnp.float32)
        total = total + jnp.einsum(
            "tc,dc->td", grad_keys, w_key, preferred_element_type=jnp.float32
        )
        return total + jnp.einsum(
            "tc,dc->td", grad_vals, w_value, preferred_element_type=jnp.float32
        )

    grad_input = grad_h1 + back_sum(input_term, share)
    matrices = (
        grad_wquery[None],
        grad_wkey[None],
        grad_wvalue[None],
        grad_wout[None],
        grad_wup[None],
        grad_wdown[None],
    )
    vectors = (
        spread(grad_bquery, D)[None],
        spread(grad_bvalue, D)[None],
        spread(grad_ckey, D)[None],
        spread(grad_cval, D)[None],
        grad_bout[None],
        grad_again[None],
        grad_ashift[None],
        spread(grad_bup, FF)[None],
        grad_bdown[None],
        grad_fgain[None],
        grad_fshift[None],
    )
    return (grad_input, matrices, vectors)


def on_device(
    tokens,
    lengths,
    w_query,
    w_key,
    w_value,
    b_query,
    b_value,
    conv_key,
    conv_value,
    w_out,
    b_out,
    attn_gain,
    attn_shift,
    w_up,
    b_up,
    w_down,
    b_down,
    ffn_gain,
    ffn_shift,
    cotangent,
):
    stacks = (
        w_query,
        w_key,
        w_value,
        b_query,
        b_value,
        conv_key,
        conv_value,
        w_out,
        b_out,
        attn_gain,
        attn_shift,
        w_up,
        b_up,
        w_down,
        b_down,
        ffn_gain,
        ffn_shift,
    )
    total_rows = tokens.shape[0]
    share = total_rows // lax.axis_size("mp")
    place = lax.axis_index("mp") * share
    resid = lax.dynamic_slice_in_dim(tokens, place, share, 0).astype(jnp.float32)
    layer = 0
    params = tuple((stack[layer] for stack in stacks))
    result, kept = layer_forward(tokens, resid, lengths, params, share)
    kept_all = [kept]
    activations = result.astype(jnp.bfloat16)
    grad_out = cotangent.astype(jnp.float32)
    matrix_list = [None] * LAYERS
    vector_list = [None] * LAYERS
    for layer in reversed(range(LAYERS)):
        params = tuple((stack[layer] for stack in stacks))
        grad_out, matrices, vectors = layer_backward(
            grad_out, kept_all[layer], params, lengths, share
        )
        matrix_list[layer] = matrices
        vector_list[layer] = vectors
    grad_wquery, grad_wkey, grad_wvalue, grad_wout, grad_wup, grad_wdown = tuple(
        (jnp.concatenate([entry[index] for entry in matrix_list], axis=0) for index in range(6))
    )
    (
        grad_bquery,
        grad_bvalue,
        grad_ckey,
        grad_cval,
        grad_bout,
        grad_again,
        grad_ashift,
        grad_bup,
        grad_bdown,
        grad_fgain,
        grad_fshift,
    ) = tuple(
        (jnp.concatenate([entry[index] for entry in vector_list], axis=0) for index in range(11))
    )
    grad_wquery, grad_wkey, grad_wvalue, grad_wout, grad_wup, grad_wdown = (
        lax.psum_scatter(grad_wquery, "dp", scatter_dimension=1, tiled=True),
        lax.psum_scatter(grad_wkey, "dp", scatter_dimension=1, tiled=True),
        lax.psum_scatter(grad_wvalue, "dp", scatter_dimension=1, tiled=True),
        lax.psum_scatter(grad_wout, "dp", scatter_dimension=2, tiled=True),
        lax.psum_scatter(grad_wup, "dp", scatter_dimension=1, tiled=True),
        lax.psum_scatter(grad_wdown, "dp", scatter_dimension=2, tiled=True),
    )
    (
        grad_bquery,
        grad_bvalue,
        grad_ckey,
        grad_cval,
        grad_bout,
        grad_again,
        grad_ashift,
        grad_bup,
        grad_bdown,
        grad_fgain,
        grad_fshift,
    ) = lax.psum(
        (
            grad_bquery,
            grad_bvalue,
            grad_ckey,
            grad_cval,
            grad_bout,
            grad_again,
            grad_ashift,
            grad_bup,
            grad_bdown,
            grad_fgain,
            grad_fshift,
        ),
        ("dp", "mp"),
    )
    return (
        activations,
        grad_out,
        grad_wquery,
        grad_wkey,
        grad_wvalue,
        grad_bquery,
        grad_bvalue,
        grad_ckey,
        grad_cval,
        grad_wout,
        grad_bout,
        grad_again,
        grad_ashift,
        grad_wup,
        grad_bup,
        grad_wdown,
        grad_bdown,
        grad_fgain,
        grad_fshift,
    )


BF = jnp.bfloat16
F32 = jnp.float32
MESH = pl.DeviceIdType.MESH
ROWS = 256
QUARTERS = 4
CHANS = D // QUARTERS
QHEADS = CHANS // HEAD_DIM
SEQ = QUARTERS * ROWS
REACH = WINDOW // 2
PREACH = POOL_WINDOW // 2 // STRIDE
OWNP = ROWS // STRIDE
KW = ROWS + 2 * REACH
KP = OWNP + 2 * PREACH
KEYS = KW + KP
QB = 128
NEAR = QB + 2 * REACH
FAR = QB // STRIDE + 2 * PREACH
COMP = 800
HALFC = COMP // 2
FRONT = 256
KVROWS = 1408
BASE = 288
PIECE = D // 8
BIG_NEG = -1e30
SCALE = HEAD_DIM ** -0.5
VROWS = 40
TILES = 2 * CHANS // 128


def nn(a, b):
    return jnp.dot(a, b, preferred_element_type=F32)


def nt(a, b):
    return lax.dot_general(a, b, (((1,), (1,)), ((), ())), preferred_element_type=F32)


def tn(a, b):
    return lax.dot_general(a, b, (((0,), (0,)), ((), ())), preferred_element_type=F32)


def rows_iota(rows, cols):
    return lax.broadcasted_iota(jnp.int32, (rows, cols), 0)


def cols_iota(rows, cols):
    return lax.broadcasted_iota(jnp.int32, (rows, cols), 1)


def mean_row(v):
    return jnp.mean(v, axis=-1, keepdims=True)


def sum_col(v):
    return jnp.sum(v, axis=0, keepdims=True)


def kernel(
    len_ref, tok, wk, wv, wq, wo, wup, wdown, bq, bv, ck, cv, bup, bo, ag, ash, bd, fg, fs, cot,
    act_out, gtok, gmats, gvec,
    W, VEC, kvf, KV, KVS, Q, CTX, P, maskn, maskf, n1, r1, y1, y1b, dg, av,
    yT, fT, gab, GKV, pt, GQ, VG,
    CR, S1, S2, ZR, HL, HR, HLL, SL, SR, GVR, GVZ,
    lsem, asend, arecv, vsend, vrecv, hsend, hrecv, rsend, rrecv, gsend, grecv,
):
    acc, n2, xT, gub = gtok, y1, yT, y1b
    dp = lax.axis_index("dp")
    z = lax.axis_index("mp")
    c = lax.rem(dp, 2)
    x = lax.rem(lax.div(dp, 2), 2)
    y = lax.div(dp, 4)
    core = (dp + 1 - 2 * c, z)
    xdev = (dp + 2 - 4 * x, z)
    ydev = (dp + 4 - 8 * y, z)
    yx = 2 * y + x
    length = len_ref[0]

    def zdev(step):
        return (dp, lax.rem(z + step, QUARTERS))

    def rcopy(src, dst, ssem, rsem, dev):
        return pltpu.make_async_remote_copy(
            src_ref=src, dst_ref=dst, send_sem=ssem, recv_sem=rsem,
            device_id=dev, device_id_type=MESH,
        )

    def loads():
        parts = [(wk, 0), (wv, CHANS), (wq, 2 * CHANS), (wo, 3 * CHANS)]
        copies = [
            pltpu.make_async_copy(src, W.at[0, z, at : at + CHANS, :], lsem.at[i])
            for i, (src, at) in enumerate(parts)
        ]
        copies.append(pltpu.make_async_copy(wup, W.at[1, z], lsem.at[4]))
        copies.append(pltpu.make_async_copy(wdown, W.at[2, z], lsem.at[5]))
        return copies

    own = loads()
    for cp in own:
        cp.start()
    HL[...] = jnp.zeros_like(HL)
    HR[...] = jnp.zeros_like(HR)
    HLL[...] = jnp.zeros_like(HLL)
    barrier = pltpu.get_barrier_semaphore()
    for dev in (core, xdev, ydev, zdev(1), zdev(2), zdev(3)):
        pl.semaphore_signal(barrier, inc=1, device_id=dev, device_id_type=MESH)
    vpack = VG.at[0:16, :]
    vpack[...] = jnp.zeros_like(vpack)
    vpack[0:1, :] = bup[...]
    vpack[1:2, CHANS : 2 * CHANS] = bv[...]
    vpack[1:2, 2 * CHANS : 3 * CHANS] = bq[...]
    vpack[2:7, 0:CHANS] = ck[...]
    vpack[2:7, CHANS : 2 * CHANS] = cv[...]
    VEC[z] = vpack[...]
    pl.semaphore_wait(barrier, 6)

    def block(j):
        return pl.ds(pl.multiple_of(j * PIECE, PIECE), PIECE)

    piece_me = c * 4 + yx
    piece_x = c * 4 + 2 * y + 1 - x
    piece_y = c * 4 + 2 * (1 - y) + x
    piece_d = c * 4 + 2 * (1 - y) + 1 - x
    LO, HI = pl.ds(0, D // 2), pl.ds(D // 2, D // 2)
    ALL = pl.ds(0, D)
    CHUNKS = 9

    def chunk(k):
        rest = lax.max(k - 3, 0)
        m = lax.select(k < 3, 0, 1 + lax.rem(rest, 2))
        s = lax.select(k < 3, k + 1, 1 + lax.div(rest, 2))
        return m, s

    def got(s):
        return lax.rem(z + QUARTERS - s, QUARTERS)

    def wz(k):
        m, s = chunk(k)
        src = W.at[m, z, block(piece_me), :]
        return rcopy(src, src, asend.at[k, 0], arecv.at[k, 0], zdev(s))

    def plane(k, which, piece, cols, dev):
        m, s = chunk(k)
        ref = W.at[m, got(s), block(piece), cols]
        return rcopy(ref, ref, asend.at[k, which], arecv.at[k, which], dev)

    def first(k):
        plane(k, 0, piece_me, ALL, core).wait_recv()
        plane(k, 1, piece_me, ALL, xdev).start()
        plane(k, 2, piece_me, ALL, ydev).start()

    def second(k):
        plane(k, 1, piece_x, ALL, xdev).wait_recv()
        plane(k, 3, piece_x, LO, ydev).start()
        plane(k, 2, piece_y, ALL, ydev).wait_recv()
        plane(k, 4, piece_y, HI, xdev).start()

    def half(j):
        return pl.ds(pl.multiple_of(j * (D // 2), D // 2), D // 2)

    def cross(k, j):
        m, s = chunk(k)
        ref = W.at[m, got(s), half(j), :]
        return rcopy(ref, ref, asend.at[k, 5], arecv.at[k, 5], core)

    def third(k):
        plane(k, 3, piece_d, LO, ydev).wait_recv()
        plane(k, 4, piece_d, HI, xdev).wait_recv()
        cross(k, c).start()

    def fourth(k):
        cross(k, 1 - c).wait_recv()

    def gather_slot(i, carry):
        for lag, stage in enumerate((first, second, third, fourth)):
            k = i - lag
            pl.when((k >= 0) & (k < CHUNKS))(lambda stage=stage, k=k: stage(k))
        return carry

    def gather_done(k, carry):
        wz(k).wait_send()
        plane(k, 1, piece_me, ALL, xdev).wait_send()
        plane(k, 2, piece_me, ALL, ydev).wait_send()
        plane(k, 3, piece_x, LO, ydev).wait_send()
        plane(k, 4, piece_y, HI, xdev).wait_send()
        cross(k, c).wait_send()
        return carry

    def vz(s):
        return rcopy(VEC.at[z], VEC.at[z], vsend.at[s - 1], vrecv.at[s - 1], zdev(s))

    def vz_in(s):
        dst = VEC.at[got(s)]
        return rcopy(dst, dst, vsend.at[s - 1], vrecv.at[s - 1], core)

    for s in (1, 2, 3):
        vz(s).start()
    for cp in own:
        cp.wait()

    def send_own(k, carry):
        wz(k).start()
        return carry

    lax.fori_loop(0, CHUNKS, send_own, 0)

    base = z * ROWS
    start = lax.select(z < 2, jnp.int32(0), jnp.int32(SEQ - COMP))
    place = pl.multiple_of(start - base + BASE + FRONT, 32)
    start = pl.multiple_of(start, 32)
    kvf[...] = jnp.zeros_like(kvf)
    for b in range(2):
        i = base + b * QB + cols_iota(1, QB)
        j = base - REACH + b * QB + rows_iota(NEAR, 1)
        ok = (jnp.abs(i - j) <= REACH) & (j >= 0) & (j < length)
        maskn[b] = jnp.where(ok, 0.0, BIG_NEG)
        j = (OWNP * z - PREACH + b * (QB // STRIDE) + rows_iota(FAR, 1)) * STRIDE
        ok = (jnp.abs(i - j) <= POOL_WINDOW // 2) & (j >= 0) & (j < length)
        maskf[b] = jnp.where(ok, 0.0, BIG_NEG)
    own_rows = pl.ds(pl.multiple_of(base, ROWS), ROWS)
    xb = tok[own_rows, :]
    acc[...] = jnp.zeros_like(acc)

    def taps(zq, t):
        return VEC[zq, 2 + t : 3 + t, 0 : 2 * CHANS]

    def strided(t):
        at = pl.ds(FRONT + BASE - POOL_WINDOW // 2 - 2 + t, KP, stride=STRIDE)
        return jnp.concatenate([kvf[i, at, :] for i in range(TILES)], axis=1)

    def tile(i):
        return slice(i * 128, (i + 1) * 128)

    def window(lo, rows):
        return jnp.concatenate([kvf[i, lo : lo + rows, :] for i in range(TILES)], axis=1)

    def attend(s, carry):
        zq = lax.rem(z + QUARTERS - s, QUARTERS)
        for blk in range(2):
            xr = tok[pl.ds(pl.multiple_of(start + blk * HALFC, 16), HALFC), :]
            kv = nt(xr, W[0, zq, 0 : 2 * CHANS, :]) + VEC[zq, 1:2, 0 : 2 * CHANS]
            pos = start + blk * HALFC + rows_iota(HALFC, 1)
            kvb = jnp.where(pos < length, kv.astype(BF).astype(F32), 0.0)
            for i in range(TILES):
                kvf[i, pl.ds(pl.multiple_of(place + blk * HALFC, 8), HALFC), :] = kvb[:, tile(i)]
        KVS[zq] = window(FRONT, COMP).astype(BF)
        KV[zq, 0:KW, :] = window(FRONT + BASE - REACH, KW).astype(BF)
        pooled = jnp.zeros((KP, 2 * CHANS), F32)
        for t in range(5):
            pooled = pooled + taps(zq, t) * strided(t)
        KV[zq, KW:KEYS, :] = pooled.astype(BF)
        qz = nt(xb, W[0, zq, 2 * CHANS : 3 * CHANS, :]) + VEC[zq, 1:2, 2 * CHANS : 3 * CHANS]
        Q[zq] = qz.astype(BF)
        for b in range(2):
            live = base + b * QB + cols_iota(1, QB) < length
            n0, f0 = b * QB, KW + b * (QB // STRIDE)
            for h in range(QHEADS):
                kl = slice(h * HEAD_DIM, (h + 1) * HEAD_DIM)
                vl = slice(CHANS + h * HEAD_DIM, CHANS + (h + 1) * HEAD_DIM)
                qh = Q[zq, b * QB : (b + 1) * QB, kl]
                sn = nt(KV[zq, n0 : n0 + NEAR, kl], qh) * SCALE + maskn[b]
                sf = nt(KV[zq, f0 : f0 + FAR, kl], qh) * SCALE + maskf[b]
                peak = jnp.maximum(
                    jnp.max(sn, axis=0, keepdims=True), jnp.max(sf, axis=0, keepdims=True)
                )
                en, ef = jnp.exp(sn - peak), jnp.exp(sf - peak)
                inv = 1.0 / (sum_col(en) + sum_col(ef))
                pn, pf = en * inv, ef * inv
                P[zq, h, b, 0:NEAR, :] = pn
                P[zq, h, b, NEAR : NEAR + FAR, :] = pf
                ct = tn(KV[zq, n0 : n0 + NEAR, vl], pn.astype(BF))
                ct = ct + tn(KV[zq, f0 : f0 + FAR, vl], pf.astype(BF))
                ct = jnp.where(live, ct, 0.0)
                CTX[zq, b * QB : (b + 1) * QB, kl] = ct.T.astype(BF)
        acc[...] += nn(CTX[zq], W[0, zq, 3 * CHANS : D, :])
        lo = lax.select(s == 0, 0, s + 3)
        lax.fori_loop(lo, lax.min(s + 4, 6), gather_slot, 0)
        return carry

    def vec_in(s, carry):
        vz_in(s).wait_recv()
        return carry

    lax.fori_loop(1, QUARTERS, vec_in, 0)
    lax.fori_loop(0, QUARTERS, attend, 0)

    def store_T(dst, v, cols):
        vt = v.T.astype(BF)
        for j in range(8):
            to = (j % 2) * 4 + j // 2
            dst[to * PIECE : (to + 1) * PIECE, cols] = vt[j * PIECE : (j + 1) * PIECE]

    def span(i, size):
        return pl.ds(pl.multiple_of(i * size, size), size)

    def norm_one(i, carry):
        rows = span(i, QB)
        res = tok[pl.ds(pl.multiple_of(base + i * QB, QB), QB), :].astype(F32)
        hid = res + (acc[rows, :] + bo[...])
        cen = hid - mean_row(hid)
        r = lax.rsqrt(mean_row(cen * cen) + epsilon)
        n = cen * r
        n1[rows, :] = n
        r1[rows, :] = r
        out = n * ag[...] + ash[...]
        y1[rows, :] = out
        y1b[rows, :] = out.astype(BF)
        store_T(yT, out, rows)
        acc[rows, :] = jnp.zeros_like(out)
        return carry

    lax.fori_loop(0, ROWS // QB, norm_one, 0)

    def feed(s, carry):
        zq = lax.rem(z + QUARTERS - s, QUARTERS)

        def up(i, carry):
            cols = span(i, ROWS)
            u = nn(y1b[...], W[1, zq, :, cols]) + VEC[zq, 0:1, cols]
            cdf = 0.5 * (1.0 + lax.erf(u * (0.5 ** 0.5)))
            dg[zq, :, cols] = cdf + u * jnp.exp(-0.5 * u * u) * ((2.0 * 3.141592653589793) ** -0.5)
            av[zq, :, cols] = (u * cdf).astype(BF)
            return carry

        def down(i, carry):
            cols = span(i, ROWS)
            acc[:, cols] += nn(av[zq], W[2, zq, :, cols])
            return carry

        lax.fori_loop(0, D // ROWS, up, 0)
        lax.fori_loop(0, D // ROWS, down, 0)
        lax.fori_loop(6 + 2 * s, lax.min(8 + 2 * s, 12), gather_slot, 0)
        return carry

    lax.fori_loop(0, QUARTERS, feed, 0)
    VG[...] = jnp.zeros_like(VG)
    GEN = 8 * QUARTERS

    def add_row(row, v):
        VG[row : row + 1, :] += sum_col(v)

    def norm_two(i, carry):
        rows = span(i, QB)
        hid = y1[rows, :] + (acc[rows, :] + bd[...])
        cen = hid - mean_row(hid)
        r = lax.rsqrt(mean_row(cen * cen) + epsilon)
        n = cen * r
        act_out[rows, :] = (n * fg[...] + fs[...]).astype(BF)
        g = cot[rows, :].astype(F32)
        add_row(GEN + 4, g * n)
        add_row(GEN + 5, g)
        e = g * fg[...]
        gh2 = r * (e - mean_row(e) - n * mean_row(e * n))
        acc[rows, :] = gh2
        gf = gh2.astype(BF)
        gab[rows, :] = gf
        gff = gf.astype(F32)
        add_row(GEN + 3, gff)
        store_T(fT, gff, rows)
        return carry

    lax.fori_loop(0, ROWS // QB, norm_two, 0)

    PARTS = 12

    def part(r):
        m = lax.select(r < 8, 1 + lax.rem(r, 2), 0)
        t = lax.select(r < 8, lax.div(r, 2), r - 8)
        return m, t

    def zq_of(t):
        return lax.rem(z + 1 + t, QUARTERS)

    def r_core(r):
        m, t = part(r)
        src = W.at[m, zq_of(t), half(1 - c), :]
        return rcopy(src, CR.at[r], rsend.at[r, 0], rrecv.at[r, 0], core)

    def blk4(r, yy, xx, cols):
        return CR.at[r, block(2 * yy + xx), cols]

    def r_stage1(r, i):
        if i < 2:
            src, dev = blk4(r, i, 1 - x, LO), xdev
        else:
            src, dev = blk4(r, 1 - y, i - 2, HI), ydev
        return rcopy(src, S1.at[r, i], rsend.at[r, 1 + i], rrecv.at[r, 1 + i], dev)

    def r_stage2(r, i):
        if i == 0:
            src, dev = blk4(r, 1 - y, x, LO), ydev
        else:
            src, dev = blk4(r, y, 1 - x, HI), xdev
        return rcopy(src, S2.at[r, i], rsend.at[r, 5 + i], rrecv.at[r, 5 + i], dev)

    def r_z(r):
        t = part(r)[1]
        src = CR.at[r, block(yx), :]
        return rcopy(src, ZR.at[r], rsend.at[r, 7], rrecv.at[r, 7], zdev(1 + t))

    def reduce1(r):
        m, t = part(r)
        r_core(r).wait_recv()
        zq = zq_of(t)

        def add(i, carry):
            mine = W[m, zq, block(4 * c + i), :].astype(F32)
            CR[r, block(i), :] = (CR[r, block(i), :].astype(F32) + mine).astype(BF)
            return carry

        lax.fori_loop(0, 4, add, 0)
        for i in range(4):
            r_stage1(r, i).start()

    def reduce2(r):
        for i in range(4):
            r_stage1(r, i).wait_recv()
        for i in range(2):
            a = blk4(r, i, x, LO)
            a[...] = (a[...].astype(F32) + S1[r, i].astype(F32)).astype(BF)
            a = blk4(r, y, i, HI)
            a[...] = (a[...].astype(F32) + S1[r, 2 + i].astype(F32)).astype(BF)
        for i in range(2):
            r_stage2(r, i).start()

    def reduce3(r):
        for i in range(2):
            r_stage2(r, i).wait_recv()
        for i, cols in enumerate((LO, HI)):
            a = blk4(r, y, x, cols)
            a[...] = (a[...].astype(F32) + S2[r, i].astype(F32)).astype(BF)
        pl.when(part(r)[1] < QUARTERS - 1)(lambda: r_z(r).start())

    def reduce_slot(i):
        for lag, stage in enumerate((reduce1, reduce2, reduce3)):
            r = i - lag
            pl.when((r >= 0) & (r < PARTS))(lambda stage=stage, r=r: stage(r))

    def weight_grad(left, right, dst, width):
        def rows(i, carry):
            at = span(i, ROWS)
            dst[at, 0:width] = nn(left[at, :], right).astype(BF)
            return carry

        lax.fori_loop(0, D // ROWS, rows, 0)

    def feed_back(s, carry):
        zq = lax.rem(z + 1 + s, QUARTERS)
        vrow = pl.multiple_of(8 * zq, 8)

        def hidden(i, carry):
            cols = span(i, ROWS)
            gact = nt(gab[...], W[2, zq, cols, :])
            gu = (gact * dg[zq, :, cols]).astype(BF)
            gub[:, cols] = gu
            VG[pl.ds(vrow, 1), cols] = sum_col(gu.astype(F32))
            return carry

        def inputs(i, carry):
            cols = span(i, ROWS)
            acc[:, cols] += nt(gub[...], W[1, zq, cols, :])
            return carry

        lax.fori_loop(0, D // ROWS, hidden, 0)
        lax.fori_loop(0, D // ROWS, inputs, 0)
        weight_grad(yT, gub[...], W.at[1, zq], D)
        r_core(2 * s).start()
        weight_grad(fT, av[zq], W.at[2, zq], D)
        r_core(2 * s + 1).start()
        pl.when(s > 0)(lambda: reduce_slot(s - 1))
        return carry

    lax.fori_loop(0, CHUNKS, gather_done, 0)
    for s in (1, 2, 3):
        vz(s).wait_send()
    lax.fori_loop(0, QUARTERS, feed_back, 0)

    def norm_back(i, carry):
        rows = span(i, QB)
        gy = acc[rows, :]
        n = n1[rows, :]
        add_row(GEN + 1, gy * n)
        add_row(GEN + 2, gy)
        e = gy * ag[...]
        gh1 = r1[rows, :] * (e - mean_row(e) - n * mean_row(e * n))
        acc[rows, :] = gh1
        ga = gh1.astype(BF)
        gab[rows, :] = ga
        gaf = ga.astype(F32)
        add_row(GEN, gaf)
        store_T(fT, gaf, rows)
        store_T(xT, tok[pl.ds(pl.multiple_of(base + i * QB, QB), QB), :].astype(F32), rows)
        return carry

    lax.fori_loop(0, ROWS // QB, norm_back, 0)

    def hl(zq):
        return rcopy(SL.at[zq], HL.at[zq], hsend.at[0, zq], hrecv.at[0, zq], zdev(3))

    def hr(zq):
        return rcopy(SR.at[zq], HR.at[zq], hsend.at[1, zq], hrecv.at[1, zq], zdev(1))

    def hll(zq):
        return rcopy(
            SL.at[zq, REACH : REACH + 16, :], HLL.at[zq], hsend.at[2, zq], hrecv.at[2, zq], zdev(2)
        )

    def attend_back(s, carry):
        zq = lax.rem(z + 1 + s, QUARTERS)
        gc = nt(gab[...], W[0, zq, 3 * CHANS : D, :])
        alive = base + rows_iota(ROWS, 1) < length
        gcb = jnp.where(alive, gc, 0.0).astype(BF)
        GKV[zq] = jnp.zeros((KEYS, 2 * CHANS), F32)
        for b in range(2):
            n0, f0 = b * QB, KW + b * (QB // STRIDE)
            for h in range(QHEADS):
                kl = slice(h * HEAD_DIM, (h + 1) * HEAD_DIM)
                vl = slice(CHANS + h * HEAD_DIM, CHANS + (h + 1) * HEAD_DIM)
                gch = gcb[b * QB : (b + 1) * QB, kl]
                qh = Q[zq, b * QB : (b + 1) * QB, kl]
                pn = P[zq, h, b, 0:NEAR, :]
                pf = P[zq, h, b, NEAR : NEAR + FAR, :]
                gpn = nt(KV[zq, n0 : n0 + NEAR, vl], gch)
                gpf = nt(KV[zq, f0 : f0 + FAR, vl], gch)
                delta = sum_col(pn * gpn) + sum_col(pf * gpf)
                gsn = (pn * (gpn - delta)).astype(BF)
                gsf = (pf * (gpf - delta)).astype(BF)
                qt = tn(KV[zq, n0 : n0 + NEAR, kl], gsn) + tn(KV[zq, f0 : f0 + FAR, kl], gsf)
                GQ[zq, b * QB : (b + 1) * QB, 2 * CHANS + h * HEAD_DIM : 2 * CHANS + (h + 1) * HEAD_DIM] = (
                    (qt * SCALE).T.astype(BF)
                )
                GKV[zq, n0 : n0 + NEAR, kl] += nn(gsn, qh) * SCALE
                GKV[zq, f0 : f0 + FAR, kl] += nn(gsf, qh) * SCALE
                GKV[zq, n0 : n0 + NEAR, vl] += nn(pn.astype(BF), gch)
                GKV[zq, f0 : f0 + FAR, vl] += nn(pf.astype(BF), gch)
        vrow = pl.multiple_of(8 * zq, 8)
        for i in range(TILES):
            kvf[i, FRONT : FRONT + COMP, :] = KVS[zq, :, tile(i)].astype(F32)
        gp = GKV[zq, KW:KEYS, :]
        for t in range(5):
            VG[pl.ds(vrow + 2 + t, 1), 0 : 2 * CHANS] = sum_col(gp * strided(t))
        SL[zq, 0:REACH, :] = GKV[zq, 0:REACH, :].astype(BF)
        SL[zq, REACH : REACH + 80, :] = GKV[zq, KW : KW + 80, :].astype(BF)
        SR[zq, 0:REACH, :] = GKV[zq, KW - REACH : KW, :].astype(BF)
        SR[zq, REACH : REACH + OWNP, :] = GKV[zq, KEYS - OWNP : KEYS, :].astype(BF)
        pl.when(z > 0)(lambda: hl(zq).start())
        pl.when(z < QUARTERS - 1)(lambda: hr(zq).start())
        pl.when(z > 1)(lambda: hll(zq).start())
        reduce_slot(3 + s)
        return carry

    lax.fori_loop(0, QUARTERS, attend_back, 0)

    def project_back(s, carry):
        zq = lax.rem(z + 1 + s, QUARTERS)
        pl.when(z < QUARTERS - 1)(lambda: hl(zq).wait_recv())
        pl.when(z > 0)(lambda: hr(zq).wait_recv())
        pl.when(z < QUARTERS - 2)(lambda: hll(zq).wait_recv())
        near = GKV.at[zq]
        near[REACH : 2 * REACH, :] += HR[zq, 0:REACH, :].astype(F32)
        near[ROWS : ROWS + REACH, :] += HL[zq, 0:REACH, :].astype(F32)
        gp = GKV[zq, KW + OWNP : KW + 2 * OWNP, :] + HR[zq, REACH : REACH + OWNP, :].astype(F32)
        gp = gp + HL[zq, REACH : REACH + OWNP, :].astype(F32)
        nxt = GKV[zq, KW + 2 * OWNP : KW + 2 * OWNP + 1, :]
        nxt = nxt + HL[zq, REACH + OWNP : REACH + OWNP + 16, :].astype(F32)[0:1, :]
        nxt = nxt + HLL[zq].astype(F32)[0:1, :]
        gp1 = jnp.concatenate([gp[1:, :], nxt], axis=0)
        fills = (
            taps(zq, 2) * gp,
            taps(zq, 3) * gp,
            taps(zq, 4) * gp + taps(zq, 0) * gp1,
            taps(zq, 1) * gp1,
        )
        for k, fill in enumerate(fills):
            for i in range(TILES):
                pt[i, pl.ds(k, OWNP, stride=STRIDE), :] = fill[:, tile(i)]
        back = jnp.concatenate([pt[i] for i in range(TILES)], axis=1)
        alive = base + rows_iota(ROWS, 1) < length
        gkv = GKV[zq, REACH : REACH + ROWS, :] + jnp.where(alive, back, 0.0)
        GQ[zq, :, 0 : 2 * CHANS] = gkv.astype(BF)
        vrow = pl.multiple_of(8 * zq, 8)
        VG[pl.ds(vrow + 1, 1), 0 : 3 * CHANS] = sum_col(GQ[zq].astype(F32))

        def inputs(i, carry):
            cols = span(i, ROWS)
            acc[:, cols] += nn(GQ[zq], W[0, zq, 0 : 3 * CHANS, cols])
            return carry

        lax.fori_loop(0, D // ROWS, inputs, 0)
        weight_grad(xT, GQ[zq], W.at[0, zq], 3 * CHANS)

        def outs(i, carry):
            at = span(i, ROWS)
            W[0, zq, at, 3 * CHANS : D] = nn(fT[at, :], CTX[zq]).astype(BF)
            return carry

        lax.fori_loop(0, D // ROWS, outs, 0)
        r_core(8 + s).start()
        reduce_slot(7 + s)
        return carry

    lax.fori_loop(0, QUARTERS, project_back, 0)
    for zq in range(QUARTERS):
        pl.when(z > 0)(lambda: hl(zq).wait_send())
        pl.when(z < QUARTERS - 1)(lambda: hr(zq).wait_send())
        pl.when(z > 1)(lambda: hll(zq).wait_send())

    def g_step(i, dev):
        return rcopy(VG, GVR.at[i], gsend.at[i], grecv.at[i], dev)

    def g_z(s):
        return rcopy(VG, GVZ.at[z], gsend.at[2 + s], grecv.at[2 + s], zdev(s))

    def g_z_in(s):
        dst = GVZ.at[got(s)]
        return rcopy(dst, dst, gsend.at[2 + s], grecv.at[2 + s], core)

    for i, dev in enumerate((core, xdev, ydev)):
        g_step(i, dev).start()
        reduce_slot(jnp.int32(11 + i))
        g_step(i, dev).wait()
        VG[...] = VG[...] + GVR[i]
    for s in (1, 2, 3):
        g_z(s).start()
    GVZ[z] = VG[...]
    for m, rs in enumerate(((8, 9, 10, 11), (0, 2, 4, 6), (1, 3, 5, 7))):
        total = CR[rs[3], block(yx), :].astype(F32)
        for r in rs[:3]:
            r_z(r).wait_recv()
            total = total + ZR[r].astype(F32)
        gmats[m] = total
    for s in (1, 2, 3):
        g_z_in(s).wait_recv()
    gvec[...] = GVZ[0] + GVZ[1] + GVZ[2] + GVZ[3]
    for s in (1, 2, 3):
        g_z(s).wait_send()

    def sent(r, carry):
        r_core(r).wait_send()
        for i in range(4):
            r_stage1(r, i).wait_send()
        for i in range(2):
            r_stage2(r, i).wait_send()
        pl.when(part(r)[1] < QUARTERS - 1)(lambda: r_z(r).wait_send())
        return carry

    lax.fori_loop(0, PARTS, sent, 0)


def unpack(
    act, gtok, gmats, gvec,
    act_out, gtok_out, gq, gk, gv, gbq, gbv, gck, gcv, go, gbo, gag, gas, gup, gbu, gdown, gbd, gfg, gfs,
):
    act_out[...] = act[...]
    gtok_out[...] = gtok[...]
    gk[...] = gmats[0, :, 0:CHANS]
    gv[...] = gmats[0, :, CHANS : 2 * CHANS]
    gq[...] = gmats[0, :, 2 * CHANS : 3 * CHANS]
    go[...] = gmats[0, :, 3 * CHANS : D].T
    gup[...] = gmats[1]
    gdown[...] = gmats[2]
    for j in range(QUARTERS):
        at = slice(j * CHANS, (j + 1) * CHANS)
        row = 8 * j
        gbu[:, j * D : (j + 1) * D] = gvec[row : row + 1, :]
        gbv[:, at] = gvec[row + 1 : row + 2, CHANS : 2 * CHANS]
        gbq[:, at] = gvec[row + 1 : row + 2, 2 * CHANS : 3 * CHANS]
        gck[:, at] = gvec[row + 2 : row + 7, 0:CHANS]
        gcv[:, at] = gvec[row + 2 : row + 7, CHANS : 2 * CHANS]
    for j, out in enumerate((gbo, gag, gas, gbd, gfg, gfs)):
        out[...] = gvec[8 * QUARTERS + j : 8 * QUARTERS + j + 1, :]


def fused_layer(
    tokens, lengths, w_query, w_key, w_value, b_query, b_value, conv_key, conv_value, w_out,
    b_out, attn_gain, attn_shift, w_up, b_up, w_down, b_down, ffn_gain, ffn_shift, cotangent,
):
    Q4 = QUARTERS
    vm = pltpu.VMEM
    dma = pltpu.SemaphoreType.DMA
    scratch = [
        vm((3, Q4, D, D), BF),
        vm((Q4, 16, D), F32),
        vm((TILES, KVROWS, 128), F32),
        vm((Q4, KEYS, 2 * CHANS), BF),
        vm((Q4, COMP, 2 * CHANS), BF),
        vm((Q4, ROWS, CHANS), BF),
        vm((Q4, ROWS, CHANS), BF),
        vm((Q4, QHEADS, 2, NEAR + FAR, QB), F32),
        vm((2, NEAR, QB), F32),
        vm((2, FAR, QB), F32),
        vm((ROWS, D), F32),
        vm((ROWS, 1), F32),
        vm((ROWS, D), F32),
        vm((ROWS, D), BF),
        vm((Q4, ROWS, D), F32),
        vm((Q4, ROWS, D), BF),
        vm((D, ROWS), BF),
        vm((D, ROWS), BF),
        vm((ROWS, D), BF),
        vm((Q4, KEYS, 2 * CHANS), F32),
        vm((TILES, ROWS, 128), F32),
        vm((Q4, ROWS, 3 * CHANS), BF),
        vm((VROWS, D), F32),
        vm((12, D // 2, D), BF),
        vm((12, 4, PIECE, D // 2), BF),
        vm((12, 2, PIECE, D // 2), BF),
        vm((12, PIECE, D), BF),
        vm((Q4, REACH + 80, 2 * CHANS), BF),
        vm((Q4, REACH + OWNP, 2 * CHANS), BF),
        vm((Q4, 16, 2 * CHANS), BF),
        vm((Q4, REACH + 80, 2 * CHANS), BF),
        vm((Q4, REACH + OWNP, 2 * CHANS), BF),
        vm((3, VROWS, D), F32),
        vm((Q4, VROWS, D), F32),
        dma((6,)),
        dma((9, 6)),
        dma((9, 6)),
        dma((3,)),
        dma((3,)),
        dma((3, Q4)),
        dma((3, Q4)),
        dma((12, 8)),
        dma((12, 8)),
        dma((6,)),
        dma((6,)),
    ]
    vspec = pl.BlockSpec(memory_space=pltpu.VMEM)
    hspec = pl.BlockSpec(memory_space=pl.ANY)
    packed = pl.pallas_call(
        kernel,
        out_shape=(
            jax.ShapeDtypeStruct((ROWS, D), BF),
            jax.ShapeDtypeStruct((ROWS, D), F32),
            jax.ShapeDtypeStruct((3, PIECE, D), F32),
            jax.ShapeDtypeStruct((VROWS, D), F32),
        ),
        in_specs=[pl.BlockSpec(memory_space=pltpu.SMEM), vspec] + [hspec] * 6 + [vspec] * 12,
        out_specs=(vspec,) * 4,
        scratch_shapes=scratch,
        compiler_params=pltpu.CompilerParams(
            collective_id=0, has_side_effects=True, vmem_limit_bytes=67043328
        ),
        name="layer",
    )(
        lengths, tokens, w_key[0].T, w_value[0].T, w_query[0].T, w_out[0], w_up[0], w_down[0],
        b_query, b_value, conv_key[0], conv_value[0], b_up, b_out, attn_gain, attn_shift, b_down,
        ffn_gain, ffn_shift, cotangent,
    )
    row = (1, D)
    shapes = [
        (ROWS, D), (PIECE, CHANS), (PIECE, CHANS), (PIECE, CHANS), row, row, (5, D), (5, D), (CHANS, PIECE),
        row, row, row, (PIECE, D), (1, FF), (PIECE, D), row, row, row,
    ]
    outs = pl.pallas_call(
        unpack,
        out_shape=[jax.ShapeDtypeStruct((ROWS, D), BF)] + [jax.ShapeDtypeStruct(v, F32) for v in shapes],
        in_specs=[vspec] * 4,
        out_specs=[vspec] * 19,
        name="unpack",
    )(*packed)
    act, gtok, gq, gk, gv, gbq, gbv, gck, gcv, go, gbo, gag, gas, gup, gbu, gdown, gbd, gfg, gfs = outs
    return (
        act, gtok, gq[None], gk[None], gv[None], gbq, gbv, gck[None], gcv[None], go[None], gbo, gag, gas,
        gup[None], gbu, gdown.T[None], gbd, gfg, gfs,
    )


def solution(mesh):
    small = mesh.shape["dp"] == 8 and mesh.shape["mp"] == QUARTERS
    return jax.shard_map(
        fused_layer if small else on_device,
        mesh=mesh,
        in_specs=(
            P("dp", None),
            P("dp"),
            P(None, None, "mp"),
            P(None, None, "mp"),
            P(None, None, "mp"),
            P(None, "mp"),
            P(None, "mp"),
            P(None, None, "mp"),
            P(None, None, "mp"),
            P(None, "mp", None),
            P(),
            P(),
            P(),
            P(None, None, "mp"),
            P(None, "mp"),
            P(None, "mp", None),
            P(),
            P(),
            P(),
            P(("dp", "mp"), None),
        ),
        out_specs=(
            P(("dp", "mp"), None),
            P(("dp", "mp"), None),
            P(None, "dp", "mp"),
            P(None, "dp", "mp"),
            P(None, "dp", "mp"),
            P(),
            P(),
            P(),
            P(),
            P(None, "mp", "dp"),
            P(),
            P(),
            P(),
            P(None, "dp", "mp"),
            P(),
            P(None, "mp", "dp"),
            P(),
            P(),
            P(),
        ),
        check_vma=False,
    )
```

```python
import jax
import jax.numpy as jnp
from jax import lax
from jax.experimental import pallas as pl
from jax.experimental.pallas import tpu as pltpu
from jax.sharding import PartitionSpec as P

D = 768
HEAD_DIM = 64
FF = 3072
WINDOW = 128
POOL_WINDOW = 512
STRIDE = 4
LAYERS = 1


block_rows = 512
mask_fill = -1000000000.0
epsilon = 1e-05


def norm_rows(hidden, gain, shift):
    center = hidden - jnp.mean(hidden, axis=-1, keepdims=True)
    spread = jnp.mean(center * center, axis=-1, keepdims=True)
    return center * lax.rsqrt(spread + epsilon) * gain + shift


def gelu_exact(values):
    return jax.nn.gelu(values, approximate=False)


def pool_rows(values, kernel):
    seqs, length, chans = values.shape
    width = kernel.shape[0]
    half = width // 2
    pooled_len = length // STRIDE
    padded = jnp.pad(values, ((0, 0), (half, width), (0, 0)))
    total = jnp.zeros((seqs, pooled_len, chans), jnp.float32)
    for offset in range(width):
        total = total + kernel[offset] * padded[:, offset : offset + STRIDE * pooled_len : STRIDE]
    return total


def block_mask(start, lengths):
    reach = WINDOW // 2
    pool_reach = POOL_WINDOW // 2 // STRIDE
    span = block_rows // STRIDE + 2 * pool_reach
    rows = start + jnp.arange(block_rows, dtype=jnp.int32)
    near_pos = start - reach + jnp.arange(block_rows + 2 * reach, dtype=jnp.int32)
    far_pos = (start // STRIDE - pool_reach + jnp.arange(span, dtype=jnp.int32)) * STRIDE
    limit = lengths[:, None, None]
    near_ok = (
        (jnp.abs(rows[:, None] - near_pos[None, :]) <= reach)[None]
        & (near_pos >= 0)[None, None]
        & (near_pos[None, None] < limit)
    )
    far_ok = (
        (jnp.abs(rows[:, None] - far_pos[None, :]) <= POOL_WINDOW // 2)[None]
        & (far_pos >= 0)[None, None]
        & (far_pos[None, None] < limit)
    )
    return jnp.concatenate([near_ok, far_ok], axis=-1)


def padded_keys(keys_loc, vals_loc, far_keys, far_vals):
    reach = WINDOW // 2
    pool_reach = POOL_WINDOW // 2 // STRIDE
    pad_near = ((0, 0), (reach, reach), (0, 0), (0, 0))
    pad_far = ((0, 0), (pool_reach, pool_reach), (0, 0), (0, 0))
    return (
        jnp.pad(keys_loc, pad_near),
        jnp.pad(vals_loc, pad_near),
        jnp.pad(far_keys, pad_far),
        jnp.pad(far_vals, pad_far),
    )


def block_inputs(start, queries, padded):
    near_k, near_v, far_k, far_v = padded
    near_len = block_rows + 2 * (WINDOW // 2)
    span = block_rows // STRIDE + 2 * (POOL_WINDOW // 2 // STRIDE)
    pool_start = start // STRIDE
    q_rows = queries[:, start : start + block_rows]
    keys_b = jnp.concatenate(
        [near_k[:, start : start + near_len], far_k[:, pool_start : pool_start + span]], axis=1
    )
    vals_b = jnp.concatenate(
        [near_v[:, start : start + near_len], far_v[:, pool_start : pool_start + span]], axis=1
    )
    return (q_rows, keys_b, vals_b)


def forward_block(q_rows, keys_b, vals_b, mask, live):
    scale = q_rows.shape[-1] ** (-0.5)
    scores = (
        jnp.einsum("sqhe,skhe->shqk", q_rows, keys_b, preferred_element_type=jnp.float32) * scale
    )
    scores = jnp.where(mask[:, None], scores, mask_fill)
    peak = jnp.max(scores, axis=-1, keepdims=True)
    expo = jnp.exp(scores - peak)
    total = jnp.sum(expo, axis=-1, keepdims=True)
    weights = (expo / total).astype(jnp.bfloat16)
    result = jnp.einsum("shqk,skhe->sqhe", weights, vals_b, preferred_element_type=jnp.float32)
    result = jnp.where(live[:, :, None, None], result, 0.0)
    return (result, peak + jnp.log(total))


def forward_skip(q_rows, keys_b, vals_b, mask, live):
    seqs, rows, heads, size = q_rows.shape
    return (
        jnp.zeros((seqs, rows, heads, size), jnp.float32),
        jnp.zeros((seqs, heads, rows, 1), jnp.float32),
    )


def backward_block(q_rows, keys_b, vals_b, mask, logsum, grad_rows):
    scale = q_rows.shape[-1] ** (-0.5)
    scores = (
        jnp.einsum("sqhe,skhe->shqk", q_rows, keys_b, preferred_element_type=jnp.float32) * scale
    )
    scores = jnp.where(mask[:, None], scores, mask_fill)
    probs = jnp.exp(scores - logsum)
    grad_probs = jnp.einsum(
        "sqhe,skhe->shqk", grad_rows, vals_b, preferred_element_type=jnp.float32
    )
    delta = jnp.sum(probs * grad_probs, axis=-1, keepdims=True)
    grad_scores = (probs * (grad_probs - delta)).astype(jnp.bfloat16)
    grad_q = (
        jnp.einsum("shqk,skhe->sqhe", grad_scores, keys_b, preferred_element_type=jnp.float32)
        * scale
    )
    grad_keys = (
        jnp.einsum("shqk,sqhe->skhe", grad_scores, q_rows, preferred_element_type=jnp.float32)
        * scale
    )
    grad_vals = jnp.einsum(
        "shqk,sqhe->skhe", probs.astype(jnp.bfloat16), grad_rows, preferred_element_type=jnp.float32
    )
    return (grad_q, grad_keys, grad_vals)


def backward_skip(q_rows, keys_b, vals_b, mask, logsum, grad_rows):
    return (
        jnp.zeros(q_rows.shape, jnp.float32),
        jnp.zeros(keys_b.shape, jnp.float32),
        jnp.zeros(vals_b.shape, jnp.float32),
    )


def attend_forward(queries, keys_loc, vals_loc, far_keys, far_vals, lengths):
    length = queries.shape[1]
    padded = padded_keys(keys_loc, vals_loc, far_keys, far_vals)
    longest = jnp.max(lengths)
    results, logsums = ([], [])
    for block in range(length // block_rows):
        start = block * block_rows
        q_rows, keys_b, vals_b = block_inputs(start, queries, padded)
        mask = block_mask(start, lengths)
        live = start + jnp.arange(block_rows, dtype=jnp.int32)[None, :] < lengths[:, None]
        result, logsum = lax.cond(
            start < longest, forward_block, forward_skip, q_rows, keys_b, vals_b, mask, live
        )
        results.append(result)
        logsums.append(logsum)
    return (jnp.concatenate(results, axis=1), logsums)


def attend_backward(
    queries, keys_loc, vals_loc, far_keys, far_vals, lengths, logsums, grad_context
):
    seqs, length, heads, size = queries.shape
    pooled_len = far_keys.shape[1]
    reach = WINDOW // 2
    pool_reach = POOL_WINDOW // 2 // STRIDE
    near_len = block_rows + 2 * reach
    span = block_rows // STRIDE + 2 * pool_reach
    padded = padded_keys(keys_loc, vals_loc, far_keys, far_vals)
    longest = jnp.max(lengths)
    grad_near_k = jnp.zeros((seqs, length + 2 * reach, heads, size), jnp.float32)
    grad_near_v = jnp.zeros((seqs, length + 2 * reach, heads, size), jnp.float32)
    grad_far_k = jnp.zeros((seqs, pooled_len + 2 * pool_reach, heads, size), jnp.float32)
    grad_far_v = jnp.zeros((seqs, pooled_len + 2 * pool_reach, heads, size), jnp.float32)
    grad_queries = []
    for block in range(length // block_rows):
        start = block * block_rows
        pool_start = start // STRIDE
        q_rows, keys_b, vals_b = block_inputs(start, queries, padded)
        mask = block_mask(start, lengths)
        grad_rows = grad_context[:, start : start + block_rows]
        grad_q, grad_keys, grad_vals = lax.cond(
            start < longest,
            backward_block,
            backward_skip,
            q_rows,
            keys_b,
            vals_b,
            mask,
            logsums[block],
            grad_rows,
        )
        grad_queries.append(grad_q)
        grad_near_k = grad_near_k.at[:, start : start + near_len].add(grad_keys[:, :near_len])
        grad_near_v = grad_near_v.at[:, start : start + near_len].add(grad_vals[:, :near_len])
        grad_far_k = grad_far_k.at[:, pool_start : pool_start + span].add(grad_keys[:, near_len:])
        grad_far_v = grad_far_v.at[:, pool_start : pool_start + span].add(grad_vals[:, near_len:])
    return (
        jnp.concatenate(grad_queries, axis=1),
        grad_near_k[:, reach : reach + length],
        grad_near_v[:, reach : reach + length],
        grad_far_k[:, pool_reach : pool_reach + pooled_len],
        grad_far_v[:, pool_reach : pool_reach + pooled_len],
    )


def row_sum(left, right, share):

    def term(start, count):
        return jnp.dot(left, right, preferred_element_type=jnp.float32)

    return lax.psum_scatter(
        term(jnp.int32(0), share * lax.axis_size("mp")), "mp", scatter_dimension=0, tiled=True
    )


def share_rows(values):
    return lax.all_gather(values, "mp", axis=0, tiled=True)


def share_back(values):
    return lax.all_gather(values, "mp", axis=0, tiled=True)


def back_sum(term, share):
    return lax.psum_scatter(
        term(jnp.int32(0), share * lax.axis_size("mp")), "mp", scatter_dimension=0, tiled=True
    )


def spread(values, width):
    whole = jnp.zeros(values.shape[:-1] + (width,), jnp.float32)
    start = lax.axis_index("mp") * values.shape[-1]
    return lax.dynamic_update_slice_in_dim(whole, values, start, values.ndim - 1)


def layer_forward(full_in, resid, lengths, params, share):
    (
        w_query,
        w_key,
        w_value,
        b_query,
        b_value,
        conv_key,
        conv_value,
        w_out,
        b_out,
        attn_gain,
        attn_shift,
        w_up,
        b_up,
        w_down,
        b_down,
        ffn_gain,
        ffn_shift,
    ) = params
    seqs = lengths.shape[0]
    total_rows = full_in.shape[0]
    length = total_rows // seqs
    chans = w_query.shape[1]
    heads = chans // HEAD_DIM
    pooled_len = length // STRIDE
    queries = (jnp.dot(full_in, w_query, preferred_element_type=jnp.float32) + b_query).astype(
        jnp.bfloat16
    )
    keys_loc = jnp.dot(full_in, w_key, preferred_element_type=jnp.float32).astype(jnp.bfloat16)
    vals_loc = (jnp.dot(full_in, w_value, preferred_element_type=jnp.float32) + b_value).astype(
        jnp.bfloat16
    )
    valid = (jnp.arange(length, dtype=jnp.int32)[None, :] < lengths[:, None]).astype(jnp.float32)[
        :, :, None
    ]
    far_keys = pool_rows(
        keys_loc.reshape(seqs, length, chans).astype(jnp.float32) * valid, conv_key
    ).astype(jnp.bfloat16)
    far_vals = pool_rows(
        vals_loc.reshape(seqs, length, chans).astype(jnp.float32) * valid, conv_value
    ).astype(jnp.bfloat16)
    context, logsums = attend_forward(
        queries.reshape(seqs, length, heads, HEAD_DIM),
        keys_loc.reshape(seqs, length, heads, HEAD_DIM),
        vals_loc.reshape(seqs, length, heads, HEAD_DIM),
        far_keys.reshape(seqs, pooled_len, heads, HEAD_DIM),
        far_vals.reshape(seqs, pooled_len, heads, HEAD_DIM),
        lengths,
    )
    context = context.reshape(total_rows, chans).astype(jnp.bfloat16)
    hidden_one = resid + (row_sum(context, w_out, share) + b_out)
    normed = norm_rows(hidden_one, attn_gain, attn_shift)
    full_normed = share_rows(normed.astype(jnp.bfloat16))
    upper = jnp.dot(full_normed, w_up, preferred_element_type=jnp.float32) + b_up
    active = gelu_exact(upper).astype(jnp.bfloat16)
    hidden_two = normed + (row_sum(active, w_down, share) + b_down)
    result = norm_rows(hidden_two, ffn_gain, ffn_shift)
    kept = (
        full_in,
        queries,
        keys_loc,
        vals_loc,
        far_keys,
        far_vals,
        logsums,
        context,
        hidden_one,
        full_normed,
        upper,
        active,
        hidden_two,
    )
    return (result, kept)


def layer_backward(grad_out, kept, params, lengths, share):
    (
        w_query,
        w_key,
        w_value,
        b_query,
        b_value,
        conv_key,
        conv_value,
        w_out,
        b_out,
        attn_gain,
        attn_shift,
        w_up,
        b_up,
        w_down,
        b_down,
        ffn_gain,
        ffn_shift,
    ) = params
    (
        full_in,
        queries,
        keys_loc,
        vals_loc,
        far_keys,
        far_vals,
        logsums,
        context,
        hidden_one,
        full_normed,
        saved_upper,
        active,
        hidden_two,
    ) = kept
    seqs = lengths.shape[0]
    total_rows = full_in.shape[0]
    length = total_rows // seqs
    chans = w_query.shape[1]
    heads = chans // HEAD_DIM
    pooled_len = length // STRIDE
    unused_two, pull_two = jax.vjp(norm_rows, hidden_two, ffn_gain, ffn_shift)
    grad_h2, grad_fgain, grad_fshift = pull_two(grad_out)
    grad_ffn = grad_h2.astype(jnp.bfloat16)
    grad_bdown = jnp.sum(grad_ffn.astype(jnp.float32), axis=0)
    full_gffn = share_back(grad_ffn)
    grad_wdown = jnp.einsum("tf,td->fd", active, full_gffn, preferred_element_type=jnp.float32)
    grad_active = jnp.einsum("td,fd->tf", full_gffn, w_down, preferred_element_type=jnp.float32)
    unused_gelu, pull_gelu = jax.vjp(gelu_exact, saved_upper)
    grad_upper = pull_gelu(grad_active)[0].astype(jnp.bfloat16)
    grad_bup = jnp.sum(grad_upper.astype(jnp.float32), axis=0)
    grad_wup = jnp.einsum("td,tf->df", full_normed, grad_upper, preferred_element_type=jnp.float32)

    def up_term(start, count):
        return jnp.einsum("tf,df->td", grad_upper, w_up, preferred_element_type=jnp.float32)

    grad_y1 = grad_h2 + back_sum(up_term, share)
    unused_one, pull_one = jax.vjp(norm_rows, hidden_one, attn_gain, attn_shift)
    grad_h1, grad_again, grad_ashift = pull_one(grad_y1)
    grad_attn = grad_h1.astype(jnp.bfloat16)
    grad_bout = jnp.sum(grad_attn.astype(jnp.float32), axis=0)
    full_gattn = share_back(grad_attn)
    grad_wout = jnp.einsum("tc,td->cd", context, full_gattn, preferred_element_type=jnp.float32)
    grad_context = jnp.einsum("td,cd->tc", full_gattn, w_out, preferred_element_type=jnp.float32)
    valid = (jnp.arange(length, dtype=jnp.int32)[None, :] < lengths[:, None]).astype(jnp.float32)[
        :, :, None
    ]
    grad_context = (grad_context.reshape(seqs, length, chans) * valid).astype(jnp.bfloat16)
    grad_q, grad_near_k, grad_near_v, grad_far_k, grad_far_v = attend_backward(
        queries.reshape(seqs, length, heads, HEAD_DIM),
        keys_loc.reshape(seqs, length, heads, HEAD_DIM),
        vals_loc.reshape(seqs, length, heads, HEAD_DIM),
        far_keys.reshape(seqs, pooled_len, heads, HEAD_DIM),
        far_vals.reshape(seqs, pooled_len, heads, HEAD_DIM),
        lengths,
        logsums,
        grad_context.reshape(seqs, length, heads, HEAD_DIM),
    )
    masked_keys = keys_loc.reshape(seqs, length, chans).astype(jnp.float32) * valid
    masked_vals = vals_loc.reshape(seqs, length, chans).astype(jnp.float32) * valid
    unused_pk, pull_key = jax.vjp(pool_rows, masked_keys, conv_key)
    grad_kpool, grad_ckey = pull_key(grad_far_k.reshape(seqs, pooled_len, chans))
    unused_pv, pull_val = jax.vjp(pool_rows, masked_vals, conv_value)
    grad_vpool, grad_cval = pull_val(grad_far_v.reshape(seqs, pooled_len, chans))
    grad_queries = grad_q.reshape(total_rows, chans).astype(jnp.bfloat16)
    grad_keys = (
        (grad_near_k.reshape(seqs, length, chans) + grad_kpool * valid)
        .reshape(total_rows, chans)
        .astype(jnp.bfloat16)
    )
    grad_vals = (
        (grad_near_v.reshape(seqs, length, chans) + grad_vpool * valid)
        .reshape(total_rows, chans)
        .astype(jnp.bfloat16)
    )
    grad_wquery = jnp.einsum("td,tc->dc", full_in, grad_queries, preferred_element_type=jnp.float32)
    grad_wkey = jnp.einsum("td,tc->dc", full_in, grad_keys, preferred_element_type=jnp.float32)
    grad_wvalue = jnp.einsum("td,tc->dc", full_in, grad_vals, preferred_element_type=jnp.float32)
    grad_bquery = jnp.sum(grad_queries.astype(jnp.float32), axis=0)
    grad_bvalue = jnp.sum(grad_vals.astype(jnp.float32), axis=0)

    def input_term(start, count):
        total = jnp.einsum("tc,dc->td", grad_queries, w_query, preferred_element_type=jnp.float32)
        total = total + jnp.einsum(
            "tc,dc->td", grad_keys, w_key, preferred_element_type=jnp.float32
        )
        return total + jnp.einsum(
            "tc,dc->td", grad_vals, w_value, preferred_element_type=jnp.float32
        )

    grad_input = grad_h1 + back_sum(input_term, share)
    matrices = (
        grad_wquery[None],
        grad_wkey[None],
        grad_wvalue[None],
        grad_wout[None],
        grad_wup[None],
        grad_wdown[None],
    )
    vectors = (
        spread(grad_bquery, D)[None],
        spread(grad_bvalue, D)[None],
        spread(grad_ckey, D)[None],
        spread(grad_cval, D)[None],
        grad_bout[None],
        grad_again[None],
        grad_ashift[None],
        spread(grad_bup, FF)[None],
        grad_bdown[None],
        grad_fgain[None],
        grad_fshift[None],
    )
    return (grad_input, matrices, vectors)


def on_device(
    tokens,
    lengths,
    w_query,
    w_key,
    w_value,
    b_query,
    b_value,
    conv_key,
    conv_value,
    w_out,
    b_out,
    attn_gain,
    attn_shift,
    w_up,
    b_up,
    w_down,
    b_down,
    ffn_gain,
    ffn_shift,
    cotangent,
):
    stacks = (
        w_query,
        w_key,
        w_value,
        b_query,
        b_value,
        conv_key,
        conv_value,
        w_out,
        b_out,
        attn_gain,
        attn_shift,
        w_up,
        b_up,
        w_down,
        b_down,
        ffn_gain,
        ffn_shift,
    )
    total_rows = tokens.shape[0]
    share = total_rows // lax.axis_size("mp")
    place = lax.axis_index("mp") * share
    resid = lax.dynamic_slice_in_dim(tokens, place, share, 0).astype(jnp.float32)
    layer = 0
    params = tuple((stack[layer] for stack in stacks))
    result, kept = layer_forward(tokens, resid, lengths, params, share)
    kept_all = [kept]
    activations = result.astype(jnp.bfloat16)
    grad_out = cotangent.astype(jnp.float32)
    matrix_list = [None] * LAYERS
    vector_list = [None] * LAYERS
    for layer in reversed(range(LAYERS)):
        params = tuple((stack[layer] for stack in stacks))
        grad_out, matrices, vectors = layer_backward(
            grad_out, kept_all[layer], params, lengths, share
        )
        matrix_list[layer] = matrices
        vector_list[layer] = vectors
    grad_wquery, grad_wkey, grad_wvalue, grad_wout, grad_wup, grad_wdown = tuple(
        (jnp.concatenate([entry[index] for entry in matrix_list], axis=0) for index in range(6))
    )
    (
        grad_bquery,
        grad_bvalue,
        grad_ckey,
        grad_cval,
        grad_bout,
        grad_again,
        grad_ashift,
        grad_bup,
        grad_bdown,
        grad_fgain,
        grad_fshift,
    ) = tuple(
        (jnp.concatenate([entry[index] for entry in vector_list], axis=0) for index in range(11))
    )
    grad_wquery, grad_wkey, grad_wvalue, grad_wout, grad_wup, grad_wdown = (
        lax.psum_scatter(grad_wquery, "dp", scatter_dimension=1, tiled=True),
        lax.psum_scatter(grad_wkey, "dp", scatter_dimension=1, tiled=True),
        lax.psum_scatter(grad_wvalue, "dp", scatter_dimension=1, tiled=True),
        lax.psum_scatter(grad_wout, "dp", scatter_dimension=2, tiled=True),
        lax.psum_scatter(grad_wup, "dp", scatter_dimension=1, tiled=True),
        lax.psum_scatter(grad_wdown, "dp", scatter_dimension=2, tiled=True),
    )
    (
        grad_bquery,
        grad_bvalue,
        grad_ckey,
        grad_cval,
        grad_bout,
        grad_again,
        grad_ashift,
        grad_bup,
        grad_bdown,
        grad_fgain,
        grad_fshift,
    ) = lax.psum(
        (
            grad_bquery,
            grad_bvalue,
            grad_ckey,
            grad_cval,
            grad_bout,
            grad_again,
            grad_ashift,
            grad_bup,
            grad_bdown,
            grad_fgain,
            grad_fshift,
        ),
        ("dp", "mp"),
    )
    return (
        activations,
        grad_out,
        grad_wquery,
        grad_wkey,
        grad_wvalue,
        grad_bquery,
        grad_bvalue,
        grad_ckey,
        grad_cval,
        grad_wout,
        grad_bout,
        grad_again,
        grad_ashift,
        grad_wup,
        grad_bup,
        grad_wdown,
        grad_bdown,
        grad_fgain,
        grad_fshift,
    )


BF = jnp.bfloat16
F32 = jnp.float32
MESH = pl.DeviceIdType.MESH
ROWS = 256
QUARTERS = 4
CHANS = D // QUARTERS
QHEADS = CHANS // HEAD_DIM
SEQ = QUARTERS * ROWS
REACH = WINDOW // 2
PREACH = POOL_WINDOW // 2 // STRIDE
OWNP = ROWS // STRIDE
KW = ROWS + 2 * REACH
KP = OWNP + 2 * PREACH
KEYS = KW + KP
QB = 128
NEAR = QB + 2 * REACH
FAR = QB // STRIDE + 2 * PREACH
COMP = 800
HALFC = COMP // 2
FRONT = 256
KVROWS = 1408
BASE = 288
PIECE = D // 8
BIG_NEG = -1e30
SCALE = HEAD_DIM ** -0.5
VROWS = 64
TILES = 2 * CHANS // 128


def nn(a, b):
    return jnp.dot(a, b, preferred_element_type=F32)


def nt(a, b):
    return lax.dot_general(a, b, (((1,), (1,)), ((), ())), preferred_element_type=F32)


def tn(a, b):
    return lax.dot_general(a, b, (((0,), (0,)), ((), ())), preferred_element_type=F32)


def rows_iota(rows, cols):
    return lax.broadcasted_iota(jnp.int32, (rows, cols), 0)


def cols_iota(rows, cols):
    return lax.broadcasted_iota(jnp.int32, (rows, cols), 1)


def mean_row(v):
    return jnp.mean(v, axis=-1, keepdims=True)


def sum_col(v):
    return jnp.sum(v, axis=0, keepdims=True)


def kernel(
    len_ref, tok, wk, wv, wq, wo, wup, wdown, bq, bv, ck, cv, bup, bo, ag, ash, bd, fg, fs, cot,
    act_out, gtok, gmats, gvec,
    W, VEC, kvf, KV, KVS, Q, CTX, P, maskn, maskf, n1, r1, y1, y1b, dg, av,
    yT, fT, gab, GKV, pt, GQ, VG,
    CR, S1, S2, ZR, HL, HR, HLL, SL, SR, GVR, GVZ, VO,
    lsem, asend, arecv, zsend, zrecv, lsend, hsend, hrecv, rsend, rrecv, zsum, gsend, grecv,
):
    acc, n2, xT, gub = gtok, y1, yT, y1b
    dp = lax.axis_index("dp")
    z = lax.axis_index("mp")
    c = lax.rem(dp, 2)
    x = lax.rem(lax.div(dp, 2), 2)
    y = lax.div(dp, 4)
    core = (dp + 1 - 2 * c, z)
    xdev = (dp + 2 - 4 * x, z)
    ydev = (dp + 4 - 8 * y, z)
    yx = 2 * y + x
    length = len_ref[0]

    def zdev(step):
        return (dp, lax.rem(z + step, QUARTERS))

    def rcopy(src, dst, ssem, rsem, dev):
        return pltpu.make_async_remote_copy(
            src_ref=src, dst_ref=dst, send_sem=ssem, recv_sem=rsem,
            device_id=dev, device_id_type=MESH,
        )

    def loads():
        parts = [(wk, 0), (wv, CHANS), (wq, 2 * CHANS), (wo, 3 * CHANS)]
        copies = [
            pltpu.make_async_copy(src, W.at[0, z, at : at + CHANS, :], lsem.at[i])
            for i, (src, at) in enumerate(parts)
        ]
        copies.append(pltpu.make_async_copy(wup, W.at[1, z], lsem.at[4]))
        copies.append(pltpu.make_async_copy(wdown, W.at[2, z], lsem.at[5]))
        return copies

    own = loads()
    for cp in own:
        cp.start()
    HL[...] = jnp.zeros_like(HL)
    HR[...] = jnp.zeros_like(HR)
    HLL[...] = jnp.zeros_like(HLL)
    for m in range(3):
        ZR[m, z] = jnp.zeros((PIECE, D), BF)
        ZR[m, QUARTERS] = jnp.zeros((PIECE, D), BF)
    barrier = pltpu.get_barrier_semaphore()
    for dev in (core, xdev, ydev, zdev(1), zdev(2), zdev(3)):
        pl.semaphore_signal(barrier, inc=1, device_id=dev, device_id_type=MESH)
    vpack = VG.at[0:16, :]
    vpack[...] = jnp.zeros_like(vpack)
    vpack[0:1, :] = bup[...]
    vpack[1:2, CHANS : 2 * CHANS] = bv[...]
    vpack[1:2, 2 * CHANS : 3 * CHANS] = bq[...]
    for t in range(5):
        vpack[2 + t : 3 + t, 0:CHANS] = ck[t]
        vpack[2 + t : 3 + t, CHANS : 2 * CHANS] = cv[t]
    VEC[z] = vpack[...]
    pl.semaphore_wait(barrier, 6)

    def block(j):
        return pl.ds(pl.multiple_of(j * PIECE, PIECE), PIECE)

    piece_me = c * 4 + yx
    piece_x = c * 4 + 2 * y + 1 - x
    piece_y = c * 4 + 2 * (1 - y) + x
    piece_d = c * 4 + 2 * (1 - y) + 1 - x
    LO, HI = pl.ds(0, D // 2), pl.ds(D // 2, D // 2)
    ALL = pl.ds(0, D)
    CHUNKS = 9
    ends = [(m, d) for d in (1, 2, 3) for m in (0, 1, 2)]
    inner = [(0, 1), (0, 2), (1, 1), (1, 2), (2, 1), (2, 2), (0, 3), (1, 3), (2, 3)]
    sources = [(1, 2, 3), (2, 0, 3), (1, 3, 0), (2, 1, 0)]
    targets = [(3, 2, 1, 0), (3, 0, 2, 1), (0, 3, 1, 2), (0, 1, 2, 3)]
    at_end = (z == 0) | (z == QUARTERS - 1)

    def table(values, bits=2):
        word = sum(v << (bits * i) for i, v in enumerate(values))
        return jnp.int32(word - (1 << 32) if word >> 31 else word)

    def lookup(word, i, bits=2):
        return lax.bitwise_and(lax.shift_right_logical(word, bits * i), (1 << bits) - 1)

    def by_place(a, b):
        return lax.select(at_end, a, b)

    mats_of = by_place(table(m for m, d in ends), table(m for m, d in inner))
    dist_of = by_place(table(d for m, d in ends), table(d for m, d in inner))
    looks_of = by_place(table((1, 2, 4, 5, 7, 8, 9), 4), table((2, 4, 7, 8, 9, 9, 9), 4))
    sends_of = by_place(table((1, 2, 4, 5, 6, 7, 8), 4), table((2, 3, 4, 5, 6, 7, 8), 4))

    def source(d):
        return lookup(table(v for row in sources for v in row), 3 * z + d - 1)

    def target(t):
        return lookup(table(v for row in targets for v in row), 4 * z + t)

    def chunk(k):
        return lookup(mats_of, k), source(lookup(dist_of, k))

    def own_z(m, up):
        src = W.at[m, z, block(piece_me), :]
        return rcopy(src, src, zsend.at[m, up], zrecv.at[m, z], (dp, z + 2 * up - 1))

    def relay(m, src, dev):
        ref = W.at[m, src, block(piece_me), :]
        return rcopy(ref, ref, lsend.at[m, src], zrecv.at[m, src], dev)

    def own_vec(up):
        src = VEC.at[z]
        return rcopy(src, src, zsend.at[3, up], zrecv.at[3, z], (dp, z + 2 * up - 1))

    def relay_vec(src, dev):
        ref = VEC.at[src]
        return rcopy(ref, ref, lsend.at[3, src], zrecv.at[3, src], dev)

    def onward(src):
        return jnp.where(src > z, z > 0, z < QUARTERS - 1)

    def next_dev(src):
        return (dp, jnp.where(src > z, z - 1, z + 1))

    def plane(k, which, piece, cols, dev):
        m, src = chunk(k)
        ref = W.at[m, src, block(piece), cols]
        return rcopy(ref, ref, asend.at[k, which], arecv.at[k, which], dev)

    def look(k):
        m, src = chunk(k)

        @pl.when(m == 0)
        def _():
            relay_vec(src, core).wait_recv()
            pl.when(onward(src))(lambda: relay_vec(src, next_dev(src)).start())

        relay(m, src, core).wait_recv()
        pl.when(onward(src))(lambda: relay(m, src, next_dev(src)).start())

    def first(k):
        plane(k, 1, piece_me, ALL, xdev).start()
        plane(k, 2, piece_me, ALL, ydev).start()

    def second(k):
        plane(k, 1, piece_x, ALL, xdev).wait_recv()
        plane(k, 3, piece_x, LO, ydev).start()
        plane(k, 2, piece_y, ALL, ydev).wait_recv()
        plane(k, 4, piece_y, HI, xdev).start()

    def half(j):
        return pl.ds(pl.multiple_of(j * (D // 2), D // 2), D // 2)

    def cross(k, j):
        m, src = chunk(k)
        ref = W.at[m, src, half(j), :]
        return rcopy(ref, ref, asend.at[k, 5], arecv.at[k, 5], core)

    def third(k):
        plane(k, 3, piece_d, LO, ydev).wait_recv()
        plane(k, 4, piece_d, HI, xdev).wait_recv()
        cross(k, c).start()

    def fourth(k):
        cross(k, 1 - c).wait_recv()

    def looks(i):
        return jnp.where(i < 0, 0, lookup(looks_of, lax.clamp(0, i, 6), 4))

    def sends(i):
        return jnp.where(i < 0, 0, jnp.where(i < 7, lookup(sends_of, lax.clamp(0, i, 6), 4), CHUNKS))

    def each(fn):
        def body(k, carry):
            fn(k)
            return carry

        return body

    def gather_slot(i, carry):
        lax.fori_loop(looks(i - 1), looks(i), each(look), 0)
        lax.fori_loop(sends(i - 1), sends(i), each(first), 0)
        for lag, stage in ((1, second), (2, third), (3, fourth)):
            k = i - lag
            pl.when((k >= 0) & (k < CHUNKS))(lambda stage=stage, k=k: stage(k))
        return carry

    def gather_done(k, carry):
        m, src = chunk(k)

        @pl.when(onward(src))
        def _():
            relay(m, src, core).wait_send()
            pl.when(m == 0)(lambda: relay_vec(src, core).wait_send())

        plane(k, 1, piece_me, ALL, xdev).wait_send()
        plane(k, 2, piece_me, ALL, ydev).wait_send()
        plane(k, 3, piece_x, LO, ydev).wait_send()
        plane(k, 4, piece_y, HI, xdev).wait_send()
        cross(k, c).wait_send()
        return carry

    def got(s):
        return lax.rem(z + QUARTERS - s, QUARTERS)

    def both(fn):
        pl.when(z > 0)(lambda: fn(0))
        pl.when(z < QUARTERS - 1)(lambda: fn(1))

    both(lambda up: own_vec(up).start())
    for m, waits in enumerate((own[:4], own[4:5], own[5:])):
        for cp in waits:
            cp.wait()
        both(lambda up: own_z(m, up).start())

    def own_sent(up):
        own_vec(up).wait_send()
        for m in range(3):
            own_z(m, up).wait_send()

    base = z * ROWS
    start = lax.select(z < 2, jnp.int32(0), jnp.int32(SEQ - COMP))
    place = pl.multiple_of(start - base + BASE + FRONT, 32)
    start = pl.multiple_of(start, 32)
    kvf[...] = jnp.zeros_like(kvf)
    for b in range(2):
        i = base + b * QB + cols_iota(1, QB)
        j = base - REACH + b * QB + rows_iota(NEAR, 1)
        ok = (jnp.abs(i - j) <= REACH) & (j >= 0) & (j < length)
        maskn[b] = jnp.where(ok, 0.0, BIG_NEG)
        j = (OWNP * z - PREACH + b * (QB // STRIDE) + rows_iota(FAR, 1)) * STRIDE
        ok = (jnp.abs(i - j) <= POOL_WINDOW // 2) & (j >= 0) & (j < length)
        maskf[b] = jnp.where(ok, 0.0, BIG_NEG)
    own_rows = pl.ds(pl.multiple_of(base, ROWS), ROWS)
    xb = tok[own_rows, :]
    acc[...] = jnp.zeros_like(acc)

    def taps(zq, t):
        return VEC[zq, 2 + t : 3 + t, 0 : 2 * CHANS]

    def strided(t):
        at = pl.ds(FRONT + BASE - POOL_WINDOW // 2 - 2 + t, KP, stride=STRIDE)
        return jnp.concatenate([kvf[i, at, :] for i in range(TILES)], axis=1)

    def tile(i):
        return slice(i * 128, (i + 1) * 128)

    def window(lo, rows):
        return jnp.concatenate([kvf[i, lo : lo + rows, :] for i in range(TILES)], axis=1)

    def quarter(s):
        return lax.select(s == 0, z, source(lax.max(s, 1)))

    def attend(s, carry):
        zq = quarter(s)
        for blk in range(2):
            xr = tok[pl.ds(pl.multiple_of(start + blk * HALFC, 16), HALFC), :]
            kv = nt(xr, W[0, zq, 0 : 2 * CHANS, :]) + VEC[zq, 1:2, 0 : 2 * CHANS]
            pos = start + blk * HALFC + rows_iota(HALFC, 1)
            kvb = jnp.where(pos < length, kv.astype(BF).astype(F32), 0.0)
            for i in range(TILES):
                kvf[i, pl.ds(pl.multiple_of(place + blk * HALFC, 8), HALFC), :] = kvb[:, tile(i)]
        KVS[zq] = window(FRONT, COMP).astype(BF)
        KV[zq, 0:KW, :] = window(FRONT + BASE - REACH, KW).astype(BF)
        pooled = jnp.zeros((KP, 2 * CHANS), F32)
        for t in range(5):
            pooled = pooled + taps(zq, t) * strided(t)
        KV[zq, KW:KEYS, :] = pooled.astype(BF)
        qz = nt(xb, W[0, zq, 2 * CHANS : 3 * CHANS, :]) + VEC[zq, 1:2, 2 * CHANS : 3 * CHANS]
        Q[zq] = qz.astype(BF)
        for b in range(2):
            live = base + b * QB + cols_iota(1, QB) < length
            n0, f0 = b * QB, KW + b * (QB // STRIDE)
            for h in range(QHEADS):
                kl = slice(h * HEAD_DIM, (h + 1) * HEAD_DIM)
                vl = slice(CHANS + h * HEAD_DIM, CHANS + (h + 1) * HEAD_DIM)
                qh = Q[zq, b * QB : (b + 1) * QB, kl]
                sn = nt(KV[zq, n0 : n0 + NEAR, kl], qh) * SCALE + maskn[b]
                sf = nt(KV[zq, f0 : f0 + FAR, kl], qh) * SCALE + maskf[b]
                peak = jnp.maximum(
                    jnp.max(sn, axis=0, keepdims=True), jnp.max(sf, axis=0, keepdims=True)
                )
                en, ef = jnp.exp(sn - peak), jnp.exp(sf - peak)
                inv = 1.0 / (sum_col(en) + sum_col(ef))
                pn, pf = en * inv, ef * inv
                P[zq, h, b, 0:NEAR, :] = pn
                P[zq, h, b, NEAR : NEAR + FAR, :] = pf
                ct = tn(KV[zq, n0 : n0 + NEAR, vl], pn.astype(BF))
                ct = ct + tn(KV[zq, f0 : f0 + FAR, vl], pf.astype(BF))
                ct = jnp.where(live, ct, 0.0)
                CTX[zq, b * QB : (b + 1) * QB, kl] = ct.T.astype(BF)
        acc[...] += nn(CTX[zq], W[0, zq, 3 * CHANS : D, :])
        lax.fori_loop(lookup_slots(s), lookup_slots(s + 1), gather_slot, 0)
        return carry

    def lookup_slots(s):
        return jnp.where(s == 0, 0, jnp.where(s == 1, 4, jnp.where(s == 2, 7, s + 7)))

    lax.fori_loop(0, QUARTERS, attend, 0)

    def store_T(dst, v, cols):
        vt = v.T.astype(BF)
        for j in range(8):
            to = (j % 2) * 4 + j // 2
            dst[to * PIECE : (to + 1) * PIECE, cols] = vt[j * PIECE : (j + 1) * PIECE]

    def span(i, size):
        if isinstance(i, int):
            return pl.ds(i * size, size)
        return pl.ds(pl.multiple_of(i * size, size), size)

    def norm_one(i, carry):
        rows = span(i, QB)
        res = tok[pl.ds(pl.multiple_of(base + i * QB, QB), QB), :].astype(F32)
        hid = res + (acc[rows, :] + bo[...])
        cen = hid - mean_row(hid)
        r = lax.rsqrt(mean_row(cen * cen) + epsilon)
        n = cen * r
        n1[rows, :] = n
        r1[rows, :] = r
        out = n * ag[...] + ash[...]
        y1[rows, :] = out
        y1b[rows, :] = out.astype(BF)
        store_T(yT, out, rows)
        acc[rows, :] = jnp.zeros_like(out)
        return carry

    lax.fori_loop(0, ROWS // QB, norm_one, 0)

    def feed(s, carry):
        zq = quarter(s)

        def up(i, carry):
            cols = span(i, ROWS)
            u = nn(y1b[...], W[1, zq, :, cols]) + VEC[zq, 0:1, cols]
            cdf = 0.5 * (1.0 + lax.erf(u * (0.5 ** 0.5)))
            dg[zq, :, cols] = cdf + u * jnp.exp(-0.5 * u * u) * ((2.0 * 3.141592653589793) ** -0.5)
            av[zq, :, cols] = (u * cdf).astype(BF)
            return carry

        for i in range(D // ROWS):
            up(i, 0)
        acc[...] += nn(av[zq], W[2, zq])
        lax.fori_loop(11, jnp.where(s == 2, 12, 11), gather_slot, 0)
        return carry

    lax.fori_loop(0, QUARTERS, feed, 0)
    VG[...] = jnp.zeros_like(VG)
    GEN = 8 * QUARTERS

    def add_row(row, v):
        VG[row : row + 1, :] += sum_col(v)

    def norm_two(i, carry):
        rows = span(i, QB)
        hid = y1[rows, :] + (acc[rows, :] + bd[...])
        cen = hid - mean_row(hid)
        r = lax.rsqrt(mean_row(cen * cen) + epsilon)
        n = cen * r
        act_out[rows, :] = (n * fg[...] + fs[...]).astype(BF)
        g = cot[rows, :].astype(F32)
        add_row(GEN + 4, g * n)
        add_row(GEN + 5, g)
        e = g * fg[...]
        gh2 = r * (e - mean_row(e) - n * mean_row(e * n))
        acc[rows, :] = gh2
        gf = gh2.astype(BF)
        gab[rows, :] = gf
        gff = gf.astype(F32)
        add_row(GEN + 3, gff)
        store_T(fT, gff, rows)
        return carry

    lax.fori_loop(0, ROWS // QB, norm_two, 0)

    PARTS = 12

    def part(r):
        m = lax.select(r < 8, 1 + lax.rem(r, 2), 0)
        t = lax.select(r < 8, lax.div(r, 2), r - 8)
        return m, t

    def r_core(r):
        m, t = part(r)
        src = W.at[m, target(t), half(1 - c), :]
        return rcopy(src, CR.at[r], rsend.at[r, 0], rrecv.at[r, 0], core)

    def blk4(r, yy, xx, cols):
        return CR.at[r, block(2 * yy + xx), cols]

    def r_stage1(r, i):
        if i < 2:
            src, dev = blk4(r, i, 1 - x, LO), xdev
        else:
            src, dev = blk4(r, 1 - y, i - 2, HI), ydev
        return rcopy(src, S1.at[r, i], rsend.at[r, 1 + i], rrecv.at[r, 1 + i], dev)

    def r_stage2(r, i):
        if i == 0:
            src, dev = blk4(r, 1 - y, x, LO), ydev
        else:
            src, dev = blk4(r, y, 1 - x, HI), xdev
        return rcopy(src, S2.at[r, i], rsend.at[r, 5 + i], rrecv.at[r, 5 + i], dev)

    def r_z(r):
        m, t = part(r)
        dst = target(t)
        left = dst < z
        slot = jnp.where(left & (dst == z - 1), QUARTERS, dst)
        src = CR.at[r, block(yx), :]
        dev = (dp, jnp.where(left, z - 1, z + 1))
        return rcopy(src, ZR.at[m, slot], rsend.at[r, 7], zsum.at[m, slot], dev)

    def z_in(m, slot):
        ref = ZR.at[m, slot]
        return rcopy(ref, ref, zsum.at[m, slot], zsum.at[m, slot], core)

    def upstream(dst):
        return jnp.where(dst < z, z < QUARTERS - 1, z > 0)

    def reduce1(r):
        m, t = part(r)
        r_core(r).wait_recv()
        zq = target(t)

        def add(i, carry):
            CR[r, block(i), :] = CR[r, block(i), :] + W[m, zq, block(4 * c + i), :]
            return carry

        lax.fori_loop(0, 4, add, 0)
        for i in range(4):
            r_stage1(r, i).start()

    def reduce2(r):
        for i in range(4):
            r_stage1(r, i).wait_recv()
        for i in range(2):
            a = blk4(r, i, x, LO)
            a[...] = a[...] + S1[r, i]
            a = blk4(r, y, i, HI)
            a[...] = a[...] + S1[r, 2 + i]
        for i in range(2):
            r_stage2(r, i).start()

    def reduce3(r):
        for i in range(2):
            r_stage2(r, i).wait_recv()
        for i, cols in enumerate((LO, HI)):
            a = blk4(r, y, x, cols)
            a[...] = a[...] + S2[r, i]
        dst = target(part(r)[1])
        pl.when((dst != z) & jnp.logical_not(upstream(dst)))(lambda: r_z(r).start())

    def reduce4(r):
        m, t = part(r)
        dst = target(t)

        @pl.when((dst != z) & upstream(dst))
        def _():
            z_in(m, dst).wait_recv()
            CR[r, block(yx), :] = CR[r, block(yx), :] + ZR[m, dst]
            r_z(r).start()

    def stage(fn, r):
        pl.when((r >= 0) & (r < PARTS))(lambda: fn(r))

    def reduce_slot(i):
        pl.when(i == 0)(lambda: reduce1(jnp.int32(0)))
        stage(reduce1, jnp.where(i < 7, i + 1, jnp.where(i == 7, -1, i)))
        stage(reduce2, i - 1)
        stage(reduce3, i - 2)
        stage(reduce4, i - 3)

    def weight_grad(left, right, dst, width):
        dst[:, 0:width] = nn(left[...], right).astype(BF)

    def feed_back(s, carry):
        zq = target(s)
        vrow = pl.multiple_of(8 * zq, 8)

        def hidden(i, carry):
            cols = span(i, ROWS)
            gact = nt(gab[...], W[2, zq, cols, :])
            gu = (gact * dg[zq, :, cols]).astype(BF)
            gub[:, cols] = gu
            VG[pl.ds(vrow, 1), cols] = sum_col(gu.astype(F32))
            return carry

        for i in range(D // ROWS):
            hidden(i, 0)
        acc[...] += nt(gub[...], W[1, zq])
        weight_grad(yT, gub[...], W.at[1, zq], D)
        r_core(2 * s).start()
        weight_grad(fT, av[zq], W.at[2, zq], D)
        r_core(2 * s + 1).start()
        pl.when(s > 0)(lambda: reduce_slot(s - 1))
        return carry

    lax.fori_loop(0, CHUNKS, gather_done, 0)
    both(own_sent)
    lax.fori_loop(0, QUARTERS, feed_back, 0)

    def norm_back(i, carry):
        rows = span(i, QB)
        gy = acc[rows, :]
        n = n1[rows, :]
        add_row(GEN + 1, gy * n)
        add_row(GEN + 2, gy)
        e = gy * ag[...]
        gh1 = r1[rows, :] * (e - mean_row(e) - n * mean_row(e * n))
        acc[rows, :] = gh1
        ga = gh1.astype(BF)
        gab[rows, :] = ga
        gaf = ga.astype(F32)
        add_row(GEN, gaf)
        store_T(fT, gaf, rows)
        store_T(xT, tok[pl.ds(pl.multiple_of(base + i * QB, QB), QB), :].astype(F32), rows)
        return carry

    lax.fori_loop(0, ROWS // QB, norm_back, 0)

    def hl(zq):
        return rcopy(SL.at[zq], HL.at[zq], hsend.at[0, zq], hrecv.at[0, zq], zdev(3))

    def hr(zq):
        return rcopy(SR.at[zq], HR.at[zq], hsend.at[1, zq], hrecv.at[1, zq], zdev(1))

    def hll(zq):
        return rcopy(
            SL.at[zq, REACH : REACH + 16, :], HLL.at[zq], hsend.at[2, zq], hrecv.at[2, zq], zdev(2)
        )

    def attend_back(s, carry):
        zq = target(s)
        gc = nt(gab[...], W[0, zq, 3 * CHANS : D, :])
        alive = base + rows_iota(ROWS, 1) < length
        gcb = jnp.where(alive, gc, 0.0).astype(BF)
        GKV[zq] = jnp.zeros((KEYS, 2 * CHANS), F32)
        for b in range(2):
            n0, f0 = b * QB, KW + b * (QB // STRIDE)
            for h in range(QHEADS):
                kl = slice(h * HEAD_DIM, (h + 1) * HEAD_DIM)
                vl = slice(CHANS + h * HEAD_DIM, CHANS + (h + 1) * HEAD_DIM)
                gch = gcb[b * QB : (b + 1) * QB, kl]
                qh = Q[zq, b * QB : (b + 1) * QB, kl]
                pn = P[zq, h, b, 0:NEAR, :]
                pf = P[zq, h, b, NEAR : NEAR + FAR, :]
                gpn = nt(KV[zq, n0 : n0 + NEAR, vl], gch)
                gpf = nt(KV[zq, f0 : f0 + FAR, vl], gch)
                delta = sum_col(pn * gpn) + sum_col(pf * gpf)
                gsn = (pn * (gpn - delta)).astype(BF)
                gsf = (pf * (gpf - delta)).astype(BF)
                qt = tn(KV[zq, n0 : n0 + NEAR, kl], gsn) + tn(KV[zq, f0 : f0 + FAR, kl], gsf)
                GQ[zq, b * QB : (b + 1) * QB, 2 * CHANS + h * HEAD_DIM : 2 * CHANS + (h + 1) * HEAD_DIM] = (
                    (qt * SCALE).T.astype(BF)
                )
                GKV[zq, n0 : n0 + NEAR, kl] += nn(gsn, qh) * SCALE
                GKV[zq, f0 : f0 + FAR, kl] += nn(gsf, qh) * SCALE
                GKV[zq, n0 : n0 + NEAR, vl] += nn(pn.astype(BF), gch)
                GKV[zq, f0 : f0 + FAR, vl] += nn(pf.astype(BF), gch)
        vrow = pl.multiple_of(8 * zq, 8)
        for i in range(TILES):
            kvf[i, FRONT : FRONT + COMP, :] = KVS[zq, :, tile(i)].astype(F32)
        gp = GKV[zq, KW:KEYS, :]
        for t in range(5):
            VG[pl.ds(vrow + 2 + t, 1), 0 : 2 * CHANS] = sum_col(gp * strided(t))
        SL[zq, 0:REACH, :] = GKV[zq, 0:REACH, :].astype(BF)
        SL[zq, REACH : REACH + 80, :] = GKV[zq, KW : KW + 80, :].astype(BF)
        SR[zq, 0:REACH, :] = GKV[zq, KW - REACH : KW, :].astype(BF)
        SR[zq, REACH : REACH + OWNP, :] = GKV[zq, KEYS - OWNP : KEYS, :].astype(BF)
        pl.when(z > 0)(lambda: hl(zq).start())
        pl.when(z < QUARTERS - 1)(lambda: hr(zq).start())
        pl.when(z > 1)(lambda: hll(zq).start())
        reduce_slot(3 + s)
        return carry

    lax.fori_loop(0, QUARTERS, attend_back, 0)

    def project_back(s, carry):
        zq = target(s)
        pl.when(z < QUARTERS - 1)(lambda: hl(zq).wait_recv())
        pl.when(z > 0)(lambda: hr(zq).wait_recv())
        pl.when(z < QUARTERS - 2)(lambda: hll(zq).wait_recv())
        near = GKV.at[zq]
        near[REACH : 2 * REACH, :] += HR[zq, 0:REACH, :].astype(F32)
        near[ROWS : ROWS + REACH, :] += HL[zq, 0:REACH, :].astype(F32)
        gp = GKV[zq, KW + OWNP : KW + 2 * OWNP, :] + HR[zq, REACH : REACH + OWNP, :].astype(F32)
        gp = gp + HL[zq, REACH : REACH + OWNP, :].astype(F32)
        nxt = GKV[zq, KW + 2 * OWNP : KW + 2 * OWNP + 1, :]
        nxt = nxt + HL[zq, REACH + OWNP : REACH + OWNP + 16, :].astype(F32)[0:1, :]
        nxt = nxt + HLL[zq].astype(F32)[0:1, :]
        gp1 = jnp.concatenate([gp[1:, :], nxt], axis=0)
        fills = (
            taps(zq, 2) * gp,
            taps(zq, 3) * gp,
            taps(zq, 4) * gp + taps(zq, 0) * gp1,
            taps(zq, 1) * gp1,
        )
        for k, fill in enumerate(fills):
            for i in range(TILES):
                pt[i, pl.ds(k, OWNP, stride=STRIDE), :] = fill[:, tile(i)]
        back = jnp.concatenate([pt[i] for i in range(TILES)], axis=1)
        alive = base + rows_iota(ROWS, 1) < length
        gkv = GKV[zq, REACH : REACH + ROWS, :] + jnp.where(alive, back, 0.0)
        GQ[zq, :, 0 : 2 * CHANS] = gkv.astype(BF)
        vrow = pl.multiple_of(8 * zq, 8)
        VG[pl.ds(vrow + 1, 1), 0 : 3 * CHANS] = sum_col(GQ[zq].astype(F32))

        acc[...] += nn(GQ[zq], W[0, zq, 0 : 3 * CHANS, :])
        weight_grad(xT, GQ[zq], W.at[0, zq], 3 * CHANS)

        W[0, zq, :, 3 * CHANS : D] = nn(fT[...], CTX[zq]).astype(BF)
        r_core(8 + s).start()
        reduce_slot(7 + s)
        return carry

    lax.fori_loop(0, QUARTERS, project_back, 0)
    for zq in range(QUARTERS):
        pl.when(z > 0)(lambda: hl(zq).wait_send())
        pl.when(z < QUARTERS - 1)(lambda: hr(zq).wait_send())
        pl.when(z > 1)(lambda: hll(zq).wait_send())

    half_row = pl.multiple_of(32 * c, 32)
    row_x = pl.multiple_of(half_row + 16 * x, 16)
    row_y = pl.multiple_of(row_x + 8 * y, 8)

    def vrows(at, size):
        return pl.ds(pl.multiple_of(at, 8), size)

    folds = [
        (core, VG.at[vrows(32 - half_row, 32), :], GVR.at[0:32], vrows(half_row, 32)),
        (xdev, VG.at[vrows(half_row + 16 - 16 * x, 16), :], GVR.at[32:48], vrows(row_x, 16)),
        (ydev, VG.at[vrows(row_x + 8 - 8 * y, 8), :], GVR.at[48:56], vrows(row_y, 8)),
    ]

    def fold(i):
        dev, src, dst, keep = folds[i]
        return rcopy(src, dst, gsend.at[i], grecv.at[i], dev)

    def fold_done(i):
        fold(i).wait()
        keep = folds[i][3]
        VG[keep, :] = VG[keep, :] + folds[i][2][...]

    def g_z(s):
        src = VG.at[vrows(row_y, 8), :]
        return rcopy(src, GVZ.at[z], gsend.at[2 + s], grecv.at[2 + s], zdev(s))

    def g_z_in(s):
        dst = GVZ.at[got(s)]
        return rcopy(dst, dst, gsend.at[2 + s], grecv.at[2 + s], core)

    opens = [
        (ydev, vrows(row_y, 8), vrows(row_x + 8 - 8 * y, 8)),
        (xdev, vrows(row_x, 16), vrows(half_row + 16 - 16 * x, 16)),
        (core, vrows(half_row, 32), vrows(32 - half_row, 32)),
    ]

    def unfold(i):
        dev, mine, other = opens[i]
        ref = VO.at[mine, :]
        return rcopy(ref, ref, gsend.at[6 + i], grecv.at[6 + i], dev)

    def unfold_done(i):
        ref = VO.at[opens[i][2], :]
        rcopy(ref, ref, gsend.at[6 + i], grecv.at[6 + i], core).wait_recv()

    def final(m):
        own_part = (11, 6, 7)[m]
        total = CR[own_part, block(yx), :].astype(F32)
        pl.when(z > 0)(lambda: z_in(m, z).wait_recv())
        pl.when(z < QUARTERS - 1)(lambda: z_in(m, QUARTERS).wait_recv())
        gmats[m] = total + ZR[m, z].astype(F32) + ZR[m, QUARTERS].astype(F32)

    def at(r):
        return jnp.int32(r)

    fold(0).start()
    reduce1(at(11))
    reduce2(at(10))
    fold_done(0)
    fold(1).start()
    reduce3(at(9))
    reduce4(at(8))
    fold_done(1)
    fold(2).start()
    reduce2(at(11))
    fold_done(2)
    for s in (1, 2, 3):
        g_z(s).start()
    GVZ[z] = VG[vrows(row_y, 8), :]
    reduce3(at(10))
    reduce4(at(9))
    for s in (1, 2, 3):
        g_z_in(s).wait_recv()
    VO[vrows(row_y, 8), :] = GVZ[0] + GVZ[1] + GVZ[2] + GVZ[3]
    unfold(0).start()
    reduce3(at(11))
    unfold_done(0)
    unfold(1).start()
    reduce4(at(10))
    final(1)
    final(2)
    unfold_done(1)
    unfold(2).start()
    final(0)
    unfold_done(2)
    gvec[...] = VO[...]
    for i in range(3):
        unfold(i).wait_send()
    for s in (1, 2, 3):
        g_z(s).wait_send()

    def sent(r, carry):
        r_core(r).wait_send()
        for i in range(4):
            r_stage1(r, i).wait_send()
        for i in range(2):
            r_stage2(r, i).wait_send()
        pl.when(part(r)[1] < QUARTERS - 1)(lambda: r_z(r).wait_send())
        return carry

    lax.fori_loop(0, PARTS, sent, 0)


def unpack(
    act, gtok, gmats, gvec,
    act_out, gtok_out, gq, gk, gv, gbq, gbv, gck, gcv, go, gbo, gag, gas, gup, gbu, gdown, gbd, gfg, gfs,
):
    act_out[...] = act[...]
    gtok_out[...] = gtok[...]
    gk[...] = gmats[0, :, 0:CHANS]
    gv[...] = gmats[0, :, CHANS : 2 * CHANS]
    gq[...] = gmats[0, :, 2 * CHANS : 3 * CHANS]
    go[...] = gmats[0, :, 3 * CHANS : D].T
    gup[...] = gmats[1]
    gdown[...] = gmats[2]
    for j in range(QUARTERS):
        at = slice(j * CHANS, (j + 1) * CHANS)
        row = 8 * j
        gbu[:, j * D : (j + 1) * D] = gvec[row : row + 1, :]
        gbv[:, at] = gvec[row + 1 : row + 2, CHANS : 2 * CHANS]
        gbq[:, at] = gvec[row + 1 : row + 2, 2 * CHANS : 3 * CHANS]
        for t in range(5):
            gck[t, :, at] = gvec[row + 2 + t : row + 3 + t, 0:CHANS]
            gcv[t, :, at] = gvec[row + 2 + t : row + 3 + t, CHANS : 2 * CHANS]
    for j, out in enumerate((gbo, gag, gas, gbd, gfg, gfs)):
        out[...] = gvec[8 * QUARTERS + j : 8 * QUARTERS + j + 1, :]


def fused_layer(
    tokens, lengths, w_query, w_key, w_value, b_query, b_value, conv_key, conv_value, w_out,
    b_out, attn_gain, attn_shift, w_up, b_up, w_down, b_down, ffn_gain, ffn_shift, cotangent,
):
    Q4 = QUARTERS
    vm = pltpu.VMEM
    dma = pltpu.SemaphoreType.DMA
    scratch = [
        vm((3, Q4, D, D), BF),
        vm((Q4, 16, D), F32),
        vm((TILES, KVROWS, 128), F32),
        vm((Q4, KEYS, 2 * CHANS), BF),
        vm((Q4, COMP, 2 * CHANS), BF),
        vm((Q4, ROWS, CHANS), BF),
        vm((Q4, ROWS, CHANS), BF),
        vm((Q4, QHEADS, 2, NEAR + FAR, QB), F32),
        vm((2, NEAR, QB), F32),
        vm((2, FAR, QB), F32),
        vm((ROWS, D), F32),
        vm((ROWS, 1), F32),
        vm((ROWS, D), F32),
        vm((ROWS, D), BF),
        vm((Q4, ROWS, D), F32),
        vm((Q4, ROWS, D), BF),
        vm((D, ROWS), BF),
        vm((D, ROWS), BF),
        vm((ROWS, D), BF),
        vm((Q4, KEYS, 2 * CHANS), F32),
        vm((TILES, ROWS, 128), F32),
        vm((Q4, ROWS, 3 * CHANS), BF),
        vm((VROWS, D), F32),
        vm((12, D // 2, D), BF),
        vm((12, 4, PIECE, D // 2), BF),
        vm((12, 2, PIECE, D // 2), BF),
        vm((3, Q4 + 1, PIECE, D), BF),
        vm((Q4, REACH + 80, 2 * CHANS), BF),
        vm((Q4, REACH + OWNP, 2 * CHANS), BF),
        vm((Q4, 16, 2 * CHANS), BF),
        vm((Q4, REACH + 80, 2 * CHANS), BF),
        vm((Q4, REACH + OWNP, 2 * CHANS), BF),
        vm((VROWS, D), F32),
        vm((Q4, 8, D), F32),
        vm((VROWS, D), F32),
        dma((6,)),
        dma((9, 6)),
        dma((9, 6)),
        dma((4, 2)),
        dma((4, Q4)),
        dma((4, Q4)),
        dma((3, Q4)),
        dma((3, Q4)),
        dma((12, 8)),
        dma((12, 7)),
        dma((3, Q4 + 1)),
        dma((9,)),
        dma((9,)),
    ]
    vspec = pl.BlockSpec(memory_space=pltpu.VMEM)
    hspec = pl.BlockSpec(memory_space=pl.ANY)
    packed = pl.pallas_call(
        kernel,
        out_shape=(
            jax.ShapeDtypeStruct((ROWS, D), BF),
            jax.ShapeDtypeStruct((ROWS, D), F32),
            jax.ShapeDtypeStruct((3, PIECE, D), F32),
            jax.ShapeDtypeStruct((VROWS, D), F32),
        ),
        in_specs=[pl.BlockSpec(memory_space=pltpu.SMEM), vspec] + [hspec] * 6 + [vspec] * 12,
        out_specs=(vspec,) * 4,
        scratch_shapes=scratch,
        compiler_params=pltpu.CompilerParams(
            collective_id=0, has_side_effects=True, vmem_limit_bytes=67043328
        ),
        name="layer",
    )(
        lengths, tokens, w_key[0].T, w_value[0].T, w_query[0].T, w_out[0], w_up[0], w_down[0],
        b_query, b_value, conv_key.transpose(1, 0, 2), conv_value.transpose(1, 0, 2), b_up, b_out, attn_gain, attn_shift, b_down,
        ffn_gain, ffn_shift, cotangent,
    )
    row = (1, D)
    shapes = [
        (ROWS, D), (PIECE, CHANS), (PIECE, CHANS), (PIECE, CHANS), row, row, (5, 1, D), (5, 1, D), (CHANS, PIECE),
        row, row, row, (PIECE, D), (1, FF), (PIECE, D), row, row, row,
    ]
    outs = pl.pallas_call(
        unpack,
        out_shape=[jax.ShapeDtypeStruct((ROWS, D), BF)] + [jax.ShapeDtypeStruct(v, F32) for v in shapes],
        in_specs=[vspec] * 4,
        out_specs=[vspec] * 19,
        name="unpack",
    )(*packed)
    act, gtok, gq, gk, gv, gbq, gbv, gck, gcv, go, gbo, gag, gas, gup, gbu, gdown, gbd, gfg, gfs = outs
    return (
        act, gtok, gq[None], gk[None], gv[None], gbq, gbv, gck.transpose(1, 0, 2), gcv.transpose(1, 0, 2), go[None], gbo, gag, gas,
        gup[None], gbu, gdown.T[None], gbd, gfg, gfs,
    )


def solution(mesh):
    small = mesh.shape["dp"] == 8 and mesh.shape["mp"] == QUARTERS
    return jax.shard_map(
        fused_layer if small else on_device,
        mesh=mesh,
        in_specs=(
            P("dp", None),
            P("dp"),
            P(None, None, "mp"),
            P(None, None, "mp"),
            P(None, None, "mp"),
            P(None, "mp"),
            P(None, "mp"),
            P(None, None, "mp"),
            P(None, None, "mp"),
            P(None, "mp", None),
            P(),
            P(),
            P(),
            P(None, None, "mp"),
            P(None, "mp"),
            P(None, "mp", None),
            P(),
            P(),
            P(),
            P(("dp", "mp"), None),
        ),
        out_specs=(
            P(("dp", "mp"), None),
            P(("dp", "mp"), None),
            P(None, "dp", "mp"),
            P(None, "dp", "mp"),
            P(None, "dp", "mp"),
            P(),
            P(),
            P(),
            P(),
            P(None, "mp", "dp"),
            P(),
            P(),
            P(),
            P(None, "dp", "mp"),
            P(),
            P(None, "mp", "dp"),
            P(),
            P(),
            P(),
        ),
        check_vma=False,
    )
```

```python
import jax
import jax.numpy as jnp
from jax import lax
from jax.experimental import pallas as pl
from jax.experimental.pallas import tpu as pltpu
from jax.sharding import PartitionSpec as P

D = 768
HEAD_DIM = 64
FF = 3072
WINDOW = 128
POOL_WINDOW = 512
STRIDE = 4
LAYERS = 1


block_rows = 512
mask_fill = -1000000000.0
epsilon = 1e-05


def norm_rows(hidden, gain, shift):
    center = hidden - jnp.mean(hidden, axis=-1, keepdims=True)
    spread = jnp.mean(center * center, axis=-1, keepdims=True)
    return center * lax.rsqrt(spread + epsilon) * gain + shift


def gelu_exact(values):
    return jax.nn.gelu(values, approximate=False)


def pool_rows(values, kernel):
    seqs, length, chans = values.shape
    width = kernel.shape[0]
    half = width // 2
    pooled_len = length // STRIDE
    padded = jnp.pad(values, ((0, 0), (half, width), (0, 0)))
    total = jnp.zeros((seqs, pooled_len, chans), jnp.float32)
    for offset in range(width):
        total = total + kernel[offset] * padded[:, offset : offset + STRIDE * pooled_len : STRIDE]
    return total


def block_mask(start, lengths):
    reach = WINDOW // 2
    pool_reach = POOL_WINDOW // 2 // STRIDE
    span = block_rows // STRIDE + 2 * pool_reach
    rows = start + jnp.arange(block_rows, dtype=jnp.int32)
    near_pos = start - reach + jnp.arange(block_rows + 2 * reach, dtype=jnp.int32)
    far_pos = (start // STRIDE - pool_reach + jnp.arange(span, dtype=jnp.int32)) * STRIDE
    limit = lengths[:, None, None]
    near_ok = (
        (jnp.abs(rows[:, None] - near_pos[None, :]) <= reach)[None]
        & (near_pos >= 0)[None, None]
        & (near_pos[None, None] < limit)
    )
    far_ok = (
        (jnp.abs(rows[:, None] - far_pos[None, :]) <= POOL_WINDOW // 2)[None]
        & (far_pos >= 0)[None, None]
        & (far_pos[None, None] < limit)
    )
    return jnp.concatenate([near_ok, far_ok], axis=-1)


def padded_keys(keys_loc, vals_loc, far_keys, far_vals):
    reach = WINDOW // 2
    pool_reach = POOL_WINDOW // 2 // STRIDE
    pad_near = ((0, 0), (reach, reach), (0, 0), (0, 0))
    pad_far = ((0, 0), (pool_reach, pool_reach), (0, 0), (0, 0))
    return (
        jnp.pad(keys_loc, pad_near),
        jnp.pad(vals_loc, pad_near),
        jnp.pad(far_keys, pad_far),
        jnp.pad(far_vals, pad_far),
    )


def block_inputs(start, queries, padded):
    near_k, near_v, far_k, far_v = padded
    near_len = block_rows + 2 * (WINDOW // 2)
    span = block_rows // STRIDE + 2 * (POOL_WINDOW // 2 // STRIDE)
    pool_start = start // STRIDE
    q_rows = queries[:, start : start + block_rows]
    keys_b = jnp.concatenate(
        [near_k[:, start : start + near_len], far_k[:, pool_start : pool_start + span]], axis=1
    )
    vals_b = jnp.concatenate(
        [near_v[:, start : start + near_len], far_v[:, pool_start : pool_start + span]], axis=1
    )
    return (q_rows, keys_b, vals_b)


def forward_block(q_rows, keys_b, vals_b, mask, live):
    scale = q_rows.shape[-1] ** (-0.5)
    scores = (
        jnp.einsum("sqhe,skhe->shqk", q_rows, keys_b, preferred_element_type=jnp.float32) * scale
    )
    scores = jnp.where(mask[:, None], scores, mask_fill)
    peak = jnp.max(scores, axis=-1, keepdims=True)
    expo = jnp.exp(scores - peak)
    total = jnp.sum(expo, axis=-1, keepdims=True)
    weights = (expo / total).astype(jnp.bfloat16)
    result = jnp.einsum("shqk,skhe->sqhe", weights, vals_b, preferred_element_type=jnp.float32)
    result = jnp.where(live[:, :, None, None], result, 0.0)
    return (result, peak + jnp.log(total))


def forward_skip(q_rows, keys_b, vals_b, mask, live):
    seqs, rows, heads, size = q_rows.shape
    return (
        jnp.zeros((seqs, rows, heads, size), jnp.float32),
        jnp.zeros((seqs, heads, rows, 1), jnp.float32),
    )


def backward_block(q_rows, keys_b, vals_b, mask, logsum, grad_rows):
    scale = q_rows.shape[-1] ** (-0.5)
    scores = (
        jnp.einsum("sqhe,skhe->shqk", q_rows, keys_b, preferred_element_type=jnp.float32) * scale
    )
    scores = jnp.where(mask[:, None], scores, mask_fill)
    probs = jnp.exp(scores - logsum)
    grad_probs = jnp.einsum(
        "sqhe,skhe->shqk", grad_rows, vals_b, preferred_element_type=jnp.float32
    )
    delta = jnp.sum(probs * grad_probs, axis=-1, keepdims=True)
    grad_scores = (probs * (grad_probs - delta)).astype(jnp.bfloat16)
    grad_q = (
        jnp.einsum("shqk,skhe->sqhe", grad_scores, keys_b, preferred_element_type=jnp.float32)
        * scale
    )
    grad_keys = (
        jnp.einsum("shqk,sqhe->skhe", grad_scores, q_rows, preferred_element_type=jnp.float32)
        * scale
    )
    grad_vals = jnp.einsum(
        "shqk,sqhe->skhe", probs.astype(jnp.bfloat16), grad_rows, preferred_element_type=jnp.float32
    )
    return (grad_q, grad_keys, grad_vals)


def backward_skip(q_rows, keys_b, vals_b, mask, logsum, grad_rows):
    return (
        jnp.zeros(q_rows.shape, jnp.float32),
        jnp.zeros(keys_b.shape, jnp.float32),
        jnp.zeros(vals_b.shape, jnp.float32),
    )


def attend_forward(queries, keys_loc, vals_loc, far_keys, far_vals, lengths):
    length = queries.shape[1]
    padded = padded_keys(keys_loc, vals_loc, far_keys, far_vals)
    longest = jnp.max(lengths)
    results, logsums = ([], [])
    for block in range(length // block_rows):
        start = block * block_rows
        q_rows, keys_b, vals_b = block_inputs(start, queries, padded)
        mask = block_mask(start, lengths)
        live = start + jnp.arange(block_rows, dtype=jnp.int32)[None, :] < lengths[:, None]
        result, logsum = lax.cond(
            start < longest, forward_block, forward_skip, q_rows, keys_b, vals_b, mask, live
        )
        results.append(result)
        logsums.append(logsum)
    return (jnp.concatenate(results, axis=1), logsums)


def attend_backward(
    queries, keys_loc, vals_loc, far_keys, far_vals, lengths, logsums, grad_context
):
    seqs, length, heads, size = queries.shape
    pooled_len = far_keys.shape[1]
    reach = WINDOW // 2
    pool_reach = POOL_WINDOW // 2 // STRIDE
    near_len = block_rows + 2 * reach
    span = block_rows // STRIDE + 2 * pool_reach
    padded = padded_keys(keys_loc, vals_loc, far_keys, far_vals)
    longest = jnp.max(lengths)
    grad_near_k = jnp.zeros((seqs, length + 2 * reach, heads, size), jnp.float32)
    grad_near_v = jnp.zeros((seqs, length + 2 * reach, heads, size), jnp.float32)
    grad_far_k = jnp.zeros((seqs, pooled_len + 2 * pool_reach, heads, size), jnp.float32)
    grad_far_v = jnp.zeros((seqs, pooled_len + 2 * pool_reach, heads, size), jnp.float32)
    grad_queries = []
    for block in range(length // block_rows):
        start = block * block_rows
        pool_start = start // STRIDE
        q_rows, keys_b, vals_b = block_inputs(start, queries, padded)
        mask = block_mask(start, lengths)
        grad_rows = grad_context[:, start : start + block_rows]
        grad_q, grad_keys, grad_vals = lax.cond(
            start < longest,
            backward_block,
            backward_skip,
            q_rows,
            keys_b,
            vals_b,
            mask,
            logsums[block],
            grad_rows,
        )
        grad_queries.append(grad_q)
        grad_near_k = grad_near_k.at[:, start : start + near_len].add(grad_keys[:, :near_len])
        grad_near_v = grad_near_v.at[:, start : start + near_len].add(grad_vals[:, :near_len])
        grad_far_k = grad_far_k.at[:, pool_start : pool_start + span].add(grad_keys[:, near_len:])
        grad_far_v = grad_far_v.at[:, pool_start : pool_start + span].add(grad_vals[:, near_len:])
    return (
        jnp.concatenate(grad_queries, axis=1),
        grad_near_k[:, reach : reach + length],
        grad_near_v[:, reach : reach + length],
        grad_far_k[:, pool_reach : pool_reach + pooled_len],
        grad_far_v[:, pool_reach : pool_reach + pooled_len],
    )


def row_sum(left, right, share):

    def term(start, count):
        return jnp.dot(left, right, preferred_element_type=jnp.float32)

    return lax.psum_scatter(
        term(jnp.int32(0), share * lax.axis_size("mp")), "mp", scatter_dimension=0, tiled=True
    )


def share_rows(values):
    return lax.all_gather(values, "mp", axis=0, tiled=True)


def share_back(values):
    return lax.all_gather(values, "mp", axis=0, tiled=True)


def back_sum(term, share):
    return lax.psum_scatter(
        term(jnp.int32(0), share * lax.axis_size("mp")), "mp", scatter_dimension=0, tiled=True
    )


def spread(values, width):
    whole = jnp.zeros(values.shape[:-1] + (width,), jnp.float32)
    start = lax.axis_index("mp") * values.shape[-1]
    return lax.dynamic_update_slice_in_dim(whole, values, start, values.ndim - 1)


def layer_forward(full_in, resid, lengths, params, share):
    (
        w_query,
        w_key,
        w_value,
        b_query,
        b_value,
        conv_key,
        conv_value,
        w_out,
        b_out,
        attn_gain,
        attn_shift,
        w_up,
        b_up,
        w_down,
        b_down,
        ffn_gain,
        ffn_shift,
    ) = params
    seqs = lengths.shape[0]
    total_rows = full_in.shape[0]
    length = total_rows // seqs
    chans = w_query.shape[1]
    heads = chans // HEAD_DIM
    pooled_len = length // STRIDE
    queries = (jnp.dot(full_in, w_query, preferred_element_type=jnp.float32) + b_query).astype(
        jnp.bfloat16
    )
    keys_loc = jnp.dot(full_in, w_key, preferred_element_type=jnp.float32).astype(jnp.bfloat16)
    vals_loc = (jnp.dot(full_in, w_value, preferred_element_type=jnp.float32) + b_value).astype(
        jnp.bfloat16
    )
    valid = (jnp.arange(length, dtype=jnp.int32)[None, :] < lengths[:, None]).astype(jnp.float32)[
        :, :, None
    ]
    far_keys = pool_rows(
        keys_loc.reshape(seqs, length, chans).astype(jnp.float32) * valid, conv_key
    ).astype(jnp.bfloat16)
    far_vals = pool_rows(
        vals_loc.reshape(seqs, length, chans).astype(jnp.float32) * valid, conv_value
    ).astype(jnp.bfloat16)
    context, logsums = attend_forward(
        queries.reshape(seqs, length, heads, HEAD_DIM),
        keys_loc.reshape(seqs, length, heads, HEAD_DIM),
        vals_loc.reshape(seqs, length, heads, HEAD_DIM),
        far_keys.reshape(seqs, pooled_len, heads, HEAD_DIM),
        far_vals.reshape(seqs, pooled_len, heads, HEAD_DIM),
        lengths,
    )
    context = context.reshape(total_rows, chans).astype(jnp.bfloat16)
    hidden_one = resid + (row_sum(context, w_out, share) + b_out)
    normed = norm_rows(hidden_one, attn_gain, attn_shift)
    full_normed = share_rows(normed.astype(jnp.bfloat16))
    upper = jnp.dot(full_normed, w_up, preferred_element_type=jnp.float32) + b_up
    active = gelu_exact(upper).astype(jnp.bfloat16)
    hidden_two = normed + (row_sum(active, w_down, share) + b_down)
    result = norm_rows(hidden_two, ffn_gain, ffn_shift)
    kept = (
        full_in,
        queries,
        keys_loc,
        vals_loc,
        far_keys,
        far_vals,
        logsums,
        context,
        hidden_one,
        full_normed,
        upper,
        active,
        hidden_two,
    )
    return (result, kept)


def layer_backward(grad_out, kept, params, lengths, share):
    (
        w_query,
        w_key,
        w_value,
        b_query,
        b_value,
        conv_key,
        conv_value,
        w_out,
        b_out,
        attn_gain,
        attn_shift,
        w_up,
        b_up,
        w_down,
        b_down,
        ffn_gain,
        ffn_shift,
    ) = params
    (
        full_in,
        queries,
        keys_loc,
        vals_loc,
        far_keys,
        far_vals,
        logsums,
        context,
        hidden_one,
        full_normed,
        saved_upper,
        active,
        hidden_two,
    ) = kept
    seqs = lengths.shape[0]
    total_rows = full_in.shape[0]
    length = total_rows // seqs
    chans = w_query.shape[1]
    heads = chans // HEAD_DIM
    pooled_len = length // STRIDE
    unused_two, pull_two = jax.vjp(norm_rows, hidden_two, ffn_gain, ffn_shift)
    grad_h2, grad_fgain, grad_fshift = pull_two(grad_out)
    grad_ffn = grad_h2.astype(jnp.bfloat16)
    grad_bdown = jnp.sum(grad_ffn.astype(jnp.float32), axis=0)
    full_gffn = share_back(grad_ffn)
    grad_wdown = jnp.einsum("tf,td->fd", active, full_gffn, preferred_element_type=jnp.float32)
    grad_active = jnp.einsum("td,fd->tf", full_gffn, w_down, preferred_element_type=jnp.float32)
    unused_gelu, pull_gelu = jax.vjp(gelu_exact, saved_upper)
    grad_upper = pull_gelu(grad_active)[0].astype(jnp.bfloat16)
    grad_bup = jnp.sum(grad_upper.astype(jnp.float32), axis=0)
    grad_wup = jnp.einsum("td,tf->df", full_normed, grad_upper, preferred_element_type=jnp.float32)

    def up_term(start, count):
        return jnp.einsum("tf,df->td", grad_upper, w_up, preferred_element_type=jnp.float32)

    grad_y1 = grad_h2 + back_sum(up_term, share)
    unused_one, pull_one = jax.vjp(norm_rows, hidden_one, attn_gain, attn_shift)
    grad_h1, grad_again, grad_ashift = pull_one(grad_y1)
    grad_attn = grad_h1.astype(jnp.bfloat16)
    grad_bout = jnp.sum(grad_attn.astype(jnp.float32), axis=0)
    full_gattn = share_back(grad_attn)
    grad_wout = jnp.einsum("tc,td->cd", context, full_gattn, preferred_element_type=jnp.float32)
    grad_context = jnp.einsum("td,cd->tc", full_gattn, w_out, preferred_element_type=jnp.float32)
    valid = (jnp.arange(length, dtype=jnp.int32)[None, :] < lengths[:, None]).astype(jnp.float32)[
        :, :, None
    ]
    grad_context = (grad_context.reshape(seqs, length, chans) * valid).astype(jnp.bfloat16)
    grad_q, grad_near_k, grad_near_v, grad_far_k, grad_far_v = attend_backward(
        queries.reshape(seqs, length, heads, HEAD_DIM),
        keys_loc.reshape(seqs, length, heads, HEAD_DIM),
        vals_loc.reshape(seqs, length, heads, HEAD_DIM),
        far_keys.reshape(seqs, pooled_len, heads, HEAD_DIM),
        far_vals.reshape(seqs, pooled_len, heads, HEAD_DIM),
        lengths,
        logsums,
        grad_context.reshape(seqs, length, heads, HEAD_DIM),
    )
    masked_keys = keys_loc.reshape(seqs, length, chans).astype(jnp.float32) * valid
    masked_vals = vals_loc.reshape(seqs, length, chans).astype(jnp.float32) * valid
    unused_pk, pull_key = jax.vjp(pool_rows, masked_keys, conv_key)
    grad_kpool, grad_ckey = pull_key(grad_far_k.reshape(seqs, pooled_len, chans))
    unused_pv, pull_val = jax.vjp(pool_rows, masked_vals, conv_value)
    grad_vpool, grad_cval = pull_val(grad_far_v.reshape(seqs, pooled_len, chans))
    grad_queries = grad_q.reshape(total_rows, chans).astype(jnp.bfloat16)
    grad_keys = (
        (grad_near_k.reshape(seqs, length, chans) + grad_kpool * valid)
        .reshape(total_rows, chans)
        .astype(jnp.bfloat16)
    )
    grad_vals = (
        (grad_near_v.reshape(seqs, length, chans) + grad_vpool * valid)
        .reshape(total_rows, chans)
        .astype(jnp.bfloat16)
    )
    grad_wquery = jnp.einsum("td,tc->dc", full_in, grad_queries, preferred_element_type=jnp.float32)
    grad_wkey = jnp.einsum("td,tc->dc", full_in, grad_keys, preferred_element_type=jnp.float32)
    grad_wvalue = jnp.einsum("td,tc->dc", full_in, grad_vals, preferred_element_type=jnp.float32)
    grad_bquery = jnp.sum(grad_queries.astype(jnp.float32), axis=0)
    grad_bvalue = jnp.sum(grad_vals.astype(jnp.float32), axis=0)

    def input_term(start, count):
        total = jnp.einsum("tc,dc->td", grad_queries, w_query, preferred_element_type=jnp.float32)
        total = total + jnp.einsum(
            "tc,dc->td", grad_keys, w_key, preferred_element_type=jnp.float32
        )
        return total + jnp.einsum(
            "tc,dc->td", grad_vals, w_value, preferred_element_type=jnp.float32
        )

    grad_input = grad_h1 + back_sum(input_term, share)
    matrices = (
        grad_wquery[None],
        grad_wkey[None],
        grad_wvalue[None],
        grad_wout[None],
        grad_wup[None],
        grad_wdown[None],
    )
    vectors = (
        spread(grad_bquery, D)[None],
        spread(grad_bvalue, D)[None],
        spread(grad_ckey, D)[None],
        spread(grad_cval, D)[None],
        grad_bout[None],
        grad_again[None],
        grad_ashift[None],
        spread(grad_bup, FF)[None],
        grad_bdown[None],
        grad_fgain[None],
        grad_fshift[None],
    )
    return (grad_input, matrices, vectors)


def on_device(
    tokens,
    lengths,
    w_query,
    w_key,
    w_value,
    b_query,
    b_value,
    conv_key,
    conv_value,
    w_out,
    b_out,
    attn_gain,
    attn_shift,
    w_up,
    b_up,
    w_down,
    b_down,
    ffn_gain,
    ffn_shift,
    cotangent,
):
    stacks = (
        w_query,
        w_key,
        w_value,
        b_query,
        b_value,
        conv_key,
        conv_value,
        w_out,
        b_out,
        attn_gain,
        attn_shift,
        w_up,
        b_up,
        w_down,
        b_down,
        ffn_gain,
        ffn_shift,
    )
    total_rows = tokens.shape[0]
    share = total_rows // lax.axis_size("mp")
    place = lax.axis_index("mp") * share
    resid = lax.dynamic_slice_in_dim(tokens, place, share, 0).astype(jnp.float32)
    layer = 0
    params = tuple((stack[layer] for stack in stacks))
    result, kept = layer_forward(tokens, resid, lengths, params, share)
    kept_all = [kept]
    activations = result.astype(jnp.bfloat16)
    grad_out = cotangent.astype(jnp.float32)
    matrix_list = [None] * LAYERS
    vector_list = [None] * LAYERS
    for layer in reversed(range(LAYERS)):
        params = tuple((stack[layer] for stack in stacks))
        grad_out, matrices, vectors = layer_backward(
            grad_out, kept_all[layer], params, lengths, share
        )
        matrix_list[layer] = matrices
        vector_list[layer] = vectors
    grad_wquery, grad_wkey, grad_wvalue, grad_wout, grad_wup, grad_wdown = tuple(
        (jnp.concatenate([entry[index] for entry in matrix_list], axis=0) for index in range(6))
    )
    (
        grad_bquery,
        grad_bvalue,
        grad_ckey,
        grad_cval,
        grad_bout,
        grad_again,
        grad_ashift,
        grad_bup,
        grad_bdown,
        grad_fgain,
        grad_fshift,
    ) = tuple(
        (jnp.concatenate([entry[index] for entry in vector_list], axis=0) for index in range(11))
    )
    grad_wquery, grad_wkey, grad_wvalue, grad_wout, grad_wup, grad_wdown = (
        lax.psum_scatter(grad_wquery, "dp", scatter_dimension=1, tiled=True),
        lax.psum_scatter(grad_wkey, "dp", scatter_dimension=1, tiled=True),
        lax.psum_scatter(grad_wvalue, "dp", scatter_dimension=1, tiled=True),
        lax.psum_scatter(grad_wout, "dp", scatter_dimension=2, tiled=True),
        lax.psum_scatter(grad_wup, "dp", scatter_dimension=1, tiled=True),
        lax.psum_scatter(grad_wdown, "dp", scatter_dimension=2, tiled=True),
    )
    (
        grad_bquery,
        grad_bvalue,
        grad_ckey,
        grad_cval,
        grad_bout,
        grad_again,
        grad_ashift,
        grad_bup,
        grad_bdown,
        grad_fgain,
        grad_fshift,
    ) = lax.psum(
        (
            grad_bquery,
            grad_bvalue,
            grad_ckey,
            grad_cval,
            grad_bout,
            grad_again,
            grad_ashift,
            grad_bup,
            grad_bdown,
            grad_fgain,
            grad_fshift,
        ),
        ("dp", "mp"),
    )
    return (
        activations,
        grad_out,
        grad_wquery,
        grad_wkey,
        grad_wvalue,
        grad_bquery,
        grad_bvalue,
        grad_ckey,
        grad_cval,
        grad_wout,
        grad_bout,
        grad_again,
        grad_ashift,
        grad_wup,
        grad_bup,
        grad_wdown,
        grad_bdown,
        grad_fgain,
        grad_fshift,
    )


BF = jnp.bfloat16
F32 = jnp.float32
MESH = pl.DeviceIdType.MESH
ROWS = 256
QUARTERS = 4
CHANS = D // QUARTERS
QHEADS = CHANS // HEAD_DIM
SEQ = QUARTERS * ROWS
REACH = WINDOW // 2
PREACH = POOL_WINDOW // 2 // STRIDE
OWNP = ROWS // STRIDE
KW = ROWS + 2 * REACH
KP = OWNP + 2 * PREACH
KEYS = KW + KP
QB = 128
NEAR = QB + 2 * REACH
FAR = QB // STRIDE + 2 * PREACH
COMP = 800
HALFC = COMP // 2
FRONT = 256
KVROWS = 1408
BASE = 288
PIECE = D // 8
BIG_NEG = -1e30
SCALE = HEAD_DIM ** -0.5
VROWS = 64
TILES = 2 * CHANS // 128


def nn(a, b):
    return jnp.dot(a, b, preferred_element_type=F32)


def nt(a, b):
    return lax.dot_general(a, b, (((1,), (1,)), ((), ())), preferred_element_type=F32)


def tn(a, b):
    return lax.dot_general(a, b, (((0,), (0,)), ((), ())), preferred_element_type=F32)


def rows_iota(rows, cols):
    return lax.broadcasted_iota(jnp.int32, (rows, cols), 0)


def cols_iota(rows, cols):
    return lax.broadcasted_iota(jnp.int32, (rows, cols), 1)


def mean_row(v):
    return jnp.mean(v, axis=-1, keepdims=True)


def sum_col(v):
    return jnp.sum(v, axis=0, keepdims=True)


def kernel(
    len_ref, tok_hbm, wk, wv, wq, wo, wup, wdown, bq, bv, ck, cv, bup, bo, ag, ash, bd, fg, fs, cot_hbm,
    act_out, gtok, gmats, gvec,
    W, VEC, kvf, KV, KVS, Q, CTX, P, maskn, maskf, n1, r1, y1, y1b, dg, av,
    yT, fT, gab, GKV, pt, GQ, VG,
    CR, S1, S2, ZR, HL, HR, HLL, SL, SR, GVR, GVZ, VO, tok, cot,
    lsem, asend, arecv, zsend, zrecv, lsend, hsend, hrecv, rsend, rrecv, zsum, gsend, grecv,
):
    acc, n2, xT, gub = gtok, y1, yT, y1b
    dp = lax.axis_index("dp")
    z = lax.axis_index("mp")
    c = lax.rem(dp, 2)
    x = lax.rem(lax.div(dp, 2), 2)
    y = lax.div(dp, 4)
    core = (dp + 1 - 2 * c, z)
    xdev = (dp + 2 - 4 * x, z)
    ydev = (dp + 4 - 8 * y, z)
    yx = 2 * y + x
    length = len_ref[0]

    def zdev(step):
        return (dp, lax.rem(z + step, QUARTERS))

    def rcopy(src, dst, ssem, rsem, dev):
        return pltpu.make_async_remote_copy(
            src_ref=src, dst_ref=dst, send_sem=ssem, recv_sem=rsem,
            device_id=dev, device_id_type=MESH,
        )

    barrier = pltpu.get_barrier_semaphore()
    for dev in (core, xdev, ydev, zdev(1), zdev(2), zdev(3)):
        pl.semaphore_signal(barrier, inc=1, device_id=dev, device_id_type=MESH)

    def loads():
        parts = [(wk, 0), (wv, CHANS), (wq, 2 * CHANS), (wo, 3 * CHANS)]
        copies = [
            pltpu.make_async_copy(src, W.at[0, z, at : at + CHANS, :], lsem.at[i])
            for i, (src, at) in enumerate(parts)
        ]
        copies.append(pltpu.make_async_copy(wup, W.at[1, z], lsem.at[4]))
        copies.append(pltpu.make_async_copy(wdown, W.at[2, z], lsem.at[5]))
        return copies

    own = loads()
    tok_in = pltpu.make_async_copy(tok_hbm, tok, lsem.at[6])
    cot_in = pltpu.make_async_copy(cot_hbm, cot, lsem.at[7])
    for cp in own:
        cp.start()
    tok_in.start()
    cot_in.start()
    vpack = VG.at[0:8, :]
    vpack[...] = jnp.zeros_like(vpack)
    vpack[0:1, :] = bup[...]
    vpack[1:2, CHANS : 2 * CHANS] = bv[...]
    vpack[1:2, 2 * CHANS : 3 * CHANS] = bq[...]
    for t in range(5):
        vpack[2 + t : 3 + t, 0:CHANS] = ck[t]
        vpack[2 + t : 3 + t, CHANS : 2 * CHANS] = cv[t]
    VEC[z] = vpack[...]
    pl.semaphore_wait(barrier, 6)

    def block(j):
        return pl.ds(pl.multiple_of(j * PIECE, PIECE), PIECE)

    piece_me = c * 4 + yx
    piece_x = c * 4 + 2 * y + 1 - x
    piece_y = c * 4 + 2 * (1 - y) + x
    piece_d = c * 4 + 2 * (1 - y) + 1 - x
    LO, HI = pl.ds(0, D // 2), pl.ds(D // 2, D // 2)
    ALL = pl.ds(0, D)
    CHUNKS = 9
    ends = [(0, 1), (1, 1), (0, 2), (1, 2), (0, 3), (2, 1), (2, 2), (1, 3), (2, 3)]
    inner = [(0, 1), (0, 2), (1, 1), (1, 2), (0, 3), (2, 1), (2, 2), (1, 3), (2, 3)]
    sources = [(1, 2, 3), (2, 0, 3), (1, 3, 0), (2, 1, 0)]
    targets = [(3, 2, 1, 0), (3, 0, 2, 1), (0, 3, 1, 2), (0, 1, 2, 3)]
    DOWN = 2
    FAR_STEPS = 2
    at_end = (z == 0) | (z == QUARTERS - 1)

    def table(values, bits=2):
        word = sum(v << (bits * i) for i, v in enumerate(values))
        return jnp.int32(word - (1 << 32) if word >> 31 else word)

    def lookup(word, i, bits=2):
        return lax.bitwise_and(lax.shift_right_logical(word, bits * i), (1 << bits) - 1)

    def by_place(a, b):
        return lax.select(at_end, a, b)

    mats_of = by_place(table(m for m, d in ends), table(m for m, d in inner))
    dist_of = by_place(table(d for m, d in ends), table(d for m, d in inner))
    looks_of = by_place(table((1, 2, 4, 5, 6, 7, 8, 9), 4), table((2, 4, 5, 7, 8, 9, 9, 9), 4))
    sends_of = by_place(table((1, 2, 4, 5, 6, 7, 8, 9), 4), table((2, 3, 4, 5, 6, 7, 8, 9), 4))

    def source(d):
        return lookup(table(v for row in sources for v in row), 3 * z + d - 1)

    def target(t):
        return lookup(table(v for row in targets for v in row), 4 * z + t)

    def chunk(k):
        return lookup(mats_of, k), source(lookup(dist_of, k))

    def is_far(k):
        return (lookup(mats_of, k) == DOWN) & (lookup(dist_of, k) < FAR_STEPS)

    def own_block(m, up, piece, sem):
        src = W.at[m, z, block(piece), :]
        return rcopy(src, src, zsend.at[sem, up], zrecv.at[sem, z], (dp, z + 2 * up - 1))

    def own_z(m, up):
        return own_block(m, up, piece_me, m)

    def far_z(up):
        return own_block(DOWN, up, piece_d, 4)

    def wants_far(up):
        to = z + 2 * up - 1
        inner_to = (to == 1) | (to == 2)
        return jnp.logical_not(inner_to) | (z == 3 - to)

    def relay(m, src, dev):
        ref = W.at[m, src, block(piece_me), :]
        return rcopy(ref, ref, lsend.at[m, src], zrecv.at[m, src], dev)

    def relay_far(src, dev):
        ref = W.at[DOWN, src, block(piece_d), :]
        return rcopy(ref, ref, lsend.at[4, src], zrecv.at[4, src], dev)

    def own_vec(up):
        src = VEC.at[z]
        return rcopy(src, src, zsend.at[3, up], zrecv.at[3, z], (dp, z + 2 * up - 1))

    def relay_vec(src, dev):
        ref = VEC.at[src]
        return rcopy(ref, ref, lsend.at[3, src], zrecv.at[3, src], dev)

    def onward(src):
        return jnp.where(src > z, z > 0, z < QUARTERS - 1)

    def next_dev(src):
        return (dp, jnp.where(src > z, z - 1, z + 1))

    def plane(k, which, piece, cols, dev):
        m, src = chunk(k)
        ref = W.at[m, src, block(piece), cols]
        return rcopy(ref, ref, asend.at[k, which], arecv.at[k, which], dev)

    def look(k):
        m, src = chunk(k)

        @pl.when(m == 0)
        def _():
            relay_vec(src, core).wait_recv()
            pl.when(onward(src))(lambda: relay_vec(src, next_dev(src)).start())

        relay(m, src, core).wait_recv()
        pl.when(onward(src))(lambda: relay(m, src, next_dev(src)).start())

        @pl.when(is_far(k))
        def _():
            relay_far(src, core).wait_recv()

    def first(k):
        plane(k, 1, piece_me, ALL, xdev).start()
        plane(k, 2, piece_me, ALL, ydev).start()

    def second(k):
        full = jnp.logical_not(is_far(k))
        plane(k, 1, piece_x, ALL, xdev).wait_recv()
        pl.when(full)(lambda: plane(k, 3, piece_x, LO, ydev).start())
        plane(k, 2, piece_y, ALL, ydev).wait_recv()
        pl.when(full)(lambda: plane(k, 4, piece_y, HI, xdev).start())

    def half(j):
        return pl.ds(pl.multiple_of(j * (D // 2), D // 2), D // 2)

    def cross(k, j):
        m, src = chunk(k)
        ref = W.at[m, src, half(j), :]
        return rcopy(ref, ref, asend.at[k, 5], arecv.at[k, 5], core)

    def third(k):
        @pl.when(jnp.logical_not(is_far(k)))
        def _():
            plane(k, 3, piece_d, LO, ydev).wait_recv()
            plane(k, 4, piece_d, HI, xdev).wait_recv()

        cross(k, c).start()

    def fourth(k):
        cross(k, 1 - c).wait_recv()

    def looks(i):
        return jnp.where(i < 0, 0, lookup(looks_of, lax.clamp(0, i, 7), 4))

    def sends(i):
        return jnp.where(i < 0, 0, lookup(sends_of, lax.clamp(0, i, 7), 4))

    def each(fn):
        def body(k, carry):
            fn(k)
            return carry

        return body

    def gather_slot(i, carry):
        lax.fori_loop(looks(i - 1), looks(i), each(look), 0)
        pl.when((i == 2) & jnp.logical_not(at_end))(lambda: both(own_down))
        lax.fori_loop(sends(i - 1), sends(i), each(first), 0)
        for lag, stage in ((1, second), (2, third), (3, fourth)):
            k = i - lag
            pl.when((k >= 0) & (k < CHUNKS))(lambda stage=stage, k=k: stage(k))
        return carry

    def gather_done(k, carry):
        m, src = chunk(k)

        @pl.when(onward(src))
        def _():
            relay(m, src, core).wait_send()
            pl.when(m == 0)(lambda: relay_vec(src, core).wait_send())

        plane(k, 1, piece_me, ALL, xdev).wait_send()
        plane(k, 2, piece_me, ALL, ydev).wait_send()

        @pl.when(jnp.logical_not(is_far(k)))
        def _():
            plane(k, 3, piece_x, LO, ydev).wait_send()
            plane(k, 4, piece_y, HI, xdev).wait_send()

        cross(k, c).wait_send()
        return carry

    def got(s):
        return lax.rem(z + QUARTERS - s, QUARTERS)

    def both(fn):
        pl.when(z > 0)(lambda: fn(0))
        pl.when(z < QUARTERS - 1)(lambda: fn(1))

    both(lambda up: own_vec(up).start())
    for m, waits in enumerate((own[:4], own[4:5], own[5:])):
        for cp in waits:
            cp.wait()
        if m != DOWN:
            both(lambda up: own_z(m, up).start())

    def own_down(up):
        own_z(DOWN, up).start()
        pl.when(wants_far(up))(lambda: far_z(up).start())

    pl.when(at_end)(lambda: both(own_down))

    def own_sent(up):
        own_vec(up).wait_send()
        for m in range(3):
            own_z(m, up).wait_send()
        pl.when(wants_far(up))(lambda: far_z(up).wait_send())

    base = z * ROWS
    start = lax.select(z < 2, jnp.int32(0), jnp.int32(SEQ - COMP))
    place = pl.multiple_of(start - base + BASE + FRONT, 32)
    start = pl.multiple_of(start, 32)
    kvf[...] = jnp.zeros_like(kvf)
    for b in range(2):
        i = base + b * QB + cols_iota(1, QB)
        j = base - REACH + b * QB + rows_iota(NEAR, 1)
        ok = (jnp.abs(i - j) <= REACH) & (j >= 0) & (j < length)
        maskn[b] = jnp.where(ok, 0.0, BIG_NEG)
        j = (OWNP * z - PREACH + b * (QB // STRIDE) + rows_iota(FAR, 1)) * STRIDE
        ok = (jnp.abs(i - j) <= POOL_WINDOW // 2) & (j >= 0) & (j < length)
        maskf[b] = jnp.where(ok, 0.0, BIG_NEG)
    own_rows = pl.ds(pl.multiple_of(base, ROWS), ROWS)
    tok_in.wait()
    cot_in.wait()
    xb = tok[own_rows, :]
    acc[...] = jnp.zeros_like(acc)

    def taps(zq, t):
        return VEC[zq, 2 + t : 3 + t, 0 : 2 * CHANS]

    def strided(t):
        at = pl.ds(FRONT + BASE - POOL_WINDOW // 2 - 2 + t, KP, stride=STRIDE)
        return jnp.concatenate([kvf[i, at, :] for i in range(TILES)], axis=1)

    def tile(i):
        return slice(i * 128, (i + 1) * 128)

    def window(lo, rows):
        return jnp.concatenate([kvf[i, lo : lo + rows, :] for i in range(TILES)], axis=1)

    def quarter(s):
        return lax.select(s == 0, z, source(lax.max(s, 1)))

    def attend(s, carry):
        zq = quarter(s)
        for blk in range(2):
            xr = tok[pl.ds(pl.multiple_of(start + blk * HALFC, 16), HALFC), :]
            kv = nt(xr, W[0, zq, 0 : 2 * CHANS, :]) + VEC[zq, 1:2, 0 : 2 * CHANS]
            pos = start + blk * HALFC + rows_iota(HALFC, 1)
            kvb = jnp.where(pos < length, kv.astype(BF).astype(F32), 0.0)
            for i in range(TILES):
                kvf[i, pl.ds(pl.multiple_of(place + blk * HALFC, 8), HALFC), :] = kvb[:, tile(i)]
        KVS[zq] = window(FRONT, COMP).astype(BF)
        KV[zq, 0:KW, :] = window(FRONT + BASE - REACH, KW).astype(BF)
        pooled = jnp.zeros((KP, 2 * CHANS), F32)
        for t in range(5):
            pooled = pooled + taps(zq, t) * strided(t)
        KV[zq, KW:KEYS, :] = pooled.astype(BF)
        qz = nt(xb, W[0, zq, 2 * CHANS : 3 * CHANS, :]) + VEC[zq, 1:2, 2 * CHANS : 3 * CHANS]
        Q[zq] = qz.astype(BF)
        for b in range(2):
            live = base + b * QB + cols_iota(1, QB) < length
            n0, f0 = b * QB, KW + b * (QB // STRIDE)
            for h in range(QHEADS):
                kl = slice(h * HEAD_DIM, (h + 1) * HEAD_DIM)
                vl = slice(CHANS + h * HEAD_DIM, CHANS + (h + 1) * HEAD_DIM)
                qh = Q[zq, b * QB : (b + 1) * QB, kl]
                sn = nt(KV[zq, n0 : n0 + NEAR, kl], qh) * SCALE + maskn[b]
                sf = nt(KV[zq, f0 : f0 + FAR, kl], qh) * SCALE + maskf[b]
                peak = jnp.maximum(
                    jnp.max(sn, axis=0, keepdims=True), jnp.max(sf, axis=0, keepdims=True)
                )
                en, ef = jnp.exp(sn - peak), jnp.exp(sf - peak)
                inv = 1.0 / (sum_col(en) + sum_col(ef))
                pn, pf = en * inv, ef * inv
                P[zq, h, b, 0:NEAR, :] = pn
                P[zq, h, b, NEAR : NEAR + FAR, :] = pf
                ct = tn(KV[zq, n0 : n0 + NEAR, vl], pn.astype(BF))
                ct = ct + tn(KV[zq, f0 : f0 + FAR, vl], pf.astype(BF))
                ct = jnp.where(live, ct, 0.0)
                CTX[zq, b * QB : (b + 1) * QB, kl] = ct.T.astype(BF)
        acc[...] += nn(CTX[zq], W[0, zq, 3 * CHANS : D, :])
        lax.fori_loop(lookup_slots(s), lookup_slots(s + 1), gather_slot, 0)
        return carry

    def lookup_slots(s):
        return jnp.where(s == 0, 0, jnp.where(s < 3, 2 + 2 * s, 8))

    lax.fori_loop(0, QUARTERS, attend, 0)

    def store_T(dst, v, cols):
        vt = v.T.astype(BF)
        for j in range(8):
            to = (j % 2) * 4 + j // 2
            dst[to * PIECE : (to + 1) * PIECE, cols] = vt[j * PIECE : (j + 1) * PIECE]

    def span(i, size):
        if isinstance(i, int):
            return pl.ds(i * size, size)
        return pl.ds(pl.multiple_of(i * size, size), size)

    def norm_one(i, carry):
        rows = span(i, QB)
        res = tok[pl.ds(pl.multiple_of(base + i * QB, QB), QB), :].astype(F32)
        hid = res + (acc[rows, :] + bo[...])
        cen = hid - mean_row(hid)
        r = lax.rsqrt(mean_row(cen * cen) + epsilon)
        n = cen * r
        n1[rows, :] = n
        r1[rows, :] = r
        out = n * ag[...] + ash[...]
        y1[rows, :] = out
        y1b[rows, :] = out.astype(BF)
        store_T(yT, out, rows)
        acc[rows, :] = jnp.zeros_like(out)
        return carry

    lax.fori_loop(0, ROWS // QB, norm_one, 0)

    def feed(s, carry):
        zq = quarter(s)

        def up(i, carry):
            cols = span(i, ROWS)
            u = nn(y1b[...], W[1, zq, :, cols]) + VEC[zq, 0:1, cols]
            cdf = 0.5 * (1.0 + lax.erf(u * (0.5 ** 0.5)))
            dg[zq, :, cols] = cdf + u * jnp.exp(-0.5 * u * u) * ((2.0 * 3.141592653589793) ** -0.5)
            av[zq, :, cols] = (u * cdf).astype(BF)
            return carry

        for i in range(D // ROWS):
            up(i, 0)
        acc[...] += nn(av[zq], W[2, zq])
        lo = jnp.where(s < 3, 8 + s, 12)
        hi = jnp.where(s < 2, 9 + s, 12)
        lax.fori_loop(lo, hi, gather_slot, 0)
        return carry

    lax.fori_loop(0, QUARTERS, feed, 0)
    VG[...] = jnp.zeros_like(VG)
    GEN = 8 * QUARTERS

    def add_row(row, v):
        VG[row : row + 1, :] += sum_col(v)

    def norm_two(i, carry):
        rows = span(i, QB)
        hid = y1[rows, :] + (acc[rows, :] + bd[...])
        cen = hid - mean_row(hid)
        r = lax.rsqrt(mean_row(cen * cen) + epsilon)
        n = cen * r
        act_out[rows, :] = (n * fg[...] + fs[...]).astype(BF)
        g = cot[rows, :].astype(F32)
        add_row(GEN + 4, g * n)
        add_row(GEN + 5, g)
        e = g * fg[...]
        gh2 = r * (e - mean_row(e) - n * mean_row(e * n))
        acc[rows, :] = gh2
        gf = gh2.astype(BF)
        gab[rows, :] = gf
        gff = gf.astype(F32)
        add_row(GEN + 3, gff)
        store_T(fT, gff, rows)
        return carry

    lax.fori_loop(0, ROWS // QB, norm_two, 0)

    PARTS = 12

    def part(r):
        m = lax.select(r < 8, 2 - lax.rem(r, 2), 0)
        t = lax.select(r < 8, lax.div(r, 2), r - 8)
        return m, t

    def r_core(r):
        m, t = part(r)
        src = W.at[m, target(t), half(1 - c), :]
        return rcopy(src, CR.at[r], rsend.at[r, 0], rrecv.at[r, 0], core)

    def blk4(r, yy, xx, cols):
        return CR.at[r, block(2 * yy + xx), cols]

    def r_stage1(r, i):
        if i < 2:
            src, dev = blk4(r, i, 1 - x, LO), xdev
        else:
            src, dev = blk4(r, 1 - y, i - 2, HI), ydev
        return rcopy(src, S1.at[r, i], rsend.at[r, 1 + i], rrecv.at[r, 1 + i], dev)

    def r_stage2(r, i):
        if i == 0:
            src, dev = blk4(r, 1 - y, x, LO), ydev
        else:
            src, dev = blk4(r, y, 1 - x, HI), xdev
        return rcopy(src, S2.at[r, i], rsend.at[r, 5 + i], rrecv.at[r, 5 + i], dev)

    def r_z(r):
        m, t = part(r)
        dst = target(t)
        left = dst < z
        slot = jnp.where(left & (dst == z - 1), QUARTERS, dst)
        src = CR.at[r, block(yx), :]
        dev = (dp, jnp.where(left, z - 1, z + 1))
        return rcopy(src, ZR.at[m, slot], rsend.at[r, 7], zsum.at[m, slot], dev)

    def z_in(m, slot):
        ref = ZR.at[m, slot]
        return rcopy(ref, ref, zsum.at[m, slot], zsum.at[m, slot], core)

    def upstream(dst):
        return jnp.where(dst < z, z < QUARTERS - 1, z > 0)

    def reduce1(r):
        m, t = part(r)
        r_core(r).wait_recv()
        zq = target(t)

        def add(i, carry):
            CR[r, block(i), :] = CR[r, block(i), :] + W[m, zq, block(4 * c + i), :]
            return carry

        lax.fori_loop(0, 4, add, 0)
        for i in range(4):
            r_stage1(r, i).start()

    def reduce2(r):
        for i in range(4):
            r_stage1(r, i).wait_recv()
        for i in range(2):
            a = blk4(r, i, x, LO)
            a[...] = a[...] + S1[r, i]
            a = blk4(r, y, i, HI)
            a[...] = a[...] + S1[r, 2 + i]
        for i in range(2):
            r_stage2(r, i).start()

    def reduce3(r):
        for i in range(2):
            r_stage2(r, i).wait_recv()
        for i, cols in enumerate((LO, HI)):
            a = blk4(r, y, x, cols)
            a[...] = a[...] + S2[r, i]
        dst = target(part(r)[1])
        pl.when((dst != z) & jnp.logical_not(upstream(dst)))(lambda: r_z(r).start())

    def reduce4(r):
        m, t = part(r)
        dst = target(t)

        @pl.when((dst != z) & upstream(dst))
        def _():
            z_in(m, dst).wait_recv()
            CR[r, block(yx), :] = CR[r, block(yx), :] + ZR[m, dst]
            r_z(r).start()

    def stage(fn, r):
        pl.when((r >= 0) & (r < PARTS))(lambda: fn(r))

    def reduce_slot(i):
        late = i > 7
        early = jnp.where(i < 2, i, jnp.where(i < 7, i + 1, -1))
        stage(reduce1, early)
        stage(reduce1, jnp.where(i == 1, 2, -1))
        stage(reduce2, i - 1)
        stage(reduce3, jnp.where(late, -1, i - 3))
        stage(reduce3, jnp.where(i == 8, 5, -1))
        stage(reduce3, jnp.where(late, i - 2, -1))
        stage(reduce4, jnp.where(i == 8, 4, -1))
        stage(reduce4, jnp.where(late, i - 3, i - 4))
        stage(reduce1, jnp.where(late, i, -1))

    def weight_grad(left, right, dst, width):
        dst[:, 0:width] = nn(left[...], right).astype(BF)

    def feed_back(s, carry):
        zq = target(s)
        vrow = pl.multiple_of(8 * zq, 8)

        def hidden(i, carry):
            cols = span(i, ROWS)
            gact = nt(gab[...], W[2, zq, cols, :])
            gu = (gact * dg[zq, :, cols]).astype(BF)
            gub[:, cols] = gu
            VG[pl.ds(vrow, 1), cols] = sum_col(gu.astype(F32))
            return carry

        for i in range(D // ROWS):
            hidden(i, 0)
        weight_grad(fT, av[zq], W.at[2, zq], D)
        r_core(2 * s).start()
        acc[...] += nt(gub[...], W[1, zq])
        weight_grad(yT, gub[...], W.at[1, zq], D)
        r_core(2 * s + 1).start()
        reduce_slot(s)
        return carry

    lax.fori_loop(0, CHUNKS, gather_done, 0)
    both(own_sent)
    lax.fori_loop(0, QUARTERS, feed_back, 0)

    def norm_back(i, carry):
        rows = span(i, QB)
        gy = acc[rows, :]
        n = n1[rows, :]
        add_row(GEN + 1, gy * n)
        add_row(GEN + 2, gy)
        e = gy * ag[...]
        gh1 = r1[rows, :] * (e - mean_row(e) - n * mean_row(e * n))
        acc[rows, :] = gh1
        ga = gh1.astype(BF)
        gab[rows, :] = ga
        gaf = ga.astype(F32)
        add_row(GEN, gaf)
        store_T(fT, gaf, rows)
        store_T(xT, tok[pl.ds(pl.multiple_of(base + i * QB, QB), QB), :].astype(F32), rows)
        return carry

    lax.fori_loop(0, ROWS // QB, norm_back, 0)

    def hl(zq):
        return rcopy(SL.at[zq], HL.at[zq], hsend.at[0, zq], hrecv.at[0, zq], zdev(3))

    def hr(zq):
        return rcopy(SR.at[zq], HR.at[zq], hsend.at[1, zq], hrecv.at[1, zq], zdev(1))

    def hll(zq):
        return rcopy(
            SL.at[zq, REACH : REACH + 16, :], HLL.at[zq], hsend.at[2, zq], hrecv.at[2, zq], zdev(2)
        )

    def attend_back(s, carry):
        zq = target(s)
        gc = nt(gab[...], W[0, zq, 3 * CHANS : D, :])
        alive = base + rows_iota(ROWS, 1) < length
        gcb = jnp.where(alive, gc, 0.0).astype(BF)
        GKV[zq] = jnp.zeros((KEYS, 2 * CHANS), F32)
        for b in range(2):
            n0, f0 = b * QB, KW + b * (QB // STRIDE)
            for h in range(QHEADS):
                kl = slice(h * HEAD_DIM, (h + 1) * HEAD_DIM)
                vl = slice(CHANS + h * HEAD_DIM, CHANS + (h + 1) * HEAD_DIM)
                gch = gcb[b * QB : (b + 1) * QB, kl]
                qh = Q[zq, b * QB : (b + 1) * QB, kl]
                pn = P[zq, h, b, 0:NEAR, :]
                pf = P[zq, h, b, NEAR : NEAR + FAR, :]
                gpn = nt(KV[zq, n0 : n0 + NEAR, vl], gch)
                gpf = nt(KV[zq, f0 : f0 + FAR, vl], gch)
                delta = sum_col(pn * gpn) + sum_col(pf * gpf)
                gsn = (pn * (gpn - delta)).astype(BF)
                gsf = (pf * (gpf - delta)).astype(BF)
                qt = tn(KV[zq, n0 : n0 + NEAR, kl], gsn) + tn(KV[zq, f0 : f0 + FAR, kl], gsf)
                GQ[zq, b * QB : (b + 1) * QB, 2 * CHANS + h * HEAD_DIM : 2 * CHANS + (h + 1) * HEAD_DIM] = (
                    (qt * SCALE).T.astype(BF)
                )
                GKV[zq, n0 : n0 + NEAR, kl] += nn(gsn, qh) * SCALE
                GKV[zq, f0 : f0 + FAR, kl] += nn(gsf, qh) * SCALE
                GKV[zq, n0 : n0 + NEAR, vl] += nn(pn.astype(BF), gch)
                GKV[zq, f0 : f0 + FAR, vl] += nn(pf.astype(BF), gch)
        vrow = pl.multiple_of(8 * zq, 8)
        for i in range(TILES):
            kvf[i, FRONT : FRONT + COMP, :] = KVS[zq, :, tile(i)].astype(F32)
        gp = GKV[zq, KW:KEYS, :]
        sums = jnp.concatenate(
            [jnp.zeros((1, CHANS), F32), sum_col(GKV[zq, 0:KW, CHANS : 2 * CHANS])], axis=1
        )
        far_at = (OWNP * z - PREACH + rows_iota(KP, 1)) * STRIDE
        for t in range(5):
            VG[pl.ds(vrow + 2 + t, 1), 0 : 2 * CHANS] = sum_col(gp * strided(t))
            to = far_at + (t - 2)
            inside = (to >= 0) & (to < length)
            sums = sums + taps(zq, t) * sum_col(jnp.where(inside, gp, 0.0))
        VG[pl.ds(vrow + 1, 1), CHANS : 2 * CHANS] = sums[:, CHANS : 2 * CHANS]
        VG[pl.ds(vrow + 1, 1), 2 * CHANS : 3 * CHANS] = sum_col(
            GQ[zq, :, 2 * CHANS : 3 * CHANS].astype(F32)
        )
        SL[zq, 0:REACH, :] = GKV[zq, 0:REACH, :].astype(BF)
        SL[zq, REACH : REACH + 80, :] = GKV[zq, KW : KW + 80, :].astype(BF)
        SR[zq, 0:REACH, :] = GKV[zq, KW - REACH : KW, :].astype(BF)
        SR[zq, REACH : REACH + OWNP, :] = GKV[zq, KEYS - OWNP : KEYS, :].astype(BF)
        pl.when(z > 0)(lambda: hl(zq).start())
        pl.when(z < QUARTERS - 1)(lambda: hr(zq).start())
        pl.when(z > 1)(lambda: hll(zq).start())
        reduce_slot(4 + s)
        return carry

    lax.fori_loop(0, QUARTERS, attend_back, 0)

    half_row = pl.multiple_of(32 * c, 32)
    row_x = pl.multiple_of(half_row + 16 * x, 16)
    row_y = pl.multiple_of(row_x + 8 * y, 8)

    def vrows(at, size):
        return pl.ds(pl.multiple_of(at, 8), size)

    folds = [
        (core, VG.at[vrows(32 - half_row, 32), :], GVR.at[0:32], vrows(half_row, 32)),
        (xdev, VG.at[vrows(half_row + 16 - 16 * x, 16), :], GVR.at[32:48], vrows(row_x, 16)),
        (ydev, VG.at[vrows(row_x + 8 - 8 * y, 8), :], GVR.at[48:56], vrows(row_y, 8)),
    ]

    def fold(i):
        dev, src, dst, keep = folds[i]
        return rcopy(src, dst, gsend.at[i], grecv.at[i], dev)

    def fold_done(i):
        fold(i).wait()
        keep = folds[i][3]
        VG[keep, :] = VG[keep, :] + folds[i][2][...]

    def g_z(s):
        src = VG.at[vrows(row_y, 8), :]
        return rcopy(src, GVZ.at[z], gsend.at[2 + s], grecv.at[2 + s], zdev(s))

    def g_z_in(s):
        dst = GVZ.at[got(s)]
        return rcopy(dst, dst, gsend.at[2 + s], grecv.at[2 + s], core)

    opens = [
        (ydev, vrows(row_y, 8), vrows(row_x + 8 - 8 * y, 8)),
        (xdev, vrows(row_x, 16), vrows(half_row + 16 - 16 * x, 16)),
        (core, vrows(half_row, 32), vrows(32 - half_row, 32)),
    ]

    def unfold(i):
        dev, mine, other = opens[i]
        ref = VO.at[mine, :]
        return rcopy(ref, ref, gsend.at[6 + i], grecv.at[6 + i], dev)

    def unfold_done(i):
        ref = VO.at[opens[i][2], :]
        rcopy(ref, ref, gsend.at[6 + i], grecv.at[6 + i], core).wait_recv()

    def vector_step(s):
        @pl.when(s == 0)
        def _():
            fold_done(0)
            fold(1).start()

        @pl.when(s == 1)
        def _():
            fold_done(1)
            fold(2).start()

        @pl.when(s == 2)
        def _():
            fold_done(2)
            for step in (1, 2, 3):
                g_z(step).start()
            GVZ[z] = VG[vrows(row_y, 8), :]

        @pl.when(s == 3)
        def _():
            for step in (1, 2, 3):
                g_z_in(step).wait_recv()
            VO[vrows(row_y, 8), :] = GVZ[0] + GVZ[1] + GVZ[2] + GVZ[3]
            unfold(0).start()

    fold(0).start()

    def project_back(s, carry):
        zq = target(s)
        pl.when(z < QUARTERS - 1)(lambda: hl(zq).wait_recv())
        pl.when(z > 0)(lambda: hr(zq).wait_recv())
        pl.when(z < QUARTERS - 2)(lambda: hll(zq).wait_recv())
        near = GKV.at[zq]

        def when(ok, v):
            return jnp.where(ok, v.astype(F32), 0.0)

        has_l, has_r, has_rr = z > 0, z < QUARTERS - 1, z < QUARTERS - 2
        near[REACH : 2 * REACH, :] += when(has_l, HR[zq, 0:REACH, :])
        near[ROWS : ROWS + REACH, :] += when(has_r, HL[zq, 0:REACH, :])
        gp = GKV[zq, KW + OWNP : KW + 2 * OWNP, :] + when(has_l, HR[zq, REACH : REACH + OWNP, :])
        gp = gp + when(has_r, HL[zq, REACH : REACH + OWNP, :])
        nxt = GKV[zq, KW + 2 * OWNP : KW + 2 * OWNP + 1, :]
        nxt = nxt + when(has_r, HL[zq, REACH + OWNP : REACH + OWNP + 16, :])[0:1, :]
        nxt = nxt + when(has_rr, HLL[zq])[0:1, :]
        gp1 = jnp.concatenate([gp[1:, :], nxt], axis=0)
        fills = (
            taps(zq, 2) * gp,
            taps(zq, 3) * gp,
            taps(zq, 4) * gp + taps(zq, 0) * gp1,
            taps(zq, 1) * gp1,
        )
        for k, fill in enumerate(fills):
            for i in range(TILES):
                pt[i, pl.ds(k, OWNP, stride=STRIDE), :] = fill[:, tile(i)]
        back = jnp.concatenate([pt[i] for i in range(TILES)], axis=1)
        alive = base + rows_iota(ROWS, 1) < length
        gkv = GKV[zq, REACH : REACH + ROWS, :] + jnp.where(alive, back, 0.0)
        GQ[zq, :, 0 : 2 * CHANS] = gkv.astype(BF)

        acc[...] += nn(GQ[zq], W[0, zq, 0 : 3 * CHANS, :])
        weight_grad(xT, GQ[zq], W.at[0, zq], 3 * CHANS)

        W[0, zq, :, 3 * CHANS : D] = nn(fT[...], CTX[zq]).astype(BF)
        r_core(8 + s).start()
        reduce_slot(8 + s)
        vector_step(s)
        return carry

    lax.fori_loop(0, QUARTERS, project_back, 0)
    for zq in range(QUARTERS):
        pl.when(z > 0)(lambda: hl(zq).wait_send())
        pl.when(z < QUARTERS - 1)(lambda: hr(zq).wait_send())
        pl.when(z > 1)(lambda: hll(zq).wait_send())

    def final(m):
        own_part = (11, 7, 6)[m]
        gmats[m] = CR[own_part, block(yx), :].astype(F32)

        def more(slot):
            z_in(m, slot).wait_recv()
            gmats[m] += ZR[m, slot].astype(F32)

        pl.when(z > 0)(lambda: more(z))
        pl.when(z < QUARTERS - 1)(lambda: more(QUARTERS))

    def at(r):
        return jnp.int32(r)

    unfold_done(0)
    unfold(1).start()
    reduce3(at(10))
    reduce4(at(9))
    reduce2(at(11))
    reduce4(at(10))
    unfold_done(1)
    unfold(2).start()
    final(1)
    final(2)
    reduce3(at(11))
    unfold_done(2)
    final(0)
    gvec[...] = VO[...]
    for i in range(3):
        unfold(i).wait_send()
    for s in (1, 2, 3):
        g_z(s).wait_send()

    def sent(r, carry):
        r_core(r).wait_send()
        for i in range(4):
            r_stage1(r, i).wait_send()
        for i in range(2):
            r_stage2(r, i).wait_send()
        pl.when(part(r)[1] < QUARTERS - 1)(lambda: r_z(r).wait_send())
        return carry

    lax.fori_loop(0, PARTS, sent, 0)


def unpack(
    act, gtok, gmats, gvec,
    act_out, gtok_out, gq, gk, gv, gbq, gbv, gck, gcv, go, gbo, gag, gas, gup, gbu, gdown, gbd, gfg, gfs,
):
    act_out[...] = act[...]
    gtok_out[...] = gtok[...]
    gk[...] = gmats[0, :, 0:CHANS]
    gv[...] = gmats[0, :, CHANS : 2 * CHANS]
    gq[...] = gmats[0, :, 2 * CHANS : 3 * CHANS]
    go[...] = gmats[0, :, 3 * CHANS : D].T
    gup[...] = gmats[1]
    gdown[...] = gmats[2]
    for j in range(QUARTERS):
        at = slice(j * CHANS, (j + 1) * CHANS)
        row = 8 * j
        gbu[:, j * D : (j + 1) * D] = gvec[row : row + 1, :]
        gbv[:, at] = gvec[row + 1 : row + 2, CHANS : 2 * CHANS]
        gbq[:, at] = gvec[row + 1 : row + 2, 2 * CHANS : 3 * CHANS]
        for t in range(5):
            gck[t, :, at] = gvec[row + 2 + t : row + 3 + t, 0:CHANS]
            gcv[t, :, at] = gvec[row + 2 + t : row + 3 + t, CHANS : 2 * CHANS]
    for j, out in enumerate((gbo, gag, gas, gbd, gfg, gfs)):
        out[...] = gvec[8 * QUARTERS + j : 8 * QUARTERS + j + 1, :]


def fused_layer(
    tokens, lengths, w_query, w_key, w_value, b_query, b_value, conv_key, conv_value, w_out,
    b_out, attn_gain, attn_shift, w_up, b_up, w_down, b_down, ffn_gain, ffn_shift, cotangent,
):
    Q4 = QUARTERS
    vm = pltpu.VMEM
    dma = pltpu.SemaphoreType.DMA
    scratch = [
        vm((3, Q4, D, D), BF),
        vm((Q4, 8, D), F32),
        vm((TILES, KVROWS, 128), F32),
        vm((Q4, KEYS, 2 * CHANS), BF),
        vm((Q4, COMP, 2 * CHANS), BF),
        vm((Q4, ROWS, CHANS), BF),
        vm((Q4, ROWS, CHANS), BF),
        vm((Q4, QHEADS, 2, NEAR + FAR, QB), F32),
        vm((2, NEAR, QB), F32),
        vm((2, FAR, QB), F32),
        vm((ROWS, D), F32),
        vm((ROWS, 1), F32),
        vm((ROWS, D), F32),
        vm((ROWS, D), BF),
        vm((Q4, ROWS, D), F32),
        vm((Q4, ROWS, D), BF),
        vm((D, ROWS), BF),
        vm((D, ROWS), BF),
        vm((ROWS, D), BF),
        vm((Q4, KEYS, 2 * CHANS), F32),
        vm((TILES, ROWS, 128), F32),
        vm((Q4, ROWS, 3 * CHANS), BF),
        vm((VROWS, D), F32),
        vm((12, D // 2, D), BF),
        vm((12, 4, PIECE, D // 2), BF),
        vm((12, 2, PIECE, D // 2), BF),
        vm((3, Q4 + 1, PIECE, D), BF),
        vm((Q4, REACH + 80, 2 * CHANS), BF),
        vm((Q4, REACH + OWNP, 2 * CHANS), BF),
        vm((Q4, 16, 2 * CHANS), BF),
        vm((Q4, REACH + 80, 2 * CHANS), BF),
        vm((Q4, REACH + OWNP, 2 * CHANS), BF),
        vm((VROWS, D), F32),
        vm((Q4, 8, D), F32),
        vm((VROWS, D), F32),
        vm((SEQ, D), BF),
        vm((ROWS, D), BF),
        dma((8,)),
        dma((9, 6)),
        dma((9, 6)),
        dma((5, 2)),
        dma((5, Q4)),
        dma((5, Q4)),
        dma((3, Q4)),
        dma((3, Q4)),
        dma((12, 8)),
        dma((12, 7)),
        dma((3, Q4 + 1)),
        dma((9,)),
        dma((9,)),
    ]
    vspec = pl.BlockSpec(memory_space=pltpu.VMEM)
    hspec = pl.BlockSpec(memory_space=pl.ANY)
    packed = pl.pallas_call(
        kernel,
        out_shape=(
            jax.ShapeDtypeStruct((ROWS, D), BF),
            jax.ShapeDtypeStruct((ROWS, D), F32),
            jax.ShapeDtypeStruct((3, PIECE, D), F32),
            jax.ShapeDtypeStruct((VROWS, D), F32),
        ),
        in_specs=[pl.BlockSpec(memory_space=pltpu.SMEM)] + [hspec] * 7 + [vspec] * 11 + [hspec],
        out_specs=(vspec,) * 4,
        scratch_shapes=scratch,
        compiler_params=pltpu.CompilerParams(
            collective_id=0, has_side_effects=True, vmem_limit_bytes=67043328
        ),
        name="layer",
    )(
        lengths, tokens, w_key[0].T, w_value[0].T, w_query[0].T, w_out[0], w_up[0], w_down[0],
        b_query, b_value, conv_key.transpose(1, 0, 2), conv_value.transpose(1, 0, 2), b_up, b_out, attn_gain, attn_shift, b_down,
        ffn_gain, ffn_shift, cotangent,
    )
    row = (1, D)
    shapes = [
        (ROWS, D), (PIECE, CHANS), (PIECE, CHANS), (PIECE, CHANS), row, row, (5, 1, D), (5, 1, D), (CHANS, PIECE),
        row, row, row, (PIECE, D), (1, FF), (PIECE, D), row, row, row,
    ]
    outs = pl.pallas_call(
        unpack,
        out_shape=[jax.ShapeDtypeStruct((ROWS, D), BF)] + [jax.ShapeDtypeStruct(v, F32) for v in shapes],
        in_specs=[vspec] * 4,
        out_specs=[vspec] * 19,
        name="unpack",
    )(*packed)
    act, gtok, gq, gk, gv, gbq, gbv, gck, gcv, go, gbo, gag, gas, gup, gbu, gdown, gbd, gfg, gfs = outs
    return (
        act, gtok, gq[None], gk[None], gv[None], gbq, gbv, gck.transpose(1, 0, 2), gcv.transpose(1, 0, 2), go[None], gbo, gag, gas,
        gup[None], gbu, gdown.T[None], gbd, gfg, gfs,
    )


def solution(mesh):
    small = mesh.shape["dp"] == 8 and mesh.shape["mp"] == QUARTERS
    return jax.shard_map(
        fused_layer if small else on_device,
        mesh=mesh,
        in_specs=(
            P("dp", None),
            P("dp"),
            P(None, None, "mp"),
            P(None, None, "mp"),
            P(None, None, "mp"),
            P(None, "mp"),
            P(None, "mp"),
            P(None, None, "mp"),
            P(None, None, "mp"),
            P(None, "mp", None),
            P(),
            P(),
            P(),
            P(None, None, "mp"),
            P(None, "mp"),
            P(None, "mp", None),
            P(),
            P(),
            P(),
            P(("dp", "mp"), None),
        ),
        out_specs=(
            P(("dp", "mp"), None),
            P(("dp", "mp"), None),
            P(None, "dp", "mp"),
            P(None, "dp", "mp"),
            P(None, "dp", "mp"),
            P(),
            P(),
            P(),
            P(),
            P(None, "mp", "dp"),
            P(),
            P(),
            P(),
            P(None, "dp", "mp"),
            P(),
            P(None, "mp", "dp"),
            P(),
            P(),
            P(),
        ),
        check_vma=False,
    )
```

```python
import jax
import jax.numpy as jnp
from jax import lax
from jax.experimental import pallas as pl
from jax.experimental.pallas import tpu as pltpu
from jax.sharding import PartitionSpec as P

D = 768
HEAD_DIM = 64
FF = 3072
WINDOW = 128
POOL_WINDOW = 512
STRIDE = 4
LAYERS = 1


block_rows = 512
mask_fill = -1000000000.0
epsilon = 1e-05


def norm_rows(hidden, gain, shift):
    center = hidden - jnp.mean(hidden, axis=-1, keepdims=True)
    spread = jnp.mean(center * center, axis=-1, keepdims=True)
    return center * lax.rsqrt(spread + epsilon) * gain + shift


def gelu_exact(values):
    return jax.nn.gelu(values, approximate=False)


def pool_rows(values, kernel):
    seqs, length, chans = values.shape
    width = kernel.shape[0]
    half = width // 2
    pooled_len = length // STRIDE
    padded = jnp.pad(values, ((0, 0), (half, width), (0, 0)))
    total = jnp.zeros((seqs, pooled_len, chans), jnp.float32)
    for offset in range(width):
        total = total + kernel[offset] * padded[:, offset : offset + STRIDE * pooled_len : STRIDE]
    return total


def block_mask(start, lengths):
    reach = WINDOW // 2
    pool_reach = POOL_WINDOW // 2 // STRIDE
    span = block_rows // STRIDE + 2 * pool_reach
    rows = start + jnp.arange(block_rows, dtype=jnp.int32)
    near_pos = start - reach + jnp.arange(block_rows + 2 * reach, dtype=jnp.int32)
    far_pos = (start // STRIDE - pool_reach + jnp.arange(span, dtype=jnp.int32)) * STRIDE
    limit = lengths[:, None, None]
    near_ok = (
        (jnp.abs(rows[:, None] - near_pos[None, :]) <= reach)[None]
        & (near_pos >= 0)[None, None]
        & (near_pos[None, None] < limit)
    )
    far_ok = (
        (jnp.abs(rows[:, None] - far_pos[None, :]) <= POOL_WINDOW // 2)[None]
        & (far_pos >= 0)[None, None]
        & (far_pos[None, None] < limit)
    )
    return jnp.concatenate([near_ok, far_ok], axis=-1)


def padded_keys(keys_loc, vals_loc, far_keys, far_vals):
    reach = WINDOW // 2
    pool_reach = POOL_WINDOW // 2 // STRIDE
    pad_near = ((0, 0), (reach, reach), (0, 0), (0, 0))
    pad_far = ((0, 0), (pool_reach, pool_reach), (0, 0), (0, 0))
    return (
        jnp.pad(keys_loc, pad_near),
        jnp.pad(vals_loc, pad_near),
        jnp.pad(far_keys, pad_far),
        jnp.pad(far_vals, pad_far),
    )


def block_inputs(start, queries, padded):
    near_k, near_v, far_k, far_v = padded
    near_len = block_rows + 2 * (WINDOW // 2)
    span = block_rows // STRIDE + 2 * (POOL_WINDOW // 2 // STRIDE)
    pool_start = start // STRIDE
    q_rows = queries[:, start : start + block_rows]
    keys_b = jnp.concatenate(
        [near_k[:, start : start + near_len], far_k[:, pool_start : pool_start + span]], axis=1
    )
    vals_b = jnp.concatenate(
        [near_v[:, start : start + near_len], far_v[:, pool_start : pool_start + span]], axis=1
    )
    return (q_rows, keys_b, vals_b)


def forward_block(q_rows, keys_b, vals_b, mask, live):
    scale = q_rows.shape[-1] ** (-0.5)
    scores = (
        jnp.einsum("sqhe,skhe->shqk", q_rows, keys_b, preferred_element_type=jnp.float32) * scale
    )
    scores = jnp.where(mask[:, None], scores, mask_fill)
    peak = jnp.max(scores, axis=-1, keepdims=True)
    expo = jnp.exp(scores - peak)
    total = jnp.sum(expo, axis=-1, keepdims=True)
    weights = (expo / total).astype(jnp.bfloat16)
    result = jnp.einsum("shqk,skhe->sqhe", weights, vals_b, preferred_element_type=jnp.float32)
    result = jnp.where(live[:, :, None, None], result, 0.0)
    return (result, peak + jnp.log(total))


def forward_skip(q_rows, keys_b, vals_b, mask, live):
    seqs, rows, heads, size = q_rows.shape
    return (
        jnp.zeros((seqs, rows, heads, size), jnp.float32),
        jnp.zeros((seqs, heads, rows, 1), jnp.float32),
    )


def backward_block(q_rows, keys_b, vals_b, mask, logsum, grad_rows):
    scale = q_rows.shape[-1] ** (-0.5)
    scores = (
        jnp.einsum("sqhe,skhe->shqk", q_rows, keys_b, preferred_element_type=jnp.float32) * scale
    )
    scores = jnp.where(mask[:, None], scores, mask_fill)
    probs = jnp.exp(scores - logsum)
    grad_probs = jnp.einsum(
        "sqhe,skhe->shqk", grad_rows, vals_b, preferred_element_type=jnp.float32
    )
    delta = jnp.sum(probs * grad_probs, axis=-1, keepdims=True)
    grad_scores = (probs * (grad_probs - delta)).astype(jnp.bfloat16)
    grad_q = (
        jnp.einsum("shqk,skhe->sqhe", grad_scores, keys_b, preferred_element_type=jnp.float32)
        * scale
    )
    grad_keys = (
        jnp.einsum("shqk,sqhe->skhe", grad_scores, q_rows, preferred_element_type=jnp.float32)
        * scale
    )
    grad_vals = jnp.einsum(
        "shqk,sqhe->skhe", probs.astype(jnp.bfloat16), grad_rows, preferred_element_type=jnp.float32
    )
    return (grad_q, grad_keys, grad_vals)


def backward_skip(q_rows, keys_b, vals_b, mask, logsum, grad_rows):
    return (
        jnp.zeros(q_rows.shape, jnp.float32),
        jnp.zeros(keys_b.shape, jnp.float32),
        jnp.zeros(vals_b.shape, jnp.float32),
    )


def attend_forward(queries, keys_loc, vals_loc, far_keys, far_vals, lengths):
    length = queries.shape[1]
    padded = padded_keys(keys_loc, vals_loc, far_keys, far_vals)
    longest = jnp.max(lengths)
    results, logsums = ([], [])
    for block in range(length // block_rows):
        start = block * block_rows
        q_rows, keys_b, vals_b = block_inputs(start, queries, padded)
        mask = block_mask(start, lengths)
        live = start + jnp.arange(block_rows, dtype=jnp.int32)[None, :] < lengths[:, None]
        result, logsum = lax.cond(
            start < longest, forward_block, forward_skip, q_rows, keys_b, vals_b, mask, live
        )
        results.append(result)
        logsums.append(logsum)
    return (jnp.concatenate(results, axis=1), logsums)


def attend_backward(
    queries, keys_loc, vals_loc, far_keys, far_vals, lengths, logsums, grad_context
):
    seqs, length, heads, size = queries.shape
    pooled_len = far_keys.shape[1]
    reach = WINDOW // 2
    pool_reach = POOL_WINDOW // 2 // STRIDE
    near_len = block_rows + 2 * reach
    span = block_rows // STRIDE + 2 * pool_reach
    padded = padded_keys(keys_loc, vals_loc, far_keys, far_vals)
    longest = jnp.max(lengths)
    grad_near_k = jnp.zeros((seqs, length + 2 * reach, heads, size), jnp.float32)
    grad_near_v = jnp.zeros((seqs, length + 2 * reach, heads, size), jnp.float32)
    grad_far_k = jnp.zeros((seqs, pooled_len + 2 * pool_reach, heads, size), jnp.float32)
    grad_far_v = jnp.zeros((seqs, pooled_len + 2 * pool_reach, heads, size), jnp.float32)
    grad_queries = []
    for block in range(length // block_rows):
        start = block * block_rows
        pool_start = start // STRIDE
        q_rows, keys_b, vals_b = block_inputs(start, queries, padded)
        mask = block_mask(start, lengths)
        grad_rows = grad_context[:, start : start + block_rows]
        grad_q, grad_keys, grad_vals = lax.cond(
            start < longest,
            backward_block,
            backward_skip,
            q_rows,
            keys_b,
            vals_b,
            mask,
            logsums[block],
            grad_rows,
        )
        grad_queries.append(grad_q)
        grad_near_k = grad_near_k.at[:, start : start + near_len].add(grad_keys[:, :near_len])
        grad_near_v = grad_near_v.at[:, start : start + near_len].add(grad_vals[:, :near_len])
        grad_far_k = grad_far_k.at[:, pool_start : pool_start + span].add(grad_keys[:, near_len:])
        grad_far_v = grad_far_v.at[:, pool_start : pool_start + span].add(grad_vals[:, near_len:])
    return (
        jnp.concatenate(grad_queries, axis=1),
        grad_near_k[:, reach : reach + length],
        grad_near_v[:, reach : reach + length],
        grad_far_k[:, pool_reach : pool_reach + pooled_len],
        grad_far_v[:, pool_reach : pool_reach + pooled_len],
    )


def row_sum(left, right, share):

    def term(start, count):
        return jnp.dot(left, right, preferred_element_type=jnp.float32)

    return lax.psum_scatter(
        term(jnp.int32(0), share * lax.axis_size("mp")), "mp", scatter_dimension=0, tiled=True
    )


def share_rows(values):
    return lax.all_gather(values, "mp", axis=0, tiled=True)


def share_back(values):
    return lax.all_gather(values, "mp", axis=0, tiled=True)


def back_sum(term, share):
    return lax.psum_scatter(
        term(jnp.int32(0), share * lax.axis_size("mp")), "mp", scatter_dimension=0, tiled=True
    )


def spread(values, width):
    whole = jnp.zeros(values.shape[:-1] + (width,), jnp.float32)
    start = lax.axis_index("mp") * values.shape[-1]
    return lax.dynamic_update_slice_in_dim(whole, values, start, values.ndim - 1)


def layer_forward(full_in, resid, lengths, params, share):
    (
        w_query,
        w_key,
        w_value,
        b_query,
        b_value,
        conv_key,
        conv_value,
        w_out,
        b_out,
        attn_gain,
        attn_shift,
        w_up,
        b_up,
        w_down,
        b_down,
        ffn_gain,
        ffn_shift,
    ) = params
    seqs = lengths.shape[0]
    total_rows = full_in.shape[0]
    length = total_rows // seqs
    chans = w_query.shape[1]
    heads = chans // HEAD_DIM
    pooled_len = length // STRIDE
    queries = (jnp.dot(full_in, w_query, preferred_element_type=jnp.float32) + b_query).astype(
        jnp.bfloat16
    )
    keys_loc = jnp.dot(full_in, w_key, preferred_element_type=jnp.float32).astype(jnp.bfloat16)
    vals_loc = (jnp.dot(full_in, w_value, preferred_element_type=jnp.float32) + b_value).astype(
        jnp.bfloat16
    )
    valid = (jnp.arange(length, dtype=jnp.int32)[None, :] < lengths[:, None]).astype(jnp.float32)[
        :, :, None
    ]
    far_keys = pool_rows(
        keys_loc.reshape(seqs, length, chans).astype(jnp.float32) * valid, conv_key
    ).astype(jnp.bfloat16)
    far_vals = pool_rows(
        vals_loc.reshape(seqs, length, chans).astype(jnp.float32) * valid, conv_value
    ).astype(jnp.bfloat16)
    context, logsums = attend_forward(
        queries.reshape(seqs, length, heads, HEAD_DIM),
        keys_loc.reshape(seqs, length, heads, HEAD_DIM),
        vals_loc.reshape(seqs, length, heads, HEAD_DIM),
        far_keys.reshape(seqs, pooled_len, heads, HEAD_DIM),
        far_vals.reshape(seqs, pooled_len, heads, HEAD_DIM),
        lengths,
    )
    context = context.reshape(total_rows, chans).astype(jnp.bfloat16)
    hidden_one = resid + (row_sum(context, w_out, share) + b_out)
    normed = norm_rows(hidden_one, attn_gain, attn_shift)
    full_normed = share_rows(normed.astype(jnp.bfloat16))
    upper = jnp.dot(full_normed, w_up, preferred_element_type=jnp.float32) + b_up
    active = gelu_exact(upper).astype(jnp.bfloat16)
    hidden_two = normed + (row_sum(active, w_down, share) + b_down)
    result = norm_rows(hidden_two, ffn_gain, ffn_shift)
    kept = (
        full_in,
        queries,
        keys_loc,
        vals_loc,
        far_keys,
        far_vals,
        logsums,
        context,
        hidden_one,
        full_normed,
        upper,
        active,
        hidden_two,
    )
    return (result, kept)


def layer_backward(grad_out, kept, params, lengths, share):
    (
        w_query,
        w_key,
        w_value,
        b_query,
        b_value,
        conv_key,
        conv_value,
        w_out,
        b_out,
        attn_gain,
        attn_shift,
        w_up,
        b_up,
        w_down,
        b_down,
        ffn_gain,
        ffn_shift,
    ) = params
    (
        full_in,
        queries,
        keys_loc,
        vals_loc,
        far_keys,
        far_vals,
        logsums,
        context,
        hidden_one,
        full_normed,
        saved_upper,
        active,
        hidden_two,
    ) = kept
    seqs = lengths.shape[0]
    total_rows = full_in.shape[0]
    length = total_rows // seqs
    chans = w_query.shape[1]
    heads = chans // HEAD_DIM
    pooled_len = length // STRIDE
    unused_two, pull_two = jax.vjp(norm_rows, hidden_two, ffn_gain, ffn_shift)
    grad_h2, grad_fgain, grad_fshift = pull_two(grad_out)
    grad_ffn = grad_h2.astype(jnp.bfloat16)
    grad_bdown = jnp.sum(grad_ffn.astype(jnp.float32), axis=0)
    full_gffn = share_back(grad_ffn)
    grad_wdown = jnp.einsum("tf,td->fd", active, full_gffn, preferred_element_type=jnp.float32)
    grad_active = jnp.einsum("td,fd->tf", full_gffn, w_down, preferred_element_type=jnp.float32)
    unused_gelu, pull_gelu = jax.vjp(gelu_exact, saved_upper)
    grad_upper = pull_gelu(grad_active)[0].astype(jnp.bfloat16)
    grad_bup = jnp.sum(grad_upper.astype(jnp.float32), axis=0)
    grad_wup = jnp.einsum("td,tf->df", full_normed, grad_upper, preferred_element_type=jnp.float32)

    def up_term(start, count):
        return jnp.einsum("tf,df->td", grad_upper, w_up, preferred_element_type=jnp.float32)

    grad_y1 = grad_h2 + back_sum(up_term, share)
    unused_one, pull_one = jax.vjp(norm_rows, hidden_one, attn_gain, attn_shift)
    grad_h1, grad_again, grad_ashift = pull_one(grad_y1)
    grad_attn = grad_h1.astype(jnp.bfloat16)
    grad_bout = jnp.sum(grad_attn.astype(jnp.float32), axis=0)
    full_gattn = share_back(grad_attn)
    grad_wout = jnp.einsum("tc,td->cd", context, full_gattn, preferred_element_type=jnp.float32)
    grad_context = jnp.einsum("td,cd->tc", full_gattn, w_out, preferred_element_type=jnp.float32)
    valid = (jnp.arange(length, dtype=jnp.int32)[None, :] < lengths[:, None]).astype(jnp.float32)[
        :, :, None
    ]
    grad_context = (grad_context.reshape(seqs, length, chans) * valid).astype(jnp.bfloat16)
    grad_q, grad_near_k, grad_near_v, grad_far_k, grad_far_v = attend_backward(
        queries.reshape(seqs, length, heads, HEAD_DIM),
        keys_loc.reshape(seqs, length, heads, HEAD_DIM),
        vals_loc.reshape(seqs, length, heads, HEAD_DIM),
        far_keys.reshape(seqs, pooled_len, heads, HEAD_DIM),
        far_vals.reshape(seqs, pooled_len, heads, HEAD_DIM),
        lengths,
        logsums,
        grad_context.reshape(seqs, length, heads, HEAD_DIM),
    )
    masked_keys = keys_loc.reshape(seqs, length, chans).astype(jnp.float32) * valid
    masked_vals = vals_loc.reshape(seqs, length, chans).astype(jnp.float32) * valid
    unused_pk, pull_key = jax.vjp(pool_rows, masked_keys, conv_key)
    grad_kpool, grad_ckey = pull_key(grad_far_k.reshape(seqs, pooled_len, chans))
    unused_pv, pull_val = jax.vjp(pool_rows, masked_vals, conv_value)
    grad_vpool, grad_cval = pull_val(grad_far_v.reshape(seqs, pooled_len, chans))
    grad_queries = grad_q.reshape(total_rows, chans).astype(jnp.bfloat16)
    grad_keys = (
        (grad_near_k.reshape(seqs, length, chans) + grad_kpool * valid)
        .reshape(total_rows, chans)
        .astype(jnp.bfloat16)
    )
    grad_vals = (
        (grad_near_v.reshape(seqs, length, chans) + grad_vpool * valid)
        .reshape(total_rows, chans)
        .astype(jnp.bfloat16)
    )
    grad_wquery = jnp.einsum("td,tc->dc", full_in, grad_queries, preferred_element_type=jnp.float32)
    grad_wkey = jnp.einsum("td,tc->dc", full_in, grad_keys, preferred_element_type=jnp.float32)
    grad_wvalue = jnp.einsum("td,tc->dc", full_in, grad_vals, preferred_element_type=jnp.float32)
    grad_bquery = jnp.sum(grad_queries.astype(jnp.float32), axis=0)
    grad_bvalue = jnp.sum(grad_vals.astype(jnp.float32), axis=0)

    def input_term(start, count):
        total = jnp.einsum("tc,dc->td", grad_queries, w_query, preferred_element_type=jnp.float32)
        total = total + jnp.einsum(
            "tc,dc->td", grad_keys, w_key, preferred_element_type=jnp.float32
        )
        return total + jnp.einsum(
            "tc,dc->td", grad_vals, w_value, preferred_element_type=jnp.float32
        )

    grad_input = grad_h1 + back_sum(input_term, share)
    matrices = (
        grad_wquery[None],
        grad_wkey[None],
        grad_wvalue[None],
        grad_wout[None],
        grad_wup[None],
        grad_wdown[None],
    )
    vectors = (
        spread(grad_bquery, D)[None],
        spread(grad_bvalue, D)[None],
        spread(grad_ckey, D)[None],
        spread(grad_cval, D)[None],
        grad_bout[None],
        grad_again[None],
        grad_ashift[None],
        spread(grad_bup, FF)[None],
        grad_bdown[None],
        grad_fgain[None],
        grad_fshift[None],
    )
    return (grad_input, matrices, vectors)


def on_device(
    tokens,
    lengths,
    w_query,
    w_key,
    w_value,
    b_query,
    b_value,
    conv_key,
    conv_value,
    w_out,
    b_out,
    attn_gain,
    attn_shift,
    w_up,
    b_up,
    w_down,
    b_down,
    ffn_gain,
    ffn_shift,
    cotangent,
):
    stacks = (
        w_query,
        w_key,
        w_value,
        b_query,
        b_value,
        conv_key,
        conv_value,
        w_out,
        b_out,
        attn_gain,
        attn_shift,
        w_up,
        b_up,
        w_down,
        b_down,
        ffn_gain,
        ffn_shift,
    )
    total_rows = tokens.shape[0]
    share = total_rows // lax.axis_size("mp")
    place = lax.axis_index("mp") * share
    resid = lax.dynamic_slice_in_dim(tokens, place, share, 0).astype(jnp.float32)
    layer = 0
    params = tuple((stack[layer] for stack in stacks))
    result, kept = layer_forward(tokens, resid, lengths, params, share)
    kept_all = [kept]
    activations = result.astype(jnp.bfloat16)
    grad_out = cotangent.astype(jnp.float32)
    matrix_list = [None] * LAYERS
    vector_list = [None] * LAYERS
    for layer in reversed(range(LAYERS)):
        params = tuple((stack[layer] for stack in stacks))
        grad_out, matrices, vectors = layer_backward(
            grad_out, kept_all[layer], params, lengths, share
        )
        matrix_list[layer] = matrices
        vector_list[layer] = vectors
    grad_wquery, grad_wkey, grad_wvalue, grad_wout, grad_wup, grad_wdown = tuple(
        (jnp.concatenate([entry[index] for entry in matrix_list], axis=0) for index in range(6))
    )
    (
        grad_bquery,
        grad_bvalue,
        grad_ckey,
        grad_cval,
        grad_bout,
        grad_again,
        grad_ashift,
        grad_bup,
        grad_bdown,
        grad_fgain,
        grad_fshift,
    ) = tuple(
        (jnp.concatenate([entry[index] for entry in vector_list], axis=0) for index in range(11))
    )
    grad_wquery, grad_wkey, grad_wvalue, grad_wout, grad_wup, grad_wdown = (
        lax.psum_scatter(grad_wquery, "dp", scatter_dimension=1, tiled=True),
        lax.psum_scatter(grad_wkey, "dp", scatter_dimension=1, tiled=True),
        lax.psum_scatter(grad_wvalue, "dp", scatter_dimension=1, tiled=True),
        lax.psum_scatter(grad_wout, "dp", scatter_dimension=2, tiled=True),
        lax.psum_scatter(grad_wup, "dp", scatter_dimension=1, tiled=True),
        lax.psum_scatter(grad_wdown, "dp", scatter_dimension=2, tiled=True),
    )
    (
        grad_bquery,
        grad_bvalue,
        grad_ckey,
        grad_cval,
        grad_bout,
        grad_again,
        grad_ashift,
        grad_bup,
        grad_bdown,
        grad_fgain,
        grad_fshift,
    ) = lax.psum(
        (
            grad_bquery,
            grad_bvalue,
            grad_ckey,
            grad_cval,
            grad_bout,
            grad_again,
            grad_ashift,
            grad_bup,
            grad_bdown,
            grad_fgain,
            grad_fshift,
        ),
        ("dp", "mp"),
    )
    return (
        activations,
        grad_out,
        grad_wquery,
        grad_wkey,
        grad_wvalue,
        grad_bquery,
        grad_bvalue,
        grad_ckey,
        grad_cval,
        grad_wout,
        grad_bout,
        grad_again,
        grad_ashift,
        grad_wup,
        grad_bup,
        grad_wdown,
        grad_bdown,
        grad_fgain,
        grad_fshift,
    )


BF = jnp.bfloat16
F32 = jnp.float32
MESH = pl.DeviceIdType.MESH
ROWS = 256
QUARTERS = 4
CHANS = D // QUARTERS
QHEADS = CHANS // HEAD_DIM
SEQ = QUARTERS * ROWS
REACH = WINDOW // 2
PREACH = POOL_WINDOW // 2 // STRIDE
OWNP = ROWS // STRIDE
KW = ROWS + 2 * REACH
KP = OWNP + 2 * PREACH
KEYS = KW + KP
QB = 128
NEAR = QB + 2 * REACH
FAR = QB // STRIDE + 2 * PREACH
COMP = 800
HALFC = COMP // 2
FRONT = 256
KVROWS = 1408
BASE = 288
PIECE = D // 8
BIG_NEG = -1e30
SCALE = HEAD_DIM ** -0.5
VROWS = 64
TILES = 2 * CHANS // 128


def nn(a, b):
    return jnp.dot(a, b, preferred_element_type=F32)


def nt(a, b):
    return lax.dot_general(a, b, (((1,), (1,)), ((), ())), preferred_element_type=F32)


def tn(a, b):
    return lax.dot_general(a, b, (((0,), (0,)), ((), ())), preferred_element_type=F32)


def rows_iota(rows, cols):
    return lax.broadcasted_iota(jnp.int32, (rows, cols), 0)


def cols_iota(rows, cols):
    return lax.broadcasted_iota(jnp.int32, (rows, cols), 1)


def mean_row(v):
    return jnp.mean(v, axis=-1, keepdims=True)


def sum_col(v):
    return jnp.sum(v, axis=0, keepdims=True)


def kernel(
    len_ref, tok_hbm, wk, wv, wq, wo, wup, wdown, bq, bv, ck, cv, bup, bo, ag, ash, bd, fg, fs, cot_hbm,
    act_out, gtok, gmats, gvec,
    W, VEC, kvf, KV, KVS, Q, CTX, P, maskn, maskf, n1, r1, y1, y1b, dg, av,
    yT, fT, gab, GKV, pt, GQ, VG,
    CR, S1, S2, ZR, HL, HR, HLL, SL, SR, GVR, GVZ, VO, tok, cot,
    lsem, asend, arecv, zsend, zrecv, lsend, hsend, hrecv, rsend, rrecv, zsum, gsend, grecv,
):
    acc, n2, xT, gub = gtok, y1, yT, y1b
    dp = lax.axis_index("dp")
    z = lax.axis_index("mp")
    c = lax.rem(dp, 2)
    x = lax.rem(lax.div(dp, 2), 2)
    y = lax.div(dp, 4)
    core = (dp + 1 - 2 * c, z)
    xdev = (dp + 2 - 4 * x, z)
    ydev = (dp + 4 - 8 * y, z)
    yx = 2 * y + x
    length = len_ref[0]

    def zdev(step):
        return (dp, lax.rem(z + step, QUARTERS))

    def rcopy(src, dst, ssem, rsem, dev):
        return pltpu.make_async_remote_copy(
            src_ref=src, dst_ref=dst, send_sem=ssem, recv_sem=rsem,
            device_id=dev, device_id_type=MESH,
        )

    barrier = pltpu.get_barrier_semaphore()
    for dev in (core, xdev, ydev, zdev(1), zdev(2), zdev(3)):
        pl.semaphore_signal(barrier, inc=1, device_id=dev, device_id_type=MESH)

    def loads():
        parts = [(wk, 0), (wv, CHANS), (wq, 2 * CHANS), (wo, 3 * CHANS)]
        copies = [
            pltpu.make_async_copy(src, W.at[0, z, at : at + CHANS, :], lsem.at[i])
            for i, (src, at) in enumerate(parts)
        ]
        copies.append(pltpu.make_async_copy(wup, W.at[1, z], lsem.at[4]))
        copies.append(pltpu.make_async_copy(wdown, W.at[2, z], lsem.at[5]))
        return copies

    own = loads()
    tok_in = pltpu.make_async_copy(tok_hbm, tok, lsem.at[6])
    cot_in = pltpu.make_async_copy(cot_hbm, cot, lsem.at[7])
    for cp in own:
        cp.start()
    tok_in.start()
    cot_in.start()
    vpack = VG.at[0:8, :]
    vpack[...] = jnp.zeros_like(vpack)
    vpack[0:1, :] = bup[...]
    vpack[1:2, CHANS : 2 * CHANS] = bv[...]
    vpack[1:2, 2 * CHANS : 3 * CHANS] = bq[...]
    for t in range(5):
        vpack[2 + t : 3 + t, 0:CHANS] = ck[t]
        vpack[2 + t : 3 + t, CHANS : 2 * CHANS] = cv[t]
    VEC[z] = vpack[...]
    pl.semaphore_wait(barrier, 6)

    def block(j):
        return pl.ds(pl.multiple_of(j * PIECE, PIECE), PIECE)

    piece_me = c * 4 + yx
    piece_x = c * 4 + 2 * y + 1 - x
    piece_y = c * 4 + 2 * (1 - y) + x
    piece_d = c * 4 + 2 * (1 - y) + 1 - x
    LO, HI = pl.ds(0, D // 2), pl.ds(D // 2, D // 2)
    ALL = pl.ds(0, D)
    CHUNKS = 9
    ends = [(0, 1), (1, 1), (0, 2), (1, 2), (0, 3), (2, 1), (2, 2), (1, 3), (2, 3)]
    inner = [(0, 1), (0, 2), (1, 1), (1, 2), (0, 3), (2, 1), (2, 2), (1, 3), (2, 3)]
    sources = [(1, 2, 3), (2, 0, 3), (1, 3, 0), (2, 1, 0)]
    targets = [(3, 2, 1, 0), (3, 0, 2, 1), (0, 3, 1, 2), (0, 1, 2, 3)]
    DOWN = 2
    FAR_STEPS = 2
    at_end = (z == 0) | (z == QUARTERS - 1)

    def table(values, bits=2):
        word = sum(v << (bits * i) for i, v in enumerate(values))
        return jnp.int32(word - (1 << 32) if word >> 31 else word)

    def lookup(word, i, bits=2):
        return lax.bitwise_and(lax.shift_right_logical(word, bits * i), (1 << bits) - 1)

    def by_place(a, b):
        return lax.select(at_end, a, b)

    mats_of = by_place(table(m for m, d in ends), table(m for m, d in inner))
    dist_of = by_place(table(d for m, d in ends), table(d for m, d in inner))
    looks_of = by_place(table((1, 2, 4, 5, 6, 7, 8, 9), 4), table((2, 4, 5, 7, 8, 9, 9, 9), 4))
    sends_of = by_place(table((1, 2, 4, 5, 6, 7, 8, 9), 4), table((2, 3, 4, 5, 6, 7, 8, 9), 4))

    def source(d):
        return lookup(table(v for row in sources for v in row), 3 * z + d - 1)

    def target(t):
        return lookup(table(v for row in targets for v in row), 4 * z + t)

    def chunk(k):
        return lookup(mats_of, k), source(lookup(dist_of, k))

    def is_far(k):
        return (lookup(mats_of, k) == DOWN) & (lookup(dist_of, k) < FAR_STEPS)

    def own_block(m, up, piece, sem):
        src = W.at[m, z, block(piece), :]
        return rcopy(src, src, zsend.at[sem, up], zrecv.at[sem, z], (dp, z + 2 * up - 1))

    def own_z(m, up):
        return own_block(m, up, piece_me, m)

    def far_z(up):
        return own_block(DOWN, up, piece_d, 4)

    def wants_far(up):
        to = z + 2 * up - 1
        inner_to = (to == 1) | (to == 2)
        return jnp.logical_not(inner_to) | (z == 3 - to)

    def relay(m, src, dev):
        ref = W.at[m, src, block(piece_me), :]
        return rcopy(ref, ref, lsend.at[m, src], zrecv.at[m, src], dev)

    def relay_far(src, dev):
        ref = W.at[DOWN, src, block(piece_d), :]
        return rcopy(ref, ref, lsend.at[4, src], zrecv.at[4, src], dev)

    def own_vec(up):
        src = VEC.at[z]
        return rcopy(src, src, zsend.at[3, up], zrecv.at[3, z], (dp, z + 2 * up - 1))

    def relay_vec(src, dev):
        ref = VEC.at[src]
        return rcopy(ref, ref, lsend.at[3, src], zrecv.at[3, src], dev)

    def onward(src):
        return jnp.where(src > z, z > 0, z < QUARTERS - 1)

    def next_dev(src):
        return (dp, jnp.where(src > z, z - 1, z + 1))

    def plane(k, which, piece, cols, dev):
        m, src = chunk(k)
        ref = W.at[m, src, block(piece), cols]
        return rcopy(ref, ref, asend.at[k, which], arecv.at[k, which], dev)

    def look(k):
        m, src = chunk(k)

        @pl.when(m == 0)
        def _():
            relay_vec(src, core).wait_recv()
            pl.when(onward(src))(lambda: relay_vec(src, next_dev(src)).start())

        relay(m, src, core).wait_recv()
        pl.when(onward(src))(lambda: relay(m, src, next_dev(src)).start())

        @pl.when(is_far(k))
        def _():
            relay_far(src, core).wait_recv()

    def first(k):
        plane(k, 1, piece_me, ALL, xdev).start()
        plane(k, 2, piece_me, ALL, ydev).start()

    def second(k):
        full = jnp.logical_not(is_far(k))
        plane(k, 1, piece_x, ALL, xdev).wait_recv()
        pl.when(full)(lambda: plane(k, 3, piece_x, LO, ydev).start())
        plane(k, 2, piece_y, ALL, ydev).wait_recv()
        pl.when(full)(lambda: plane(k, 4, piece_y, HI, xdev).start())

    def half(j):
        return pl.ds(pl.multiple_of(j * (D // 2), D // 2), D // 2)

    def cross(k, j):
        m, src = chunk(k)
        ref = W.at[m, src, half(j), :]
        return rcopy(ref, ref, asend.at[k, 5], arecv.at[k, 5], core)

    def third(k):
        @pl.when(jnp.logical_not(is_far(k)))
        def _():
            plane(k, 3, piece_d, LO, ydev).wait_recv()
            plane(k, 4, piece_d, HI, xdev).wait_recv()

        cross(k, c).start()

    def fourth(k):
        cross(k, 1 - c).wait_recv()

    def looks(i):
        return jnp.where(i < 0, 0, lookup(looks_of, lax.clamp(0, i, 7), 4))

    def sends(i):
        return jnp.where(i < 0, 0, lookup(sends_of, lax.clamp(0, i, 7), 4))

    def each(fn):
        def body(k, carry):
            fn(k)
            return carry

        return body

    def gather_slot(i, carry):
        lax.fori_loop(looks(i - 1), looks(i), each(look), 0)
        pl.when((i == 2) & jnp.logical_not(at_end))(lambda: both(own_down))
        lax.fori_loop(sends(i - 1), sends(i), each(first), 0)
        for lag, stage in ((1, second), (2, third), (3, fourth)):
            k = i - lag
            pl.when((k >= 0) & (k < CHUNKS))(lambda stage=stage, k=k: stage(k))
        return carry

    def gather_done(k, carry):
        m, src = chunk(k)

        @pl.when(onward(src))
        def _():
            relay(m, src, core).wait_send()
            pl.when(m == 0)(lambda: relay_vec(src, core).wait_send())

        plane(k, 1, piece_me, ALL, xdev).wait_send()
        plane(k, 2, piece_me, ALL, ydev).wait_send()

        @pl.when(jnp.logical_not(is_far(k)))
        def _():
            plane(k, 3, piece_x, LO, ydev).wait_send()
            plane(k, 4, piece_y, HI, xdev).wait_send()

        cross(k, c).wait_send()
        return carry

    def got(s):
        return lax.rem(z + QUARTERS - s, QUARTERS)

    def both(fn):
        pl.when(z > 0)(lambda: fn(0))
        pl.when(z < QUARTERS - 1)(lambda: fn(1))

    both(lambda up: own_vec(up).start())
    for m, waits in enumerate((own[:4], own[4:5], own[5:])):
        for cp in waits:
            cp.wait()
        if m != DOWN:
            both(lambda up: own_z(m, up).start())

    def own_down(up):
        own_z(DOWN, up).start()
        pl.when(wants_far(up))(lambda: far_z(up).start())

    pl.when(at_end)(lambda: both(own_down))

    def own_sent(up):
        own_vec(up).wait_send()
        for m in range(3):
            own_z(m, up).wait_send()
        pl.when(wants_far(up))(lambda: far_z(up).wait_send())

    base = z * ROWS
    start = lax.select(z < 2, jnp.int32(0), jnp.int32(SEQ - COMP))
    place = pl.multiple_of(start - base + BASE + FRONT, 32)
    start = pl.multiple_of(start, 32)
    kvf[...] = jnp.zeros_like(kvf)
    for b in range(2):
        i = base + b * QB + cols_iota(1, QB)
        j = base - REACH + b * QB + rows_iota(NEAR, 1)
        ok = (jnp.abs(i - j) <= REACH) & (j >= 0) & (j < length)
        maskn[b] = jnp.where(ok, 0.0, BIG_NEG)
        j = (OWNP * z - PREACH + b * (QB // STRIDE) + rows_iota(FAR, 1)) * STRIDE
        ok = (jnp.abs(i - j) <= POOL_WINDOW // 2) & (j >= 0) & (j < length)
        maskf[b] = jnp.where(ok, 0.0, BIG_NEG)
    own_rows = pl.ds(pl.multiple_of(base, ROWS), ROWS)
    tok_in.wait()
    cot_in.wait()
    xb = tok[own_rows, :]
    acc[...] = jnp.zeros_like(acc)

    def taps(zq, t):
        return VEC[zq, 2 + t : 3 + t, 0 : 2 * CHANS]

    def strided(t):
        at = pl.ds(FRONT + BASE - POOL_WINDOW // 2 - 2 + t, KP, stride=STRIDE)
        return jnp.concatenate([kvf[i, at, :] for i in range(TILES)], axis=1)

    def tile(i):
        return slice(i * 128, (i + 1) * 128)

    def window(lo, rows):
        return jnp.concatenate([kvf[i, lo : lo + rows, :] for i in range(TILES)], axis=1)

    def quarter(s):
        return lax.select(s == 0, z, source(lax.max(s, 1)))

    def attend(s, carry):
        zq = quarter(s)
        for blk in range(2):
            xr = tok[pl.ds(pl.multiple_of(start + blk * HALFC, 16), HALFC), :]
            kv = nt(xr, W[0, zq, 0 : 2 * CHANS, :]) + VEC[zq, 1:2, 0 : 2 * CHANS]
            pos = start + blk * HALFC + rows_iota(HALFC, 1)
            kvb = jnp.where(pos < length, kv.astype(BF).astype(F32), 0.0)
            for i in range(TILES):
                kvf[i, pl.ds(pl.multiple_of(place + blk * HALFC, 8), HALFC), :] = kvb[:, tile(i)]
        KVS[zq] = window(FRONT, COMP).astype(BF)
        KV[zq, 0:KW, :] = window(FRONT + BASE - REACH, KW).astype(BF)
        pooled = jnp.zeros((KP, 2 * CHANS), F32)
        for t in range(5):
            pooled = pooled + taps(zq, t) * strided(t)
        KV[zq, KW:KEYS, :] = pooled.astype(BF)
        qz = nt(xb, W[0, zq, 2 * CHANS : 3 * CHANS, :]) + VEC[zq, 1:2, 2 * CHANS : 3 * CHANS]
        Q[zq] = qz.astype(BF)
        for b in range(2):
            live = base + b * QB + cols_iota(1, QB) < length
            n0, f0 = b * QB, KW + b * (QB // STRIDE)
            for h in range(QHEADS):
                kl = slice(h * HEAD_DIM, (h + 1) * HEAD_DIM)
                vl = slice(CHANS + h * HEAD_DIM, CHANS + (h + 1) * HEAD_DIM)
                qh = Q[zq, b * QB : (b + 1) * QB, kl]
                sn = nt(KV[zq, n0 : n0 + NEAR, kl], qh) * SCALE + maskn[b]
                sf = nt(KV[zq, f0 : f0 + FAR, kl], qh) * SCALE + maskf[b]
                peak = jnp.maximum(
                    jnp.max(sn, axis=0, keepdims=True), jnp.max(sf, axis=0, keepdims=True)
                )
                en, ef = jnp.exp(sn - peak), jnp.exp(sf - peak)
                inv = 1.0 / (sum_col(en) + sum_col(ef))
                pn, pf = en * inv, ef * inv
                P[zq, h, b, 0:NEAR, :] = pn
                P[zq, h, b, NEAR : NEAR + FAR, :] = pf
                ct = tn(KV[zq, n0 : n0 + NEAR, vl], pn.astype(BF))
                ct = ct + tn(KV[zq, f0 : f0 + FAR, vl], pf.astype(BF))
                ct = jnp.where(live, ct, 0.0)
                CTX[zq, b * QB : (b + 1) * QB, kl] = ct.T.astype(BF)
        acc[...] += nn(CTX[zq], W[0, zq, 3 * CHANS : D, :])
        lax.fori_loop(lookup_slots(s), lookup_slots(s + 1), gather_slot, 0)
        return carry

    def lookup_slots(s):
        return jnp.where(s == 0, 0, jnp.where(s < 3, 2 + 2 * s, 8))

    lax.fori_loop(0, QUARTERS, attend, 0)

    def store_T(dst, v, cols):
        vt = v.T.astype(BF)
        for j in range(8):
            to = (j % 2) * 4 + j // 2
            dst[to * PIECE : (to + 1) * PIECE, cols] = vt[j * PIECE : (j + 1) * PIECE]

    def span(i, size):
        if isinstance(i, int):
            return pl.ds(i * size, size)
        return pl.ds(pl.multiple_of(i * size, size), size)

    def norm_one(i, carry):
        rows = span(i, QB)
        res = tok[pl.ds(pl.multiple_of(base + i * QB, QB), QB), :].astype(F32)
        hid = res + (acc[rows, :] + bo[...])
        cen = hid - mean_row(hid)
        r = lax.rsqrt(mean_row(cen * cen) + epsilon)
        n = cen * r
        n1[rows, :] = n
        r1[rows, :] = r
        out = n * ag[...] + ash[...]
        y1[rows, :] = out
        y1b[rows, :] = out.astype(BF)
        store_T(yT, out, rows)
        acc[rows, :] = jnp.zeros_like(out)
        return carry

    lax.fori_loop(0, ROWS // QB, norm_one, 0)

    def feed(s, carry):
        zq = quarter(s)

        def up(i, carry):
            cols = span(i, ROWS)
            u = nn(y1b[...], W[1, zq, :, cols]) + VEC[zq, 0:1, cols]
            cdf = 0.5 * (1.0 + lax.erf(u * (0.5 ** 0.5)))
            dg[zq, :, cols] = cdf + u * jnp.exp(-0.5 * u * u) * ((2.0 * 3.141592653589793) ** -0.5)
            av[zq, :, cols] = (u * cdf).astype(BF)
            return carry

        for i in range(D // ROWS):
            up(i, 0)
        acc[...] += nn(av[zq], W[2, zq])
        lo = jnp.where(s < 3, 8 + s, 12)
        hi = jnp.where(s < 2, 9 + s, 12)
        lax.fori_loop(lo, hi, gather_slot, 0)
        return carry

    lax.fori_loop(0, QUARTERS, feed, 0)
    VG[...] = jnp.zeros_like(VG)
    GEN = 8 * QUARTERS

    def add_row(row, v):
        VG[row : row + 1, :] += sum_col(v)

    def norm_two(i, carry):
        rows = span(i, QB)
        hid = y1[rows, :] + (acc[rows, :] + bd[...])
        cen = hid - mean_row(hid)
        r = lax.rsqrt(mean_row(cen * cen) + epsilon)
        n = cen * r
        act_out[rows, :] = (n * fg[...] + fs[...]).astype(BF)
        g = cot[rows, :].astype(F32)
        add_row(GEN + 4, g * n)
        add_row(GEN + 5, g)
        e = g * fg[...]
        gh2 = r * (e - mean_row(e) - n * mean_row(e * n))
        acc[rows, :] = gh2
        gf = gh2.astype(BF)
        gab[rows, :] = gf
        gff = gf.astype(F32)
        add_row(GEN + 3, gff)
        store_T(fT, gff, rows)
        return carry

    lax.fori_loop(0, ROWS // QB, norm_two, 0)

    PARTS = 12

    def part(r):
        m = lax.select(r < 8, 2 - lax.rem(r, 2), 0)
        t = lax.select(r < 8, lax.div(r, 2), r - 8)
        return m, t

    def r_core(r):
        m, t = part(r)
        src = W.at[m, target(t), half(1 - c), :]
        return rcopy(src, CR.at[r], rsend.at[r, 0], rrecv.at[r, 0], core)

    def blk4(r, yy, xx, cols):
        return CR.at[r, block(2 * yy + xx), cols]

    def r_stage1(r, i):
        if i < 2:
            src, dev = blk4(r, i, 1 - x, LO), xdev
        else:
            src, dev = blk4(r, 1 - y, i - 2, HI), ydev
        return rcopy(src, S1.at[r, i], rsend.at[r, 1 + i], rrecv.at[r, 1 + i], dev)

    def r_stage2(r, i):
        if i == 0:
            src, dev = blk4(r, 1 - y, x, LO), ydev
        else:
            src, dev = blk4(r, y, 1 - x, HI), xdev
        return rcopy(src, S2.at[r, i], rsend.at[r, 5 + i], rrecv.at[r, 5 + i], dev)

    def r_z(r):
        m, t = part(r)
        dst = target(t)
        left = dst < z
        slot = jnp.where(left & (dst == z - 1), QUARTERS, dst)
        src = CR.at[r, block(yx), :]
        dev = (dp, jnp.where(left, z - 1, z + 1))
        return rcopy(src, ZR.at[m, slot], rsend.at[r, 7], zsum.at[m, slot], dev)

    def z_in(m, slot):
        ref = ZR.at[m, slot]
        return rcopy(ref, ref, zsum.at[m, slot], zsum.at[m, slot], core)

    def upstream(dst):
        return jnp.where(dst < z, z < QUARTERS - 1, z > 0)

    def reduce1(r):
        m, t = part(r)
        r_core(r).wait_recv()
        zq = target(t)

        def add(i, carry):
            CR[r, block(i), :] = CR[r, block(i), :] + W[m, zq, block(4 * c + i), :]
            return carry

        lax.fori_loop(0, 4, add, 0)
        for i in range(4):
            r_stage1(r, i).start()

    def reduce2(r):
        for i in range(4):
            r_stage1(r, i).wait_recv()
        for i in range(2):
            a = blk4(r, i, x, LO)
            a[...] = a[...] + S1[r, i]
            a = blk4(r, y, i, HI)
            a[...] = a[...] + S1[r, 2 + i]
        for i in range(2):
            r_stage2(r, i).start()

    def reduce3(r):
        for i in range(2):
            r_stage2(r, i).wait_recv()
        for i, cols in enumerate((LO, HI)):
            a = blk4(r, y, x, cols)
            a[...] = a[...] + S2[r, i]
        dst = target(part(r)[1])
        pl.when((dst != z) & jnp.logical_not(upstream(dst)))(lambda: r_z(r).start())

    def reduce4(r):
        m, t = part(r)
        dst = target(t)

        @pl.when((dst != z) & upstream(dst))
        def _():
            z_in(m, dst).wait_recv()
            CR[r, block(yx), :] = CR[r, block(yx), :] + ZR[m, dst]
            r_z(r).start()

    def stage(fn, ok, r):
        pl.when(ok)(lambda: fn(r))

    def weight_grad(left, right, dst, width):
        dst[:, 0:width] = nn(left[...], right).astype(BF)

    def feed_back(s, carry):
        zq = target(s)
        vrow = pl.multiple_of(8 * zq, 8)

        def hidden(i, carry):
            cols = span(i, ROWS)
            gact = nt(gab[...], W[2, zq, cols, :])
            gu = (gact * dg[zq, :, cols]).astype(BF)
            gub[:, cols] = gu
            VG[pl.ds(vrow, 1), cols] = sum_col(gu.astype(F32))
            return carry

        for i in range(D // ROWS):
            hidden(i, 0)
        weight_grad(fT, av[zq], W.at[2, zq], D)
        r_core(2 * s).start()
        acc[...] += nt(gub[...], W[1, zq])
        weight_grad(yT, gub[...], W.at[1, zq], D)
        r_core(2 * s + 1).start()
        reduce1(jnp.where(s < 2, s, s + 1))
        stage(reduce1, s == 1, jnp.int32(2))
        stage(reduce2, s == 3, jnp.int32(0))
        return carry

    lax.fori_loop(0, CHUNKS, gather_done, 0)
    both(own_sent)
    lax.fori_loop(0, QUARTERS, feed_back, 0)

    def norm_back(i, carry):
        rows = span(i, QB)
        gy = acc[rows, :]
        n = n1[rows, :]
        add_row(GEN + 1, gy * n)
        add_row(GEN + 2, gy)
        e = gy * ag[...]
        gh1 = r1[rows, :] * (e - mean_row(e) - n * mean_row(e * n))
        acc[rows, :] = gh1
        ga = gh1.astype(BF)
        gab[rows, :] = ga
        gaf = ga.astype(F32)
        add_row(GEN, gaf)
        store_T(fT, gaf, rows)
        store_T(xT, tok[pl.ds(pl.multiple_of(base + i * QB, QB), QB), :].astype(F32), rows)
        return carry

    lax.fori_loop(0, ROWS // QB, norm_back, 0)

    def hl(zq):
        return rcopy(SL.at[zq], HL.at[zq], hsend.at[0, zq], hrecv.at[0, zq], zdev(3))

    def hr(zq):
        return rcopy(SR.at[zq], HR.at[zq], hsend.at[1, zq], hrecv.at[1, zq], zdev(1))

    def hll(zq):
        return rcopy(
            SL.at[zq, REACH : REACH + 16, :], HLL.at[zq], hsend.at[2, zq], hrecv.at[2, zq], zdev(2)
        )

    def attend_back(s, carry):
        zq = lookup(table((0, 3, 1, 2)), s)
        gc = nt(gab[...], W[0, zq, 3 * CHANS : D, :])
        alive = base + rows_iota(ROWS, 1) < length
        gcb = jnp.where(alive, gc, 0.0).astype(BF)
        GKV[zq] = jnp.zeros((KEYS, 2 * CHANS), F32)
        for b in range(2):
            n0, f0 = b * QB, KW + b * (QB // STRIDE)
            for h in range(QHEADS):
                kl = slice(h * HEAD_DIM, (h + 1) * HEAD_DIM)
                vl = slice(CHANS + h * HEAD_DIM, CHANS + (h + 1) * HEAD_DIM)
                gch = gcb[b * QB : (b + 1) * QB, kl]
                qh = Q[zq, b * QB : (b + 1) * QB, kl]
                pn = P[zq, h, b, 0:NEAR, :]
                pf = P[zq, h, b, NEAR : NEAR + FAR, :]
                gpn = nt(KV[zq, n0 : n0 + NEAR, vl], gch)
                gpf = nt(KV[zq, f0 : f0 + FAR, vl], gch)
                delta = sum_col(pn * gpn) + sum_col(pf * gpf)
                gsn = (pn * (gpn - delta)).astype(BF)
                gsf = (pf * (gpf - delta)).astype(BF)
                qt = tn(KV[zq, n0 : n0 + NEAR, kl], gsn) + tn(KV[zq, f0 : f0 + FAR, kl], gsf)
                GQ[zq, b * QB : (b + 1) * QB, 2 * CHANS + h * HEAD_DIM : 2 * CHANS + (h + 1) * HEAD_DIM] = (
                    (qt * SCALE).T.astype(BF)
                )
                GKV[zq, n0 : n0 + NEAR, kl] += nn(gsn, qh) * SCALE
                GKV[zq, f0 : f0 + FAR, kl] += nn(gsf, qh) * SCALE
                GKV[zq, n0 : n0 + NEAR, vl] += nn(pn.astype(BF), gch)
                GKV[zq, f0 : f0 + FAR, vl] += nn(pf.astype(BF), gch)
        vrow = pl.multiple_of(8 * zq, 8)
        for i in range(TILES):
            kvf[i, FRONT : FRONT + COMP, :] = KVS[zq, :, tile(i)].astype(F32)
        gp = GKV[zq, KW:KEYS, :]
        sums = jnp.concatenate(
            [jnp.zeros((1, CHANS), F32), sum_col(GKV[zq, 0:KW, CHANS : 2 * CHANS])], axis=1
        )
        far_at = (OWNP * z - PREACH + rows_iota(KP, 1)) * STRIDE
        for t in range(5):
            VG[pl.ds(vrow + 2 + t, 1), 0 : 2 * CHANS] = sum_col(gp * strided(t))
            to = far_at + (t - 2)
            inside = (to >= 0) & (to < length)
            sums = sums + taps(zq, t) * sum_col(jnp.where(inside, gp, 0.0))
        VG[pl.ds(vrow + 1, 1), CHANS : 2 * CHANS] = sums[:, CHANS : 2 * CHANS]
        VG[pl.ds(vrow + 1, 1), 2 * CHANS : 3 * CHANS] = sum_col(
            GQ[zq, :, 2 * CHANS : 3 * CHANS].astype(F32)
        )
        SL[zq, 0:REACH, :] = GKV[zq, 0:REACH, :].astype(BF)
        SL[zq, REACH : REACH + 80, :] = GKV[zq, KW : KW + 80, :].astype(BF)
        SR[zq, 0:REACH, :] = GKV[zq, KW - REACH : KW, :].astype(BF)
        SR[zq, REACH : REACH + OWNP, :] = GKV[zq, KEYS - OWNP : KEYS, :].astype(BF)
        pl.when(z > 0)(lambda: hl(zq).start())
        pl.when(z < QUARTERS - 1)(lambda: hr(zq).start())
        pl.when(z > 1)(lambda: hll(zq).start())
        stage(reduce1, s == 0, jnp.int32(5))
        reduce2(s + 1)
        stage(reduce3, s == 3, jnp.int32(0))
        return carry

    lax.fori_loop(0, QUARTERS, attend_back, 0)

    half_row = pl.multiple_of(32 * c, 32)
    row_x = pl.multiple_of(half_row + 16 * x, 16)
    row_y = pl.multiple_of(row_x + 8 * y, 8)

    def vrows(at, size):
        return pl.ds(pl.multiple_of(at, 8), size)

    folds = [
        (core, VG.at[vrows(32 - half_row, 32), :], GVR.at[0:32], vrows(half_row, 32)),
        (xdev, VG.at[vrows(half_row + 16 - 16 * x, 16), :], GVR.at[32:48], vrows(row_x, 16)),
        (ydev, VG.at[vrows(row_x + 8 - 8 * y, 8), :], GVR.at[48:56], vrows(row_y, 8)),
    ]

    def fold(i):
        dev, src, dst, keep = folds[i]
        return rcopy(src, dst, gsend.at[i], grecv.at[i], dev)

    def fold_done(i):
        fold(i).wait()
        keep = folds[i][3]
        VG[keep, :] = VG[keep, :] + folds[i][2][...]

    def g_z(s):
        src = VG.at[vrows(row_y, 8), :]
        return rcopy(src, GVZ.at[z], gsend.at[2 + s], grecv.at[2 + s], zdev(s))

    def g_z_in(s):
        dst = GVZ.at[got(s)]
        return rcopy(dst, dst, gsend.at[2 + s], grecv.at[2 + s], core)

    opens = [
        (ydev, vrows(row_y, 8), vrows(row_x + 8 - 8 * y, 8)),
        (xdev, vrows(row_x, 16), vrows(half_row + 16 - 16 * x, 16)),
        (core, vrows(half_row, 32), vrows(32 - half_row, 32)),
    ]

    def unfold(i):
        dev, mine, other = opens[i]
        ref = VO.at[mine, :]
        return rcopy(ref, ref, gsend.at[6 + i], grecv.at[6 + i], dev)

    def unfold_done(i):
        ref = VO.at[opens[i][2], :]
        rcopy(ref, ref, gsend.at[6 + i], grecv.at[6 + i], core).wait_recv()

    def vector_two():
        fold_done(0)
        fold(1).start()

    def vector_three():
        fold_done(1)
        fold(2).start()

    def vector_z():
        fold_done(2)
        for step in (1, 2, 3):
            g_z(step).start()
        GVZ[z] = VG[vrows(row_y, 8), :]

    def vector_back():
        for step in (1, 2, 3):
            g_z_in(step).wait_recv()
        VO[vrows(row_y, 8), :] = GVZ[0] + GVZ[1] + GVZ[2] + GVZ[3]
        unfold(0).start()

    fold(0).start()

    def project_back(s, carry):
        zq = target(s)
        pl.when(z < QUARTERS - 1)(lambda: hl(zq).wait_recv())
        pl.when(z > 0)(lambda: hr(zq).wait_recv())
        pl.when(z < QUARTERS - 2)(lambda: hll(zq).wait_recv())
        near = GKV.at[zq]

        def when(ok, v):
            return jnp.where(ok, v.astype(F32), 0.0)

        has_l, has_r, has_rr = z > 0, z < QUARTERS - 1, z < QUARTERS - 2
        near[REACH : 2 * REACH, :] += when(has_l, HR[zq, 0:REACH, :])
        near[ROWS : ROWS + REACH, :] += when(has_r, HL[zq, 0:REACH, :])
        gp = GKV[zq, KW + OWNP : KW + 2 * OWNP, :] + when(has_l, HR[zq, REACH : REACH + OWNP, :])
        gp = gp + when(has_r, HL[zq, REACH : REACH + OWNP, :])
        nxt = GKV[zq, KW + 2 * OWNP : KW + 2 * OWNP + 1, :]
        nxt = nxt + when(has_r, HL[zq, REACH + OWNP : REACH + OWNP + 16, :])[0:1, :]
        nxt = nxt + when(has_rr, HLL[zq])[0:1, :]
        gp1 = jnp.concatenate([gp[1:, :], nxt], axis=0)
        fills = (
            taps(zq, 2) * gp,
            taps(zq, 3) * gp,
            taps(zq, 4) * gp + taps(zq, 0) * gp1,
            taps(zq, 1) * gp1,
        )
        for k, fill in enumerate(fills):
            for i in range(TILES):
                pt[i, pl.ds(k, OWNP, stride=STRIDE), :] = fill[:, tile(i)]
        back = jnp.concatenate([pt[i] for i in range(TILES)], axis=1)
        alive = base + rows_iota(ROWS, 1) < length
        gkv = GKV[zq, REACH : REACH + ROWS, :] + jnp.where(alive, back, 0.0)
        GQ[zq, :, 0 : 2 * CHANS] = gkv.astype(BF)

        acc[...] += nn(GQ[zq], W[0, zq, 0 : 3 * CHANS, :])
        weight_grad(xT, GQ[zq], W.at[0, zq], 3 * CHANS)

        W[0, zq, :, 3 * CHANS : D] = nn(fT[...], CTX[zq]).astype(BF)
        r_core(8 + s).start()
        stage(reduce2, s == 0, jnp.int32(5))
        stage(reduce3, s > 0, s)
        stage(reduce4, s > 0, s - 1)
        stage(reduce1, s < 3, 8 + s)
        pl.when(s == 0)(vector_two)
        return carry

    lax.fori_loop(0, QUARTERS, project_back, 0)
    for zq in range(QUARTERS):
        pl.when(z > 0)(lambda: hl(zq).wait_send())
        pl.when(z < QUARTERS - 1)(lambda: hr(zq).wait_send())
        pl.when(z > 1)(lambda: hll(zq).wait_send())

    def final(m):
        own_part = (11, 7, 6)[m]
        gmats[m] = CR[own_part, block(yx), :].astype(F32)

        def more(slot):
            z_in(m, slot).wait_recv()
            gmats[m] += ZR[m, slot].astype(F32)

        pl.when(z > 0)(lambda: more(z))
        pl.when(z < QUARTERS - 1)(lambda: more(QUARTERS))

    def at(r):
        return jnp.int32(r)

    reduce2(at(8))
    vector_three()
    reduce1(at(6))
    reduce3(at(4))
    reduce4(at(3))
    reduce2(at(9))
    reduce1(at(7))
    reduce3(at(5))
    reduce4(at(4))
    reduce2(at(10))
    reduce1(at(11))
    reduce4(at(5))
    reduce3(at(8))
    vector_z()
    reduce3(at(9))
    reduce4(at(8))
    reduce2(at(6))
    reduce3(at(10))
    reduce4(at(9))
    vector_back()
    reduce2(at(7))
    reduce4(at(10))
    unfold_done(0)
    unfold(1).start()
    reduce2(at(11))
    reduce3(at(6))
    final(2)
    reduce3(at(7))
    final(1)
    unfold_done(1)
    unfold(2).start()
    reduce3(at(11))
    final(0)
    unfold_done(2)
    gvec[...] = VO[...]
    for i in range(3):
        unfold(i).wait_send()
    for s in (1, 2, 3):
        g_z(s).wait_send()

    def sent(r, carry):
        r_core(r).wait_send()
        for i in range(4):
            r_stage1(r, i).wait_send()
        for i in range(2):
            r_stage2(r, i).wait_send()
        pl.when(part(r)[1] < QUARTERS - 1)(lambda: r_z(r).wait_send())
        return carry

    lax.fori_loop(0, PARTS, sent, 0)


def unpack(
    act, gtok, gmats, gvec,
    act_out, gtok_out, gq, gk, gv, gbq, gbv, gck, gcv, go, gbo, gag, gas, gup, gbu, gdown, gbd, gfg, gfs,
):
    act_out[...] = act[...]
    gtok_out[...] = gtok[...]
    gk[...] = gmats[0, :, 0:CHANS]
    gv[...] = gmats[0, :, CHANS : 2 * CHANS]
    gq[...] = gmats[0, :, 2 * CHANS : 3 * CHANS]
    go[...] = gmats[0, :, 3 * CHANS : D].T
    gup[...] = gmats[1]
    gdown[...] = gmats[2]
    for j in range(QUARTERS):
        at = slice(j * CHANS, (j + 1) * CHANS)
        row = 8 * j
        gbu[:, j * D : (j + 1) * D] = gvec[row : row + 1, :]
        gbv[:, at] = gvec[row + 1 : row + 2, CHANS : 2 * CHANS]
        gbq[:, at] = gvec[row + 1 : row + 2, 2 * CHANS : 3 * CHANS]
        for t in range(5):
            gck[t, :, at] = gvec[row + 2 + t : row + 3 + t, 0:CHANS]
            gcv[t, :, at] = gvec[row + 2 + t : row + 3 + t, CHANS : 2 * CHANS]
    for j, out in enumerate((gbo, gag, gas, gbd, gfg, gfs)):
        out[...] = gvec[8 * QUARTERS + j : 8 * QUARTERS + j + 1, :]


def fused_layer(
    tokens, lengths, w_query, w_key, w_value, b_query, b_value, conv_key, conv_value, w_out,
    b_out, attn_gain, attn_shift, w_up, b_up, w_down, b_down, ffn_gain, ffn_shift, cotangent,
):
    Q4 = QUARTERS
    vm = pltpu.VMEM
    dma = pltpu.SemaphoreType.DMA
    scratch = [
        vm((3, Q4, D, D), BF),
        vm((Q4, 8, D), F32),
        vm((TILES, KVROWS, 128), F32),
        vm((Q4, KEYS, 2 * CHANS), BF),
        vm((Q4, COMP, 2 * CHANS), BF),
        vm((Q4, ROWS, CHANS), BF),
        vm((Q4, ROWS, CHANS), BF),
        vm((Q4, QHEADS, 2, NEAR + FAR, QB), F32),
        vm((2, NEAR, QB), F32),
        vm((2, FAR, QB), F32),
        vm((ROWS, D), F32),
        vm((ROWS, 1), F32),
        vm((ROWS, D), F32),
        vm((ROWS, D), BF),
        vm((Q4, ROWS, D), F32),
        vm((Q4, ROWS, D), BF),
        vm((D, ROWS), BF),
        vm((D, ROWS), BF),
        vm((ROWS, D), BF),
        vm((Q4, KEYS, 2 * CHANS), F32),
        vm((TILES, ROWS, 128), F32),
        vm((Q4, ROWS, 3 * CHANS), BF),
        vm((VROWS, D), F32),
        vm((12, D // 2, D), BF),
        vm((12, 4, PIECE, D // 2), BF),
        vm((12, 2, PIECE, D // 2), BF),
        vm((3, Q4 + 1, PIECE, D), BF),
        vm((Q4, REACH + 80, 2 * CHANS), BF),
        vm((Q4, REACH + OWNP, 2 * CHANS), BF),
        vm((Q4, 16, 2 * CHANS), BF),
        vm((Q4, REACH + 80, 2 * CHANS), BF),
        vm((Q4, REACH + OWNP, 2 * CHANS), BF),
        vm((VROWS, D), F32),
        vm((Q4, 8, D), F32),
        vm((VROWS, D), F32),
        vm((SEQ, D), BF),
        vm((ROWS, D), BF),
        dma((8,)),
        dma((9, 6)),
        dma((9, 6)),
        dma((5, 2)),
        dma((5, Q4)),
        dma((5, Q4)),
        dma((3, Q4)),
        dma((3, Q4)),
        dma((12, 8)),
        dma((12, 7)),
        dma((3, Q4 + 1)),
        dma((9,)),
        dma((9,)),
    ]
    vspec = pl.BlockSpec(memory_space=pltpu.VMEM)
    hspec = pl.BlockSpec(memory_space=pl.ANY)
    packed = pl.pallas_call(
        kernel,
        out_shape=(
            jax.ShapeDtypeStruct((ROWS, D), BF),
            jax.ShapeDtypeStruct((ROWS, D), F32),
            jax.ShapeDtypeStruct((3, PIECE, D), F32),
            jax.ShapeDtypeStruct((VROWS, D), F32),
        ),
        in_specs=[pl.BlockSpec(memory_space=pltpu.SMEM)] + [hspec] * 7 + [vspec] * 11 + [hspec],
        out_specs=(vspec,) * 4,
        scratch_shapes=scratch,
        compiler_params=pltpu.CompilerParams(
            collective_id=0, has_side_effects=True, vmem_limit_bytes=67043328
        ),
        name="layer",
    )(
        lengths, tokens, w_key[0].T, w_value[0].T, w_query[0].T, w_out[0], w_up[0], w_down[0],
        b_query, b_value, conv_key.transpose(1, 0, 2), conv_value.transpose(1, 0, 2), b_up, b_out, attn_gain, attn_shift, b_down,
        ffn_gain, ffn_shift, cotangent,
    )
    row = (1, D)
    shapes = [
        (ROWS, D), (PIECE, CHANS), (PIECE, CHANS), (PIECE, CHANS), row, row, (5, 1, D), (5, 1, D), (CHANS, PIECE),
        row, row, row, (PIECE, D), (1, FF), (PIECE, D), row, row, row,
    ]
    outs = pl.pallas_call(
        unpack,
        out_shape=[jax.ShapeDtypeStruct((ROWS, D), BF)] + [jax.ShapeDtypeStruct(v, F32) for v in shapes],
        in_specs=[vspec] * 4,
        out_specs=[vspec] * 19,
        name="unpack",
    )(*packed)
    act, gtok, gq, gk, gv, gbq, gbv, gck, gcv, go, gbo, gag, gas, gup, gbu, gdown, gbd, gfg, gfs = outs
    return (
        act, gtok, gq[None], gk[None], gv[None], gbq, gbv, gck.transpose(1, 0, 2), gcv.transpose(1, 0, 2), go[None], gbo, gag, gas,
        gup[None], gbu, gdown.T[None], gbd, gfg, gfs,
    )


def solution(mesh):
    small = mesh.shape["dp"] == 8 and mesh.shape["mp"] == QUARTERS
    return jax.shard_map(
        fused_layer if small else on_device,
        mesh=mesh,
        in_specs=(
            P("dp", None),
            P("dp"),
            P(None, None, "mp"),
            P(None, None, "mp"),
            P(None, None, "mp"),
            P(None, "mp"),
            P(None, "mp"),
            P(None, None, "mp"),
            P(None, None, "mp"),
            P(None, "mp", None),
            P(),
            P(),
            P(),
            P(None, None, "mp"),
            P(None, "mp"),
            P(None, "mp", None),
            P(),
            P(),
            P(),
            P(("dp", "mp"), None),
        ),
        out_specs=(
            P(("dp", "mp"), None),
            P(("dp", "mp"), None),
            P(None, "dp", "mp"),
            P(None, "dp", "mp"),
            P(None, "dp", "mp"),
            P(),
            P(),
            P(),
            P(),
            P(None, "mp", "dp"),
            P(),
            P(),
            P(),
            P(None, "dp", "mp"),
            P(),
            P(None, "mp", "dp"),
            P(),
            P(),
            P(),
        ),
        check_vma=False,
    )
```

```python
import jax
import jax.numpy as jnp
from jax import lax
from jax.experimental import pallas as pl
from jax.experimental.pallas import tpu as pltpu
from jax.sharding import PartitionSpec as P

D = 768
HEAD_DIM = 64
FF = 3072
WINDOW = 128
POOL_WINDOW = 512
STRIDE = 4
LAYERS = 1


block_rows = 512
mask_fill = -1000000000.0
epsilon = 1e-05


def norm_rows(hidden, gain, shift):
    center = hidden - jnp.mean(hidden, axis=-1, keepdims=True)
    spread = jnp.mean(center * center, axis=-1, keepdims=True)
    return center * lax.rsqrt(spread + epsilon) * gain + shift


def gelu_exact(values):
    return jax.nn.gelu(values, approximate=False)


def pool_rows(values, kernel):
    seqs, length, chans = values.shape
    width = kernel.shape[0]
    half = width // 2
    pooled_len = length // STRIDE
    padded = jnp.pad(values, ((0, 0), (half, width), (0, 0)))
    total = jnp.zeros((seqs, pooled_len, chans), jnp.float32)
    for offset in range(width):
        total = total + kernel[offset] * padded[:, offset : offset + STRIDE * pooled_len : STRIDE]
    return total


def block_mask(start, lengths):
    reach = WINDOW // 2
    pool_reach = POOL_WINDOW // 2 // STRIDE
    span = block_rows // STRIDE + 2 * pool_reach
    rows = start + jnp.arange(block_rows, dtype=jnp.int32)
    near_pos = start - reach + jnp.arange(block_rows + 2 * reach, dtype=jnp.int32)
    far_pos = (start // STRIDE - pool_reach + jnp.arange(span, dtype=jnp.int32)) * STRIDE
    limit = lengths[:, None, None]
    near_ok = (
        (jnp.abs(rows[:, None] - near_pos[None, :]) <= reach)[None]
        & (near_pos >= 0)[None, None]
        & (near_pos[None, None] < limit)
    )
    far_ok = (
        (jnp.abs(rows[:, None] - far_pos[None, :]) <= POOL_WINDOW // 2)[None]
        & (far_pos >= 0)[None, None]
        & (far_pos[None, None] < limit)
    )
    return jnp.concatenate([near_ok, far_ok], axis=-1)


def padded_keys(keys_loc, vals_loc, far_keys, far_vals):
    reach = WINDOW // 2
    pool_reach = POOL_WINDOW // 2 // STRIDE
    pad_near = ((0, 0), (reach, reach), (0, 0), (0, 0))
    pad_far = ((0, 0), (pool_reach, pool_reach), (0, 0), (0, 0))
    return (
        jnp.pad(keys_loc, pad_near),
        jnp.pad(vals_loc, pad_near),
        jnp.pad(far_keys, pad_far),
        jnp.pad(far_vals, pad_far),
    )


def block_inputs(start, queries, padded):
    near_k, near_v, far_k, far_v = padded
    near_len = block_rows + 2 * (WINDOW // 2)
    span = block_rows // STRIDE + 2 * (POOL_WINDOW // 2 // STRIDE)
    pool_start = start // STRIDE
    q_rows = queries[:, start : start + block_rows]
    keys_b = jnp.concatenate(
        [near_k[:, start : start + near_len], far_k[:, pool_start : pool_start + span]], axis=1
    )
    vals_b = jnp.concatenate(
        [near_v[:, start : start + near_len], far_v[:, pool_start : pool_start + span]], axis=1
    )
    return (q_rows, keys_b, vals_b)


def forward_block(q_rows, keys_b, vals_b, mask, live):
    scale = q_rows.shape[-1] ** (-0.5)
    scores = (
        jnp.einsum("sqhe,skhe->shqk", q_rows, keys_b, preferred_element_type=jnp.float32) * scale
    )
    scores = jnp.where(mask[:, None], scores, mask_fill)
    peak = jnp.max(scores, axis=-1, keepdims=True)
    expo = jnp.exp(scores - peak)
    total = jnp.sum(expo, axis=-1, keepdims=True)
    weights = (expo / total).astype(jnp.bfloat16)
    result = jnp.einsum("shqk,skhe->sqhe", weights, vals_b, preferred_element_type=jnp.float32)
    result = jnp.where(live[:, :, None, None], result, 0.0)
    return (result, peak + jnp.log(total))


def forward_skip(q_rows, keys_b, vals_b, mask, live):
    seqs, rows, heads, size = q_rows.shape
    return (
        jnp.zeros((seqs, rows, heads, size), jnp.float32),
        jnp.zeros((seqs, heads, rows, 1), jnp.float32),
    )


def backward_block(q_rows, keys_b, vals_b, mask, logsum, grad_rows):
    scale = q_rows.shape[-1] ** (-0.5)
    scores = (
        jnp.einsum("sqhe,skhe->shqk", q_rows, keys_b, preferred_element_type=jnp.float32) * scale
    )
    scores = jnp.where(mask[:, None], scores, mask_fill)
    probs = jnp.exp(scores - logsum)
    grad_probs = jnp.einsum(
        "sqhe,skhe->shqk", grad_rows, vals_b, preferred_element_type=jnp.float32
    )
    delta = jnp.sum(probs * grad_probs, axis=-1, keepdims=True)
    grad_scores = (probs * (grad_probs - delta)).astype(jnp.bfloat16)
    grad_q = (
        jnp.einsum("shqk,skhe->sqhe", grad_scores, keys_b, preferred_element_type=jnp.float32)
        * scale
    )
    grad_keys = (
        jnp.einsum("shqk,sqhe->skhe", grad_scores, q_rows, preferred_element_type=jnp.float32)
        * scale
    )
    grad_vals = jnp.einsum(
        "shqk,sqhe->skhe", probs.astype(jnp.bfloat16), grad_rows, preferred_element_type=jnp.float32
    )
    return (grad_q, grad_keys, grad_vals)


def backward_skip(q_rows, keys_b, vals_b, mask, logsum, grad_rows):
    return (
        jnp.zeros(q_rows.shape, jnp.float32),
        jnp.zeros(keys_b.shape, jnp.float32),
        jnp.zeros(vals_b.shape, jnp.float32),
    )


def attend_forward(queries, keys_loc, vals_loc, far_keys, far_vals, lengths):
    length = queries.shape[1]
    padded = padded_keys(keys_loc, vals_loc, far_keys, far_vals)
    longest = jnp.max(lengths)
    results, logsums = ([], [])
    for block in range(length // block_rows):
        start = block * block_rows
        q_rows, keys_b, vals_b = block_inputs(start, queries, padded)
        mask = block_mask(start, lengths)
        live = start + jnp.arange(block_rows, dtype=jnp.int32)[None, :] < lengths[:, None]
        result, logsum = lax.cond(
            start < longest, forward_block, forward_skip, q_rows, keys_b, vals_b, mask, live
        )
        results.append(result)
        logsums.append(logsum)
    return (jnp.concatenate(results, axis=1), logsums)


def attend_backward(
    queries, keys_loc, vals_loc, far_keys, far_vals, lengths, logsums, grad_context
):
    seqs, length, heads, size = queries.shape
    pooled_len = far_keys.shape[1]
    reach = WINDOW // 2
    pool_reach = POOL_WINDOW // 2 // STRIDE
    near_len = block_rows + 2 * reach
    span = block_rows // STRIDE + 2 * pool_reach
    padded = padded_keys(keys_loc, vals_loc, far_keys, far_vals)
    longest = jnp.max(lengths)
    grad_near_k = jnp.zeros((seqs, length + 2 * reach, heads, size), jnp.float32)
    grad_near_v = jnp.zeros((seqs, length + 2 * reach, heads, size), jnp.float32)
    grad_far_k = jnp.zeros((seqs, pooled_len + 2 * pool_reach, heads, size), jnp.float32)
    grad_far_v = jnp.zeros((seqs, pooled_len + 2 * pool_reach, heads, size), jnp.float32)
    grad_queries = []
    for block in range(length // block_rows):
        start = block * block_rows
        pool_start = start // STRIDE
        q_rows, keys_b, vals_b = block_inputs(start, queries, padded)
        mask = block_mask(start, lengths)
        grad_rows = grad_context[:, start : start + block_rows]
        grad_q, grad_keys, grad_vals = lax.cond(
            start < longest,
            backward_block,
            backward_skip,
            q_rows,
            keys_b,
            vals_b,
            mask,
            logsums[block],
            grad_rows,
        )
        grad_queries.append(grad_q)
        grad_near_k = grad_near_k.at[:, start : start + near_len].add(grad_keys[:, :near_len])
        grad_near_v = grad_near_v.at[:, start : start + near_len].add(grad_vals[:, :near_len])
        grad_far_k = grad_far_k.at[:, pool_start : pool_start + span].add(grad_keys[:, near_len:])
        grad_far_v = grad_far_v.at[:, pool_start : pool_start + span].add(grad_vals[:, near_len:])
    return (
        jnp.concatenate(grad_queries, axis=1),
        grad_near_k[:, reach : reach + length],
        grad_near_v[:, reach : reach + length],
        grad_far_k[:, pool_reach : pool_reach + pooled_len],
        grad_far_v[:, pool_reach : pool_reach + pooled_len],
    )


def row_sum(left, right, share):

    def term(start, count):
        return jnp.dot(left, right, preferred_element_type=jnp.float32)

    return lax.psum_scatter(
        term(jnp.int32(0), share * lax.axis_size("mp")), "mp", scatter_dimension=0, tiled=True
    )


def share_rows(values):
    return lax.all_gather(values, "mp", axis=0, tiled=True)


def share_back(values):
    return lax.all_gather(values, "mp", axis=0, tiled=True)


def back_sum(term, share):
    return lax.psum_scatter(
        term(jnp.int32(0), share * lax.axis_size("mp")), "mp", scatter_dimension=0, tiled=True
    )


def spread(values, width):
    whole = jnp.zeros(values.shape[:-1] + (width,), jnp.float32)
    start = lax.axis_index("mp") * values.shape[-1]
    return lax.dynamic_update_slice_in_dim(whole, values, start, values.ndim - 1)


def layer_forward(full_in, resid, lengths, params, share):
    (
        w_query,
        w_key,
        w_value,
        b_query,
        b_value,
        conv_key,
        conv_value,
        w_out,
        b_out,
        attn_gain,
        attn_shift,
        w_up,
        b_up,
        w_down,
        b_down,
        ffn_gain,
        ffn_shift,
    ) = params
    seqs = lengths.shape[0]
    total_rows = full_in.shape[0]
    length = total_rows // seqs
    chans = w_query.shape[1]
    heads = chans // HEAD_DIM
    pooled_len = length // STRIDE
    queries = (jnp.dot(full_in, w_query, preferred_element_type=jnp.float32) + b_query).astype(
        jnp.bfloat16
    )
    keys_loc = jnp.dot(full_in, w_key, preferred_element_type=jnp.float32).astype(jnp.bfloat16)
    vals_loc = (jnp.dot(full_in, w_value, preferred_element_type=jnp.float32) + b_value).astype(
        jnp.bfloat16
    )
    valid = (jnp.arange(length, dtype=jnp.int32)[None, :] < lengths[:, None]).astype(jnp.float32)[
        :, :, None
    ]
    far_keys = pool_rows(
        keys_loc.reshape(seqs, length, chans).astype(jnp.float32) * valid, conv_key
    ).astype(jnp.bfloat16)
    far_vals = pool_rows(
        vals_loc.reshape(seqs, length, chans).astype(jnp.float32) * valid, conv_value
    ).astype(jnp.bfloat16)
    context, logsums = attend_forward(
        queries.reshape(seqs, length, heads, HEAD_DIM),
        keys_loc.reshape(seqs, length, heads, HEAD_DIM),
        vals_loc.reshape(seqs, length, heads, HEAD_DIM),
        far_keys.reshape(seqs, pooled_len, heads, HEAD_DIM),
        far_vals.reshape(seqs, pooled_len, heads, HEAD_DIM),
        lengths,
    )
    context = context.reshape(total_rows, chans).astype(jnp.bfloat16)
    hidden_one = resid + (row_sum(context, w_out, share) + b_out)
    normed = norm_rows(hidden_one, attn_gain, attn_shift)
    full_normed = share_rows(normed.astype(jnp.bfloat16))
    upper = jnp.dot(full_normed, w_up, preferred_element_type=jnp.float32) + b_up
    active = gelu_exact(upper).astype(jnp.bfloat16)
    hidden_two = normed + (row_sum(active, w_down, share) + b_down)
    result = norm_rows(hidden_two, ffn_gain, ffn_shift)
    kept = (
        full_in,
        queries,
        keys_loc,
        vals_loc,
        far_keys,
        far_vals,
        logsums,
        context,
        hidden_one,
        full_normed,
        upper,
        active,
        hidden_two,
    )
    return (result, kept)


def layer_backward(grad_out, kept, params, lengths, share):
    (
        w_query,
        w_key,
        w_value,
        b_query,
        b_value,
        conv_key,
        conv_value,
        w_out,
        b_out,
        attn_gain,
        attn_shift,
        w_up,
        b_up,
        w_down,
        b_down,
        ffn_gain,
        ffn_shift,
    ) = params
    (
        full_in,
        queries,
        keys_loc,
        vals_loc,
        far_keys,
        far_vals,
        logsums,
        context,
        hidden_one,
        full_normed,
        saved_upper,
        active,
        hidden_two,
    ) = kept
    seqs = lengths.shape[0]
    total_rows = full_in.shape[0]
    length = total_rows // seqs
    chans = w_query.shape[1]
    heads = chans // HEAD_DIM
    pooled_len = length // STRIDE
    unused_two, pull_two = jax.vjp(norm_rows, hidden_two, ffn_gain, ffn_shift)
    grad_h2, grad_fgain, grad_fshift = pull_two(grad_out)
    grad_ffn = grad_h2.astype(jnp.bfloat16)
    grad_bdown = jnp.sum(grad_ffn.astype(jnp.float32), axis=0)
    full_gffn = share_back(grad_ffn)
    grad_wdown = jnp.einsum("tf,td->fd", active, full_gffn, preferred_element_type=jnp.float32)
    grad_active = jnp.einsum("td,fd->tf", full_gffn, w_down, preferred_element_type=jnp.float32)
    unused_gelu, pull_gelu = jax.vjp(gelu_exact, saved_upper)
    grad_upper = pull_gelu(grad_active)[0].astype(jnp.bfloat16)
    grad_bup = jnp.sum(grad_upper.astype(jnp.float32), axis=0)
    grad_wup = jnp.einsum("td,tf->df", full_normed, grad_upper, preferred_element_type=jnp.float32)

    def up_term(start, count):
        return jnp.einsum("tf,df->td", grad_upper, w_up, preferred_element_type=jnp.float32)

    grad_y1 = grad_h2 + back_sum(up_term, share)
    unused_one, pull_one = jax.vjp(norm_rows, hidden_one, attn_gain, attn_shift)
    grad_h1, grad_again, grad_ashift = pull_one(grad_y1)
    grad_attn = grad_h1.astype(jnp.bfloat16)
    grad_bout = jnp.sum(grad_attn.astype(jnp.float32), axis=0)
    full_gattn = share_back(grad_attn)
    grad_wout = jnp.einsum("tc,td->cd", context, full_gattn, preferred_element_type=jnp.float32)
    grad_context = jnp.einsum("td,cd->tc", full_gattn, w_out, preferred_element_type=jnp.float32)
    valid = (jnp.arange(length, dtype=jnp.int32)[None, :] < lengths[:, None]).astype(jnp.float32)[
        :, :, None
    ]
    grad_context = (grad_context.reshape(seqs, length, chans) * valid).astype(jnp.bfloat16)
    grad_q, grad_near_k, grad_near_v, grad_far_k, grad_far_v = attend_backward(
        queries.reshape(seqs, length, heads, HEAD_DIM),
        keys_loc.reshape(seqs, length, heads, HEAD_DIM),
        vals_loc.reshape(seqs, length, heads, HEAD_DIM),
        far_keys.reshape(seqs, pooled_len, heads, HEAD_DIM),
        far_vals.reshape(seqs, pooled_len, heads, HEAD_DIM),
        lengths,
        logsums,
        grad_context.reshape(seqs, length, heads, HEAD_DIM),
    )
    masked_keys = keys_loc.reshape(seqs, length, chans).astype(jnp.float32) * valid
    masked_vals = vals_loc.reshape(seqs, length, chans).astype(jnp.float32) * valid
    unused_pk, pull_key = jax.vjp(pool_rows, masked_keys, conv_key)
    grad_kpool, grad_ckey = pull_key(grad_far_k.reshape(seqs, pooled_len, chans))
    unused_pv, pull_val = jax.vjp(pool_rows, masked_vals, conv_value)
    grad_vpool, grad_cval = pull_val(grad_far_v.reshape(seqs, pooled_len, chans))
    grad_queries = grad_q.reshape(total_rows, chans).astype(jnp.bfloat16)
    grad_keys = (
        (grad_near_k.reshape(seqs, length, chans) + grad_kpool * valid)
        .reshape(total_rows, chans)
        .astype(jnp.bfloat16)
    )
    grad_vals = (
        (grad_near_v.reshape(seqs, length, chans) + grad_vpool * valid)
        .reshape(total_rows, chans)
        .astype(jnp.bfloat16)
    )
    grad_wquery = jnp.einsum("td,tc->dc", full_in, grad_queries, preferred_element_type=jnp.float32)
    grad_wkey = jnp.einsum("td,tc->dc", full_in, grad_keys, preferred_element_type=jnp.float32)
    grad_wvalue = jnp.einsum("td,tc->dc", full_in, grad_vals, preferred_element_type=jnp.float32)
    grad_bquery = jnp.sum(grad_queries.astype(jnp.float32), axis=0)
    grad_bvalue = jnp.sum(grad_vals.astype(jnp.float32), axis=0)

    def input_term(start, count):
        total = jnp.einsum("tc,dc->td", grad_queries, w_query, preferred_element_type=jnp.float32)
        total = total + jnp.einsum(
            "tc,dc->td", grad_keys, w_key, preferred_element_type=jnp.float32
        )
        return total + jnp.einsum(
            "tc,dc->td", grad_vals, w_value, preferred_element_type=jnp.float32
        )

    grad_input = grad_h1 + back_sum(input_term, share)
    matrices = (
        grad_wquery[None],
        grad_wkey[None],
        grad_wvalue[None],
        grad_wout[None],
        grad_wup[None],
        grad_wdown[None],
    )
    vectors = (
        spread(grad_bquery, D)[None],
        spread(grad_bvalue, D)[None],
        spread(grad_ckey, D)[None],
        spread(grad_cval, D)[None],
        grad_bout[None],
        grad_again[None],
        grad_ashift[None],
        spread(grad_bup, FF)[None],
        grad_bdown[None],
        grad_fgain[None],
        grad_fshift[None],
    )
    return (grad_input, matrices, vectors)


def on_device(
    tokens,
    lengths,
    w_query,
    w_key,
    w_value,
    b_query,
    b_value,
    conv_key,
    conv_value,
    w_out,
    b_out,
    attn_gain,
    attn_shift,
    w_up,
    b_up,
    w_down,
    b_down,
    ffn_gain,
    ffn_shift,
    cotangent,
):
    stacks = (
        w_query,
        w_key,
        w_value,
        b_query,
        b_value,
        conv_key,
        conv_value,
        w_out,
        b_out,
        attn_gain,
        attn_shift,
        w_up,
        b_up,
        w_down,
        b_down,
        ffn_gain,
        ffn_shift,
    )
    total_rows = tokens.shape[0]
    share = total_rows // lax.axis_size("mp")
    place = lax.axis_index("mp") * share
    resid = lax.dynamic_slice_in_dim(tokens, place, share, 0).astype(jnp.float32)
    layer = 0
    params = tuple((stack[layer] for stack in stacks))
    result, kept = layer_forward(tokens, resid, lengths, params, share)
    kept_all = [kept]
    activations = result.astype(jnp.bfloat16)
    grad_out = cotangent.astype(jnp.float32)
    matrix_list = [None] * LAYERS
    vector_list = [None] * LAYERS
    for layer in reversed(range(LAYERS)):
        params = tuple((stack[layer] for stack in stacks))
        grad_out, matrices, vectors = layer_backward(
            grad_out, kept_all[layer], params, lengths, share
        )
        matrix_list[layer] = matrices
        vector_list[layer] = vectors
    grad_wquery, grad_wkey, grad_wvalue, grad_wout, grad_wup, grad_wdown = tuple(
        (jnp.concatenate([entry[index] for entry in matrix_list], axis=0) for index in range(6))
    )
    (
        grad_bquery,
        grad_bvalue,
        grad_ckey,
        grad_cval,
        grad_bout,
        grad_again,
        grad_ashift,
        grad_bup,
        grad_bdown,
        grad_fgain,
        grad_fshift,
    ) = tuple(
        (jnp.concatenate([entry[index] for entry in vector_list], axis=0) for index in range(11))
    )
    grad_wquery, grad_wkey, grad_wvalue, grad_wout, grad_wup, grad_wdown = (
        lax.psum_scatter(grad_wquery, "dp", scatter_dimension=1, tiled=True),
        lax.psum_scatter(grad_wkey, "dp", scatter_dimension=1, tiled=True),
        lax.psum_scatter(grad_wvalue, "dp", scatter_dimension=1, tiled=True),
        lax.psum_scatter(grad_wout, "dp", scatter_dimension=2, tiled=True),
        lax.psum_scatter(grad_wup, "dp", scatter_dimension=1, tiled=True),
        lax.psum_scatter(grad_wdown, "dp", scatter_dimension=2, tiled=True),
    )
    (
        grad_bquery,
        grad_bvalue,
        grad_ckey,
        grad_cval,
        grad_bout,
        grad_again,
        grad_ashift,
        grad_bup,
        grad_bdown,
        grad_fgain,
        grad_fshift,
    ) = lax.psum(
        (
            grad_bquery,
            grad_bvalue,
            grad_ckey,
            grad_cval,
            grad_bout,
            grad_again,
            grad_ashift,
            grad_bup,
            grad_bdown,
            grad_fgain,
            grad_fshift,
        ),
        ("dp", "mp"),
    )
    return (
        activations,
        grad_out,
        grad_wquery,
        grad_wkey,
        grad_wvalue,
        grad_bquery,
        grad_bvalue,
        grad_ckey,
        grad_cval,
        grad_wout,
        grad_bout,
        grad_again,
        grad_ashift,
        grad_wup,
        grad_bup,
        grad_wdown,
        grad_bdown,
        grad_fgain,
        grad_fshift,
    )


BF = jnp.bfloat16
F32 = jnp.float32
MESH = pl.DeviceIdType.MESH
ROWS = 256
QUARTERS = 4
CHANS = D // QUARTERS
QHEADS = CHANS // HEAD_DIM
SEQ = QUARTERS * ROWS
REACH = WINDOW // 2
PREACH = POOL_WINDOW // 2 // STRIDE
OWNP = ROWS // STRIDE
KW = ROWS + 2 * REACH
KP = OWNP + 2 * PREACH
KEYS = KW + KP
QB = 128
NEAR = QB + 2 * REACH
FAR = QB // STRIDE + 2 * PREACH
COMP = 800
HALFC = COMP // 2
FRONT = 256
KVROWS = 1408
BASE = 288
PIECE = D // 8
BIG_NEG = -1e30
SCALE = HEAD_DIM ** -0.5
VROWS = 64
TILES = 2 * CHANS // 128


def nn(a, b):
    return jnp.dot(a, b, preferred_element_type=F32)


def nt(a, b):
    return lax.dot_general(a, b, (((1,), (1,)), ((), ())), preferred_element_type=F32)


def tn(a, b):
    return lax.dot_general(a, b, (((0,), (0,)), ((), ())), preferred_element_type=F32)


def rows_iota(rows, cols):
    return lax.broadcasted_iota(jnp.int32, (rows, cols), 0)


def cols_iota(rows, cols):
    return lax.broadcasted_iota(jnp.int32, (rows, cols), 1)


def mean_row(v):
    return jnp.mean(v, axis=-1, keepdims=True)


def sum_col(v):
    return jnp.sum(v, axis=0, keepdims=True)


def kernel(
    len_hbm, tok_hbm, wk, wv, wq, wo, wup, wdown, bq_h, bv_h, ck_h, cv_h, bup_h, bo_h, ag_h, ash_h, bd_h, fg_h, fs_h, cot_hbm,
    act_hbm, gtok_hbm, gmats_hbm, gvec_hbm,
    W, VEC, kvf, KV, KVS, Q, CTX, P, maskn, maskf, n1, r1, y1, y1b, dg, av,
    yT, fT, gab, GKV, pt, GQ, VG,
    CR, S1, S2, ZR, HL, HR, HLL, SL, SR, GVR, GVZ, VO, tok, cot,
    len_ref, bq, bv, ck, cv, bup, bo, ag, ash, bd, fg, fs, act_out, gtok, gmats,
    ssem, osem, lsem, asend, arecv, zsend, zrecv, lsend, hsend, hrecv, rsend, rrecv, zsum, gsend, grecv,
):
    acc, n2, xT, gub = gtok, y1, yT, y1b
    dp = lax.axis_index("dp")
    z = lax.axis_index("mp")
    c = lax.rem(dp, 2)
    x = lax.rem(lax.div(dp, 2), 2)
    y = lax.div(dp, 4)
    core = (dp + 1 - 2 * c, z)
    xdev = (dp + 2 - 4 * x, z)
    ydev = (dp + 4 - 8 * y, z)
    yx = 2 * y + x

    def zdev(step):
        return (dp, lax.rem(z + step, QUARTERS))

    def rcopy(src, dst, ssem, rsem, dev):
        return pltpu.make_async_remote_copy(
            src_ref=src, dst_ref=dst, send_sem=ssem, recv_sem=rsem,
            device_id=dev, device_id_type=MESH,
        )

    barrier = pltpu.get_barrier_semaphore()
    for dev in (core, xdev, ydev, zdev(1), zdev(2), zdev(3)):
        pl.semaphore_signal(barrier, inc=1, device_id=dev, device_id_type=MESH)

    def loads():
        parts = [(wk, 0), (wv, CHANS), (wq, 2 * CHANS), (wo, 3 * CHANS)]
        copies = [
            pltpu.make_async_copy(src, W.at[0, z, at : at + CHANS, :], lsem.at[i])
            for i, (src, at) in enumerate(parts)
        ]
        copies.append(pltpu.make_async_copy(wup, W.at[1, z], lsem.at[4]))
        copies.append(pltpu.make_async_copy(wdown, W.at[2, z], lsem.at[5]))
        return copies

    small = [
        pltpu.make_async_copy(src, dst, ssem.at[i])
        for i, (src, dst) in enumerate(
            (
                (bup_h, bup), (bv_h, bv), (bq_h, bq), (ck_h, ck), (cv_h, cv), (len_hbm, len_ref),
                (bo_h, bo), (ag_h, ag), (ash_h, ash), (bd_h, bd), (fg_h, fg), (fs_h, fs),
            )
        )
    ]
    outs = [
        pltpu.make_async_copy(src, dst, osem.at[i])
        for i, (src, dst) in enumerate(
            (
                (act_out, act_hbm), (gtok, gtok_hbm), (gmats.at[0], gmats_hbm.at[0]),
                (gmats.at[1], gmats_hbm.at[1]), (gmats.at[2], gmats_hbm.at[2]), (VO, gvec_hbm),
            )
        )
    ]
    for cp in small[:6]:
        cp.start()
    own = loads()
    tok_in = pltpu.make_async_copy(tok_hbm, tok, lsem.at[6])
    cot_in = pltpu.make_async_copy(cot_hbm, cot, lsem.at[7])
    for cp in own:
        cp.start()
    tok_in.start()
    for cp in small[6:]:
        cp.start()
    cot_in.start()
    for cp in small[:6]:
        cp.wait()
    length = len_ref[0]
    vpack = VG.at[0:8, :]
    vpack[...] = jnp.zeros_like(vpack)
    vpack[0:1, :] = bup[...]
    vpack[1:2, CHANS : 2 * CHANS] = bv[...]
    vpack[1:2, 2 * CHANS : 3 * CHANS] = bq[...]
    for t in range(5):
        vpack[2 + t : 3 + t, 0:CHANS] = ck[t]
        vpack[2 + t : 3 + t, CHANS : 2 * CHANS] = cv[t]
    VEC[z] = vpack[...]
    pl.semaphore_wait(barrier, 6)

    def block(j):
        return pl.ds(pl.multiple_of(j * PIECE, PIECE), PIECE)

    piece_me = c * 4 + yx
    piece_x = c * 4 + 2 * y + 1 - x
    piece_y = c * 4 + 2 * (1 - y) + x
    piece_d = c * 4 + 2 * (1 - y) + 1 - x
    LO, HI = pl.ds(0, D // 2), pl.ds(D // 2, D // 2)
    ALL = pl.ds(0, D)
    CHUNKS = 9
    ends = [(0, 1), (1, 1), (0, 2), (1, 2), (0, 3), (2, 1), (2, 2), (1, 3), (2, 3)]
    inner = [(0, 1), (0, 2), (1, 1), (1, 2), (0, 3), (2, 1), (2, 2), (1, 3), (2, 3)]
    sources = [(1, 2, 3), (2, 0, 3), (1, 3, 0), (2, 1, 0)]
    targets = [(3, 2, 1, 0), (3, 0, 2, 1), (0, 3, 1, 2), (0, 1, 2, 3)]
    DOWN = 2
    FAR_STEPS = 2
    at_end = (z == 0) | (z == QUARTERS - 1)

    def table(values, bits=2):
        word = sum(v << (bits * i) for i, v in enumerate(values))
        return jnp.int32(word - (1 << 32) if word >> 31 else word)

    def lookup(word, i, bits=2):
        return lax.bitwise_and(lax.shift_right_logical(word, bits * i), (1 << bits) - 1)

    def by_place(a, b):
        return lax.select(at_end, a, b)

    mats_of = by_place(table(m for m, d in ends), table(m for m, d in inner))
    dist_of = by_place(table(d for m, d in ends), table(d for m, d in inner))
    looks_of = by_place(table((1, 2, 4, 5, 6, 7, 8, 9), 4), table((2, 4, 5, 7, 8, 9, 9, 9), 4))
    sends_of = by_place(table((1, 2, 4, 5, 6, 7, 8, 9), 4), table((2, 3, 4, 5, 6, 7, 8, 9), 4))

    def source(d):
        return lookup(table(v for row in sources for v in row), 3 * z + d - 1)

    def target(t):
        return lookup(table(v for row in targets for v in row), 4 * z + t)

    def chunk(k):
        return lookup(mats_of, k), source(lookup(dist_of, k))

    def is_far(k):
        return (lookup(mats_of, k) == DOWN) & (lookup(dist_of, k) < FAR_STEPS)

    def own_block(m, up, piece, sem):
        src = W.at[m, z, block(piece), :]
        return rcopy(src, src, zsend.at[sem, up], zrecv.at[sem, z], (dp, z + 2 * up - 1))

    def own_z(m, up):
        return own_block(m, up, piece_me, m)

    def far_z(up):
        return own_block(DOWN, up, piece_d, 4)

    def wants_far(up):
        to = z + 2 * up - 1
        inner_to = (to == 1) | (to == 2)
        return jnp.logical_not(inner_to) | (z == 3 - to)

    def relay(m, src, dev):
        ref = W.at[m, src, block(piece_me), :]
        return rcopy(ref, ref, lsend.at[m, src], zrecv.at[m, src], dev)

    def relay_far(src, dev):
        ref = W.at[DOWN, src, block(piece_d), :]
        return rcopy(ref, ref, lsend.at[4, src], zrecv.at[4, src], dev)

    def own_vec(up):
        src = VEC.at[z]
        return rcopy(src, src, zsend.at[3, up], zrecv.at[3, z], (dp, z + 2 * up - 1))

    def relay_vec(src, dev):
        ref = VEC.at[src]
        return rcopy(ref, ref, lsend.at[3, src], zrecv.at[3, src], dev)

    def onward(src):
        return jnp.where(src > z, z > 0, z < QUARTERS - 1)

    def next_dev(src):
        return (dp, jnp.where(src > z, z - 1, z + 1))

    def plane(k, which, piece, cols, dev):
        m, src = chunk(k)
        ref = W.at[m, src, block(piece), cols]
        return rcopy(ref, ref, asend.at[k], arecv.at[k, (which - 1) // 2], dev)

    def look(k):
        m, src = chunk(k)

        @pl.when(m == 0)
        def _():
            relay_vec(src, core).wait_recv()
            pl.when(onward(src))(lambda: relay_vec(src, next_dev(src)).start())

        relay(m, src, core).wait_recv()
        pl.when(onward(src))(lambda: relay(m, src, next_dev(src)).start())

        @pl.when(is_far(k))
        def _():
            relay_far(src, core).wait_recv()

    def first(k):
        plane(k, 1, piece_me, ALL, xdev).start()
        plane(k, 2, piece_me, ALL, ydev).start()

    def rows_of(count):
        return W.at[0, 0, 0:count, :]

    def wait_rows(sem, count):
        pltpu.make_async_copy(rows_of(count), rows_of(count), sem).wait()

    def second(k):
        wait_rows(arecv.at[k, 0], 2 * PIECE)

        @pl.when(jnp.logical_not(is_far(k)))
        def _():
            plane(k, 3, piece_x, LO, ydev).start()
            plane(k, 4, piece_y, HI, xdev).start()

    def half(j):
        return pl.ds(pl.multiple_of(j * (D // 2), D // 2), D // 2)

    def cross(k, j):
        m, src = chunk(k)
        ref = W.at[m, src, half(j), :]
        return rcopy(ref, ref, asend.at[k], arecv.at[k, 2], core)

    def third(k):
        pl.when(jnp.logical_not(is_far(k)))(lambda: wait_rows(arecv.at[k, 1], PIECE))
        cross(k, c).start()

    def fourth(k):
        cross(k, 1 - c).wait_recv()

    def looks(i):
        return jnp.where(i < 0, 0, lookup(looks_of, lax.clamp(0, i, 7), 4))

    def sends(i):
        return jnp.where(i < 0, 0, lookup(sends_of, lax.clamp(0, i, 7), 4))

    def each(fn):
        def body(k, carry):
            fn(k)
            return carry

        return body

    def gather_slot(i, carry):
        lax.fori_loop(looks(i - 1), looks(i), each(look), 0)
        pl.when((i == 2) & jnp.logical_not(at_end))(lambda: both(own_down))
        lax.fori_loop(sends(i - 1), sends(i), each(first), 0)
        for lag, stage in ((1, second), (2, third), (3, fourth)):
            k = i - lag
            pl.when((k >= 0) & (k < CHUNKS))(lambda stage=stage, k=k: stage(k))
        return carry

    def gather_done(k, carry):
        m, src = chunk(k)

        @pl.when(onward(src))
        def _():
            relay(m, src, core).wait_send()
            pl.when(m == 0)(lambda: relay_vec(src, core).wait_send())

        far = is_far(k)
        pl.when(far)(lambda: wait_rows(asend.at[k], 6 * PIECE))
        pl.when(jnp.logical_not(far))(lambda: wait_rows(asend.at[k], 7 * PIECE))
        return carry

    def got(s):
        return lax.rem(z + QUARTERS - s, QUARTERS)

    def both(fn):
        pl.when(z > 0)(lambda: fn(0))
        pl.when(z < QUARTERS - 1)(lambda: fn(1))

    both(lambda up: own_vec(up).start())
    for m, waits in enumerate((own[:4], own[4:5], own[5:])):
        for cp in waits:
            cp.wait()
        if m != DOWN:
            both(lambda up: own_z(m, up).start())

    def own_down(up):
        own_z(DOWN, up).start()
        pl.when(wants_far(up))(lambda: far_z(up).start())

    pl.when(at_end)(lambda: both(own_down))

    def own_sent(up):
        own_vec(up).wait_send()
        for m in range(3):
            own_z(m, up).wait_send()
        pl.when(wants_far(up))(lambda: far_z(up).wait_send())

    base = z * ROWS
    start = lax.select(z < 2, jnp.int32(0), jnp.int32(SEQ - COMP))
    place = pl.multiple_of(start - base + BASE + FRONT, 32)
    start = pl.multiple_of(start, 32)
    kvf[...] = jnp.zeros_like(kvf)
    for b in range(2):
        i = base + b * QB + cols_iota(1, QB)
        j = base - REACH + b * QB + rows_iota(NEAR, 1)
        ok = (jnp.abs(i - j) <= REACH) & (j >= 0) & (j < length)
        maskn[b] = jnp.where(ok, 0.0, BIG_NEG)
        j = (OWNP * z - PREACH + b * (QB // STRIDE) + rows_iota(FAR, 1)) * STRIDE
        ok = (jnp.abs(i - j) <= POOL_WINDOW // 2) & (j >= 0) & (j < length)
        maskf[b] = jnp.where(ok, 0.0, BIG_NEG)
    own_rows = pl.ds(pl.multiple_of(base, ROWS), ROWS)
    tok_in.wait()
    cot_in.wait()
    for cp in small[6:]:
        cp.wait()
    xb = tok[own_rows, :]
    acc[...] = jnp.zeros_like(acc)

    def taps(zq, t):
        return VEC[zq, 2 + t : 3 + t, 0 : 2 * CHANS]

    def strided(t):
        at = pl.ds(FRONT + BASE - POOL_WINDOW // 2 - 2 + t, KP, stride=STRIDE)
        return jnp.concatenate([kvf[i, at, :] for i in range(TILES)], axis=1)

    def tile(i):
        return slice(i * 128, (i + 1) * 128)

    def window(lo, rows):
        return jnp.concatenate([kvf[i, lo : lo + rows, :] for i in range(TILES)], axis=1)

    def quarter(s):
        return lax.select(s == 0, z, source(lax.max(s, 1)))

    def attend(s, carry):
        zq = quarter(s)
        for blk in range(2):
            xr = tok[pl.ds(pl.multiple_of(start + blk * HALFC, 16), HALFC), :]
            kv = nt(xr, W[0, zq, 0 : 2 * CHANS, :]) + VEC[zq, 1:2, 0 : 2 * CHANS]
            pos = start + blk * HALFC + rows_iota(HALFC, 1)
            kvb = jnp.where(pos < length, kv.astype(BF).astype(F32), 0.0)
            for i in range(TILES):
                kvf[i, pl.ds(pl.multiple_of(place + blk * HALFC, 8), HALFC), :] = kvb[:, tile(i)]
        KVS[zq] = window(FRONT, COMP).astype(BF)
        KV[zq, 0:KW, :] = window(FRONT + BASE - REACH, KW).astype(BF)
        pooled = jnp.zeros((KP, 2 * CHANS), F32)
        for t in range(5):
            pooled = pooled + taps(zq, t) * strided(t)
        KV[zq, KW:KEYS, :] = pooled.astype(BF)
        qz = nt(xb, W[0, zq, 2 * CHANS : 3 * CHANS, :]) + VEC[zq, 1:2, 2 * CHANS : 3 * CHANS]
        Q[zq] = qz.astype(BF)
        for b in range(2):
            live = base + b * QB + cols_iota(1, QB) < length
            n0, f0 = b * QB, KW + b * (QB // STRIDE)
            for h in range(QHEADS):
                kl = slice(h * HEAD_DIM, (h + 1) * HEAD_DIM)
                vl = slice(CHANS + h * HEAD_DIM, CHANS + (h + 1) * HEAD_DIM)
                qh = Q[zq, b * QB : (b + 1) * QB, kl]
                sn = nt(KV[zq, n0 : n0 + NEAR, kl], qh) * SCALE + maskn[b]
                sf = nt(KV[zq, f0 : f0 + FAR, kl], qh) * SCALE + maskf[b]
                peak = jnp.maximum(
                    jnp.max(sn, axis=0, keepdims=True), jnp.max(sf, axis=0, keepdims=True)
                )
                en, ef = jnp.exp(sn - peak), jnp.exp(sf - peak)
                inv = 1.0 / (sum_col(en) + sum_col(ef))
                pn, pf = en * inv, ef * inv
                P[zq, h, b, 0:NEAR, :] = pn
                P[zq, h, b, NEAR : NEAR + FAR, :] = pf
                ct = tn(KV[zq, n0 : n0 + NEAR, vl], pn.astype(BF))
                ct = ct + tn(KV[zq, f0 : f0 + FAR, vl], pf.astype(BF))
                ct = jnp.where(live, ct, 0.0)
                CTX[zq, b * QB : (b + 1) * QB, kl] = ct.T.astype(BF)
        acc[...] += nn(CTX[zq], W[0, zq, 3 * CHANS : D, :])
        lax.fori_loop(lookup_slots(s), lookup_slots(s + 1), gather_slot, 0)
        return carry

    def lookup_slots(s):
        return jnp.where(s == 0, 0, jnp.where(s < 3, 2 + 2 * s, 8))

    lax.fori_loop(0, QUARTERS, attend, 0)

    def store_T(dst, v, cols):
        vt = v.T.astype(BF)
        for j in range(8):
            to = (j % 2) * 4 + j // 2
            dst[to * PIECE : (to + 1) * PIECE, cols] = vt[j * PIECE : (j + 1) * PIECE]

    def span(i, size):
        if isinstance(i, int):
            return pl.ds(i * size, size)
        return pl.ds(pl.multiple_of(i * size, size), size)

    def norm_one(i, carry):
        rows = span(i, QB)
        res = tok[pl.ds(pl.multiple_of(base + i * QB, QB), QB), :].astype(F32)
        hid = res + (acc[rows, :] + bo[...])
        cen = hid - mean_row(hid)
        r = lax.rsqrt(mean_row(cen * cen) + epsilon)
        n = cen * r
        n1[rows, :] = n
        r1[rows, :] = r
        out = n * ag[...] + ash[...]
        y1[rows, :] = out
        y1b[rows, :] = out.astype(BF)
        store_T(yT, out, rows)
        acc[rows, :] = jnp.zeros_like(out)
        return carry

    lax.fori_loop(0, ROWS // QB, norm_one, 0)

    def feed(s, carry):
        zq = quarter(s)

        def up(i, carry):
            cols = span(i, ROWS)
            u = nn(y1b[...], W[1, zq, :, cols]) + VEC[zq, 0:1, cols]
            cdf = 0.5 * (1.0 + lax.erf(u * (0.5 ** 0.5)))
            dg[zq, :, cols] = cdf + u * jnp.exp(-0.5 * u * u) * ((2.0 * 3.141592653589793) ** -0.5)
            av[zq, :, cols] = (u * cdf).astype(BF)
            return carry

        for i in range(D // ROWS):
            up(i, 0)
        acc[...] += nn(av[zq], W[2, zq])
        lo = jnp.where(s < 3, 8 + s, 12)
        hi = jnp.where(s < 2, 9 + s, 12)
        lax.fori_loop(lo, hi, gather_slot, 0)
        return carry

    lax.fori_loop(0, QUARTERS, feed, 0)
    VG[...] = jnp.zeros_like(VG)
    GEN = 8 * QUARTERS

    def add_row(row, v):
        VG[row : row + 1, :] += sum_col(v)

    def norm_two(i, carry):
        rows = span(i, QB)
        hid = y1[rows, :] + (acc[rows, :] + bd[...])
        cen = hid - mean_row(hid)
        r = lax.rsqrt(mean_row(cen * cen) + epsilon)
        n = cen * r
        act_out[rows, :] = (n * fg[...] + fs[...]).astype(BF)
        g = cot[rows, :].astype(F32)
        add_row(GEN + 4, g * n)
        add_row(GEN + 5, g)
        e = g * fg[...]
        gh2 = r * (e - mean_row(e) - n * mean_row(e * n))
        acc[rows, :] = gh2
        gf = gh2.astype(BF)
        gab[rows, :] = gf
        gff = gf.astype(F32)
        add_row(GEN + 3, gff)
        store_T(fT, gff, rows)
        return carry

    lax.fori_loop(0, ROWS // QB, norm_two, 0)
    outs[0].start()

    PARTS = 12

    def part(r):
        m = lax.select(r < 8, 2 - lax.rem(r, 2), 0)
        t = lax.select(r < 8, lax.div(r, 2), r - 8)
        return m, t

    def r_core(r):
        m, t = part(r)
        src = W.at[m, target(t), half(1 - c), :]
        return rcopy(src, CR.at[r], rsend.at[r], rrecv.at[r, 0], core)

    def blk4(r, yy, xx, cols):
        return CR.at[r, block(2 * yy + xx), cols]

    def r_stage1(r, i):
        if i < 2:
            src, dev = blk4(r, i, 1 - x, LO), xdev
        else:
            src, dev = blk4(r, 1 - y, i - 2, HI), ydev
        return rcopy(src, S1.at[r, i], rsend.at[r], rrecv.at[r, 1], dev)

    def r_stage2(r, i):
        if i == 0:
            src, dev = blk4(r, 1 - y, x, LO), ydev
        else:
            src, dev = blk4(r, y, 1 - x, HI), xdev
        return rcopy(src, S2.at[r, i], rsend.at[r], rrecv.at[r, 2], dev)

    def r_z(r):
        m, t = part(r)
        dst = target(t)
        left = dst < z
        slot = jnp.where(left & (dst == z - 1), QUARTERS, dst)
        src = CR.at[r, block(yx), :]
        dev = (dp, jnp.where(left, z - 1, z + 1))
        return rcopy(src, ZR.at[m, slot], rsend.at[r], zsum.at[m, slot], dev)

    def z_in(m, slot):
        ref = ZR.at[m, slot]
        return rcopy(ref, ref, zsum.at[m, slot], zsum.at[m, slot], core)

    def upstream(dst):
        return jnp.where(dst < z, z < QUARTERS - 1, z > 0)

    def reduce1(r):
        m, t = part(r)
        r_core(r).wait_recv()
        zq = target(t)

        def add(i, carry):
            CR[r, block(i), :] = CR[r, block(i), :] + W[m, zq, block(4 * c + i), :]
            return carry

        lax.fori_loop(0, 4, add, 0)
        for i in range(4):
            r_stage1(r, i).start()

    def reduce2(r):
        pltpu.make_async_copy(S1.at[r], S1.at[r], rrecv.at[r, 1]).wait()
        for i in range(2):
            a = blk4(r, i, x, LO)
            a[...] = a[...] + S1[r, i]
            a = blk4(r, y, i, HI)
            a[...] = a[...] + S1[r, 2 + i]
        for i in range(2):
            r_stage2(r, i).start()

    def reduce3(r):
        pltpu.make_async_copy(S2.at[r], S2.at[r], rrecv.at[r, 2]).wait()
        for i, cols in enumerate((LO, HI)):
            a = blk4(r, y, x, cols)
            a[...] = a[...] + S2[r, i]
        dst = target(part(r)[1])
        pl.when((dst != z) & jnp.logical_not(upstream(dst)))(lambda: r_z(r).start())

    def reduce4(r):
        m, t = part(r)
        dst = target(t)

        @pl.when((dst != z) & upstream(dst))
        def _():
            z_in(m, dst).wait_recv()
            CR[r, block(yx), :] = CR[r, block(yx), :] + ZR[m, dst]
            r_z(r).start()

    def stage(fn, ok, r):
        pl.when(ok)(lambda: fn(r))

    def weight_grad(left, right, dst, width):
        dst[:, 0:width] = nn(left[...], right).astype(BF)

    def feed_back(s, carry):
        zq = target(s)
        vrow = pl.multiple_of(8 * zq, 8)

        def hidden(i, carry):
            cols = span(i, ROWS)
            gact = nt(gab[...], W[2, zq, cols, :])
            gu = (gact * dg[zq, :, cols]).astype(BF)
            gub[:, cols] = gu
            VG[pl.ds(vrow, 1), cols] = sum_col(gu.astype(F32))
            return carry

        for i in range(D // ROWS):
            hidden(i, 0)
        weight_grad(fT, av[zq], W.at[2, zq], D)
        r_core(2 * s).start()
        acc[...] += nt(gub[...], W[1, zq])
        weight_grad(yT, gub[...], W.at[1, zq], D)
        r_core(2 * s + 1).start()
        reduce1(jnp.where(s < 2, s, s + 1))
        stage(reduce1, s == 1, jnp.int32(2))
        stage(reduce2, s == 3, jnp.int32(0))
        return carry

    lax.fori_loop(0, CHUNKS, gather_done, 0)
    both(own_sent)
    lax.fori_loop(0, QUARTERS, feed_back, 0)

    def norm_back(i, carry):
        rows = span(i, QB)
        gy = acc[rows, :]
        n = n1[rows, :]
        add_row(GEN + 1, gy * n)
        add_row(GEN + 2, gy)
        e = gy * ag[...]
        gh1 = r1[rows, :] * (e - mean_row(e) - n * mean_row(e * n))
        acc[rows, :] = gh1
        ga = gh1.astype(BF)
        gab[rows, :] = ga
        gaf = ga.astype(F32)
        add_row(GEN, gaf)
        store_T(fT, gaf, rows)
        store_T(xT, tok[pl.ds(pl.multiple_of(base + i * QB, QB), QB), :].astype(F32), rows)
        return carry

    lax.fori_loop(0, ROWS // QB, norm_back, 0)

    def hl(zq):
        return rcopy(SL.at[zq], HL.at[zq], hsend.at[0], hrecv.at[0, zq], zdev(3))

    def hr(zq):
        return rcopy(SR.at[zq], HR.at[zq], hsend.at[1], hrecv.at[1, zq], zdev(1))

    def hll(zq):
        return rcopy(
            SL.at[zq, REACH : REACH + 16, :], HLL.at[zq], hsend.at[2], hrecv.at[2, zq], zdev(2)
        )

    def attend_back(s, carry):
        zq = lookup(table((0, 3, 1, 2)), s)
        gc = nt(gab[...], W[0, zq, 3 * CHANS : D, :])
        alive = base + rows_iota(ROWS, 1) < length
        gcb = jnp.where(alive, gc, 0.0).astype(BF)
        GKV[zq] = jnp.zeros((KEYS, 2 * CHANS), F32)
        for b in range(2):
            n0, f0 = b * QB, KW + b * (QB // STRIDE)
            for h in range(QHEADS):
                kl = slice(h * HEAD_DIM, (h + 1) * HEAD_DIM)
                vl = slice(CHANS + h * HEAD_DIM, CHANS + (h + 1) * HEAD_DIM)
                gch = gcb[b * QB : (b + 1) * QB, kl]
                qh = Q[zq, b * QB : (b + 1) * QB, kl]
                pn = P[zq, h, b, 0:NEAR, :]
                pf = P[zq, h, b, NEAR : NEAR + FAR, :]
                gpn = nt(KV[zq, n0 : n0 + NEAR, vl], gch)
                gpf = nt(KV[zq, f0 : f0 + FAR, vl], gch)
                delta = sum_col(pn * gpn) + sum_col(pf * gpf)
                gsn = (pn * (gpn - delta)).astype(BF)
                gsf = (pf * (gpf - delta)).astype(BF)
                qt = tn(KV[zq, n0 : n0 + NEAR, kl], gsn) + tn(KV[zq, f0 : f0 + FAR, kl], gsf)
                GQ[zq, b * QB : (b + 1) * QB, 2 * CHANS + h * HEAD_DIM : 2 * CHANS + (h + 1) * HEAD_DIM] = (
                    (qt * SCALE).T.astype(BF)
                )
                GKV[zq, n0 : n0 + NEAR, kl] += nn(gsn, qh) * SCALE
                GKV[zq, f0 : f0 + FAR, kl] += nn(gsf, qh) * SCALE
                GKV[zq, n0 : n0 + NEAR, vl] += nn(pn.astype(BF), gch)
                GKV[zq, f0 : f0 + FAR, vl] += nn(pf.astype(BF), gch)
        vrow = pl.multiple_of(8 * zq, 8)
        for i in range(TILES):
            kvf[i, FRONT : FRONT + COMP, :] = KVS[zq, :, tile(i)].astype(F32)
        gp = GKV[zq, KW:KEYS, :]
        sums = jnp.concatenate(
            [jnp.zeros((1, CHANS), F32), sum_col(GKV[zq, 0:KW, CHANS : 2 * CHANS])], axis=1
        )
        far_at = (OWNP * z - PREACH + rows_iota(KP, 1)) * STRIDE
        for t in range(5):
            VG[pl.ds(vrow + 2 + t, 1), 0 : 2 * CHANS] = sum_col(gp * strided(t))
            to = far_at + (t - 2)
            inside = (to >= 0) & (to < length)
            sums = sums + taps(zq, t) * sum_col(jnp.where(inside, gp, 0.0))
        VG[pl.ds(vrow + 1, 1), CHANS : 2 * CHANS] = sums[:, CHANS : 2 * CHANS]
        VG[pl.ds(vrow + 1, 1), 2 * CHANS : 3 * CHANS] = sum_col(
            GQ[zq, :, 2 * CHANS : 3 * CHANS].astype(F32)
        )
        SL[zq, 0:REACH, :] = GKV[zq, 0:REACH, :].astype(BF)
        SL[zq, REACH : REACH + 80, :] = GKV[zq, KW : KW + 80, :].astype(BF)
        SR[zq, 0:REACH, :] = GKV[zq, KW - REACH : KW, :].astype(BF)
        SR[zq, REACH : REACH + OWNP, :] = GKV[zq, KEYS - OWNP : KEYS, :].astype(BF)
        pl.when(z > 0)(lambda: hl(zq).start())
        pl.when(z < QUARTERS - 1)(lambda: hr(zq).start())
        pl.when(z > 1)(lambda: hll(zq).start())
        stage(reduce1, s == 0, jnp.int32(5))
        reduce2(s + 1)
        stage(reduce3, s == 3, jnp.int32(0))
        return carry

    lax.fori_loop(0, QUARTERS, attend_back, 0)

    half_row = pl.multiple_of(32 * c, 32)
    row_x = pl.multiple_of(half_row + 16 * x, 16)
    row_y = pl.multiple_of(row_x + 8 * y, 8)

    def vrows(at, size):
        return pl.ds(pl.multiple_of(at, 8), size)

    folds = [
        (core, VG.at[vrows(32 - half_row, 32), :], GVR.at[0:32], vrows(half_row, 32)),
        (xdev, VG.at[vrows(half_row + 16 - 16 * x, 16), :], GVR.at[32:48], vrows(row_x, 16)),
        (ydev, VG.at[vrows(row_x + 8 - 8 * y, 8), :], GVR.at[48:56], vrows(row_y, 8)),
    ]

    def fold(i):
        dev, src, dst, keep = folds[i]
        return rcopy(src, dst, gsend.at[i], grecv.at[i], dev)

    def fold_done(i):
        fold(i).wait()
        keep = folds[i][3]
        VG[keep, :] = VG[keep, :] + folds[i][2][...]

    def g_z(s):
        src = VG.at[vrows(row_y, 8), :]
        return rcopy(src, GVZ.at[z], gsend.at[2 + s], grecv.at[2 + s], zdev(s))

    def g_z_in(s):
        dst = GVZ.at[got(s)]
        return rcopy(dst, dst, gsend.at[2 + s], grecv.at[2 + s], core)

    opens = [
        (ydev, vrows(row_y, 8), vrows(row_x + 8 - 8 * y, 8)),
        (xdev, vrows(row_x, 16), vrows(half_row + 16 - 16 * x, 16)),
        (core, vrows(half_row, 32), vrows(32 - half_row, 32)),
    ]

    def unfold(i):
        dev, mine, other = opens[i]
        ref = VO.at[mine, :]
        return rcopy(ref, ref, gsend.at[6 + i], grecv.at[6 + i], dev)

    def unfold_done(i):
        ref = VO.at[opens[i][2], :]
        rcopy(ref, ref, gsend.at[6 + i], grecv.at[6 + i], core).wait_recv()

    def vector_two():
        fold_done(0)
        fold(1).start()

    def vector_three():
        fold_done(1)
        fold(2).start()

    def vector_z():
        fold_done(2)
        for step in (1, 2, 3):
            g_z(step).start()
        GVZ[z] = VG[vrows(row_y, 8), :]

    def vector_back():
        for step in (1, 2, 3):
            g_z_in(step).wait_recv()
        VO[vrows(row_y, 8), :] = GVZ[0] + GVZ[1] + GVZ[2] + GVZ[3]
        unfold(0).start()

    fold(0).start()

    def project_back(s, carry):
        zq = target(s)
        pl.when(z < QUARTERS - 1)(lambda: hl(zq).wait_recv())
        pl.when(z > 0)(lambda: hr(zq).wait_recv())
        pl.when(z < QUARTERS - 2)(lambda: hll(zq).wait_recv())
        near = GKV.at[zq]

        def when(ok, v):
            return jnp.where(ok, v.astype(F32), 0.0)

        has_l, has_r, has_rr = z > 0, z < QUARTERS - 1, z < QUARTERS - 2
        near[REACH : 2 * REACH, :] += when(has_l, HR[zq, 0:REACH, :])
        near[ROWS : ROWS + REACH, :] += when(has_r, HL[zq, 0:REACH, :])
        gp = GKV[zq, KW + OWNP : KW + 2 * OWNP, :] + when(has_l, HR[zq, REACH : REACH + OWNP, :])
        gp = gp + when(has_r, HL[zq, REACH : REACH + OWNP, :])
        nxt = GKV[zq, KW + 2 * OWNP : KW + 2 * OWNP + 1, :]
        nxt = nxt + when(has_r, HL[zq, REACH + OWNP : REACH + OWNP + 16, :])[0:1, :]
        nxt = nxt + when(has_rr, HLL[zq])[0:1, :]
        gp1 = jnp.concatenate([gp[1:, :], nxt], axis=0)
        fills = (
            taps(zq, 2) * gp,
            taps(zq, 3) * gp,
            taps(zq, 4) * gp + taps(zq, 0) * gp1,
            taps(zq, 1) * gp1,
        )
        for k, fill in enumerate(fills):
            for i in range(TILES):
                pt[i, pl.ds(k, OWNP, stride=STRIDE), :] = fill[:, tile(i)]
        back = jnp.concatenate([pt[i] for i in range(TILES)], axis=1)
        alive = base + rows_iota(ROWS, 1) < length
        gkv = GKV[zq, REACH : REACH + ROWS, :] + jnp.where(alive, back, 0.0)
        GQ[zq, :, 0 : 2 * CHANS] = gkv.astype(BF)

        acc[...] += nn(GQ[zq], W[0, zq, 0 : 3 * CHANS, :])
        weight_grad(xT, GQ[zq], W.at[0, zq], 3 * CHANS)

        W[0, zq, :, 3 * CHANS : D] = nn(fT[...], CTX[zq]).astype(BF)
        r_core(8 + s).start()
        stage(reduce2, s == 0, jnp.int32(5))
        stage(reduce3, s > 0, s)
        stage(reduce4, s > 0, s - 1)
        stage(reduce1, s < 3, 8 + s)
        pl.when(s == 0)(vector_two)
        return carry

    lax.fori_loop(0, QUARTERS, project_back, 0)
    outs[1].start()

    def wait_all(ref, sem):
        pltpu.make_async_copy(ref, ref, sem).wait()

    pl.when(z > 0)(lambda: wait_all(SL, hsend.at[0]))
    pl.when(z < QUARTERS - 1)(lambda: wait_all(SR, hsend.at[1]))
    pl.when(z > 1)(lambda: wait_all(HLL, hsend.at[2]))

    def final(m):
        own_part = (11, 7, 6)[m]
        gmats[m] = CR[own_part, block(yx), :].astype(F32)

        def more(slot):
            z_in(m, slot).wait_recv()
            gmats[m] += ZR[m, slot].astype(F32)

        pl.when(z > 0)(lambda: more(z))
        pl.when(z < QUARTERS - 1)(lambda: more(QUARTERS))
        outs[2 + m].start()

    def at(r):
        return jnp.int32(r)

    reduce2(at(8))
    vector_three()
    reduce1(at(6))
    reduce3(at(4))
    reduce4(at(3))
    reduce2(at(9))
    reduce1(at(7))
    reduce3(at(5))
    reduce4(at(4))
    reduce2(at(10))
    reduce1(at(11))
    reduce4(at(5))
    reduce3(at(8))
    vector_z()
    reduce3(at(9))
    reduce4(at(8))
    reduce2(at(6))
    reduce3(at(10))
    reduce4(at(9))
    vector_back()
    reduce2(at(7))
    reduce4(at(10))
    unfold_done(0)
    unfold(1).start()
    reduce2(at(11))
    reduce3(at(6))
    final(2)
    reduce3(at(7))
    final(1)
    unfold_done(1)
    unfold(2).start()
    reduce3(at(11))
    final(0)
    unfold_done(2)
    outs[5].start()
    for i in range(3):
        unfold(i).wait_send()
    for s in (1, 2, 3):
        g_z(s).wait_send()

    def sent(r, carry):
        own_part = part(r)[1] == QUARTERS - 1
        pl.when(own_part)(lambda: wait_rows(rsend.at[r], 7 * PIECE))
        pl.when(jnp.logical_not(own_part))(lambda: wait_rows(rsend.at[r], 8 * PIECE))
        return carry

    lax.fori_loop(0, PARTS, sent, 0)
    for cp in outs:
        cp.wait()


def unpack(
    act, gtok, gmats, gvec,
    act_out, gtok_out, gq, gk, gv, gbq, gbv, gck, gcv, go, gbo, gag, gas, gup, gbu, gdown, gbd, gfg, gfs,
):
    act_out[...] = act[...]
    gtok_out[...] = gtok[...]
    gk[...] = gmats[0, :, 0:CHANS]
    gv[...] = gmats[0, :, CHANS : 2 * CHANS]
    gq[...] = gmats[0, :, 2 * CHANS : 3 * CHANS]
    go[...] = gmats[0, :, 3 * CHANS : D].T
    gup[...] = gmats[1]
    gdown[...] = gmats[2]
    for j in range(QUARTERS):
        at = slice(j * CHANS, (j + 1) * CHANS)
        row = 8 * j
        gbu[:, j * D : (j + 1) * D] = gvec[row : row + 1, :]
        gbv[:, at] = gvec[row + 1 : row + 2, CHANS : 2 * CHANS]
        gbq[:, at] = gvec[row + 1 : row + 2, 2 * CHANS : 3 * CHANS]
        for t in range(5):
            gck[t, :, at] = gvec[row + 2 + t : row + 3 + t, 0:CHANS]
            gcv[t, :, at] = gvec[row + 2 + t : row + 3 + t, CHANS : 2 * CHANS]
    for j, out in enumerate((gbo, gag, gas, gbd, gfg, gfs)):
        out[...] = gvec[8 * QUARTERS + j : 8 * QUARTERS + j + 1, :]


def fused_layer(
    tokens, lengths, w_query, w_key, w_value, b_query, b_value, conv_key, conv_value, w_out,
    b_out, attn_gain, attn_shift, w_up, b_up, w_down, b_down, ffn_gain, ffn_shift, cotangent,
):
    Q4 = QUARTERS
    vm = pltpu.VMEM
    dma = pltpu.SemaphoreType.DMA
    scratch = [
        vm((3, Q4, D, D), BF),
        vm((Q4, 8, D), F32),
        vm((TILES, KVROWS, 128), F32),
        vm((Q4, KEYS, 2 * CHANS), BF),
        vm((Q4, COMP, 2 * CHANS), BF),
        vm((Q4, ROWS, CHANS), BF),
        vm((Q4, ROWS, CHANS), BF),
        vm((Q4, QHEADS, 2, NEAR + FAR, QB), F32),
        vm((2, NEAR, QB), F32),
        vm((2, FAR, QB), F32),
        vm((ROWS, D), F32),
        vm((ROWS, 1), F32),
        vm((ROWS, D), F32),
        vm((ROWS, D), BF),
        vm((Q4, ROWS, D), F32),
        vm((Q4, ROWS, D), BF),
        vm((D, ROWS), BF),
        vm((D, ROWS), BF),
        vm((ROWS, D), BF),
        vm((Q4, KEYS, 2 * CHANS), F32),
        vm((TILES, ROWS, 128), F32),
        vm((Q4, ROWS, 3 * CHANS), BF),
        vm((VROWS, D), F32),
        vm((12, D // 2, D), BF),
        vm((12, 4, PIECE, D // 2), BF),
        vm((12, 2, PIECE, D // 2), BF),
        vm((3, Q4 + 1, PIECE, D), BF),
        vm((Q4, REACH + 80, 2 * CHANS), BF),
        vm((Q4, REACH + OWNP, 2 * CHANS), BF),
        vm((Q4, 16, 2 * CHANS), BF),
        vm((Q4, REACH + 80, 2 * CHANS), BF),
        vm((Q4, REACH + OWNP, 2 * CHANS), BF),
        vm((VROWS, D), F32),
        vm((Q4, 8, D), F32),
        vm((VROWS, D), F32),
        vm((SEQ, D), BF),
        vm((ROWS, D), BF),
        pltpu.SMEM((1,), jnp.int32),
        vm((1, CHANS), F32),
        vm((1, CHANS), F32),
        vm((5, 1, CHANS), F32),
        vm((5, 1, CHANS), F32),
        vm((1, D), F32),
        vm((1, D), F32),
        vm((1, D), F32),
        vm((1, D), F32),
        vm((1, D), F32),
        vm((1, D), F32),
        vm((1, D), F32),
        vm((ROWS, D), BF),
        vm((ROWS, D), F32),
        vm((3, PIECE, D), F32),
        dma((12,)),
        dma((6,)),
        dma((8,)),
        dma((9,)),
        dma((9, 3)),
        dma((5, 2)),
        dma((5, Q4)),
        dma((5, Q4)),
        dma((3,)),
        dma((3, Q4)),
        dma((12,)),
        dma((12, 3)),
        dma((3, Q4 + 1)),
        dma((9,)),
        dma((9,)),
    ]
    vspec = pl.BlockSpec(memory_space=pltpu.VMEM)
    hspec = pl.BlockSpec(memory_space=pl.ANY)
    packed = pl.pallas_call(
        kernel,
        out_shape=(
            jax.ShapeDtypeStruct((ROWS, D), BF),
            jax.ShapeDtypeStruct((ROWS, D), F32),
            jax.ShapeDtypeStruct((3, PIECE, D), F32),
            jax.ShapeDtypeStruct((VROWS, D), F32),
        ),
        in_specs=[hspec] * 20,
        out_specs=(hspec,) * 4,
        scratch_shapes=scratch,
        compiler_params=pltpu.CompilerParams(
            collective_id=0, has_side_effects=True, vmem_limit_bytes=67043328
        ),
        name="layer",
    )(
        lengths, tokens, w_key[0].T, w_value[0].T, w_query[0].T, w_out[0], w_up[0], w_down[0],
        b_query, b_value, conv_key.transpose(1, 0, 2), conv_value.transpose(1, 0, 2), b_up, b_out, attn_gain, attn_shift, b_down,
        ffn_gain, ffn_shift, cotangent,
    )
    row = (1, D)
    shapes = [
        (ROWS, D), (PIECE, CHANS), (PIECE, CHANS), (PIECE, CHANS), row, row, (5, 1, D), (5, 1, D), (CHANS, PIECE),
        row, row, row, (PIECE, D), (1, FF), (PIECE, D), row, row, row,
    ]
    outs = pl.pallas_call(
        unpack,
        out_shape=[jax.ShapeDtypeStruct((ROWS, D), BF)] + [jax.ShapeDtypeStruct(v, F32) for v in shapes],
        in_specs=[vspec] * 4,
        out_specs=[vspec] * 19,
        name="unpack",
    )(*packed)
    act, gtok, gq, gk, gv, gbq, gbv, gck, gcv, go, gbo, gag, gas, gup, gbu, gdown, gbd, gfg, gfs = outs
    return (
        act, gtok, gq[None], gk[None], gv[None], gbq, gbv, gck.transpose(1, 0, 2), gcv.transpose(1, 0, 2), go[None], gbo, gag, gas,
        gup[None], gbu, gdown.T[None], gbd, gfg, gfs,
    )


def solution(mesh):
    small = mesh.shape["dp"] == 8 and mesh.shape["mp"] == QUARTERS
    return jax.shard_map(
        fused_layer if small else on_device,
        mesh=mesh,
        in_specs=(
            P("dp", None),
            P("dp"),
            P(None, None, "mp"),
            P(None, None, "mp"),
            P(None, None, "mp"),
            P(None, "mp"),
            P(None, "mp"),
            P(None, None, "mp"),
            P(None, None, "mp"),
            P(None, "mp", None),
            P(),
            P(),
            P(),
            P(None, None, "mp"),
            P(None, "mp"),
            P(None, "mp", None),
            P(),
            P(),
            P(),
            P(("dp", "mp"), None),
        ),
        out_specs=(
            P(("dp", "mp"), None),
            P(("dp", "mp"), None),
            P(None, "dp", "mp"),
            P(None, "dp", "mp"),
            P(None, "dp", "mp"),
            P(),
            P(),
            P(),
            P(),
            P(None, "mp", "dp"),
            P(),
            P(),
            P(),
            P(None, "dp", "mp"),
            P(),
            P(None, "mp", "dp"),
            P(),
            P(),
            P(),
        ),
        check_vma=False,
    )
```

```python
import jax
import jax.numpy as jnp
from jax import lax
from jax.experimental import pallas as pl
from jax.experimental.pallas import tpu as pltpu
from jax.sharding import PartitionSpec as P

D = 768
HEAD_DIM = 64
FF = 3072
WINDOW = 128
POOL_WINDOW = 512
STRIDE = 4
LAYERS = 1


block_rows = 512
mask_fill = -1000000000.0
epsilon = 1e-05


def norm_rows(hidden, gain, shift):
    center = hidden - jnp.mean(hidden, axis=-1, keepdims=True)
    spread = jnp.mean(center * center, axis=-1, keepdims=True)
    return center * lax.rsqrt(spread + epsilon) * gain + shift


def gelu_exact(values):
    return jax.nn.gelu(values, approximate=False)


def pool_rows(values, kernel):
    seqs, length, chans = values.shape
    width = kernel.shape[0]
    half = width // 2
    pooled_len = length // STRIDE
    padded = jnp.pad(values, ((0, 0), (half, width), (0, 0)))
    total = jnp.zeros((seqs, pooled_len, chans), jnp.float32)
    for offset in range(width):
        total = total + kernel[offset] * padded[:, offset : offset + STRIDE * pooled_len : STRIDE]
    return total


def block_mask(start, lengths):
    reach = WINDOW // 2
    pool_reach = POOL_WINDOW // 2 // STRIDE
    span = block_rows // STRIDE + 2 * pool_reach
    rows = start + jnp.arange(block_rows, dtype=jnp.int32)
    near_pos = start - reach + jnp.arange(block_rows + 2 * reach, dtype=jnp.int32)
    far_pos = (start // STRIDE - pool_reach + jnp.arange(span, dtype=jnp.int32)) * STRIDE
    limit = lengths[:, None, None]
    near_ok = (
        (jnp.abs(rows[:, None] - near_pos[None, :]) <= reach)[None]
        & (near_pos >= 0)[None, None]
        & (near_pos[None, None] < limit)
    )
    far_ok = (
        (jnp.abs(rows[:, None] - far_pos[None, :]) <= POOL_WINDOW // 2)[None]
        & (far_pos >= 0)[None, None]
        & (far_pos[None, None] < limit)
    )
    return jnp.concatenate([near_ok, far_ok], axis=-1)


def padded_keys(keys_loc, vals_loc, far_keys, far_vals):
    reach = WINDOW // 2
    pool_reach = POOL_WINDOW // 2 // STRIDE
    pad_near = ((0, 0), (reach, reach), (0, 0), (0, 0))
    pad_far = ((0, 0), (pool_reach, pool_reach), (0, 0), (0, 0))
    return (
        jnp.pad(keys_loc, pad_near),
        jnp.pad(vals_loc, pad_near),
        jnp.pad(far_keys, pad_far),
        jnp.pad(far_vals, pad_far),
    )


def block_inputs(start, queries, padded):
    near_k, near_v, far_k, far_v = padded
    near_len = block_rows + 2 * (WINDOW // 2)
    span = block_rows // STRIDE + 2 * (POOL_WINDOW // 2 // STRIDE)
    pool_start = start // STRIDE
    q_rows = queries[:, start : start + block_rows]
    keys_b = jnp.concatenate(
        [near_k[:, start : start + near_len], far_k[:, pool_start : pool_start + span]], axis=1
    )
    vals_b = jnp.concatenate(
        [near_v[:, start : start + near_len], far_v[:, pool_start : pool_start + span]], axis=1
    )
    return (q_rows, keys_b, vals_b)


def forward_block(q_rows, keys_b, vals_b, mask, live):
    scale = q_rows.shape[-1] ** (-0.5)
    scores = (
        jnp.einsum("sqhe,skhe->shqk", q_rows, keys_b, preferred_element_type=jnp.float32) * scale
    )
    scores = jnp.where(mask[:, None], scores, mask_fill)
    peak = jnp.max(scores, axis=-1, keepdims=True)
    expo = jnp.exp(scores - peak)
    total = jnp.sum(expo, axis=-1, keepdims=True)
    weights = (expo / total).astype(jnp.bfloat16)
    result = jnp.einsum("shqk,skhe->sqhe", weights, vals_b, preferred_element_type=jnp.float32)
    result = jnp.where(live[:, :, None, None], result, 0.0)
    return (result, peak + jnp.log(total))


def forward_skip(q_rows, keys_b, vals_b, mask, live):
    seqs, rows, heads, size = q_rows.shape
    return (
        jnp.zeros((seqs, rows, heads, size), jnp.float32),
        jnp.zeros((seqs, heads, rows, 1), jnp.float32),
    )


def backward_block(q_rows, keys_b, vals_b, mask, logsum, grad_rows):
    scale = q_rows.shape[-1] ** (-0.5)
    scores = (
        jnp.einsum("sqhe,skhe->shqk", q_rows, keys_b, preferred_element_type=jnp.float32) * scale
    )
    scores = jnp.where(mask[:, None], scores, mask_fill)
    probs = jnp.exp(scores - logsum)
    grad_probs = jnp.einsum(
        "sqhe,skhe->shqk", grad_rows, vals_b, preferred_element_type=jnp.float32
    )
    delta = jnp.sum(probs * grad_probs, axis=-1, keepdims=True)
    grad_scores = (probs * (grad_probs - delta)).astype(jnp.bfloat16)
    grad_q = (
        jnp.einsum("shqk,skhe->sqhe", grad_scores, keys_b, preferred_element_type=jnp.float32)
        * scale
    )
    grad_keys = (
        jnp.einsum("shqk,sqhe->skhe", grad_scores, q_rows, preferred_element_type=jnp.float32)
        * scale
    )
    grad_vals = jnp.einsum(
        "shqk,sqhe->skhe", probs.astype(jnp.bfloat16), grad_rows, preferred_element_type=jnp.float32
    )
    return (grad_q, grad_keys, grad_vals)


def backward_skip(q_rows, keys_b, vals_b, mask, logsum, grad_rows):
    return (
        jnp.zeros(q_rows.shape, jnp.float32),
        jnp.zeros(keys_b.shape, jnp.float32),
        jnp.zeros(vals_b.shape, jnp.float32),
    )


def attend_forward(queries, keys_loc, vals_loc, far_keys, far_vals, lengths):
    length = queries.shape[1]
    padded = padded_keys(keys_loc, vals_loc, far_keys, far_vals)
    longest = jnp.max(lengths)
    results, logsums = ([], [])
    for block in range(length // block_rows):
        start = block * block_rows
        q_rows, keys_b, vals_b = block_inputs(start, queries, padded)
        mask = block_mask(start, lengths)
        live = start + jnp.arange(block_rows, dtype=jnp.int32)[None, :] < lengths[:, None]
        result, logsum = lax.cond(
            start < longest, forward_block, forward_skip, q_rows, keys_b, vals_b, mask, live
        )
        results.append(result)
        logsums.append(logsum)
    return (jnp.concatenate(results, axis=1), logsums)


def attend_backward(
    queries, keys_loc, vals_loc, far_keys, far_vals, lengths, logsums, grad_context
):
    seqs, length, heads, size = queries.shape
    pooled_len = far_keys.shape[1]
    reach = WINDOW // 2
    pool_reach = POOL_WINDOW // 2 // STRIDE
    near_len = block_rows + 2 * reach
    span = block_rows // STRIDE + 2 * pool_reach
    padded = padded_keys(keys_loc, vals_loc, far_keys, far_vals)
    longest = jnp.max(lengths)
    grad_near_k = jnp.zeros((seqs, length + 2 * reach, heads, size), jnp.float32)
    grad_near_v = jnp.zeros((seqs, length + 2 * reach, heads, size), jnp.float32)
    grad_far_k = jnp.zeros((seqs, pooled_len + 2 * pool_reach, heads, size), jnp.float32)
    grad_far_v = jnp.zeros((seqs, pooled_len + 2 * pool_reach, heads, size), jnp.float32)
    grad_queries = []
    for block in range(length // block_rows):
        start = block * block_rows
        pool_start = start // STRIDE
        q_rows, keys_b, vals_b = block_inputs(start, queries, padded)
        mask = block_mask(start, lengths)
        grad_rows = grad_context[:, start : start + block_rows]
        grad_q, grad_keys, grad_vals = lax.cond(
            start < longest,
            backward_block,
            backward_skip,
            q_rows,
            keys_b,
            vals_b,
            mask,
            logsums[block],
            grad_rows,
        )
        grad_queries.append(grad_q)
        grad_near_k = grad_near_k.at[:, start : start + near_len].add(grad_keys[:, :near_len])
        grad_near_v = grad_near_v.at[:, start : start + near_len].add(grad_vals[:, :near_len])
        grad_far_k = grad_far_k.at[:, pool_start : pool_start + span].add(grad_keys[:, near_len:])
        grad_far_v = grad_far_v.at[:, pool_start : pool_start + span].add(grad_vals[:, near_len:])
    return (
        jnp.concatenate(grad_queries, axis=1),
        grad_near_k[:, reach : reach + length],
        grad_near_v[:, reach : reach + length],
        grad_far_k[:, pool_reach : pool_reach + pooled_len],
        grad_far_v[:, pool_reach : pool_reach + pooled_len],
    )


def row_sum(left, right, share):

    def term(start, count):
        return jnp.dot(left, right, preferred_element_type=jnp.float32)

    return lax.psum_scatter(
        term(jnp.int32(0), share * lax.axis_size("mp")), "mp", scatter_dimension=0, tiled=True
    )


def share_rows(values):
    return lax.all_gather(values, "mp", axis=0, tiled=True)


def share_back(values):
    return lax.all_gather(values, "mp", axis=0, tiled=True)


def back_sum(term, share):
    return lax.psum_scatter(
        term(jnp.int32(0), share * lax.axis_size("mp")), "mp", scatter_dimension=0, tiled=True
    )


def spread(values, width):
    whole = jnp.zeros(values.shape[:-1] + (width,), jnp.float32)
    start = lax.axis_index("mp") * values.shape[-1]
    return lax.dynamic_update_slice_in_dim(whole, values, start, values.ndim - 1)


def layer_forward(full_in, resid, lengths, params, share):
    (
        w_query,
        w_key,
        w_value,
        b_query,
        b_value,
        conv_key,
        conv_value,
        w_out,
        b_out,
        attn_gain,
        attn_shift,
        w_up,
        b_up,
        w_down,
        b_down,
        ffn_gain,
        ffn_shift,
    ) = params
    seqs = lengths.shape[0]
    total_rows = full_in.shape[0]
    length = total_rows // seqs
    chans = w_query.shape[1]
    heads = chans // HEAD_DIM
    pooled_len = length // STRIDE
    queries = (jnp.dot(full_in, w_query, preferred_element_type=jnp.float32) + b_query).astype(
        jnp.bfloat16
    )
    keys_loc = jnp.dot(full_in, w_key, preferred_element_type=jnp.float32).astype(jnp.bfloat16)
    vals_loc = (jnp.dot(full_in, w_value, preferred_element_type=jnp.float32) + b_value).astype(
        jnp.bfloat16
    )
    valid = (jnp.arange(length, dtype=jnp.int32)[None, :] < lengths[:, None]).astype(jnp.float32)[
        :, :, None
    ]
    far_keys = pool_rows(
        keys_loc.reshape(seqs, length, chans).astype(jnp.float32) * valid, conv_key
    ).astype(jnp.bfloat16)
    far_vals = pool_rows(
        vals_loc.reshape(seqs, length, chans).astype(jnp.float32) * valid, conv_value
    ).astype(jnp.bfloat16)
    context, logsums = attend_forward(
        queries.reshape(seqs, length, heads, HEAD_DIM),
        keys_loc.reshape(seqs, length, heads, HEAD_DIM),
        vals_loc.reshape(seqs, length, heads, HEAD_DIM),
        far_keys.reshape(seqs, pooled_len, heads, HEAD_DIM),
        far_vals.reshape(seqs, pooled_len, heads, HEAD_DIM),
        lengths,
    )
    context = context.reshape(total_rows, chans).astype(jnp.bfloat16)
    hidden_one = resid + (row_sum(context, w_out, share) + b_out)
    normed = norm_rows(hidden_one, attn_gain, attn_shift)
    full_normed = share_rows(normed.astype(jnp.bfloat16))
    upper = jnp.dot(full_normed, w_up, preferred_element_type=jnp.float32) + b_up
    active = gelu_exact(upper).astype(jnp.bfloat16)
    hidden_two = normed + (row_sum(active, w_down, share) + b_down)
    result = norm_rows(hidden_two, ffn_gain, ffn_shift)
    kept = (
        full_in,
        queries,
        keys_loc,
        vals_loc,
        far_keys,
        far_vals,
        logsums,
        context,
        hidden_one,
        full_normed,
        upper,
        active,
        hidden_two,
    )
    return (result, kept)


def layer_backward(grad_out, kept, params, lengths, share):
    (
        w_query,
        w_key,
        w_value,
        b_query,
        b_value,
        conv_key,
        conv_value,
        w_out,
        b_out,
        attn_gain,
        attn_shift,
        w_up,
        b_up,
        w_down,
        b_down,
        ffn_gain,
        ffn_shift,
    ) = params
    (
        full_in,
        queries,
        keys_loc,
        vals_loc,
        far_keys,
        far_vals,
        logsums,
        context,
        hidden_one,
        full_normed,
        saved_upper,
        active,
        hidden_two,
    ) = kept
    seqs = lengths.shape[0]
    total_rows = full_in.shape[0]
    length = total_rows // seqs
    chans = w_query.shape[1]
    heads = chans // HEAD_DIM
    pooled_len = length // STRIDE
    unused_two, pull_two = jax.vjp(norm_rows, hidden_two, ffn_gain, ffn_shift)
    grad_h2, grad_fgain, grad_fshift = pull_two(grad_out)
    grad_ffn = grad_h2.astype(jnp.bfloat16)
    grad_bdown = jnp.sum(grad_ffn.astype(jnp.float32), axis=0)
    full_gffn = share_back(grad_ffn)
    grad_wdown = jnp.einsum("tf,td->fd", active, full_gffn, preferred_element_type=jnp.float32)
    grad_active = jnp.einsum("td,fd->tf", full_gffn, w_down, preferred_element_type=jnp.float32)
    unused_gelu, pull_gelu = jax.vjp(gelu_exact, saved_upper)
    grad_upper = pull_gelu(grad_active)[0].astype(jnp.bfloat16)
    grad_bup = jnp.sum(grad_upper.astype(jnp.float32), axis=0)
    grad_wup = jnp.einsum("td,tf->df", full_normed, grad_upper, preferred_element_type=jnp.float32)

    def up_term(start, count):
        return jnp.einsum("tf,df->td", grad_upper, w_up, preferred_element_type=jnp.float32)

    grad_y1 = grad_h2 + back_sum(up_term, share)
    unused_one, pull_one = jax.vjp(norm_rows, hidden_one, attn_gain, attn_shift)
    grad_h1, grad_again, grad_ashift = pull_one(grad_y1)
    grad_attn = grad_h1.astype(jnp.bfloat16)
    grad_bout = jnp.sum(grad_attn.astype(jnp.float32), axis=0)
    full_gattn = share_back(grad_attn)
    grad_wout = jnp.einsum("tc,td->cd", context, full_gattn, preferred_element_type=jnp.float32)
    grad_context = jnp.einsum("td,cd->tc", full_gattn, w_out, preferred_element_type=jnp.float32)
    valid = (jnp.arange(length, dtype=jnp.int32)[None, :] < lengths[:, None]).astype(jnp.float32)[
        :, :, None
    ]
    grad_context = (grad_context.reshape(seqs, length, chans) * valid).astype(jnp.bfloat16)
    grad_q, grad_near_k, grad_near_v, grad_far_k, grad_far_v = attend_backward(
        queries.reshape(seqs, length, heads, HEAD_DIM),
        keys_loc.reshape(seqs, length, heads, HEAD_DIM),
        vals_loc.reshape(seqs, length, heads, HEAD_DIM),
        far_keys.reshape(seqs, pooled_len, heads, HEAD_DIM),
        far_vals.reshape(seqs, pooled_len, heads, HEAD_DIM),
        lengths,
        logsums,
        grad_context.reshape(seqs, length, heads, HEAD_DIM),
    )
    masked_keys = keys_loc.reshape(seqs, length, chans).astype(jnp.float32) * valid
    masked_vals = vals_loc.reshape(seqs, length, chans).astype(jnp.float32) * valid
    unused_pk, pull_key = jax.vjp(pool_rows, masked_keys, conv_key)
    grad_kpool, grad_ckey = pull_key(grad_far_k.reshape(seqs, pooled_len, chans))
    unused_pv, pull_val = jax.vjp(pool_rows, masked_vals, conv_value)
    grad_vpool, grad_cval = pull_val(grad_far_v.reshape(seqs, pooled_len, chans))
    grad_queries = grad_q.reshape(total_rows, chans).astype(jnp.bfloat16)
    grad_keys = (
        (grad_near_k.reshape(seqs, length, chans) + grad_kpool * valid)
        .reshape(total_rows, chans)
        .astype(jnp.bfloat16)
    )
    grad_vals = (
        (grad_near_v.reshape(seqs, length, chans) + grad_vpool * valid)
        .reshape(total_rows, chans)
        .astype(jnp.bfloat16)
    )
    grad_wquery = jnp.einsum("td,tc->dc", full_in, grad_queries, preferred_element_type=jnp.float32)
    grad_wkey = jnp.einsum("td,tc->dc", full_in, grad_keys, preferred_element_type=jnp.float32)
    grad_wvalue = jnp.einsum("td,tc->dc", full_in, grad_vals, preferred_element_type=jnp.float32)
    grad_bquery = jnp.sum(grad_queries.astype(jnp.float32), axis=0)
    grad_bvalue = jnp.sum(grad_vals.astype(jnp.float32), axis=0)

    def input_term(start, count):
        total = jnp.einsum("tc,dc->td", grad_queries, w_query, preferred_element_type=jnp.float32)
        total = total + jnp.einsum(
            "tc,dc->td", grad_keys, w_key, preferred_element_type=jnp.float32
        )
        return total + jnp.einsum(
            "tc,dc->td", grad_vals, w_value, preferred_element_type=jnp.float32
        )

    grad_input = grad_h1 + back_sum(input_term, share)
    matrices = (
        grad_wquery[None],
        grad_wkey[None],
        grad_wvalue[None],
        grad_wout[None],
        grad_wup[None],
        grad_wdown[None],
    )
    vectors = (
        spread(grad_bquery, D)[None],
        spread(grad_bvalue, D)[None],
        spread(grad_ckey, D)[None],
        spread(grad_cval, D)[None],
        grad_bout[None],
        grad_again[None],
        grad_ashift[None],
        spread(grad_bup, FF)[None],
        grad_bdown[None],
        grad_fgain[None],
        grad_fshift[None],
    )
    return (grad_input, matrices, vectors)


def on_device(
    tokens,
    lengths,
    w_query,
    w_key,
    w_value,
    b_query,
    b_value,
    conv_key,
    conv_value,
    w_out,
    b_out,
    attn_gain,
    attn_shift,
    w_up,
    b_up,
    w_down,
    b_down,
    ffn_gain,
    ffn_shift,
    cotangent,
):
    stacks = (
        w_query,
        w_key,
        w_value,
        b_query,
        b_value,
        conv_key,
        conv_value,
        w_out,
        b_out,
        attn_gain,
        attn_shift,
        w_up,
        b_up,
        w_down,
        b_down,
        ffn_gain,
        ffn_shift,
    )
    total_rows = tokens.shape[0]
    share = total_rows // lax.axis_size("mp")
    place = lax.axis_index("mp") * share
    resid = lax.dynamic_slice_in_dim(tokens, place, share, 0).astype(jnp.float32)
    layer = 0
    params = tuple((stack[layer] for stack in stacks))
    result, kept = layer_forward(tokens, resid, lengths, params, share)
    kept_all = [kept]
    activations = result.astype(jnp.bfloat16)
    grad_out = cotangent.astype(jnp.float32)
    matrix_list = [None] * LAYERS
    vector_list = [None] * LAYERS
    for layer in reversed(range(LAYERS)):
        params = tuple((stack[layer] for stack in stacks))
        grad_out, matrices, vectors = layer_backward(
            grad_out, kept_all[layer], params, lengths, share
        )
        matrix_list[layer] = matrices
        vector_list[layer] = vectors
    grad_wquery, grad_wkey, grad_wvalue, grad_wout, grad_wup, grad_wdown = tuple(
        (jnp.concatenate([entry[index] for entry in matrix_list], axis=0) for index in range(6))
    )
    (
        grad_bquery,
        grad_bvalue,
        grad_ckey,
        grad_cval,
        grad_bout,
        grad_again,
        grad_ashift,
        grad_bup,
        grad_bdown,
        grad_fgain,
        grad_fshift,
    ) = tuple(
        (jnp.concatenate([entry[index] for entry in vector_list], axis=0) for index in range(11))
    )
    grad_wquery, grad_wkey, grad_wvalue, grad_wout, grad_wup, grad_wdown = (
        lax.psum_scatter(grad_wquery, "dp", scatter_dimension=1, tiled=True),
        lax.psum_scatter(grad_wkey, "dp", scatter_dimension=1, tiled=True),
        lax.psum_scatter(grad_wvalue, "dp", scatter_dimension=1, tiled=True),
        lax.psum_scatter(grad_wout, "dp", scatter_dimension=2, tiled=True),
        lax.psum_scatter(grad_wup, "dp", scatter_dimension=1, tiled=True),
        lax.psum_scatter(grad_wdown, "dp", scatter_dimension=2, tiled=True),
    )
    (
        grad_bquery,
        grad_bvalue,
        grad_ckey,
        grad_cval,
        grad_bout,
        grad_again,
        grad_ashift,
        grad_bup,
        grad_bdown,
        grad_fgain,
        grad_fshift,
    ) = lax.psum(
        (
            grad_bquery,
            grad_bvalue,
            grad_ckey,
            grad_cval,
            grad_bout,
            grad_again,
            grad_ashift,
            grad_bup,
            grad_bdown,
            grad_fgain,
            grad_fshift,
        ),
        ("dp", "mp"),
    )
    return (
        activations,
        grad_out,
        grad_wquery,
        grad_wkey,
        grad_wvalue,
        grad_bquery,
        grad_bvalue,
        grad_ckey,
        grad_cval,
        grad_wout,
        grad_bout,
        grad_again,
        grad_ashift,
        grad_wup,
        grad_bup,
        grad_wdown,
        grad_bdown,
        grad_fgain,
        grad_fshift,
    )


BF = jnp.bfloat16
F32 = jnp.float32
MESH = pl.DeviceIdType.MESH
ROWS = 256
QUARTERS = 4
CHANS = D // QUARTERS
QHEADS = CHANS // HEAD_DIM
SEQ = QUARTERS * ROWS
REACH = WINDOW // 2
PREACH = POOL_WINDOW // 2 // STRIDE
OWNP = ROWS // STRIDE
KW = ROWS + 2 * REACH
KP = OWNP + 2 * PREACH
KEYS = KW + KP
QB = 128
NEAR = QB + 2 * REACH
FAR = QB // STRIDE + 2 * PREACH
COMP = 800
HALFC = COMP // 2
FRONT = 256
KVROWS = 1408
BASE = 288
PIECE = D // 8
BIG_NEG = -1e30
SCALE = HEAD_DIM ** -0.5
VROWS = 64
TILES = 2 * CHANS // 128


def nn(a, b):
    return jnp.dot(a, b, preferred_element_type=F32)


def nt(a, b):
    return lax.dot_general(a, b, (((1,), (1,)), ((), ())), preferred_element_type=F32)


def tn(a, b):
    return lax.dot_general(a, b, (((0,), (0,)), ((), ())), preferred_element_type=F32)


def rows_iota(rows, cols):
    return lax.broadcasted_iota(jnp.int32, (rows, cols), 0)


def cols_iota(rows, cols):
    return lax.broadcasted_iota(jnp.int32, (rows, cols), 1)


def mean_row(v):
    return jnp.mean(v, axis=-1, keepdims=True)


def sum_col(v):
    return jnp.sum(v, axis=0, keepdims=True)


def kernel(
    len_hbm, tok_hbm, wk, wv, wq, wo, wup, wdown, bq_h, bv_h, ck_h, cv_h, bup_h, bo_h, ag_h, ash_h, bd_h, fg_h, fs_h, cot_hbm,
    act_hbm, gtok_hbm, gmats_hbm, gvec_hbm,
    W, VEC, kvf, KV, KVS, Q, CTX, P, maskn, maskf, n1, r1, y1, y1b, dg, av,
    yT, fT, gab, GKV, pt, GQ, VG,
    CR, S1, S2, ZR, ZF, HL, HR, HLL, SL, SR, GVR, GVZ, VO, tok, cot,
    len_ref, bq, bv, ck, cv, bup, bo, ag, ash, bd, fg, fs, act_out, gtok, gmats,
    ssem, osem, lsem, asend, arecv, zsend, zrecv, lsend, hsend, hrecv, rsend, rrecv, zsum, zfsum, gsend, grecv,
):
    acc, n2, xT, gub = gtok, y1, yT, y1b
    dp = lax.axis_index("dp")
    z = lax.axis_index("mp")
    c = lax.rem(dp, 2)
    x = lax.rem(lax.div(dp, 2), 2)
    y = lax.div(dp, 4)
    core = (dp + 1 - 2 * c, z)
    xdev = (dp + 2 - 4 * x, z)
    ydev = (dp + 4 - 8 * y, z)
    yx = 2 * y + x

    def zdev(step):
        return (dp, lax.rem(z + step, QUARTERS))

    def rcopy(src, dst, ssem, rsem, dev):
        return pltpu.make_async_remote_copy(
            src_ref=src, dst_ref=dst, send_sem=ssem, recv_sem=rsem,
            device_id=dev, device_id_type=MESH,
        )

    barrier = pltpu.get_barrier_semaphore()
    for dev in (core, xdev, ydev, zdev(1), zdev(2), zdev(3)):
        pl.semaphore_signal(barrier, inc=1, device_id=dev, device_id_type=MESH)

    def loads():
        parts = [(wk, 0), (wv, CHANS), (wq, 2 * CHANS), (wo, 3 * CHANS)]
        copies = [
            pltpu.make_async_copy(src, W.at[0, z, at : at + CHANS, :], lsem.at[i])
            for i, (src, at) in enumerate(parts)
        ]
        copies.append(pltpu.make_async_copy(wup, W.at[1, z], lsem.at[4]))
        copies.append(pltpu.make_async_copy(wdown, W.at[2, z], lsem.at[5]))
        return copies

    small = [
        pltpu.make_async_copy(src, dst, ssem.at[i])
        for i, (src, dst) in enumerate(
            (
                (bup_h, bup), (bv_h, bv), (bq_h, bq), (ck_h, ck), (cv_h, cv), (len_hbm, len_ref),
                (bo_h, bo), (ag_h, ag), (ash_h, ash), (bd_h, bd), (fg_h, fg), (fs_h, fs),
            )
        )
    ]
    outs = [
        pltpu.make_async_copy(src, dst, osem.at[i])
        for i, (src, dst) in enumerate(
            (
                (act_out, act_hbm), (gtok, gtok_hbm), (gmats.at[0], gmats_hbm.at[0]),
                (gmats.at[1], gmats_hbm.at[1]), (gmats.at[2], gmats_hbm.at[2]), (VO, gvec_hbm),
            )
        )
    ]
    for cp in small[:6]:
        cp.start()
    own = loads()
    tok_in = pltpu.make_async_copy(tok_hbm, tok, lsem.at[6])
    cot_in = pltpu.make_async_copy(cot_hbm, cot, lsem.at[7])
    for cp in own:
        cp.start()
    tok_in.start()
    for cp in small[6:]:
        cp.start()
    cot_in.start()
    for cp in small[:6]:
        cp.wait()
    length = len_ref[0]
    vpack = VG.at[0:8, :]
    vpack[...] = jnp.zeros_like(vpack)
    vpack[0:1, :] = bup[...]
    vpack[1:2, CHANS : 2 * CHANS] = bv[...]
    vpack[1:2, 2 * CHANS : 3 * CHANS] = bq[...]
    for t in range(5):
        vpack[2 + t : 3 + t, 0:CHANS] = ck[t]
        vpack[2 + t : 3 + t, CHANS : 2 * CHANS] = cv[t]
    VEC[z] = vpack[...]
    pl.semaphore_wait(barrier, 6)

    def block(j):
        return pl.ds(pl.multiple_of(j * PIECE, PIECE), PIECE)

    piece_me = c * 4 + yx
    piece_x = c * 4 + 2 * y + 1 - x
    piece_y = c * 4 + 2 * (1 - y) + x
    piece_d = c * 4 + 2 * (1 - y) + 1 - x
    LO, HI = pl.ds(0, D // 2), pl.ds(D // 2, D // 2)
    ALL = pl.ds(0, D)
    CHUNKS = 9
    ends = [(0, 1), (1, 1), (0, 2), (1, 2), (0, 3), (2, 1), (2, 2), (1, 3), (2, 3)]
    inner = [(0, 1), (0, 2), (1, 1), (1, 2), (0, 3), (2, 1), (2, 2), (1, 3), (2, 3)]
    sources = [(1, 2, 3), (2, 0, 3), (1, 3, 0), (2, 1, 0)]
    targets = [(3, 2, 1, 0), (3, 0, 2, 1), (0, 3, 1, 2), (0, 1, 2, 3)]
    DOWN = 2
    FAR_STEPS = 2
    at_end = (z == 0) | (z == QUARTERS - 1)

    def table(values, bits=2):
        word = sum(v << (bits * i) for i, v in enumerate(values))
        return jnp.int32(word - (1 << 32) if word >> 31 else word)

    def lookup(word, i, bits=2):
        return lax.bitwise_and(lax.shift_right_logical(word, bits * i), (1 << bits) - 1)

    def by_place(a, b):
        return lax.select(at_end, a, b)

    mats_of = by_place(table(m for m, d in ends), table(m for m, d in inner))
    dist_of = by_place(table(d for m, d in ends), table(d for m, d in inner))
    looks_of = by_place(table((1, 2, 4, 5, 6, 7, 8, 9), 4), table((2, 4, 5, 7, 8, 9, 9, 9), 4))
    sends_of = by_place(table((1, 2, 4, 5, 6, 7, 8, 9), 4), table((2, 3, 4, 5, 6, 7, 8, 9), 4))

    def source(d):
        return lookup(table(v for row in sources for v in row), 3 * z + d - 1)

    def target(t):
        return lookup(table(v for row in targets for v in row), 4 * z + t)

    def chunk(k):
        return lookup(mats_of, k), source(lookup(dist_of, k))

    def is_far(k):
        return (lookup(mats_of, k) == DOWN) & (lookup(dist_of, k) < FAR_STEPS)

    def own_block(m, up, piece, sem):
        src = W.at[m, z, block(piece), :]
        return rcopy(src, src, zsend.at[sem, up], zrecv.at[sem, z], (dp, z + 2 * up - 1))

    def own_z(m, up):
        return own_block(m, up, piece_me, m)

    def far_z(up):
        return own_block(DOWN, up, piece_d, 4)

    def wants_far(up):
        to = z + 2 * up - 1
        inner_to = (to == 1) | (to == 2)
        return jnp.logical_not(inner_to) | (z == 3 - to)

    def relay(m, src, dev):
        ref = W.at[m, src, block(piece_me), :]
        return rcopy(ref, ref, lsend.at[m, src], zrecv.at[m, src], dev)

    def relay_far(src, dev):
        ref = W.at[DOWN, src, block(piece_d), :]
        return rcopy(ref, ref, lsend.at[4, src], zrecv.at[4, src], dev)

    def own_vec(up):
        src = VEC.at[z]
        return rcopy(src, src, zsend.at[3, up], zrecv.at[3, z], (dp, z + 2 * up - 1))

    def relay_vec(src, dev):
        ref = VEC.at[src]
        return rcopy(ref, ref, lsend.at[3, src], zrecv.at[3, src], dev)

    def onward(src):
        return jnp.where(src > z, z > 0, z < QUARTERS - 1)

    def next_dev(src):
        return (dp, jnp.where(src > z, z - 1, z + 1))

    def plane(k, which, piece, cols, dev):
        m, src = chunk(k)
        ref = W.at[m, src, block(piece), cols]
        return rcopy(ref, ref, asend.at[k], arecv.at[k, (which - 1) // 2], dev)

    def look(k):
        m, src = chunk(k)

        @pl.when(m == 0)
        def _():
            relay_vec(src, core).wait_recv()
            pl.when(onward(src))(lambda: relay_vec(src, next_dev(src)).start())

        relay(m, src, core).wait_recv()
        pl.when(onward(src))(lambda: relay(m, src, next_dev(src)).start())

        @pl.when(is_far(k))
        def _():
            relay_far(src, core).wait_recv()

    def first(k):
        plane(k, 1, piece_me, ALL, xdev).start()
        plane(k, 2, piece_me, ALL, ydev).start()

    def rows_of(count):
        return W.at[0, 0, 0:count, :]

    def wait_rows(sem, count):
        pltpu.make_async_copy(rows_of(count), rows_of(count), sem).wait()

    def second(k):
        wait_rows(arecv.at[k, 0], 2 * PIECE)

        @pl.when(jnp.logical_not(is_far(k)))
        def _():
            plane(k, 3, piece_x, LO, ydev).start()
            plane(k, 4, piece_y, HI, xdev).start()

    def half(j):
        return pl.ds(pl.multiple_of(j * (D // 2), D // 2), D // 2)

    def cross(k, j):
        m, src = chunk(k)
        ref = W.at[m, src, half(j), :]
        return rcopy(ref, ref, asend.at[k], arecv.at[k, 2], core)

    def third(k):
        pl.when(jnp.logical_not(is_far(k)))(lambda: wait_rows(arecv.at[k, 1], PIECE))
        cross(k, c).start()

    def fourth(k):
        cross(k, 1 - c).wait_recv()

    def looks(i):
        return jnp.where(i < 0, 0, lookup(looks_of, lax.clamp(0, i, 7), 4))

    def sends(i):
        return jnp.where(i < 0, 0, lookup(sends_of, lax.clamp(0, i, 7), 4))

    def each(fn):
        def body(k, carry):
            fn(k)
            return carry

        return body

    def gather_slot(i, carry):
        lax.fori_loop(looks(i - 1), looks(i), each(look), 0)
        pl.when((i == 2) & jnp.logical_not(at_end))(lambda: both(own_down))
        lax.fori_loop(sends(i - 1), sends(i), each(first), 0)
        for lag, stage in ((1, second), (2, third), (3, fourth)):
            k = i - lag
            pl.when((k >= 0) & (k < CHUNKS))(lambda stage=stage, k=k: stage(k))
        return carry

    def gather_done(k, carry):
        m, src = chunk(k)

        @pl.when(onward(src))
        def _():
            relay(m, src, core).wait_send()
            pl.when(m == 0)(lambda: relay_vec(src, core).wait_send())

        far = is_far(k)
        pl.when(far)(lambda: wait_rows(asend.at[k], 6 * PIECE))
        pl.when(jnp.logical_not(far))(lambda: wait_rows(asend.at[k], 7 * PIECE))
        return carry

    def got(s):
        return lax.rem(z + QUARTERS - s, QUARTERS)

    def both(fn):
        pl.when(z > 0)(lambda: fn(0))
        pl.when(z < QUARTERS - 1)(lambda: fn(1))

    both(lambda up: own_vec(up).start())
    for m, waits in enumerate((own[:4], own[4:5], own[5:])):
        for cp in waits:
            cp.wait()
        if m != DOWN:
            both(lambda up: own_z(m, up).start())

    def own_down(up):
        own_z(DOWN, up).start()
        pl.when(wants_far(up))(lambda: far_z(up).start())

    pl.when(at_end)(lambda: both(own_down))

    def own_sent(up):
        own_vec(up).wait_send()
        for m in range(3):
            own_z(m, up).wait_send()
        pl.when(wants_far(up))(lambda: far_z(up).wait_send())

    base = z * ROWS
    start = lax.select(z < 2, jnp.int32(0), jnp.int32(SEQ - COMP))
    place = pl.multiple_of(start - base + BASE + FRONT, 32)
    start = pl.multiple_of(start, 32)
    kvf[...] = jnp.zeros_like(kvf)
    for b in range(2):
        i = base + b * QB + cols_iota(1, QB)
        j = base - REACH + b * QB + rows_iota(NEAR, 1)
        ok = (jnp.abs(i - j) <= REACH) & (j >= 0) & (j < length)
        maskn[b] = jnp.where(ok, 0.0, BIG_NEG)
        j = (OWNP * z - PREACH + b * (QB // STRIDE) + rows_iota(FAR, 1)) * STRIDE
        ok = (jnp.abs(i - j) <= POOL_WINDOW // 2) & (j >= 0) & (j < length)
        maskf[b] = jnp.where(ok, 0.0, BIG_NEG)
    own_rows = pl.ds(pl.multiple_of(base, ROWS), ROWS)
    tok_in.wait()
    cot_in.wait()
    for cp in small[6:]:
        cp.wait()
    xb = tok[own_rows, :]
    acc[...] = jnp.zeros_like(acc)

    def taps(zq, t):
        return VEC[zq, 2 + t : 3 + t, 0 : 2 * CHANS]

    def strided(t):
        at = pl.ds(FRONT + BASE - POOL_WINDOW // 2 - 2 + t, KP, stride=STRIDE)
        return jnp.concatenate([kvf[i, at, :] for i in range(TILES)], axis=1)

    def tile(i):
        return slice(i * 128, (i + 1) * 128)

    def window(lo, rows):
        return jnp.concatenate([kvf[i, lo : lo + rows, :] for i in range(TILES)], axis=1)

    def quarter(s):
        return lax.select(s == 0, z, source(lax.max(s, 1)))

    def attend(s, carry):
        zq = quarter(s)
        for blk in range(2):
            xr = tok[pl.ds(pl.multiple_of(start + blk * HALFC, 16), HALFC), :]
            kv = nt(xr, W[0, zq, 0 : 2 * CHANS, :]) + VEC[zq, 1:2, 0 : 2 * CHANS]
            pos = start + blk * HALFC + rows_iota(HALFC, 1)
            kvb = jnp.where(pos < length, kv.astype(BF).astype(F32), 0.0)
            for i in range(TILES):
                kvf[i, pl.ds(pl.multiple_of(place + blk * HALFC, 8), HALFC), :] = kvb[:, tile(i)]
        KVS[zq] = window(FRONT, COMP).astype(BF)
        KV[zq, 0:KW, :] = window(FRONT + BASE - REACH, KW).astype(BF)
        pooled = jnp.zeros((KP, 2 * CHANS), F32)
        for t in range(5):
            pooled = pooled + taps(zq, t) * strided(t)
        KV[zq, KW:KEYS, :] = pooled.astype(BF)
        qz = nt(xb, W[0, zq, 2 * CHANS : 3 * CHANS, :]) + VEC[zq, 1:2, 2 * CHANS : 3 * CHANS]
        Q[zq] = qz.astype(BF)
        for b in range(2):
            live = base + b * QB + cols_iota(1, QB) < length
            n0, f0 = b * QB, KW + b * (QB // STRIDE)
            for h in range(QHEADS):
                kl = slice(h * HEAD_DIM, (h + 1) * HEAD_DIM)
                vl = slice(CHANS + h * HEAD_DIM, CHANS + (h + 1) * HEAD_DIM)
                qh = Q[zq, b * QB : (b + 1) * QB, kl]
                sn = nt(KV[zq, n0 : n0 + NEAR, kl], qh) * SCALE + maskn[b]
                sf = nt(KV[zq, f0 : f0 + FAR, kl], qh) * SCALE + maskf[b]
                peak = jnp.maximum(
                    jnp.max(sn, axis=0, keepdims=True), jnp.max(sf, axis=0, keepdims=True)
                )
                en, ef = jnp.exp(sn - peak), jnp.exp(sf - peak)
                inv = 1.0 / (sum_col(en) + sum_col(ef))
                pn, pf = en * inv, ef * inv
                P[zq, h, b, 0:NEAR, :] = pn
                P[zq, h, b, NEAR : NEAR + FAR, :] = pf
                ct = tn(KV[zq, n0 : n0 + NEAR, vl], pn.astype(BF))
                ct = ct + tn(KV[zq, f0 : f0 + FAR, vl], pf.astype(BF))
                ct = jnp.where(live, ct, 0.0)
                CTX[zq, b * QB : (b + 1) * QB, kl] = ct.T.astype(BF)
        acc[...] += nn(CTX[zq], W[0, zq, 3 * CHANS : D, :])
        lax.fori_loop(lookup_slots(s), lookup_slots(s + 1), gather_slot, 0)
        return carry

    def lookup_slots(s):
        return jnp.where(s == 0, 0, jnp.where(s < 3, 2 + 2 * s, 8))

    lax.fori_loop(0, QUARTERS, attend, 0)

    def store_T(dst, v, cols):
        vt = v.T.astype(BF)
        for j in range(8):
            to = (j % 2) * 4 + j // 2
            dst[to * PIECE : (to + 1) * PIECE, cols] = vt[j * PIECE : (j + 1) * PIECE]

    def span(i, size):
        if isinstance(i, int):
            return pl.ds(i * size, size)
        return pl.ds(pl.multiple_of(i * size, size), size)

    def norm_one(i, carry):
        rows = span(i, QB)
        res = tok[pl.ds(pl.multiple_of(base + i * QB, QB), QB), :].astype(F32)
        hid = res + (acc[rows, :] + bo[...])
        cen = hid - mean_row(hid)
        r = lax.rsqrt(mean_row(cen * cen) + epsilon)
        n = cen * r
        n1[rows, :] = n
        r1[rows, :] = r
        out = n * ag[...] + ash[...]
        y1[rows, :] = out
        y1b[rows, :] = out.astype(BF)
        store_T(yT, out, rows)
        acc[rows, :] = jnp.zeros_like(out)
        return carry

    lax.fori_loop(0, ROWS // QB, norm_one, 0)

    def feed(s, carry):
        zq = quarter(s)

        def up(i, carry):
            cols = span(i, ROWS)
            u = nn(y1b[...], W[1, zq, :, cols]) + VEC[zq, 0:1, cols]
            cdf = 0.5 * (1.0 + lax.erf(u * (0.5 ** 0.5)))
            dg[zq, :, cols] = cdf + u * jnp.exp(-0.5 * u * u) * ((2.0 * 3.141592653589793) ** -0.5)
            av[zq, :, cols] = (u * cdf).astype(BF)
            return carry

        for i in range(D // ROWS):
            up(i, 0)
        acc[...] += nn(av[zq], W[2, zq])
        lo = jnp.where(s < 3, 8 + s, 12)
        hi = jnp.where(s < 2, 9 + s, 12)
        lax.fori_loop(lo, hi, gather_slot, 0)
        return carry

    lax.fori_loop(0, QUARTERS, feed, 0)
    VG[...] = jnp.zeros_like(VG)
    GEN = 8 * QUARTERS

    def add_row(row, v):
        VG[row : row + 1, :] += sum_col(v)

    def norm_two(i, carry):
        rows = span(i, QB)
        hid = y1[rows, :] + (acc[rows, :] + bd[...])
        cen = hid - mean_row(hid)
        r = lax.rsqrt(mean_row(cen * cen) + epsilon)
        n = cen * r
        act_out[rows, :] = (n * fg[...] + fs[...]).astype(BF)
        g = cot[rows, :].astype(F32)
        add_row(GEN + 4, g * n)
        add_row(GEN + 5, g)
        e = g * fg[...]
        gh2 = r * (e - mean_row(e) - n * mean_row(e * n))
        acc[rows, :] = gh2
        gf = gh2.astype(BF)
        gab[rows, :] = gf
        gff = gf.astype(F32)
        add_row(GEN + 3, gff)
        store_T(fT, gff, rows)
        return carry

    lax.fori_loop(0, ROWS // QB, norm_two, 0)
    outs[0].start()

    PARTS = 12

    def part(r):
        m = lax.select(r < 8, 2 - lax.rem(r, 2), 0)
        t = lax.select(r < 8, lax.div(r, 2), r - 8)
        return m, t

    def r_core(r):
        m, t = part(r)
        src = W.at[m, target(t), half(1 - c), :]
        return rcopy(src, CR.at[r], rsend.at[r], rrecv.at[r, 0], core)

    def blk4(r, yy, xx, cols):
        return CR.at[r, block(2 * yy + xx), cols]

    THIRD = D // 3
    wide = (LO, HI, D // 2, ALL)
    thin = (pl.ds(0, THIRD), pl.ds(THIRD, THIRD), THIRD, pl.ds(0, 2 * THIRD))
    LAST = pl.ds(2 * THIRD, THIRD)
    OWN_DOWN = 6

    def narrow(r):
        m, t = part(r)
        return (m == DOWN) & (t < QUARTERS - 1)

    def by_width(r, fn):
        pl.when(narrow(r))(lambda: fn(thin))
        pl.when(jnp.logical_not(narrow(r)))(lambda: fn(wide))

    def r_stage1(r, i, cut):
        if i < 2:
            src, dev = blk4(r, i, 1 - x, cut[0]), xdev
        else:
            src, dev = blk4(r, 1 - y, i - 2, cut[1]), ydev
        return rcopy(src, S1.at[r, i, :, 0 : cut[2]], rsend.at[r], rrecv.at[r, 1], dev)

    def r_stage2(r, i, cut):
        if i == 0:
            src, dev = blk4(r, 1 - y, x, cut[0]), ydev
        else:
            src, dev = blk4(r, y, 1 - x, cut[1]), xdev
        return rcopy(src, S2.at[r, i, :, 0 : cut[2]], rsend.at[r], rrecv.at[r, 2], dev)

    def onto(r):
        dst = target(part(r)[1])
        left = dst < z
        slot = jnp.where(left & (dst == z - 1), QUARTERS, dst)
        return slot, (dp, jnp.where(left, z - 1, z + 1))

    def r_z(r, cut):
        slot, dev = onto(r)
        m = part(r)[0]
        src = CR.at[r, block(yx), cut[3]]
        return rcopy(src, ZR.at[m, slot, :, cut[3]], rsend.at[r], zsum.at[m, slot], dev)

    def z_wait(m, slot, cut):
        ref = ZR.at[m, slot, :, cut[3]]
        pltpu.make_async_copy(ref, ref, zsum.at[m, slot]).wait()

    def r_zf(r):
        slot, dev = onto(r)
        return rcopy(CR.at[r, :, LAST], ZF.at[slot], rsend.at[r], zfsum.at[slot], dev)

    def take_zf(r, slot):
        ref = ZF.at[slot]
        pltpu.make_async_copy(ref, ref, zfsum.at[slot]).wait()
        CR[r, :, LAST] = CR[r, :, LAST] + ZF[slot]

    def upstream(dst):
        return jnp.where(dst < z, z < QUARTERS - 1, z > 0)

    def reduce1(r):
        m, t = part(r)
        r_core(r).wait_recv()
        zq = target(t)

        def add(i, carry):
            CR[r, block(i), :] = CR[r, block(i), :] + W[m, zq, block(4 * c + i), :]
            return carry

        lax.fori_loop(0, 4, add, 0)

        @pl.when(r == OWN_DOWN)
        def _():
            pl.when(z > 0)(lambda: take_zf(r, z))
            pl.when(z < QUARTERS - 1)(lambda: take_zf(r, jnp.int32(QUARTERS)))

        def go(cut):
            for i in range(4):
                r_stage1(r, i, cut).start()

        by_width(r, go)
        pl.when(narrow(r) & jnp.logical_not(upstream(zq)))(lambda: r_zf(r).start())

    def reduce_f(r):
        dst = target(part(r)[1])

        @pl.when(upstream(dst))
        def _():
            take_zf(r, dst)
            r_zf(r).start()

    def reduce2(r):
        def go(cut):
            ref = S1.at[r, :, :, 0 : cut[2]]
            pltpu.make_async_copy(ref, ref, rrecv.at[r, 1]).wait()
            for i in range(2):
                a = blk4(r, i, x, cut[0])
                a[...] = a[...] + S1[r, i, :, 0 : cut[2]]
                a = blk4(r, y, i, cut[1])
                a[...] = a[...] + S1[r, 2 + i, :, 0 : cut[2]]
            for i in range(2):
                r_stage2(r, i, cut).start()

        by_width(r, go)

    def reduce3(r):
        dst = target(part(r)[1])

        def go(cut):
            ref = S2.at[r, :, :, 0 : cut[2]]
            pltpu.make_async_copy(ref, ref, rrecv.at[r, 2]).wait()
            for i in range(2):
                a = blk4(r, y, x, cut[i])
                a[...] = a[...] + S2[r, i, :, 0 : cut[2]]
            pl.when((dst != z) & jnp.logical_not(upstream(dst)))(lambda: r_z(r, cut).start())

        by_width(r, go)

    def reduce4(r):
        m, t = part(r)
        dst = target(t)

        def go(cut):
            @pl.when((dst != z) & upstream(dst))
            def _():
                z_wait(m, dst, cut)
                a = CR.at[r, block(yx), cut[3]]
                a[...] = a[...] + ZR[m, dst, :, cut[3]]
                r_z(r, cut).start()

        by_width(r, go)

    def stage(fn, ok, r):
        pl.when(ok)(lambda: fn(r))

    def weight_grad(left, right, dst, width):
        dst[:, 0:width] = nn(left[...], right).astype(BF)

    def feed_back(s, carry):
        zq = target(s)
        vrow = pl.multiple_of(8 * zq, 8)

        def hidden(i, carry):
            cols = span(i, ROWS)
            gact = nt(gab[...], W[2, zq, cols, :])
            gu = (gact * dg[zq, :, cols]).astype(BF)
            gub[:, cols] = gu
            VG[pl.ds(vrow, 1), cols] = sum_col(gu.astype(F32))
            return carry

        for i in range(D // ROWS):
            hidden(i, 0)
        weight_grad(fT, av[zq], W.at[2, zq], D)
        r_core(2 * s).start()
        acc[...] += nt(gub[...], W[1, zq])
        weight_grad(yT, gub[...], W.at[1, zq], D)
        r_core(2 * s + 1).start()
        reduce1(jnp.where(s < 2, s, s + 1))
        stage(reduce1, s == 1, jnp.int32(2))
        stage(reduce2, s == 3, jnp.int32(0))
        return carry

    lax.fori_loop(0, CHUNKS, gather_done, 0)
    both(own_sent)
    lax.fori_loop(0, QUARTERS, feed_back, 0)

    def norm_back(i, carry):
        rows = span(i, QB)
        gy = acc[rows, :]
        n = n1[rows, :]
        add_row(GEN + 1, gy * n)
        add_row(GEN + 2, gy)
        e = gy * ag[...]
        gh1 = r1[rows, :] * (e - mean_row(e) - n * mean_row(e * n))
        acc[rows, :] = gh1
        ga = gh1.astype(BF)
        gab[rows, :] = ga
        gaf = ga.astype(F32)
        add_row(GEN, gaf)
        store_T(fT, gaf, rows)
        store_T(xT, tok[pl.ds(pl.multiple_of(base + i * QB, QB), QB), :].astype(F32), rows)
        return carry

    lax.fori_loop(0, ROWS // QB, norm_back, 0)

    def hl(zq):
        return rcopy(SL.at[zq], HL.at[zq], hsend.at[0], hrecv.at[0, zq], zdev(3))

    def hr(zq):
        return rcopy(SR.at[zq], HR.at[zq], hsend.at[1], hrecv.at[1, zq], zdev(1))

    def hll(zq):
        return rcopy(
            SL.at[zq, REACH : REACH + 16, :], HLL.at[zq], hsend.at[2], hrecv.at[2, zq], zdev(2)
        )

    def attend_back(s, carry):
        zq = lookup(table((3, 0, 2, 1)), s)
        gc = nt(gab[...], W[0, zq, 3 * CHANS : D, :])
        alive = base + rows_iota(ROWS, 1) < length
        gcb = jnp.where(alive, gc, 0.0).astype(BF)
        GKV[zq] = jnp.zeros((KEYS, 2 * CHANS), F32)
        for b in range(2):
            n0, f0 = b * QB, KW + b * (QB // STRIDE)
            for h in range(QHEADS):
                kl = slice(h * HEAD_DIM, (h + 1) * HEAD_DIM)
                vl = slice(CHANS + h * HEAD_DIM, CHANS + (h + 1) * HEAD_DIM)
                gch = gcb[b * QB : (b + 1) * QB, kl]
                qh = Q[zq, b * QB : (b + 1) * QB, kl]
                pn = P[zq, h, b, 0:NEAR, :]
                pf = P[zq, h, b, NEAR : NEAR + FAR, :]
                gpn = nt(KV[zq, n0 : n0 + NEAR, vl], gch)
                gpf = nt(KV[zq, f0 : f0 + FAR, vl], gch)
                delta = sum_col(pn * gpn) + sum_col(pf * gpf)
                gsn = (pn * (gpn - delta)).astype(BF)
                gsf = (pf * (gpf - delta)).astype(BF)
                qt = tn(KV[zq, n0 : n0 + NEAR, kl], gsn) + tn(KV[zq, f0 : f0 + FAR, kl], gsf)
                GQ[zq, b * QB : (b + 1) * QB, 2 * CHANS + h * HEAD_DIM : 2 * CHANS + (h + 1) * HEAD_DIM] = (
                    (qt * SCALE).T.astype(BF)
                )
                GKV[zq, n0 : n0 + NEAR, kl] += nn(gsn, qh) * SCALE
                GKV[zq, f0 : f0 + FAR, kl] += nn(gsf, qh) * SCALE
                GKV[zq, n0 : n0 + NEAR, vl] += nn(pn.astype(BF), gch)
                GKV[zq, f0 : f0 + FAR, vl] += nn(pf.astype(BF), gch)
        vrow = pl.multiple_of(8 * zq, 8)
        for i in range(TILES):
            kvf[i, FRONT : FRONT + COMP, :] = KVS[zq, :, tile(i)].astype(F32)
        gp = GKV[zq, KW:KEYS, :]
        sums = jnp.concatenate(
            [jnp.zeros((1, CHANS), F32), sum_col(GKV[zq, 0:KW, CHANS : 2 * CHANS])], axis=1
        )
        far_at = (OWNP * z - PREACH + rows_iota(KP, 1)) * STRIDE
        for t in range(5):
            VG[pl.ds(vrow + 2 + t, 1), 0 : 2 * CHANS] = sum_col(gp * strided(t))
            to = far_at + (t - 2)
            inside = (to >= 0) & (to < length)
            sums = sums + taps(zq, t) * sum_col(jnp.where(inside, gp, 0.0))
        VG[pl.ds(vrow + 1, 1), CHANS : 2 * CHANS] = sums[:, CHANS : 2 * CHANS]
        VG[pl.ds(vrow + 1, 1), 2 * CHANS : 3 * CHANS] = sum_col(
            GQ[zq, :, 2 * CHANS : 3 * CHANS].astype(F32)
        )
        SL[zq, 0:REACH, :] = GKV[zq, 0:REACH, :].astype(BF)
        SL[zq, REACH : REACH + 80, :] = GKV[zq, KW : KW + 80, :].astype(BF)
        SR[zq, 0:REACH, :] = GKV[zq, KW - REACH : KW, :].astype(BF)
        SR[zq, REACH : REACH + OWNP, :] = GKV[zq, KEYS - OWNP : KEYS, :].astype(BF)
        pl.when(z > 0)(lambda: hl(zq).start())
        pl.when(z < QUARTERS - 1)(lambda: hr(zq).start())
        pl.when(z > 1)(lambda: hll(zq).start())
        stage(reduce1, s == 0, jnp.int32(5))
        reduce2(s + 1)
        stage(reduce3, s == 3, jnp.int32(0))
        stage(reduce_f, s > 0, jnp.where(s == 1, 0, jnp.where(s == 2, 4, 2)))
        return carry

    lax.fori_loop(0, QUARTERS, attend_back, 0)

    half_row = pl.multiple_of(32 * c, 32)
    row_x = pl.multiple_of(half_row + 16 * x, 16)
    row_y = pl.multiple_of(row_x + 8 * y, 8)

    def vrows(at, size):
        return pl.ds(pl.multiple_of(at, 8), size)

    folds = [
        (core, VG.at[vrows(32 - half_row, 32), :], GVR.at[0:32], vrows(half_row, 32)),
        (xdev, VG.at[vrows(half_row + 16 - 16 * x, 16), :], GVR.at[32:48], vrows(row_x, 16)),
        (ydev, VG.at[vrows(row_x + 8 - 8 * y, 8), :], GVR.at[48:56], vrows(row_y, 8)),
    ]

    def fold(i):
        dev, src, dst, keep = folds[i]
        return rcopy(src, dst, gsend.at[i], grecv.at[i], dev)

    def fold_done(i):
        fold(i).wait()
        keep = folds[i][3]
        VG[keep, :] = VG[keep, :] + folds[i][2][...]

    def g_z(s):
        src = VG.at[vrows(row_y, 8), :]
        return rcopy(src, GVZ.at[z], gsend.at[2 + s], grecv.at[2 + s], zdev(s))

    def g_z_in(s):
        dst = GVZ.at[got(s)]
        return rcopy(dst, dst, gsend.at[2 + s], grecv.at[2 + s], core)

    opens = [
        (ydev, vrows(row_y, 8), vrows(row_x + 8 - 8 * y, 8)),
        (xdev, vrows(row_x, 16), vrows(half_row + 16 - 16 * x, 16)),
        (core, vrows(half_row, 32), vrows(32 - half_row, 32)),
    ]

    def unfold(i):
        dev, mine, other = opens[i]
        ref = VO.at[mine, :]
        return rcopy(ref, ref, gsend.at[6 + i], grecv.at[6 + i], dev)

    def unfold_done(i):
        ref = VO.at[opens[i][2], :]
        rcopy(ref, ref, gsend.at[6 + i], grecv.at[6 + i], core).wait_recv()

    def vector_two():
        fold_done(0)
        fold(1).start()

    def vector_three():
        fold_done(1)
        fold(2).start()

    def vector_z():
        fold_done(2)
        for step in (1, 2, 3):
            g_z(step).start()
        GVZ[z] = VG[vrows(row_y, 8), :]

    def vector_back():
        for step in (1, 2, 3):
            g_z_in(step).wait_recv()
        VO[vrows(row_y, 8), :] = GVZ[0] + GVZ[1] + GVZ[2] + GVZ[3]
        unfold(0).start()

    fold(0).start()

    def project_back(s, carry):
        zq = target(s)
        pl.when(z < QUARTERS - 1)(lambda: hl(zq).wait_recv())
        pl.when(z > 0)(lambda: hr(zq).wait_recv())
        pl.when(z < QUARTERS - 2)(lambda: hll(zq).wait_recv())
        near = GKV.at[zq]

        def when(ok, v):
            return jnp.where(ok, v.astype(F32), 0.0)

        has_l, has_r, has_rr = z > 0, z < QUARTERS - 1, z < QUARTERS - 2
        near[REACH : 2 * REACH, :] += when(has_l, HR[zq, 0:REACH, :])
        near[ROWS : ROWS + REACH, :] += when(has_r, HL[zq, 0:REACH, :])
        gp = GKV[zq, KW + OWNP : KW + 2 * OWNP, :] + when(has_l, HR[zq, REACH : REACH + OWNP, :])
        gp = gp + when(has_r, HL[zq, REACH : REACH + OWNP, :])
        nxt = GKV[zq, KW + 2 * OWNP : KW + 2 * OWNP + 1, :]
        nxt = nxt + when(has_r, HL[zq, REACH + OWNP : REACH + OWNP + 16, :])[0:1, :]
        nxt = nxt + when(has_rr, HLL[zq])[0:1, :]
        gp1 = jnp.concatenate([gp[1:, :], nxt], axis=0)
        fills = (
            taps(zq, 2) * gp,
            taps(zq, 3) * gp,
            taps(zq, 4) * gp + taps(zq, 0) * gp1,
            taps(zq, 1) * gp1,
        )
        for k, fill in enumerate(fills):
            for i in range(TILES):
                pt[i, pl.ds(k, OWNP, stride=STRIDE), :] = fill[:, tile(i)]
        back = jnp.concatenate([pt[i] for i in range(TILES)], axis=1)
        alive = base + rows_iota(ROWS, 1) < length
        gkv = GKV[zq, REACH : REACH + ROWS, :] + jnp.where(alive, back, 0.0)
        GQ[zq, :, 0 : 2 * CHANS] = gkv.astype(BF)

        acc[...] += nn(GQ[zq], W[0, zq, 0 : 3 * CHANS, :])
        weight_grad(xT, GQ[zq], W.at[0, zq], 3 * CHANS)

        W[0, zq, :, 3 * CHANS : D] = nn(fT[...], CTX[zq]).astype(BF)
        r_core(8 + s).start()
        stage(reduce2, s == 0, jnp.int32(5))
        stage(reduce3, s > 0, s)
        stage(reduce4, s > 1, s - 2)
        stage(reduce1, s < 3, 8 + s)
        stage(reduce1, s == 1, jnp.int32(7))
        pl.when(s == 0)(vector_two)
        return carry

    lax.fori_loop(0, QUARTERS, project_back, 0)
    outs[1].start()

    def wait_all(ref, sem):
        pltpu.make_async_copy(ref, ref, sem).wait()

    pl.when(z > 0)(lambda: wait_all(SL, hsend.at[0]))
    pl.when(z < QUARTERS - 1)(lambda: wait_all(SR, hsend.at[1]))
    pl.when(z > 1)(lambda: wait_all(HLL, hsend.at[2]))

    def final(m):
        own_part = (11, 7, 6)[m]
        gmats[m] = CR[own_part, block(yx), :].astype(F32)

        def more(slot):
            cut = thin if m == DOWN else wide
            z_wait(m, slot, cut)
            at = gmats.at[m, :, cut[3]]
            at[...] += ZR[m, slot, :, cut[3]].astype(F32)

        pl.when(z > 0)(lambda: more(z))
        pl.when(z < QUARTERS - 1)(lambda: more(QUARTERS))
        outs[2 + m].start()

    def at(r):
        return jnp.int32(r)

    reduce2(at(8))
    vector_three()
    reduce1(at(6))
    reduce3(at(4))
    reduce4(at(2))
    reduce2(at(9))
    reduce1(at(11))
    reduce3(at(5))
    reduce4(at(3))
    reduce2(at(10))
    reduce2(at(7))
    reduce4(at(4))
    reduce3(at(8))
    vector_z()
    reduce4(at(5))
    reduce3(at(9))
    reduce4(at(8))
    reduce2(at(6))
    reduce3(at(10))
    reduce4(at(9))
    vector_back()
    reduce2(at(11))
    reduce4(at(10))
    reduce3(at(7))
    final(1)
    unfold_done(0)
    unfold(1).start()
    reduce3(at(6))
    final(2)
    unfold_done(1)
    unfold(2).start()
    reduce3(at(11))
    final(0)
    unfold_done(2)
    outs[5].start()
    for i in range(3):
        unfold(i).wait_send()
    for s in (1, 2, 3):
        g_z(s).wait_send()

    def sent(r, carry):
        own_part = part(r)[1] == QUARTERS - 1
        pl.when(own_part)(lambda: wait_rows(rsend.at[r], 7 * PIECE))
        pl.when(jnp.logical_not(own_part))(lambda: wait_rows(rsend.at[r], 8 * PIECE))
        return carry

    lax.fori_loop(0, PARTS, sent, 0)
    for cp in outs:
        cp.wait()


def unpack(
    act, gtok, gmats, gvec,
    act_out, gtok_out, gq, gk, gv, gbq, gbv, gck, gcv, go, gbo, gag, gas, gup, gbu, gdown, gbd, gfg, gfs,
):
    act_out[...] = act[...]
    gtok_out[...] = gtok[...]
    gk[...] = gmats[0, :, 0:CHANS]
    gv[...] = gmats[0, :, CHANS : 2 * CHANS]
    gq[...] = gmats[0, :, 2 * CHANS : 3 * CHANS]
    go[...] = gmats[0, :, 3 * CHANS : D].T
    gup[...] = gmats[1]
    gdown[...] = gmats[2]
    for j in range(QUARTERS):
        at = slice(j * CHANS, (j + 1) * CHANS)
        row = 8 * j
        gbu[:, j * D : (j + 1) * D] = gvec[row : row + 1, :]
        gbv[:, at] = gvec[row + 1 : row + 2, CHANS : 2 * CHANS]
        gbq[:, at] = gvec[row + 1 : row + 2, 2 * CHANS : 3 * CHANS]
        for t in range(5):
            gck[t, :, at] = gvec[row + 2 + t : row + 3 + t, 0:CHANS]
            gcv[t, :, at] = gvec[row + 2 + t : row + 3 + t, CHANS : 2 * CHANS]
    for j, out in enumerate((gbo, gag, gas, gbd, gfg, gfs)):
        out[...] = gvec[8 * QUARTERS + j : 8 * QUARTERS + j + 1, :]


def fused_layer(
    tokens, lengths, w_query, w_key, w_value, b_query, b_value, conv_key, conv_value, w_out,
    b_out, attn_gain, attn_shift, w_up, b_up, w_down, b_down, ffn_gain, ffn_shift, cotangent,
):
    Q4 = QUARTERS
    vm = pltpu.VMEM
    dma = pltpu.SemaphoreType.DMA
    scratch = [
        vm((3, Q4, D, D), BF),
        vm((Q4, 8, D), F32),
        vm((TILES, KVROWS, 128), F32),
        vm((Q4, KEYS, 2 * CHANS), BF),
        vm((Q4, COMP, 2 * CHANS), BF),
        vm((Q4, ROWS, CHANS), BF),
        vm((Q4, ROWS, CHANS), BF),
        vm((Q4, QHEADS, 2, NEAR + FAR, QB), F32),
        vm((2, NEAR, QB), F32),
        vm((2, FAR, QB), F32),
        vm((ROWS, D), F32),
        vm((ROWS, 1), F32),
        vm((ROWS, D), F32),
        vm((ROWS, D), BF),
        vm((Q4, ROWS, D), F32),
        vm((Q4, ROWS, D), BF),
        vm((D, ROWS), BF),
        vm((D, ROWS), BF),
        vm((ROWS, D), BF),
        vm((Q4, KEYS, 2 * CHANS), F32),
        vm((TILES, ROWS, 128), F32),
        vm((Q4, ROWS, 3 * CHANS), BF),
        vm((VROWS, D), F32),
        vm((12, D // 2, D), BF),
        vm((12, 4, PIECE, D // 2), BF),
        vm((12, 2, PIECE, D // 2), BF),
        vm((3, Q4 + 1, PIECE, D), BF),
        vm((Q4 + 1, D // 2, D // 3), BF),
        vm((Q4, REACH + 80, 2 * CHANS), BF),
        vm((Q4, REACH + OWNP, 2 * CHANS), BF),
        vm((Q4, 16, 2 * CHANS), BF),
        vm((Q4, REACH + 80, 2 * CHANS), BF),
        vm((Q4, REACH + OWNP, 2 * CHANS), BF),
        vm((VROWS, D), F32),
        vm((Q4, 8, D), F32),
        vm((VROWS, D), F32),
        vm((SEQ, D), BF),
        vm((ROWS, D), BF),
        pltpu.SMEM((1,), jnp.int32),
        vm((1, CHANS), F32),
        vm((1, CHANS), F32),
        vm((5, 1, CHANS), F32),
        vm((5, 1, CHANS), F32),
        vm((1, D), F32),
        vm((1, D), F32),
        vm((1, D), F32),
        vm((1, D), F32),
        vm((1, D), F32),
        vm((1, D), F32),
        vm((1, D), F32),
        vm((ROWS, D), BF),
        vm((ROWS, D), F32),
        vm((3, PIECE, D), F32),
        dma((12,)),
        dma((6,)),
        dma((8,)),
        dma((9,)),
        dma((9, 3)),
        dma((5, 2)),
        dma((5, Q4)),
        dma((5, Q4)),
        dma((3,)),
        dma((3, Q4)),
        dma((12,)),
        dma((12, 3)),
        dma((3, Q4 + 1)),
        dma((Q4 + 1,)),
        dma((9,)),
        dma((9,)),
    ]
    vspec = pl.BlockSpec(memory_space=pltpu.VMEM)
    hspec = pl.BlockSpec(memory_space=pl.ANY)
    packed = pl.pallas_call(
        kernel,
        out_shape=(
            jax.ShapeDtypeStruct((ROWS, D), BF),
            jax.ShapeDtypeStruct((ROWS, D), F32),
            jax.ShapeDtypeStruct((3, PIECE, D), F32),
            jax.ShapeDtypeStruct((VROWS, D), F32),
        ),
        in_specs=[hspec] * 20,
        out_specs=(hspec,) * 4,
        scratch_shapes=scratch,
        compiler_params=pltpu.CompilerParams(
            collective_id=0, has_side_effects=True, vmem_limit_bytes=67043328
        ),
        name="layer",
    )(
        lengths, tokens, w_key[0].T, w_value[0].T, w_query[0].T, w_out[0], w_up[0], w_down[0],
        b_query, b_value, conv_key.transpose(1, 0, 2), conv_value.transpose(1, 0, 2), b_up, b_out, attn_gain, attn_shift, b_down,
        ffn_gain, ffn_shift, cotangent,
    )
    row = (1, D)
    shapes = [
        (ROWS, D), (PIECE, CHANS), (PIECE, CHANS), (PIECE, CHANS), row, row, (5, 1, D), (5, 1, D), (CHANS, PIECE),
        row, row, row, (PIECE, D), (1, FF), (PIECE, D), row, row, row,
    ]
    outs = pl.pallas_call(
        unpack,
        out_shape=[jax.ShapeDtypeStruct((ROWS, D), BF)] + [jax.ShapeDtypeStruct(v, F32) for v in shapes],
        in_specs=[vspec] * 4,
        out_specs=[vspec] * 19,
        name="unpack",
    )(*packed)
    act, gtok, gq, gk, gv, gbq, gbv, gck, gcv, go, gbo, gag, gas, gup, gbu, gdown, gbd, gfg, gfs = outs
    return (
        act, gtok, gq[None], gk[None], gv[None], gbq, gbv, gck.transpose(1, 0, 2), gcv.transpose(1, 0, 2), go[None], gbo, gag, gas,
        gup[None], gbu, gdown.T[None], gbd, gfg, gfs,
    )


def solution(mesh):
    small = mesh.shape["dp"] == 8 and mesh.shape["mp"] == QUARTERS
    return jax.shard_map(
        fused_layer if small else on_device,
        mesh=mesh,
        in_specs=(
            P("dp", None),
            P("dp"),
            P(None, None, "mp"),
            P(None, None, "mp"),
            P(None, None, "mp"),
            P(None, "mp"),
            P(None, "mp"),
            P(None, None, "mp"),
            P(None, None, "mp"),
            P(None, "mp", None),
            P(),
            P(),
            P(),
            P(None, None, "mp"),
            P(None, "mp"),
            P(None, "mp", None),
            P(),
            P(),
            P(),
            P(("dp", "mp"), None),
        ),
        out_specs=(
            P(("dp", "mp"), None),
            P(("dp", "mp"), None),
            P(None, "dp", "mp"),
            P(None, "dp", "mp"),
            P(None, "dp", "mp"),
            P(),
            P(),
            P(),
            P(),
            P(None, "mp", "dp"),
            P(),
            P(),
            P(),
            P(None, "dp", "mp"),
            P(),
            P(None, "mp", "dp"),
            P(),
            P(),
            P(),
        ),
        check_vma=False,
    )
```

```python
import jax
import jax.numpy as jnp
from jax import lax
from jax.experimental import pallas as pl
from jax.experimental.pallas import tpu as pltpu
from jax.sharding import PartitionSpec as P

D = 768
HEAD_DIM = 64
FF = 3072
WINDOW = 128
POOL_WINDOW = 512
STRIDE = 4
LAYERS = 1


block_rows = 512
mask_fill = -1000000000.0
epsilon = 1e-05


def norm_rows(hidden, gain, shift):
    center = hidden - jnp.mean(hidden, axis=-1, keepdims=True)
    spread = jnp.mean(center * center, axis=-1, keepdims=True)
    return center * lax.rsqrt(spread + epsilon) * gain + shift


def gelu_exact(values):
    return jax.nn.gelu(values, approximate=False)


def pool_rows(values, kernel):
    seqs, length, chans = values.shape
    width = kernel.shape[0]
    half = width // 2
    pooled_len = length // STRIDE
    padded = jnp.pad(values, ((0, 0), (half, width), (0, 0)))
    total = jnp.zeros((seqs, pooled_len, chans), jnp.float32)
    for offset in range(width):
        total = total + kernel[offset] * padded[:, offset : offset + STRIDE * pooled_len : STRIDE]
    return total


def block_mask(start, lengths):
    reach = WINDOW // 2
    pool_reach = POOL_WINDOW // 2 // STRIDE
    span = block_rows // STRIDE + 2 * pool_reach
    rows = start + jnp.arange(block_rows, dtype=jnp.int32)
    near_pos = start - reach + jnp.arange(block_rows + 2 * reach, dtype=jnp.int32)
    far_pos = (start // STRIDE - pool_reach + jnp.arange(span, dtype=jnp.int32)) * STRIDE
    limit = lengths[:, None, None]
    near_ok = (
        (jnp.abs(rows[:, None] - near_pos[None, :]) <= reach)[None]
        & (near_pos >= 0)[None, None]
        & (near_pos[None, None] < limit)
    )
    far_ok = (
        (jnp.abs(rows[:, None] - far_pos[None, :]) <= POOL_WINDOW // 2)[None]
        & (far_pos >= 0)[None, None]
        & (far_pos[None, None] < limit)
    )
    return jnp.concatenate([near_ok, far_ok], axis=-1)


def padded_keys(keys_loc, vals_loc, far_keys, far_vals):
    reach = WINDOW // 2
    pool_reach = POOL_WINDOW // 2 // STRIDE
    pad_near = ((0, 0), (reach, reach), (0, 0), (0, 0))
    pad_far = ((0, 0), (pool_reach, pool_reach), (0, 0), (0, 0))
    return (
        jnp.pad(keys_loc, pad_near),
        jnp.pad(vals_loc, pad_near),
        jnp.pad(far_keys, pad_far),
        jnp.pad(far_vals, pad_far),
    )


def block_inputs(start, queries, padded):
    near_k, near_v, far_k, far_v = padded
    near_len = block_rows + 2 * (WINDOW // 2)
    span = block_rows // STRIDE + 2 * (POOL_WINDOW // 2 // STRIDE)
    pool_start = start // STRIDE
    q_rows = queries[:, start : start + block_rows]
    keys_b = jnp.concatenate(
        [near_k[:, start : start + near_len], far_k[:, pool_start : pool_start + span]], axis=1
    )
    vals_b = jnp.concatenate(
        [near_v[:, start : start + near_len], far_v[:, pool_start : pool_start + span]], axis=1
    )
    return (q_rows, keys_b, vals_b)


def forward_block(q_rows, keys_b, vals_b, mask, live):
    scale = q_rows.shape[-1] ** (-0.5)
    scores = (
        jnp.einsum("sqhe,skhe->shqk", q_rows, keys_b, preferred_element_type=jnp.float32) * scale
    )
    scores = jnp.where(mask[:, None], scores, mask_fill)
    peak = jnp.max(scores, axis=-1, keepdims=True)
    expo = jnp.exp(scores - peak)
    total = jnp.sum(expo, axis=-1, keepdims=True)
    weights = (expo / total).astype(jnp.bfloat16)
    result = jnp.einsum("shqk,skhe->sqhe", weights, vals_b, preferred_element_type=jnp.float32)
    result = jnp.where(live[:, :, None, None], result, 0.0)
    return (result, peak + jnp.log(total))


def forward_skip(q_rows, keys_b, vals_b, mask, live):
    seqs, rows, heads, size = q_rows.shape
    return (
        jnp.zeros((seqs, rows, heads, size), jnp.float32),
        jnp.zeros((seqs, heads, rows, 1), jnp.float32),
    )


def backward_block(q_rows, keys_b, vals_b, mask, logsum, grad_rows):
    scale = q_rows.shape[-1] ** (-0.5)
    scores = (
        jnp.einsum("sqhe,skhe->shqk", q_rows, keys_b, preferred_element_type=jnp.float32) * scale
    )
    scores = jnp.where(mask[:, None], scores, mask_fill)
    probs = jnp.exp(scores - logsum)
    grad_probs = jnp.einsum(
        "sqhe,skhe->shqk", grad_rows, vals_b, preferred_element_type=jnp.float32
    )
    delta = jnp.sum(probs * grad_probs, axis=-1, keepdims=True)
    grad_scores = (probs * (grad_probs - delta)).astype(jnp.bfloat16)
    grad_q = (
        jnp.einsum("shqk,skhe->sqhe", grad_scores, keys_b, preferred_element_type=jnp.float32)
        * scale
    )
    grad_keys = (
        jnp.einsum("shqk,sqhe->skhe", grad_scores, q_rows, preferred_element_type=jnp.float32)
        * scale
    )
    grad_vals = jnp.einsum(
        "shqk,sqhe->skhe", probs.astype(jnp.bfloat16), grad_rows, preferred_element_type=jnp.float32
    )
    return (grad_q, grad_keys, grad_vals)


def backward_skip(q_rows, keys_b, vals_b, mask, logsum, grad_rows):
    return (
        jnp.zeros(q_rows.shape, jnp.float32),
        jnp.zeros(keys_b.shape, jnp.float32),
        jnp.zeros(vals_b.shape, jnp.float32),
    )


def attend_forward(queries, keys_loc, vals_loc, far_keys, far_vals, lengths):
    length = queries.shape[1]
    padded = padded_keys(keys_loc, vals_loc, far_keys, far_vals)
    longest = jnp.max(lengths)
    results, logsums = ([], [])
    for block in range(length // block_rows):
        start = block * block_rows
        q_rows, keys_b, vals_b = block_inputs(start, queries, padded)
        mask = block_mask(start, lengths)
        live = start + jnp.arange(block_rows, dtype=jnp.int32)[None, :] < lengths[:, None]
        result, logsum = lax.cond(
            start < longest, forward_block, forward_skip, q_rows, keys_b, vals_b, mask, live
        )
        results.append(result)
        logsums.append(logsum)
    return (jnp.concatenate(results, axis=1), logsums)


def attend_backward(
    queries, keys_loc, vals_loc, far_keys, far_vals, lengths, logsums, grad_context
):
    seqs, length, heads, size = queries.shape
    pooled_len = far_keys.shape[1]
    reach = WINDOW // 2
    pool_reach = POOL_WINDOW // 2 // STRIDE
    near_len = block_rows + 2 * reach
    span = block_rows // STRIDE + 2 * pool_reach
    padded = padded_keys(keys_loc, vals_loc, far_keys, far_vals)
    longest = jnp.max(lengths)
    grad_near_k = jnp.zeros((seqs, length + 2 * reach, heads, size), jnp.float32)
    grad_near_v = jnp.zeros((seqs, length + 2 * reach, heads, size), jnp.float32)
    grad_far_k = jnp.zeros((seqs, pooled_len + 2 * pool_reach, heads, size), jnp.float32)
    grad_far_v = jnp.zeros((seqs, pooled_len + 2 * pool_reach, heads, size), jnp.float32)
    grad_queries = []
    for block in range(length // block_rows):
        start = block * block_rows
        pool_start = start // STRIDE
        q_rows, keys_b, vals_b = block_inputs(start, queries, padded)
        mask = block_mask(start, lengths)
        grad_rows = grad_context[:, start : start + block_rows]
        grad_q, grad_keys, grad_vals = lax.cond(
            start < longest,
            backward_block,
            backward_skip,
            q_rows,
            keys_b,
            vals_b,
            mask,
            logsums[block],
            grad_rows,
        )
        grad_queries.append(grad_q)
        grad_near_k = grad_near_k.at[:, start : start + near_len].add(grad_keys[:, :near_len])
        grad_near_v = grad_near_v.at[:, start : start + near_len].add(grad_vals[:, :near_len])
        grad_far_k = grad_far_k.at[:, pool_start : pool_start + span].add(grad_keys[:, near_len:])
        grad_far_v = grad_far_v.at[:, pool_start : pool_start + span].add(grad_vals[:, near_len:])
    return (
        jnp.concatenate(grad_queries, axis=1),
        grad_near_k[:, reach : reach + length],
        grad_near_v[:, reach : reach + length],
        grad_far_k[:, pool_reach : pool_reach + pooled_len],
        grad_far_v[:, pool_reach : pool_reach + pooled_len],
    )


def row_sum(left, right, share):

    def term(start, count):
        return jnp.dot(left, right, preferred_element_type=jnp.float32)

    return lax.psum_scatter(
        term(jnp.int32(0), share * lax.axis_size("mp")), "mp", scatter_dimension=0, tiled=True
    )


def share_rows(values):
    return lax.all_gather(values, "mp", axis=0, tiled=True)


def share_back(values):
    return lax.all_gather(values, "mp", axis=0, tiled=True)


def back_sum(term, share):
    return lax.psum_scatter(
        term(jnp.int32(0), share * lax.axis_size("mp")), "mp", scatter_dimension=0, tiled=True
    )


def spread(values, width):
    whole = jnp.zeros(values.shape[:-1] + (width,), jnp.float32)
    start = lax.axis_index("mp") * values.shape[-1]
    return lax.dynamic_update_slice_in_dim(whole, values, start, values.ndim - 1)


def layer_forward(full_in, resid, lengths, params, share):
    (
        w_query,
        w_key,
        w_value,
        b_query,
        b_value,
        conv_key,
        conv_value,
        w_out,
        b_out,
        attn_gain,
        attn_shift,
        w_up,
        b_up,
        w_down,
        b_down,
        ffn_gain,
        ffn_shift,
    ) = params
    seqs = lengths.shape[0]
    total_rows = full_in.shape[0]
    length = total_rows // seqs
    chans = w_query.shape[1]
    heads = chans // HEAD_DIM
    pooled_len = length // STRIDE
    queries = (jnp.dot(full_in, w_query, preferred_element_type=jnp.float32) + b_query).astype(
        jnp.bfloat16
    )
    keys_loc = jnp.dot(full_in, w_key, preferred_element_type=jnp.float32).astype(jnp.bfloat16)
    vals_loc = (jnp.dot(full_in, w_value, preferred_element_type=jnp.float32) + b_value).astype(
        jnp.bfloat16
    )
    valid = (jnp.arange(length, dtype=jnp.int32)[None, :] < lengths[:, None]).astype(jnp.float32)[
        :, :, None
    ]
    far_keys = pool_rows(
        keys_loc.reshape(seqs, length, chans).astype(jnp.float32) * valid, conv_key
    ).astype(jnp.bfloat16)
    far_vals = pool_rows(
        vals_loc.reshape(seqs, length, chans).astype(jnp.float32) * valid, conv_value
    ).astype(jnp.bfloat16)
    context, logsums = attend_forward(
        queries.reshape(seqs, length, heads, HEAD_DIM),
        keys_loc.reshape(seqs, length, heads, HEAD_DIM),
        vals_loc.reshape(seqs, length, heads, HEAD_DIM),
        far_keys.reshape(seqs, pooled_len, heads, HEAD_DIM),
        far_vals.reshape(seqs, pooled_len, heads, HEAD_DIM),
        lengths,
    )
    context = context.reshape(total_rows, chans).astype(jnp.bfloat16)
    hidden_one = resid + (row_sum(context, w_out, share) + b_out)
    normed = norm_rows(hidden_one, attn_gain, attn_shift)
    full_normed = share_rows(normed.astype(jnp.bfloat16))
    upper = jnp.dot(full_normed, w_up, preferred_element_type=jnp.float32) + b_up
    active = gelu_exact(upper).astype(jnp.bfloat16)
    hidden_two = normed + (row_sum(active, w_down, share) + b_down)
    result = norm_rows(hidden_two, ffn_gain, ffn_shift)
    kept = (
        full_in,
        queries,
        keys_loc,
        vals_loc,
        far_keys,
        far_vals,
        logsums,
        context,
        hidden_one,
        full_normed,
        upper,
        active,
        hidden_two,
    )
    return (result, kept)


def layer_backward(grad_out, kept, params, lengths, share):
    (
        w_query,
        w_key,
        w_value,
        b_query,
        b_value,
        conv_key,
        conv_value,
        w_out,
        b_out,
        attn_gain,
        attn_shift,
        w_up,
        b_up,
        w_down,
        b_down,
        ffn_gain,
        ffn_shift,
    ) = params
    (
        full_in,
        queries,
        keys_loc,
        vals_loc,
        far_keys,
        far_vals,
        logsums,
        context,
        hidden_one,
        full_normed,
        saved_upper,
        active,
        hidden_two,
    ) = kept
    seqs = lengths.shape[0]
    total_rows = full_in.shape[0]
    length = total_rows // seqs
    chans = w_query.shape[1]
    heads = chans // HEAD_DIM
    pooled_len = length // STRIDE
    unused_two, pull_two = jax.vjp(norm_rows, hidden_two, ffn_gain, ffn_shift)
    grad_h2, grad_fgain, grad_fshift = pull_two(grad_out)
    grad_ffn = grad_h2.astype(jnp.bfloat16)
    grad_bdown = jnp.sum(grad_ffn.astype(jnp.float32), axis=0)
    full_gffn = share_back(grad_ffn)
    grad_wdown = jnp.einsum("tf,td->fd", active, full_gffn, preferred_element_type=jnp.float32)
    grad_active = jnp.einsum("td,fd->tf", full_gffn, w_down, preferred_element_type=jnp.float32)
    unused_gelu, pull_gelu = jax.vjp(gelu_exact, saved_upper)
    grad_upper = pull_gelu(grad_active)[0].astype(jnp.bfloat16)
    grad_bup = jnp.sum(grad_upper.astype(jnp.float32), axis=0)
    grad_wup = jnp.einsum("td,tf->df", full_normed, grad_upper, preferred_element_type=jnp.float32)

    def up_term(start, count):
        return jnp.einsum("tf,df->td", grad_upper, w_up, preferred_element_type=jnp.float32)

    grad_y1 = grad_h2 + back_sum(up_term, share)
    unused_one, pull_one = jax.vjp(norm_rows, hidden_one, attn_gain, attn_shift)
    grad_h1, grad_again, grad_ashift = pull_one(grad_y1)
    grad_attn = grad_h1.astype(jnp.bfloat16)
    grad_bout = jnp.sum(grad_attn.astype(jnp.float32), axis=0)
    full_gattn = share_back(grad_attn)
    grad_wout = jnp.einsum("tc,td->cd", context, full_gattn, preferred_element_type=jnp.float32)
    grad_context = jnp.einsum("td,cd->tc", full_gattn, w_out, preferred_element_type=jnp.float32)
    valid = (jnp.arange(length, dtype=jnp.int32)[None, :] < lengths[:, None]).astype(jnp.float32)[
        :, :, None
    ]
    grad_context = (grad_context.reshape(seqs, length, chans) * valid).astype(jnp.bfloat16)
    grad_q, grad_near_k, grad_near_v, grad_far_k, grad_far_v = attend_backward(
        queries.reshape(seqs, length, heads, HEAD_DIM),
        keys_loc.reshape(seqs, length, heads, HEAD_DIM),
        vals_loc.reshape(seqs, length, heads, HEAD_DIM),
        far_keys.reshape(seqs, pooled_len, heads, HEAD_DIM),
        far_vals.reshape(seqs, pooled_len, heads, HEAD_DIM),
        lengths,
        logsums,
        grad_context.reshape(seqs, length, heads, HEAD_DIM),
    )
    masked_keys = keys_loc.reshape(seqs, length, chans).astype(jnp.float32) * valid
    masked_vals = vals_loc.reshape(seqs, length, chans).astype(jnp.float32) * valid
    unused_pk, pull_key = jax.vjp(pool_rows, masked_keys, conv_key)
    grad_kpool, grad_ckey = pull_key(grad_far_k.reshape(seqs, pooled_len, chans))
    unused_pv, pull_val = jax.vjp(pool_rows, masked_vals, conv_value)
    grad_vpool, grad_cval = pull_val(grad_far_v.reshape(seqs, pooled_len, chans))
    grad_queries = grad_q.reshape(total_rows, chans).astype(jnp.bfloat16)
    grad_keys = (
        (grad_near_k.reshape(seqs, length, chans) + grad_kpool * valid)
        .reshape(total_rows, chans)
        .astype(jnp.bfloat16)
    )
    grad_vals = (
        (grad_near_v.reshape(seqs, length, chans) + grad_vpool * valid)
        .reshape(total_rows, chans)
        .astype(jnp.bfloat16)
    )
    grad_wquery = jnp.einsum("td,tc->dc", full_in, grad_queries, preferred_element_type=jnp.float32)
    grad_wkey = jnp.einsum("td,tc->dc", full_in, grad_keys, preferred_element_type=jnp.float32)
    grad_wvalue = jnp.einsum("td,tc->dc", full_in, grad_vals, preferred_element_type=jnp.float32)
    grad_bquery = jnp.sum(grad_queries.astype(jnp.float32), axis=0)
    grad_bvalue = jnp.sum(grad_vals.astype(jnp.float32), axis=0)

    def input_term(start, count):
        total = jnp.einsum("tc,dc->td", grad_queries, w_query, preferred_element_type=jnp.float32)
        total = total + jnp.einsum(
            "tc,dc->td", grad_keys, w_key, preferred_element_type=jnp.float32
        )
        return total + jnp.einsum(
            "tc,dc->td", grad_vals, w_value, preferred_element_type=jnp.float32
        )

    grad_input = grad_h1 + back_sum(input_term, share)
    matrices = (
        grad_wquery[None],
        grad_wkey[None],
        grad_wvalue[None],
        grad_wout[None],
        grad_wup[None],
        grad_wdown[None],
    )
    vectors = (
        spread(grad_bquery, D)[None],
        spread(grad_bvalue, D)[None],
        spread(grad_ckey, D)[None],
        spread(grad_cval, D)[None],
        grad_bout[None],
        grad_again[None],
        grad_ashift[None],
        spread(grad_bup, FF)[None],
        grad_bdown[None],
        grad_fgain[None],
        grad_fshift[None],
    )
    return (grad_input, matrices, vectors)


def on_device(
    tokens,
    lengths,
    w_query,
    w_key,
    w_value,
    b_query,
    b_value,
    conv_key,
    conv_value,
    w_out,
    b_out,
    attn_gain,
    attn_shift,
    w_up,
    b_up,
    w_down,
    b_down,
    ffn_gain,
    ffn_shift,
    cotangent,
):
    stacks = (
        w_query,
        w_key,
        w_value,
        b_query,
        b_value,
        conv_key,
        conv_value,
        w_out,
        b_out,
        attn_gain,
        attn_shift,
        w_up,
        b_up,
        w_down,
        b_down,
        ffn_gain,
        ffn_shift,
    )
    total_rows = tokens.shape[0]
    share = total_rows // lax.axis_size("mp")
    place = lax.axis_index("mp") * share
    resid = lax.dynamic_slice_in_dim(tokens, place, share, 0).astype(jnp.float32)
    layer = 0
    params = tuple((stack[layer] for stack in stacks))
    result, kept = layer_forward(tokens, resid, lengths, params, share)
    kept_all = [kept]
    activations = result.astype(jnp.bfloat16)
    grad_out = cotangent.astype(jnp.float32)
    matrix_list = [None] * LAYERS
    vector_list = [None] * LAYERS
    for layer in reversed(range(LAYERS)):
        params = tuple((stack[layer] for stack in stacks))
        grad_out, matrices, vectors = layer_backward(
            grad_out, kept_all[layer], params, lengths, share
        )
        matrix_list[layer] = matrices
        vector_list[layer] = vectors
    grad_wquery, grad_wkey, grad_wvalue, grad_wout, grad_wup, grad_wdown = tuple(
        (jnp.concatenate([entry[index] for entry in matrix_list], axis=0) for index in range(6))
    )
    (
        grad_bquery,
        grad_bvalue,
        grad_ckey,
        grad_cval,
        grad_bout,
        grad_again,
        grad_ashift,
        grad_bup,
        grad_bdown,
        grad_fgain,
        grad_fshift,
    ) = tuple(
        (jnp.concatenate([entry[index] for entry in vector_list], axis=0) for index in range(11))
    )
    grad_wquery, grad_wkey, grad_wvalue, grad_wout, grad_wup, grad_wdown = (
        lax.psum_scatter(grad_wquery, "dp", scatter_dimension=1, tiled=True),
        lax.psum_scatter(grad_wkey, "dp", scatter_dimension=1, tiled=True),
        lax.psum_scatter(grad_wvalue, "dp", scatter_dimension=1, tiled=True),
        lax.psum_scatter(grad_wout, "dp", scatter_dimension=2, tiled=True),
        lax.psum_scatter(grad_wup, "dp", scatter_dimension=1, tiled=True),
        lax.psum_scatter(grad_wdown, "dp", scatter_dimension=2, tiled=True),
    )
    (
        grad_bquery,
        grad_bvalue,
        grad_ckey,
        grad_cval,
        grad_bout,
        grad_again,
        grad_ashift,
        grad_bup,
        grad_bdown,
        grad_fgain,
        grad_fshift,
    ) = lax.psum(
        (
            grad_bquery,
            grad_bvalue,
            grad_ckey,
            grad_cval,
            grad_bout,
            grad_again,
            grad_ashift,
            grad_bup,
            grad_bdown,
            grad_fgain,
            grad_fshift,
        ),
        ("dp", "mp"),
    )
    return (
        activations,
        grad_out,
        grad_wquery,
        grad_wkey,
        grad_wvalue,
        grad_bquery,
        grad_bvalue,
        grad_ckey,
        grad_cval,
        grad_wout,
        grad_bout,
        grad_again,
        grad_ashift,
        grad_wup,
        grad_bup,
        grad_wdown,
        grad_bdown,
        grad_fgain,
        grad_fshift,
    )


BF = jnp.bfloat16
F32 = jnp.float32
MESH = pl.DeviceIdType.MESH
ROWS = 256
QUARTERS = 4
CHANS = D // QUARTERS
QHEADS = CHANS // HEAD_DIM
SEQ = QUARTERS * ROWS
REACH = WINDOW // 2
PREACH = POOL_WINDOW // 2 // STRIDE
OWNP = ROWS // STRIDE
KW = ROWS + 2 * REACH
KP = OWNP + 2 * PREACH
KEYS = KW + KP
QB = 128
NEAR = QB + 2 * REACH
FAR = QB // STRIDE + 2 * PREACH
COMP = 800
HALFC = COMP // 2
FRONT = 256
KVROWS = 1408
BASE = 288
PIECE = D // 8
BIG_NEG = -1e30
SCALE = HEAD_DIM ** -0.5
VROWS = 64
TILES = 2 * CHANS // 128


def nn(a, b):
    return jnp.dot(a, b, preferred_element_type=F32)


def nt(a, b):
    return lax.dot_general(a, b, (((1,), (1,)), ((), ())), preferred_element_type=F32)


def tn(a, b):
    return lax.dot_general(a, b, (((0,), (0,)), ((), ())), preferred_element_type=F32)


def rows_iota(rows, cols):
    return lax.broadcasted_iota(jnp.int32, (rows, cols), 0)


def cols_iota(rows, cols):
    return lax.broadcasted_iota(jnp.int32, (rows, cols), 1)


def mean_row(v):
    return jnp.mean(v, axis=-1, keepdims=True)


def sum_col(v):
    return jnp.sum(v, axis=0, keepdims=True)


def kernel(
    len_hbm, tok_hbm, wk, wv, wq, wo, wup, wdown, bq_h, bv_h, ck_h, cv_h, bup_h, bo_h, ag_h, ash_h, bd_h, fg_h, fs_h, cot_hbm,
    act_hbm, gtok_hbm, gmats_hbm, gvec_hbm,
    W, VEC, kvf, KV, KVS, Q, CTX, P, maskn, maskf, n1, r1, y1, y1b, dg, av,
    yT, fT, gab, GKV, pt, GQ, VG,
    CR, S1, S2, ZR, ZF, HL, HR, HLL, SL, SR, GVR, GVZ, VO, tok, cot,
    len_ref, bq, bv, ck, cv, bup, bo, ag, ash, bd, fg, fs, act_out, gtok, gmats,
    ssem, osem, lsem, asend, arecv, zsend, zrecv, lsend, hsend, hrecv, rsend, rrecv, zsum, zfsum, gsend, grecv,
):
    acc, n2, xT, gub = gtok, y1, yT, y1b
    dp = lax.axis_index("dp")
    z = lax.axis_index("mp")
    c = lax.rem(dp, 2)
    x = lax.rem(lax.div(dp, 2), 2)
    y = lax.div(dp, 4)
    core = (dp + 1 - 2 * c, z)
    xdev = (dp + 2 - 4 * x, z)
    ydev = (dp + 4 - 8 * y, z)
    yx = 2 * y + x

    def zdev(step):
        return (dp, lax.rem(z + step, QUARTERS))

    def rcopy(src, dst, ssem, rsem, dev):
        return pltpu.make_async_remote_copy(
            src_ref=src, dst_ref=dst, send_sem=ssem, recv_sem=rsem,
            device_id=dev, device_id_type=MESH,
        )

    barrier = pltpu.get_barrier_semaphore()
    for dev in (core, xdev, ydev, zdev(1), zdev(2), zdev(3)):
        pl.semaphore_signal(barrier, inc=1, device_id=dev, device_id_type=MESH)

    def loads():
        parts = [(wk, 0), (wv, CHANS), (wq, 2 * CHANS), (wo, 3 * CHANS)]
        copies = [
            pltpu.make_async_copy(src, W.at[0, z, at : at + CHANS, :], lsem.at[i])
            for i, (src, at) in enumerate(parts)
        ]
        copies.append(pltpu.make_async_copy(wup, W.at[1, z], lsem.at[4]))
        copies.append(pltpu.make_async_copy(wdown, W.at[2, z], lsem.at[5]))
        return copies

    small = [
        pltpu.make_async_copy(src, dst, ssem.at[i])
        for i, (src, dst) in enumerate(
            (
                (bup_h, bup), (bv_h, bv), (bq_h, bq), (ck_h, ck), (cv_h, cv), (len_hbm, len_ref),
                (bo_h, bo), (ag_h, ag), (ash_h, ash), (bd_h, bd), (fg_h, fg), (fs_h, fs),
            )
        )
    ]
    outs = [
        pltpu.make_async_copy(src, dst, osem.at[i])
        for i, (src, dst) in enumerate(
            (
                (act_out, act_hbm), (gtok, gtok_hbm), (gmats.at[0], gmats_hbm.at[0]),
                (gmats.at[1], gmats_hbm.at[1]), (gmats.at[2], gmats_hbm.at[2]), (VO, gvec_hbm),
            )
        )
    ]
    for cp in small[:6]:
        cp.start()
    own = loads()
    tok_in = pltpu.make_async_copy(tok_hbm, tok, lsem.at[6])
    cot_in = pltpu.make_async_copy(cot_hbm, cot, lsem.at[7])
    for cp in own:
        cp.start()
    tok_in.start()
    for cp in small[6:]:
        cp.start()
    cot_in.start()
    for cp in small[:6]:
        cp.wait()
    length = len_ref[0]
    vpack = VG.at[0:8, :]
    vpack[...] = jnp.zeros_like(vpack)
    vpack[0:1, :] = bup[...]
    vpack[1:2, CHANS : 2 * CHANS] = bv[...]
    vpack[1:2, 2 * CHANS : 3 * CHANS] = bq[...]
    for t in range(5):
        vpack[2 + t : 3 + t, 0:CHANS] = ck[t]
        vpack[2 + t : 3 + t, CHANS : 2 * CHANS] = cv[t]
    VEC[z] = vpack[...]
    pl.semaphore_wait(barrier, 6)

    def block(j):
        return pl.ds(pl.multiple_of(j * PIECE, PIECE), PIECE)

    piece_me = c * 4 + yx
    piece_x = c * 4 + 2 * y + 1 - x
    piece_y = c * 4 + 2 * (1 - y) + x
    piece_d = c * 4 + 2 * (1 - y) + 1 - x
    LO, HI = pl.ds(0, D // 2), pl.ds(D // 2, D // 2)
    ALL = pl.ds(0, D)
    CHUNKS = 9
    ends = [(0, 1), (1, 1), (0, 2), (1, 2), (0, 3), (2, 1), (2, 2), (1, 3), (2, 3)]
    inner = [(0, 1), (0, 2), (1, 1), (1, 2), (0, 3), (2, 1), (2, 2), (1, 3), (2, 3)]
    sources = [(1, 2, 3), (2, 0, 3), (1, 3, 0), (2, 1, 0)]
    targets = [(3, 2, 1, 0), (3, 0, 2, 1), (0, 3, 1, 2), (0, 1, 2, 3)]
    DOWN = 2
    FAR_STEPS = 2
    at_end = (z == 0) | (z == QUARTERS - 1)

    def table(values, bits=2):
        word = sum(v << (bits * i) for i, v in enumerate(values))
        return jnp.int32(word - (1 << 32) if word >> 31 else word)

    def lookup(word, i, bits=2):
        return lax.bitwise_and(lax.shift_right_logical(word, bits * i), (1 << bits) - 1)

    def by_place(a, b):
        return lax.select(at_end, a, b)

    mats_of = by_place(table(m for m, d in ends), table(m for m, d in inner))
    dist_of = by_place(table(d for m, d in ends), table(d for m, d in inner))
    looks_of = by_place(table((1, 2, 4, 5, 6, 7, 8, 9), 4), table((2, 4, 5, 7, 8, 9, 9, 9), 4))
    sends_of = by_place(table((1, 2, 4, 5, 6, 7, 8, 9), 4), table((2, 3, 4, 5, 6, 7, 8, 9), 4))

    def source(d):
        return lookup(table(v for row in sources for v in row), 3 * z + d - 1)

    def target(t):
        return lookup(table(v for row in targets for v in row), 4 * z + t)

    def chunk(k):
        return lookup(mats_of, k), source(lookup(dist_of, k))

    def is_far(k):
        return (lookup(mats_of, k) == DOWN) & (lookup(dist_of, k) < FAR_STEPS)

    def own_block(m, up, piece, sem):
        src = W.at[m, z, block(piece), :]
        return rcopy(src, src, zsend.at[sem, up], zrecv.at[sem, z], (dp, z + 2 * up - 1))

    def own_z(m, up):
        return own_block(m, up, piece_me, m)

    def far_z(up):
        return own_block(DOWN, up, piece_d, 4)

    def wants_far(up):
        to = z + 2 * up - 1
        inner_to = (to == 1) | (to == 2)
        return jnp.logical_not(inner_to) | (z == 3 - to)

    def relay(m, src, dev):
        ref = W.at[m, src, block(piece_me), :]
        return rcopy(ref, ref, lsend.at[m, src], zrecv.at[m, src], dev)

    def relay_far(src, dev):
        ref = W.at[DOWN, src, block(piece_d), :]
        return rcopy(ref, ref, lsend.at[4, src], zrecv.at[4, src], dev)

    def own_vec(up):
        src = VEC.at[z]
        return rcopy(src, src, zsend.at[3, up], zrecv.at[3, z], (dp, z + 2 * up - 1))

    def relay_vec(src, dev):
        ref = VEC.at[src]
        return rcopy(ref, ref, lsend.at[3, src], zrecv.at[3, src], dev)

    def onward(src):
        return jnp.where(src > z, z > 0, z < QUARTERS - 1)

    def next_dev(src):
        return (dp, jnp.where(src > z, z - 1, z + 1))

    def plane(k, which, piece, cols, dev):
        m, src = chunk(k)
        ref = W.at[m, src, block(piece), cols]
        return rcopy(ref, ref, asend.at[k], arecv.at[k, (which - 1) // 2], dev)

    def look(k):
        m, src = chunk(k)

        @pl.when(m == 0)
        def _():
            relay_vec(src, core).wait_recv()
            pl.when(onward(src))(lambda: relay_vec(src, next_dev(src)).start())

        relay(m, src, core).wait_recv()
        pl.when(onward(src))(lambda: relay(m, src, next_dev(src)).start())

        @pl.when(is_far(k))
        def _():
            relay_far(src, core).wait_recv()

        pl.when(at_end)(lambda: first(k))

    LAST_CHUNK = CHUNKS - 1

    def cross_piece(k, piece):
        m, src = chunk(k)
        ref = W.at[m, src, block(piece), :]
        return rcopy(ref, ref, asend.at[k], arecv.at[k, 2], core)

    def first(k):
        plane(k, 1, piece_me, ALL, xdev).start()
        plane(k, 2, piece_me, ALL, ydev).start()
        pl.when(k == LAST_CHUNK)(lambda: cross_piece(k, piece_me).start())

    def rows_of(count):
        return W.at[0, 0, 0:count, :]

    def wait_rows(sem, count):
        pltpu.make_async_copy(rows_of(count), rows_of(count), sem).wait()

    def second(k):
        wait_rows(arecv.at[k, 0], 2 * PIECE)

        @pl.when(jnp.logical_not(is_far(k)))
        def _():
            plane(k, 3, piece_x, LO, ydev).start()
            plane(k, 4, piece_y, HI, xdev).start()

        @pl.when(k == LAST_CHUNK)
        def _():
            cross_piece(k, piece_x).start()
            cross_piece(k, piece_y).start()

    def half(j):
        return pl.ds(pl.multiple_of(j * (D // 2), D // 2), D // 2)

    def cross(k, j):
        m, src = chunk(k)
        ref = W.at[m, src, half(j), :]
        return rcopy(ref, ref, asend.at[k], arecv.at[k, 2], core)

    def third(k):
        pl.when(jnp.logical_not(is_far(k)))(lambda: wait_rows(arecv.at[k, 1], PIECE))
        pl.when(k < LAST_CHUNK)(lambda: cross(k, c).start())
        pl.when(k == LAST_CHUNK)(lambda: cross_piece(k, piece_d).start())

    def fourth(k):
        cross(k, 1 - c).wait_recv()

    def looks(i):
        return jnp.where(i < 0, 0, lookup(looks_of, lax.clamp(0, i, 7), 4))

    def sends(i):
        return jnp.where(i < 0, 0, lookup(sends_of, lax.clamp(0, i, 7), 4))

    def each(fn):
        def body(k, carry):
            fn(k)
            return carry

        return body

    def gather_slot(i, carry):
        lax.fori_loop(looks(i - 1), looks(i), each(look), 0)
        pl.when((i == 2) & jnp.logical_not(at_end))(lambda: both(own_down))
        lo = jnp.where(at_end, sends(i), sends(i - 1))
        lax.fori_loop(lo, sends(i), each(first), 0)
        for lag, stage in ((1, second), (2, third), (3, fourth)):
            k = i - lag
            pl.when((k >= 0) & (k < CHUNKS))(lambda stage=stage, k=k: stage(k))
        return carry

    def gather_done(k, carry):
        m, src = chunk(k)

        @pl.when(onward(src))
        def _():
            relay(m, src, core).wait_send()
            pl.when(m == 0)(lambda: relay_vec(src, core).wait_send())

        far = is_far(k)
        pl.when(far)(lambda: wait_rows(asend.at[k], 6 * PIECE))
        pl.when(jnp.logical_not(far))(lambda: wait_rows(asend.at[k], 7 * PIECE))
        return carry

    def got(s):
        return lax.rem(z + QUARTERS - s, QUARTERS)

    def both(fn):
        pl.when(z > 0)(lambda: fn(0))
        pl.when(z < QUARTERS - 1)(lambda: fn(1))

    both(lambda up: own_vec(up).start())
    for m, waits in enumerate((own[:4], own[4:5], own[5:])):
        for cp in waits:
            cp.wait()
        if m != DOWN:
            both(lambda up: own_z(m, up).start())

    def own_down(up):
        own_z(DOWN, up).start()
        pl.when(wants_far(up))(lambda: far_z(up).start())

    pl.when(at_end)(lambda: both(own_down))

    def own_sent(up):
        own_vec(up).wait_send()
        for m in range(3):
            own_z(m, up).wait_send()
        pl.when(wants_far(up))(lambda: far_z(up).wait_send())

    base = z * ROWS
    start = lax.select(z < 2, jnp.int32(0), jnp.int32(SEQ - COMP))
    place = pl.multiple_of(start - base + BASE + FRONT, 32)
    start = pl.multiple_of(start, 32)
    kvf[...] = jnp.zeros_like(kvf)
    for b in range(2):
        i = base + b * QB + cols_iota(1, QB)
        j = base - REACH + b * QB + rows_iota(NEAR, 1)
        ok = (jnp.abs(i - j) <= REACH) & (j >= 0) & (j < length)
        maskn[b] = jnp.where(ok, 0.0, BIG_NEG)
        j = (OWNP * z - PREACH + b * (QB // STRIDE) + rows_iota(FAR, 1)) * STRIDE
        ok = (jnp.abs(i - j) <= POOL_WINDOW // 2) & (j >= 0) & (j < length)
        maskf[b] = jnp.where(ok, 0.0, BIG_NEG)
    own_rows = pl.ds(pl.multiple_of(base, ROWS), ROWS)
    tok_in.wait()
    cot_in.wait()
    for cp in small[6:]:
        cp.wait()
    xb = tok[own_rows, :]
    acc[...] = jnp.zeros_like(acc)

    def taps(zq, t):
        return VEC[zq, 2 + t : 3 + t, 0 : 2 * CHANS]

    def strided(t):
        at = pl.ds(FRONT + BASE - POOL_WINDOW // 2 - 2 + t, KP, stride=STRIDE)
        return jnp.concatenate([kvf[i, at, :] for i in range(TILES)], axis=1)

    def tile(i):
        return slice(i * 128, (i + 1) * 128)

    def window(lo, rows):
        return jnp.concatenate([kvf[i, lo : lo + rows, :] for i in range(TILES)], axis=1)

    def quarter(s):
        return lax.select(s == 0, z, source(lax.max(s, 1)))

    def attend(s, carry):
        zq = quarter(s)
        for blk in range(2):
            xr = tok[pl.ds(pl.multiple_of(start + blk * HALFC, 16), HALFC), :]
            kv = nt(xr, W[0, zq, 0 : 2 * CHANS, :]) + VEC[zq, 1:2, 0 : 2 * CHANS]
            pos = start + blk * HALFC + rows_iota(HALFC, 1)
            kvb = jnp.where(pos < length, kv.astype(BF).astype(F32), 0.0)
            for i in range(TILES):
                kvf[i, pl.ds(pl.multiple_of(place + blk * HALFC, 8), HALFC), :] = kvb[:, tile(i)]
        KVS[zq] = window(FRONT, COMP).astype(BF)
        KV[zq, 0:KW, :] = window(FRONT + BASE - REACH, KW).astype(BF)
        pooled = jnp.zeros((KP, 2 * CHANS), F32)
        for t in range(5):
            pooled = pooled + taps(zq, t) * strided(t)
        KV[zq, KW:KEYS, :] = pooled.astype(BF)
        qz = nt(xb, W[0, zq, 2 * CHANS : 3 * CHANS, :]) + VEC[zq, 1:2, 2 * CHANS : 3 * CHANS]
        Q[zq] = qz.astype(BF)
        for b in range(2):
            live = base + b * QB + cols_iota(1, QB) < length
            n0, f0 = b * QB, KW + b * (QB // STRIDE)
            for h in range(QHEADS):
                kl = slice(h * HEAD_DIM, (h + 1) * HEAD_DIM)
                vl = slice(CHANS + h * HEAD_DIM, CHANS + (h + 1) * HEAD_DIM)
                qh = Q[zq, b * QB : (b + 1) * QB, kl]
                sn = nt(KV[zq, n0 : n0 + NEAR, kl], qh) * SCALE + maskn[b]
                sf = nt(KV[zq, f0 : f0 + FAR, kl], qh) * SCALE + maskf[b]
                peak = jnp.maximum(
                    jnp.max(sn, axis=0, keepdims=True), jnp.max(sf, axis=0, keepdims=True)
                )
                en, ef = jnp.exp(sn - peak), jnp.exp(sf - peak)
                inv = 1.0 / (sum_col(en) + sum_col(ef))
                pn, pf = en * inv, ef * inv
                P[zq, h, b, 0:NEAR, :] = pn
                P[zq, h, b, NEAR : NEAR + FAR, :] = pf
                ct = tn(KV[zq, n0 : n0 + NEAR, vl], pn.astype(BF))
                ct = ct + tn(KV[zq, f0 : f0 + FAR, vl], pf.astype(BF))
                ct = jnp.where(live, ct, 0.0)
                CTX[zq, b * QB : (b + 1) * QB, kl] = ct.T.astype(BF)
        acc[...] += nn(CTX[zq], W[0, zq, 3 * CHANS : D, :])
        lax.fori_loop(lookup_slots(s), lookup_slots(s + 1), gather_slot, 0)
        return carry

    def lookup_slots(s):
        return jnp.where(s == 0, 0, jnp.where(s < 3, 2 + 2 * s, 8))

    lax.fori_loop(0, QUARTERS, attend, 0)

    def store_T(dst, v, cols):
        vt = v.T.astype(BF)
        for j in range(8):
            to = (j % 2) * 4 + j // 2
            dst[to * PIECE : (to + 1) * PIECE, cols] = vt[j * PIECE : (j + 1) * PIECE]

    def span(i, size):
        if isinstance(i, int):
            return pl.ds(i * size, size)
        return pl.ds(pl.multiple_of(i * size, size), size)

    def norm_one(i, carry):
        rows = span(i, QB)
        res = tok[pl.ds(pl.multiple_of(base + i * QB, QB), QB), :].astype(F32)
        hid = res + (acc[rows, :] + bo[...])
        cen = hid - mean_row(hid)
        r = lax.rsqrt(mean_row(cen * cen) + epsilon)
        n = cen * r
        n1[rows, :] = n
        r1[rows, :] = r
        out = n * ag[...] + ash[...]
        y1[rows, :] = out
        y1b[rows, :] = out.astype(BF)
        store_T(yT, out, rows)
        acc[rows, :] = jnp.zeros_like(out)
        return carry

    lax.fori_loop(0, ROWS // QB, norm_one, 0)

    def most_gathered():
        lax.fori_loop(0, CHUNKS - 1, gather_done, 0)

    def feed(s, carry):
        zq = quarter(s)

        def up(i, carry):
            cols = span(i, ROWS)
            u = nn(y1b[...], W[1, zq, :, cols]) + VEC[zq, 0:1, cols]
            cdf = 0.5 * (1.0 + lax.erf(u * (0.5 ** 0.5)))
            dg[zq, :, cols] = cdf + u * jnp.exp(-0.5 * u * u) * ((2.0 * 3.141592653589793) ** -0.5)
            av[zq, :, cols] = (u * cdf).astype(BF)
            return carry

        for i in range(D // ROWS):
            up(i, 0)
        pl.when(s == QUARTERS - 1)(most_gathered)
        lax.fori_loop(8 + s, 9 + s, gather_slot, 0)
        acc[...] += nn(av[zq], W[2, zq])
        return carry

    lax.fori_loop(0, QUARTERS, feed, 0)
    VG[...] = jnp.zeros_like(VG)
    GEN = 8 * QUARTERS

    def add_row(row, v):
        VG[row : row + 1, :] += sum_col(v)

    def norm_two(i, carry):
        rows = span(i, QB)
        hid = y1[rows, :] + (acc[rows, :] + bd[...])
        cen = hid - mean_row(hid)
        r = lax.rsqrt(mean_row(cen * cen) + epsilon)
        n = cen * r
        act_out[rows, :] = (n * fg[...] + fs[...]).astype(BF)
        g = cot[rows, :].astype(F32)
        add_row(GEN + 4, g * n)
        add_row(GEN + 5, g)
        e = g * fg[...]
        gh2 = r * (e - mean_row(e) - n * mean_row(e * n))
        acc[rows, :] = gh2
        gf = gh2.astype(BF)
        gab[rows, :] = gf
        gff = gf.astype(F32)
        add_row(GEN + 3, gff)
        store_T(fT, gff, rows)
        return carry

    lax.fori_loop(0, ROWS // QB, norm_two, 0)
    outs[0].start()

    PARTS = 12

    def part(r):
        m = lax.select(r < 8, 2 - lax.rem(r, 2), 0)
        t = lax.select(r < 8, lax.div(r, 2), r - 8)
        return m, t

    def r_core(r):
        m, t = part(r)
        src = W.at[m, target(t), half(1 - c), :]
        return rcopy(src, CR.at[r], rsend.at[r], rrecv.at[r, 0], core)

    def blk4(r, yy, xx, cols):
        return CR.at[r, block(2 * yy + xx), cols]

    THIRD = D // 3
    wide = (LO, HI, D // 2, ALL)
    thin = (pl.ds(0, THIRD), pl.ds(THIRD, THIRD), THIRD, pl.ds(0, 2 * THIRD))
    LAST = pl.ds(2 * THIRD, THIRD)
    OWN_DOWN = 6

    def narrow(r):
        m, t = part(r)
        return (m == DOWN) & (t < QUARTERS - 1)

    def by_width(r, fn):
        pl.when(narrow(r))(lambda: fn(thin))
        pl.when(jnp.logical_not(narrow(r)))(lambda: fn(wide))

    def r_stage1(r, i, cut):
        if i < 2:
            src, dev = blk4(r, i, 1 - x, cut[0]), xdev
        else:
            src, dev = blk4(r, 1 - y, i - 2, cut[1]), ydev
        return rcopy(src, S1.at[r, i, :, 0 : cut[2]], rsend.at[r], rrecv.at[r, 1], dev)

    def r_stage2(r, i, cut):
        if i == 0:
            src, dev = blk4(r, 1 - y, x, cut[0]), ydev
        else:
            src, dev = blk4(r, y, 1 - x, cut[1]), xdev
        return rcopy(src, S2.at[r, i, :, 0 : cut[2]], rsend.at[r], rrecv.at[r, 2], dev)

    def onto(r):
        dst = target(part(r)[1])
        left = dst < z
        slot = jnp.where(left & (dst == z - 1), QUARTERS, dst)
        return slot, (dp, jnp.where(left, z - 1, z + 1))

    def r_z(r, cut):
        slot, dev = onto(r)
        m = part(r)[0]
        src = CR.at[r, block(yx), cut[3]]
        return rcopy(src, ZR.at[m, slot, :, cut[3]], rsend.at[r], zsum.at[m, slot], dev)

    def z_wait(m, slot, cut):
        ref = ZR.at[m, slot, :, cut[3]]
        pltpu.make_async_copy(ref, ref, zsum.at[m, slot]).wait()

    def r_zf(r):
        slot, dev = onto(r)
        return rcopy(CR.at[r, :, LAST], ZF.at[slot], rsend.at[r], zfsum.at[slot], dev)

    def take_zf(r, slot):
        ref = ZF.at[slot]
        pltpu.make_async_copy(ref, ref, zfsum.at[slot]).wait()
        CR[r, :, LAST] = CR[r, :, LAST] + ZF[slot]

    def upstream(dst):
        return jnp.where(dst < z, z < QUARTERS - 1, z > 0)

    def reduce1(r):
        m, t = part(r)
        r_core(r).wait_recv()
        zq = target(t)

        def add(i, carry):
            CR[r, block(i), :] = CR[r, block(i), :] + W[m, zq, block(4 * c + i), :]
            return carry

        lax.fori_loop(0, 4, add, 0)

        @pl.when(r == OWN_DOWN)
        def _():
            pl.when(z > 0)(lambda: take_zf(r, z))
            pl.when(z < QUARTERS - 1)(lambda: take_zf(r, jnp.int32(QUARTERS)))

        def go(cut):
            for i in range(4):
                r_stage1(r, i, cut).start()

        by_width(r, go)
        pl.when(narrow(r) & jnp.logical_not(upstream(zq)))(lambda: r_zf(r).start())

    def reduce_f(r):
        dst = target(part(r)[1])

        @pl.when(upstream(dst))
        def _():
            take_zf(r, dst)
            r_zf(r).start()

    def reduce2(r):
        def go(cut):
            ref = S1.at[r, :, :, 0 : cut[2]]
            pltpu.make_async_copy(ref, ref, rrecv.at[r, 1]).wait()
            for i in range(2):
                a = blk4(r, i, x, cut[0])
                a[...] = a[...] + S1[r, i, :, 0 : cut[2]]
                a = blk4(r, y, i, cut[1])
                a[...] = a[...] + S1[r, 2 + i, :, 0 : cut[2]]
            for i in range(2):
                r_stage2(r, i, cut).start()

        by_width(r, go)

    def reduce3(r):
        dst = target(part(r)[1])

        def go(cut):
            ref = S2.at[r, :, :, 0 : cut[2]]
            pltpu.make_async_copy(ref, ref, rrecv.at[r, 2]).wait()
            for i in range(2):
                a = blk4(r, y, x, cut[i])
                a[...] = a[...] + S2[r, i, :, 0 : cut[2]]
            pl.when((dst != z) & jnp.logical_not(upstream(dst)))(lambda: r_z(r, cut).start())

        by_width(r, go)

    def reduce4(r):
        m, t = part(r)
        dst = target(t)

        def go(cut):
            @pl.when((dst != z) & upstream(dst))
            def _():
                z_wait(m, dst, cut)
                a = CR.at[r, block(yx), cut[3]]
                a[...] = a[...] + ZR[m, dst, :, cut[3]]
                r_z(r, cut).start()

        by_width(r, go)

    def stage(fn, ok, r):
        pl.when(ok)(lambda: fn(r))

    def weight_grad(left, right, dst, width):
        dst[:, 0:width] = nn(left[...], right).astype(BF)

    def feed_back(s, carry):
        zq = target(s)
        vrow = pl.multiple_of(8 * zq, 8)

        def hidden(i, carry):
            cols = span(i, ROWS)
            gact = nt(gab[...], W[2, zq, cols, :])
            gu = (gact * dg[zq, :, cols]).astype(BF)
            gub[:, cols] = gu
            VG[pl.ds(vrow, 1), cols] = sum_col(gu.astype(F32))
            return carry

        for i in range(D // ROWS):
            hidden(i, 0)
        weight_grad(fT, av[zq], W.at[2, zq], D)
        r_core(2 * s).start()
        acc[...] += nt(gub[...], W[1, zq])
        weight_grad(yT, gub[...], W.at[1, zq], D)
        r_core(2 * s + 1).start()
        reduce1(jnp.where(s < 2, s, s + 1))
        stage(reduce1, s == 1, jnp.int32(2))
        stage(reduce2, s == 3, jnp.int32(0))
        return carry

    gather_done(jnp.int32(LAST_CHUNK), 0)
    both(own_sent)
    lax.fori_loop(0, QUARTERS, feed_back, 0)

    def norm_back(i, carry):
        rows = span(i, QB)
        gy = acc[rows, :]
        n = n1[rows, :]
        add_row(GEN + 1, gy * n)
        add_row(GEN + 2, gy)
        e = gy * ag[...]
        gh1 = r1[rows, :] * (e - mean_row(e) - n * mean_row(e * n))
        acc[rows, :] = gh1
        ga = gh1.astype(BF)
        gab[rows, :] = ga
        gaf = ga.astype(F32)
        add_row(GEN, gaf)
        store_T(fT, gaf, rows)
        store_T(xT, tok[pl.ds(pl.multiple_of(base + i * QB, QB), QB), :].astype(F32), rows)
        return carry

    lax.fori_loop(0, ROWS // QB, norm_back, 0)

    def hl(zq):
        return rcopy(SL.at[zq], HL.at[zq], hsend.at[0], hrecv.at[0, zq], zdev(3))

    def hr(zq):
        return rcopy(SR.at[zq], HR.at[zq], hsend.at[1], hrecv.at[1, zq], zdev(1))

    def hll(zq):
        return rcopy(
            SL.at[zq, REACH : REACH + 16, :], HLL.at[zq], hsend.at[2], hrecv.at[2, zq], zdev(2)
        )

    def attend_back(s, carry):
        zq = lookup(table((3, 0, 2, 1)), s)
        gc = nt(gab[...], W[0, zq, 3 * CHANS : D, :])
        alive = base + rows_iota(ROWS, 1) < length
        gcb = jnp.where(alive, gc, 0.0).astype(BF)
        GKV[zq] = jnp.zeros((KEYS, 2 * CHANS), F32)
        for b in range(2):
            n0, f0 = b * QB, KW + b * (QB // STRIDE)
            for h in range(QHEADS):
                kl = slice(h * HEAD_DIM, (h + 1) * HEAD_DIM)
                vl = slice(CHANS + h * HEAD_DIM, CHANS + (h + 1) * HEAD_DIM)
                gch = gcb[b * QB : (b + 1) * QB, kl]
                qh = Q[zq, b * QB : (b + 1) * QB, kl]
                pn = P[zq, h, b, 0:NEAR, :]
                pf = P[zq, h, b, NEAR : NEAR + FAR, :]
                gpn = nt(KV[zq, n0 : n0 + NEAR, vl], gch)
                gpf = nt(KV[zq, f0 : f0 + FAR, vl], gch)
                delta = sum_col(pn * gpn) + sum_col(pf * gpf)
                gsn = (pn * (gpn - delta)).astype(BF)
                gsf = (pf * (gpf - delta)).astype(BF)
                qt = tn(KV[zq, n0 : n0 + NEAR, kl], gsn) + tn(KV[zq, f0 : f0 + FAR, kl], gsf)
                GQ[zq, b * QB : (b + 1) * QB, 2 * CHANS + h * HEAD_DIM : 2 * CHANS + (h + 1) * HEAD_DIM] = (
                    (qt * SCALE).T.astype(BF)
                )
                GKV[zq, n0 : n0 + NEAR, kl] += nn(gsn, qh) * SCALE
                GKV[zq, f0 : f0 + FAR, kl] += nn(gsf, qh) * SCALE
                GKV[zq, n0 : n0 + NEAR, vl] += nn(pn.astype(BF), gch)
                GKV[zq, f0 : f0 + FAR, vl] += nn(pf.astype(BF), gch)
        vrow = pl.multiple_of(8 * zq, 8)
        for i in range(TILES):
            kvf[i, FRONT : FRONT + COMP, :] = KVS[zq, :, tile(i)].astype(F32)
        gp = GKV[zq, KW:KEYS, :]
        sums = jnp.concatenate(
            [jnp.zeros((1, CHANS), F32), sum_col(GKV[zq, 0:KW, CHANS : 2 * CHANS])], axis=1
        )
        far_at = (OWNP * z - PREACH + rows_iota(KP, 1)) * STRIDE
        for t in range(5):
            VG[pl.ds(vrow + 2 + t, 1), 0 : 2 * CHANS] = sum_col(gp * strided(t))
            to = far_at + (t - 2)
            inside = (to >= 0) & (to < length)
            sums = sums + taps(zq, t) * sum_col(jnp.where(inside, gp, 0.0))
        VG[pl.ds(vrow + 1, 1), CHANS : 2 * CHANS] = sums[:, CHANS : 2 * CHANS]
        VG[pl.ds(vrow + 1, 1), 2 * CHANS : 3 * CHANS] = sum_col(
            GQ[zq, :, 2 * CHANS : 3 * CHANS].astype(F32)
        )
        SL[zq, 0:REACH, :] = GKV[zq, 0:REACH, :].astype(BF)
        SL[zq, REACH : REACH + 80, :] = GKV[zq, KW : KW + 80, :].astype(BF)
        SR[zq, 0:REACH, :] = GKV[zq, KW - REACH : KW, :].astype(BF)
        SR[zq, REACH : REACH + OWNP, :] = GKV[zq, KEYS - OWNP : KEYS, :].astype(BF)
        pl.when(z > 0)(lambda: hl(zq).start())
        pl.when(z < QUARTERS - 1)(lambda: hr(zq).start())
        pl.when(z > 1)(lambda: hll(zq).start())
        stage(reduce1, s == 0, jnp.int32(5))
        reduce2(s + 1)
        stage(reduce3, s == 3, jnp.int32(0))
        stage(reduce_f, s > 0, jnp.where(s == 1, 0, jnp.where(s == 2, 4, 2)))
        return carry

    lax.fori_loop(0, QUARTERS, attend_back, 0)

    half_row = pl.multiple_of(32 * c, 32)
    row_x = pl.multiple_of(half_row + 16 * x, 16)
    row_y = pl.multiple_of(row_x + 8 * y, 8)

    def vrows(at, size):
        return pl.ds(pl.multiple_of(at, 8), size)

    folds = [
        (core, VG.at[vrows(32 - half_row, 32), :], GVR.at[0:32], vrows(half_row, 32)),
        (xdev, VG.at[vrows(half_row + 16 - 16 * x, 16), :], GVR.at[32:48], vrows(row_x, 16)),
        (ydev, VG.at[vrows(row_x + 8 - 8 * y, 8), :], GVR.at[48:56], vrows(row_y, 8)),
    ]

    def fold(i):
        dev, src, dst, keep = folds[i]
        return rcopy(src, dst, gsend.at[i], grecv.at[i], dev)

    def fold_done(i):
        fold(i).wait()
        keep = folds[i][3]
        VG[keep, :] = VG[keep, :] + folds[i][2][...]

    def g_z(s):
        src = VG.at[vrows(row_y, 8), :]
        return rcopy(src, GVZ.at[z], gsend.at[2 + s], grecv.at[2 + s], zdev(s))

    def g_z_in(s):
        dst = GVZ.at[got(s)]
        return rcopy(dst, dst, gsend.at[2 + s], grecv.at[2 + s], core)

    opens = [
        (ydev, vrows(row_y, 8), vrows(row_x + 8 - 8 * y, 8)),
        (xdev, vrows(row_x, 16), vrows(half_row + 16 - 16 * x, 16)),
        (core, vrows(half_row, 32), vrows(32 - half_row, 32)),
    ]

    def unfold(i):
        dev, mine, other = opens[i]
        ref = VO.at[mine, :]
        return rcopy(ref, ref, gsend.at[6 + i], grecv.at[6 + i], dev)

    def unfold_done(i):
        ref = VO.at[opens[i][2], :]
        rcopy(ref, ref, gsend.at[6 + i], grecv.at[6 + i], core).wait_recv()

    def vector_two():
        fold_done(0)
        fold(1).start()

    def vector_three():
        fold_done(1)
        fold(2).start()

    def vector_z():
        fold_done(2)
        for step in (1, 2, 3):
            g_z(step).start()
        GVZ[z] = VG[vrows(row_y, 8), :]

    def vector_back():
        for step in (1, 2, 3):
            g_z_in(step).wait_recv()
        VO[vrows(row_y, 8), :] = GVZ[0] + GVZ[1] + GVZ[2] + GVZ[3]
        unfold(0).start()

    fold(0).start()

    def project_back(s, carry):
        zq = target(s)
        pl.when(z < QUARTERS - 1)(lambda: hl(zq).wait_recv())
        pl.when(z > 0)(lambda: hr(zq).wait_recv())
        pl.when(z < QUARTERS - 2)(lambda: hll(zq).wait_recv())
        near = GKV.at[zq]

        def when(ok, v):
            return jnp.where(ok, v.astype(F32), 0.0)

        has_l, has_r, has_rr = z > 0, z < QUARTERS - 1, z < QUARTERS - 2
        near[REACH : 2 * REACH, :] += when(has_l, HR[zq, 0:REACH, :])
        near[ROWS : ROWS + REACH, :] += when(has_r, HL[zq, 0:REACH, :])
        gp = GKV[zq, KW + OWNP : KW + 2 * OWNP, :] + when(has_l, HR[zq, REACH : REACH + OWNP, :])
        gp = gp + when(has_r, HL[zq, REACH : REACH + OWNP, :])
        nxt = GKV[zq, KW + 2 * OWNP : KW + 2 * OWNP + 1, :]
        nxt = nxt + when(has_r, HL[zq, REACH + OWNP : REACH + OWNP + 16, :])[0:1, :]
        nxt = nxt + when(has_rr, HLL[zq])[0:1, :]
        gp1 = jnp.concatenate([gp[1:, :], nxt], axis=0)
        fills = (
            taps(zq, 2) * gp,
            taps(zq, 3) * gp,
            taps(zq, 4) * gp + taps(zq, 0) * gp1,
            taps(zq, 1) * gp1,
        )
        for k, fill in enumerate(fills):
            for i in range(TILES):
                pt[i, pl.ds(k, OWNP, stride=STRIDE), :] = fill[:, tile(i)]
        back = jnp.concatenate([pt[i] for i in range(TILES)], axis=1)
        alive = base + rows_iota(ROWS, 1) < length
        gkv = GKV[zq, REACH : REACH + ROWS, :] + jnp.where(alive, back, 0.0)
        GQ[zq, :, 0 : 2 * CHANS] = gkv.astype(BF)

        acc[...] += nn(GQ[zq], W[0, zq, 0 : 3 * CHANS, :])
        weight_grad(xT, GQ[zq], W.at[0, zq], 3 * CHANS)

        W[0, zq, :, 3 * CHANS : D] = nn(fT[...], CTX[zq]).astype(BF)
        r_core(8 + s).start()
        stage(reduce2, s == 0, jnp.int32(5))
        stage(reduce3, s > 0, s)
        stage(reduce4, s > 1, s - 2)
        stage(reduce1, s < 3, 8 + s)
        stage(reduce1, s == 1, jnp.int32(7))
        pl.when(s == 0)(vector_two)
        return carry

    lax.fori_loop(0, QUARTERS, project_back, 0)
    outs[1].start()

    def wait_all(ref, sem):
        pltpu.make_async_copy(ref, ref, sem).wait()

    pl.when(z > 0)(lambda: wait_all(SL, hsend.at[0]))
    pl.when(z < QUARTERS - 1)(lambda: wait_all(SR, hsend.at[1]))
    pl.when(z > 1)(lambda: wait_all(HLL, hsend.at[2]))

    def final(m):
        own_part = (11, 7, 6)[m]
        gmats[m] = CR[own_part, block(yx), :].astype(F32)

        def more(slot):
            cut = thin if m == DOWN else wide
            z_wait(m, slot, cut)
            at = gmats.at[m, :, cut[3]]
            at[...] += ZR[m, slot, :, cut[3]].astype(F32)

        pl.when(z > 0)(lambda: more(z))
        pl.when(z < QUARTERS - 1)(lambda: more(QUARTERS))
        outs[2 + m].start()

    def at(r):
        return jnp.int32(r)

    reduce2(at(8))
    vector_three()
    reduce1(at(6))
    reduce3(at(4))
    reduce4(at(2))
    reduce2(at(9))
    reduce1(at(11))
    reduce3(at(5))
    reduce4(at(3))
    reduce2(at(10))
    reduce2(at(7))
    reduce4(at(4))
    reduce3(at(8))
    vector_z()
    reduce4(at(5))
    reduce3(at(9))
    reduce4(at(8))
    reduce2(at(6))
    reduce3(at(10))
    reduce4(at(9))
    vector_back()
    reduce2(at(11))
    reduce4(at(10))
    reduce3(at(7))
    final(1)
    unfold_done(0)
    unfold(1).start()
    reduce3(at(6))
    final(2)
    unfold_done(1)
    unfold(2).start()
    reduce3(at(11))
    final(0)
    unfold_done(2)
    outs[5].start()
    for i in range(3):
        unfold(i).wait_send()
    for s in (1, 2, 3):
        g_z(s).wait_send()

    def sent(r, carry):
        own_part = part(r)[1] == QUARTERS - 1
        pl.when(own_part)(lambda: wait_rows(rsend.at[r], 7 * PIECE))
        pl.when(jnp.logical_not(own_part))(lambda: wait_rows(rsend.at[r], 8 * PIECE))
        return carry

    lax.fori_loop(0, PARTS, sent, 0)
    for cp in outs:
        cp.wait()


def unpack(
    act, gtok, gmats, gvec,
    act_out, gtok_out, gq, gk, gv, gbq, gbv, gck, gcv, go, gbo, gag, gas, gup, gbu, gdown, gbd, gfg, gfs,
):
    act_out[...] = act[...]
    gtok_out[...] = gtok[...]
    gk[...] = gmats[0, :, 0:CHANS]
    gv[...] = gmats[0, :, CHANS : 2 * CHANS]
    gq[...] = gmats[0, :, 2 * CHANS : 3 * CHANS]
    go[...] = gmats[0, :, 3 * CHANS : D].T
    gup[...] = gmats[1]
    gdown[...] = gmats[2]
    for j in range(QUARTERS):
        at = slice(j * CHANS, (j + 1) * CHANS)
        row = 8 * j
        gbu[:, j * D : (j + 1) * D] = gvec[row : row + 1, :]
        gbv[:, at] = gvec[row + 1 : row + 2, CHANS : 2 * CHANS]
        gbq[:, at] = gvec[row + 1 : row + 2, 2 * CHANS : 3 * CHANS]
        for t in range(5):
            gck[t, :, at] = gvec[row + 2 + t : row + 3 + t, 0:CHANS]
            gcv[t, :, at] = gvec[row + 2 + t : row + 3 + t, CHANS : 2 * CHANS]
    for j, out in enumerate((gbo, gag, gas, gbd, gfg, gfs)):
        out[...] = gvec[8 * QUARTERS + j : 8 * QUARTERS + j + 1, :]


def fused_layer(
    tokens, lengths, w_query, w_key, w_value, b_query, b_value, conv_key, conv_value, w_out,
    b_out, attn_gain, attn_shift, w_up, b_up, w_down, b_down, ffn_gain, ffn_shift, cotangent,
):
    Q4 = QUARTERS
    vm = pltpu.VMEM
    dma = pltpu.SemaphoreType.DMA
    scratch = [
        vm((3, Q4, D, D), BF),
        vm((Q4, 8, D), F32),
        vm((TILES, KVROWS, 128), F32),
        vm((Q4, KEYS, 2 * CHANS), BF),
        vm((Q4, COMP, 2 * CHANS), BF),
        vm((Q4, ROWS, CHANS), BF),
        vm((Q4, ROWS, CHANS), BF),
        vm((Q4, QHEADS, 2, NEAR + FAR, QB), F32),
        vm((2, NEAR, QB), F32),
        vm((2, FAR, QB), F32),
        vm((ROWS, D), F32),
        vm((ROWS, 1), F32),
        vm((ROWS, D), F32),
        vm((ROWS, D), BF),
        vm((Q4, ROWS, D), F32),
        vm((Q4, ROWS, D), BF),
        vm((D, ROWS), BF),
        vm((D, ROWS), BF),
        vm((ROWS, D), BF),
        vm((Q4, KEYS, 2 * CHANS), F32),
        vm((TILES, ROWS, 128), F32),
        vm((Q4, ROWS, 3 * CHANS), BF),
        vm((VROWS, D), F32),
        vm((12, D // 2, D), BF),
        vm((12, 4, PIECE, D // 2), BF),
        vm((12, 2, PIECE, D // 2), BF),
        vm((3, Q4 + 1, PIECE, D), BF),
        vm((Q4 + 1, D // 2, D // 3), BF),
        vm((Q4, REACH + 80, 2 * CHANS), BF),
        vm((Q4, REACH + OWNP, 2 * CHANS), BF),
        vm((Q4, 16, 2 * CHANS), BF),
        vm((Q4, REACH + 80, 2 * CHANS), BF),
        vm((Q4, REACH + OWNP, 2 * CHANS), BF),
        vm((VROWS, D), F32),
        vm((Q4, 8, D), F32),
        vm((VROWS, D), F32),
        vm((SEQ, D), BF),
        vm((ROWS, D), BF),
        pltpu.SMEM((1,), jnp.int32),
        vm((1, CHANS), F32),
        vm((1, CHANS), F32),
        vm((5, 1, CHANS), F32),
        vm((5, 1, CHANS), F32),
        vm((1, D), F32),
        vm((1, D), F32),
        vm((1, D), F32),
        vm((1, D), F32),
        vm((1, D), F32),
        vm((1, D), F32),
        vm((1, D), F32),
        vm((ROWS, D), BF),
        vm((ROWS, D), F32),
        vm((3, PIECE, D), F32),
        dma((12,)),
        dma((6,)),
        dma((8,)),
        dma((9,)),
        dma((9, 3)),
        dma((5, 2)),
        dma((5, Q4)),
        dma((5, Q4)),
        dma((3,)),
        dma((3, Q4)),
        dma((12,)),
        dma((12, 3)),
        dma((3, Q4 + 1)),
        dma((Q4 + 1,)),
        dma((9,)),
        dma((9,)),
    ]
    vspec = pl.BlockSpec(memory_space=pltpu.VMEM)
    hspec = pl.BlockSpec(memory_space=pl.ANY)
    packed = pl.pallas_call(
        kernel,
        out_shape=(
            jax.ShapeDtypeStruct((ROWS, D), BF),
            jax.ShapeDtypeStruct((ROWS, D), F32),
            jax.ShapeDtypeStruct((3, PIECE, D), F32),
            jax.ShapeDtypeStruct((VROWS, D), F32),
        ),
        in_specs=[hspec] * 20,
        out_specs=(hspec,) * 4,
        scratch_shapes=scratch,
        compiler_params=pltpu.CompilerParams(
            collective_id=0, has_side_effects=True, vmem_limit_bytes=67043328
        ),
        name="layer",
    )(
        lengths, tokens, w_key[0].T, w_value[0].T, w_query[0].T, w_out[0], w_up[0], w_down[0],
        b_query, b_value, conv_key.transpose(1, 0, 2), conv_value.transpose(1, 0, 2), b_up, b_out, attn_gain, attn_shift, b_down,
        ffn_gain, ffn_shift, cotangent,
    )
    row = (1, D)
    shapes = [
        (ROWS, D), (PIECE, CHANS), (PIECE, CHANS), (PIECE, CHANS), row, row, (5, 1, D), (5, 1, D), (CHANS, PIECE),
        row, row, row, (PIECE, D), (1, FF), (PIECE, D), row, row, row,
    ]
    outs = pl.pallas_call(
        unpack,
        out_shape=[jax.ShapeDtypeStruct((ROWS, D), BF)] + [jax.ShapeDtypeStruct(v, F32) for v in shapes],
        in_specs=[vspec] * 4,
        out_specs=[vspec] * 19,
        name="unpack",
    )(*packed)
    act, gtok, gq, gk, gv, gbq, gbv, gck, gcv, go, gbo, gag, gas, gup, gbu, gdown, gbd, gfg, gfs = outs
    return (
        act, gtok, gq[None], gk[None], gv[None], gbq, gbv, gck.transpose(1, 0, 2), gcv.transpose(1, 0, 2), go[None], gbo, gag, gas,
        gup[None], gbu, gdown.T[None], gbd, gfg, gfs,
    )


def solution(mesh):
    small = mesh.shape["dp"] == 8 and mesh.shape["mp"] == QUARTERS
    return jax.shard_map(
        fused_layer if small else on_device,
        mesh=mesh,
        in_specs=(
            P("dp", None),
            P("dp"),
            P(None, None, "mp"),
            P(None, None, "mp"),
            P(None, None, "mp"),
            P(None, "mp"),
            P(None, "mp"),
            P(None, None, "mp"),
            P(None, None, "mp"),
            P(None, "mp", None),
            P(),
            P(),
            P(),
            P(None, None, "mp"),
            P(None, "mp"),
            P(None, "mp", None),
            P(),
            P(),
            P(),
            P(("dp", "mp"), None),
        ),
        out_specs=(
            P(("dp", "mp"), None),
            P(("dp", "mp"), None),
            P(None, "dp", "mp"),
            P(None, "dp", "mp"),
            P(None, "dp", "mp"),
            P(),
            P(),
            P(),
            P(),
            P(None, "mp", "dp"),
            P(),
            P(),
            P(),
            P(None, "dp", "mp"),
            P(),
            P(None, "mp", "dp"),
            P(),
            P(),
            P(),
        ),
        check_vma=False,
    )
```

```python
import jax
import jax.numpy as jnp
from jax import lax
from jax.experimental import pallas as pl
from jax.experimental.pallas import tpu as pltpu
from jax.sharding import PartitionSpec as P

D = 768
HEAD_DIM = 64
FF = 3072
WINDOW = 128
POOL_WINDOW = 512
STRIDE = 4
LAYERS = 1


block_rows = 512
mask_fill = -1000000000.0
epsilon = 1e-05


def norm_rows(hidden, gain, shift):
    center = hidden - jnp.mean(hidden, axis=-1, keepdims=True)
    spread = jnp.mean(center * center, axis=-1, keepdims=True)
    return center * lax.rsqrt(spread + epsilon) * gain + shift


def gelu_exact(values):
    return jax.nn.gelu(values, approximate=False)


def pool_rows(values, kernel):
    seqs, length, chans = values.shape
    width = kernel.shape[0]
    half = width // 2
    pooled_len = length // STRIDE
    padded = jnp.pad(values, ((0, 0), (half, width), (0, 0)))
    total = jnp.zeros((seqs, pooled_len, chans), jnp.float32)
    for offset in range(width):
        total = total + kernel[offset] * padded[:, offset : offset + STRIDE * pooled_len : STRIDE]
    return total


def block_mask(start, lengths):
    reach = WINDOW // 2
    pool_reach = POOL_WINDOW // 2 // STRIDE
    span = block_rows // STRIDE + 2 * pool_reach
    rows = start + jnp.arange(block_rows, dtype=jnp.int32)
    near_pos = start - reach + jnp.arange(block_rows + 2 * reach, dtype=jnp.int32)
    far_pos = (start // STRIDE - pool_reach + jnp.arange(span, dtype=jnp.int32)) * STRIDE
    limit = lengths[:, None, None]
    near_ok = (
        (jnp.abs(rows[:, None] - near_pos[None, :]) <= reach)[None]
        & (near_pos >= 0)[None, None]
        & (near_pos[None, None] < limit)
    )
    far_ok = (
        (jnp.abs(rows[:, None] - far_pos[None, :]) <= POOL_WINDOW // 2)[None]
        & (far_pos >= 0)[None, None]
        & (far_pos[None, None] < limit)
    )
    return jnp.concatenate([near_ok, far_ok], axis=-1)


def padded_keys(keys_loc, vals_loc, far_keys, far_vals):
    reach = WINDOW // 2
    pool_reach = POOL_WINDOW // 2 // STRIDE
    pad_near = ((0, 0), (reach, reach), (0, 0), (0, 0))
    pad_far = ((0, 0), (pool_reach, pool_reach), (0, 0), (0, 0))
    return (
        jnp.pad(keys_loc, pad_near),
        jnp.pad(vals_loc, pad_near),
        jnp.pad(far_keys, pad_far),
        jnp.pad(far_vals, pad_far),
    )


def block_inputs(start, queries, padded):
    near_k, near_v, far_k, far_v = padded
    near_len = block_rows + 2 * (WINDOW // 2)
    span = block_rows // STRIDE + 2 * (POOL_WINDOW // 2 // STRIDE)
    pool_start = start // STRIDE
    q_rows = queries[:, start : start + block_rows]
    keys_b = jnp.concatenate(
        [near_k[:, start : start + near_len], far_k[:, pool_start : pool_start + span]], axis=1
    )
    vals_b = jnp.concatenate(
        [near_v[:, start : start + near_len], far_v[:, pool_start : pool_start + span]], axis=1
    )
    return (q_rows, keys_b, vals_b)


def forward_block(q_rows, keys_b, vals_b, mask, live):
    scale = q_rows.shape[-1] ** (-0.5)
    scores = (
        jnp.einsum("sqhe,skhe->shqk", q_rows, keys_b, preferred_element_type=jnp.float32) * scale
    )
    scores = jnp.where(mask[:, None], scores, mask_fill)
    peak = jnp.max(scores, axis=-1, keepdims=True)
    expo = jnp.exp(scores - peak)
    total = jnp.sum(expo, axis=-1, keepdims=True)
    weights = (expo / total).astype(jnp.bfloat16)
    result = jnp.einsum("shqk,skhe->sqhe", weights, vals_b, preferred_element_type=jnp.float32)
    result = jnp.where(live[:, :, None, None], result, 0.0)
    return (result, peak + jnp.log(total))


def forward_skip(q_rows, keys_b, vals_b, mask, live):
    seqs, rows, heads, size = q_rows.shape
    return (
        jnp.zeros((seqs, rows, heads, size), jnp.float32),
        jnp.zeros((seqs, heads, rows, 1), jnp.float32),
    )


def backward_block(q_rows, keys_b, vals_b, mask, logsum, grad_rows):
    scale = q_rows.shape[-1] ** (-0.5)
    scores = (
        jnp.einsum("sqhe,skhe->shqk", q_rows, keys_b, preferred_element_type=jnp.float32) * scale
    )
    scores = jnp.where(mask[:, None], scores, mask_fill)
    probs = jnp.exp(scores - logsum)
    grad_probs = jnp.einsum(
        "sqhe,skhe->shqk", grad_rows, vals_b, preferred_element_type=jnp.float32
    )
    delta = jnp.sum(probs * grad_probs, axis=-1, keepdims=True)
    grad_scores = (probs * (grad_probs - delta)).astype(jnp.bfloat16)
    grad_q = (
        jnp.einsum("shqk,skhe->sqhe", grad_scores, keys_b, preferred_element_type=jnp.float32)
        * scale
    )
    grad_keys = (
        jnp.einsum("shqk,sqhe->skhe", grad_scores, q_rows, preferred_element_type=jnp.float32)
        * scale
    )
    grad_vals = jnp.einsum(
        "shqk,sqhe->skhe", probs.astype(jnp.bfloat16), grad_rows, preferred_element_type=jnp.float32
    )
    return (grad_q, grad_keys, grad_vals)


def backward_skip(q_rows, keys_b, vals_b, mask, logsum, grad_rows):
    return (
        jnp.zeros(q_rows.shape, jnp.float32),
        jnp.zeros(keys_b.shape, jnp.float32),
        jnp.zeros(vals_b.shape, jnp.float32),
    )


def attend_forward(queries, keys_loc, vals_loc, far_keys, far_vals, lengths):
    length = queries.shape[1]
    padded = padded_keys(keys_loc, vals_loc, far_keys, far_vals)
    longest = jnp.max(lengths)
    results, logsums = ([], [])
    for block in range(length // block_rows):
        start = block * block_rows
        q_rows, keys_b, vals_b = block_inputs(start, queries, padded)
        mask = block_mask(start, lengths)
        live = start + jnp.arange(block_rows, dtype=jnp.int32)[None, :] < lengths[:, None]
        result, logsum = lax.cond(
            start < longest, forward_block, forward_skip, q_rows, keys_b, vals_b, mask, live
        )
        results.append(result)
        logsums.append(logsum)
    return (jnp.concatenate(results, axis=1), logsums)


def attend_backward(
    queries, keys_loc, vals_loc, far_keys, far_vals, lengths, logsums, grad_context
):
    seqs, length, heads, size = queries.shape
    pooled_len = far_keys.shape[1]
    reach = WINDOW // 2
    pool_reach = POOL_WINDOW // 2 // STRIDE
    near_len = block_rows + 2 * reach
    span = block_rows // STRIDE + 2 * pool_reach
    padded = padded_keys(keys_loc, vals_loc, far_keys, far_vals)
    longest = jnp.max(lengths)
    grad_near_k = jnp.zeros((seqs, length + 2 * reach, heads, size), jnp.float32)
    grad_near_v = jnp.zeros((seqs, length + 2 * reach, heads, size), jnp.float32)
    grad_far_k = jnp.zeros((seqs, pooled_len + 2 * pool_reach, heads, size), jnp.float32)
    grad_far_v = jnp.zeros((seqs, pooled_len + 2 * pool_reach, heads, size), jnp.float32)
    grad_queries = []
    for block in range(length // block_rows):
        start = block * block_rows
        pool_start = start // STRIDE
        q_rows, keys_b, vals_b = block_inputs(start, queries, padded)
        mask = block_mask(start, lengths)
        grad_rows = grad_context[:, start : start + block_rows]
        grad_q, grad_keys, grad_vals = lax.cond(
            start < longest,
            backward_block,
            backward_skip,
            q_rows,
            keys_b,
            vals_b,
            mask,
            logsums[block],
            grad_rows,
        )
        grad_queries.append(grad_q)
        grad_near_k = grad_near_k.at[:, start : start + near_len].add(grad_keys[:, :near_len])
        grad_near_v = grad_near_v.at[:, start : start + near_len].add(grad_vals[:, :near_len])
        grad_far_k = grad_far_k.at[:, pool_start : pool_start + span].add(grad_keys[:, near_len:])
        grad_far_v = grad_far_v.at[:, pool_start : pool_start + span].add(grad_vals[:, near_len:])
    return (
        jnp.concatenate(grad_queries, axis=1),
        grad_near_k[:, reach : reach + length],
        grad_near_v[:, reach : reach + length],
        grad_far_k[:, pool_reach : pool_reach + pooled_len],
        grad_far_v[:, pool_reach : pool_reach + pooled_len],
    )


def row_sum(left, right, share):

    def term(start, count):
        return jnp.dot(left, right, preferred_element_type=jnp.float32)

    return lax.psum_scatter(
        term(jnp.int32(0), share * lax.axis_size("mp")), "mp", scatter_dimension=0, tiled=True
    )


def share_rows(values):
    return lax.all_gather(values, "mp", axis=0, tiled=True)


def share_back(values):
    return lax.all_gather(values, "mp", axis=0, tiled=True)


def back_sum(term, share):
    return lax.psum_scatter(
        term(jnp.int32(0), share * lax.axis_size("mp")), "mp", scatter_dimension=0, tiled=True
    )


def spread(values, width):
    whole = jnp.zeros(values.shape[:-1] + (width,), jnp.float32)
    start = lax.axis_index("mp") * values.shape[-1]
    return lax.dynamic_update_slice_in_dim(whole, values, start, values.ndim - 1)


def layer_forward(full_in, resid, lengths, params, share):
    (
        w_query,
        w_key,
        w_value,
        b_query,
        b_value,
        conv_key,
        conv_value,
        w_out,
        b_out,
        attn_gain,
        attn_shift,
        w_up,
        b_up,
        w_down,
        b_down,
        ffn_gain,
        ffn_shift,
    ) = params
    seqs = lengths.shape[0]
    total_rows = full_in.shape[0]
    length = total_rows // seqs
    chans = w_query.shape[1]
    heads = chans // HEAD_DIM
    pooled_len = length // STRIDE
    queries = (jnp.dot(full_in, w_query, preferred_element_type=jnp.float32) + b_query).astype(
        jnp.bfloat16
    )
    keys_loc = jnp.dot(full_in, w_key, preferred_element_type=jnp.float32).astype(jnp.bfloat16)
    vals_loc = (jnp.dot(full_in, w_value, preferred_element_type=jnp.float32) + b_value).astype(
        jnp.bfloat16
    )
    valid = (jnp.arange(length, dtype=jnp.int32)[None, :] < lengths[:, None]).astype(jnp.float32)[
        :, :, None
    ]
    far_keys = pool_rows(
        keys_loc.reshape(seqs, length, chans).astype(jnp.float32) * valid, conv_key
    ).astype(jnp.bfloat16)
    far_vals = pool_rows(
        vals_loc.reshape(seqs, length, chans).astype(jnp.float32) * valid, conv_value
    ).astype(jnp.bfloat16)
    context, logsums = attend_forward(
        queries.reshape(seqs, length, heads, HEAD_DIM),
        keys_loc.reshape(seqs, length, heads, HEAD_DIM),
        vals_loc.reshape(seqs, length, heads, HEAD_DIM),
        far_keys.reshape(seqs, pooled_len, heads, HEAD_DIM),
        far_vals.reshape(seqs, pooled_len, heads, HEAD_DIM),
        lengths,
    )
    context = context.reshape(total_rows, chans).astype(jnp.bfloat16)
    hidden_one = resid + (row_sum(context, w_out, share) + b_out)
    normed = norm_rows(hidden_one, attn_gain, attn_shift)
    full_normed = share_rows(normed.astype(jnp.bfloat16))
    upper = jnp.dot(full_normed, w_up, preferred_element_type=jnp.float32) + b_up
    active = gelu_exact(upper).astype(jnp.bfloat16)
    hidden_two = normed + (row_sum(active, w_down, share) + b_down)
    result = norm_rows(hidden_two, ffn_gain, ffn_shift)
    kept = (
        full_in,
        queries,
        keys_loc,
        vals_loc,
        far_keys,
        far_vals,
        logsums,
        context,
        hidden_one,
        full_normed,
        upper,
        active,
        hidden_two,
    )
    return (result, kept)


def layer_backward(grad_out, kept, params, lengths, share):
    (
        w_query,
        w_key,
        w_value,
        b_query,
        b_value,
        conv_key,
        conv_value,
        w_out,
        b_out,
        attn_gain,
        attn_shift,
        w_up,
        b_up,
        w_down,
        b_down,
        ffn_gain,
        ffn_shift,
    ) = params
    (
        full_in,
        queries,
        keys_loc,
        vals_loc,
        far_keys,
        far_vals,
        logsums,
        context,
        hidden_one,
        full_normed,
        saved_upper,
        active,
        hidden_two,
    ) = kept
    seqs = lengths.shape[0]
    total_rows = full_in.shape[0]
    length = total_rows // seqs
    chans = w_query.shape[1]
    heads = chans // HEAD_DIM
    pooled_len = length // STRIDE
    unused_two, pull_two = jax.vjp(norm_rows, hidden_two, ffn_gain, ffn_shift)
    grad_h2, grad_fgain, grad_fshift = pull_two(grad_out)
    grad_ffn = grad_h2.astype(jnp.bfloat16)
    grad_bdown = jnp.sum(grad_ffn.astype(jnp.float32), axis=0)
    full_gffn = share_back(grad_ffn)
    grad_wdown = jnp.einsum("tf,td->fd", active, full_gffn, preferred_element_type=jnp.float32)
    grad_active = jnp.einsum("td,fd->tf", full_gffn, w_down, preferred_element_type=jnp.float32)
    unused_gelu, pull_gelu = jax.vjp(gelu_exact, saved_upper)
    grad_upper = pull_gelu(grad_active)[0].astype(jnp.bfloat16)
    grad_bup = jnp.sum(grad_upper.astype(jnp.float32), axis=0)
    grad_wup = jnp.einsum("td,tf->df", full_normed, grad_upper, preferred_element_type=jnp.float32)

    def up_term(start, count):
        return jnp.einsum("tf,df->td", grad_upper, w_up, preferred_element_type=jnp.float32)

    grad_y1 = grad_h2 + back_sum(up_term, share)
    unused_one, pull_one = jax.vjp(norm_rows, hidden_one, attn_gain, attn_shift)
    grad_h1, grad_again, grad_ashift = pull_one(grad_y1)
    grad_attn = grad_h1.astype(jnp.bfloat16)
    grad_bout = jnp.sum(grad_attn.astype(jnp.float32), axis=0)
    full_gattn = share_back(grad_attn)
    grad_wout = jnp.einsum("tc,td->cd", context, full_gattn, preferred_element_type=jnp.float32)
    grad_context = jnp.einsum("td,cd->tc", full_gattn, w_out, preferred_element_type=jnp.float32)
    valid = (jnp.arange(length, dtype=jnp.int32)[None, :] < lengths[:, None]).astype(jnp.float32)[
        :, :, None
    ]
    grad_context = (grad_context.reshape(seqs, length, chans) * valid).astype(jnp.bfloat16)
    grad_q, grad_near_k, grad_near_v, grad_far_k, grad_far_v = attend_backward(
        queries.reshape(seqs, length, heads, HEAD_DIM),
        keys_loc.reshape(seqs, length, heads, HEAD_DIM),
        vals_loc.reshape(seqs, length, heads, HEAD_DIM),
        far_keys.reshape(seqs, pooled_len, heads, HEAD_DIM),
        far_vals.reshape(seqs, pooled_len, heads, HEAD_DIM),
        lengths,
        logsums,
        grad_context.reshape(seqs, length, heads, HEAD_DIM),
    )
    masked_keys = keys_loc.reshape(seqs, length, chans).astype(jnp.float32) * valid
    masked_vals = vals_loc.reshape(seqs, length, chans).astype(jnp.float32) * valid
    unused_pk, pull_key = jax.vjp(pool_rows, masked_keys, conv_key)
    grad_kpool, grad_ckey = pull_key(grad_far_k.reshape(seqs, pooled_len, chans))
    unused_pv, pull_val = jax.vjp(pool_rows, masked_vals, conv_value)
    grad_vpool, grad_cval = pull_val(grad_far_v.reshape(seqs, pooled_len, chans))
    grad_queries = grad_q.reshape(total_rows, chans).astype(jnp.bfloat16)
    grad_keys = (
        (grad_near_k.reshape(seqs, length, chans) + grad_kpool * valid)
        .reshape(total_rows, chans)
        .astype(jnp.bfloat16)
    )
    grad_vals = (
        (grad_near_v.reshape(seqs, length, chans) + grad_vpool * valid)
        .reshape(total_rows, chans)
        .astype(jnp.bfloat16)
    )
    grad_wquery = jnp.einsum("td,tc->dc", full_in, grad_queries, preferred_element_type=jnp.float32)
    grad_wkey = jnp.einsum("td,tc->dc", full_in, grad_keys, preferred_element_type=jnp.float32)
    grad_wvalue = jnp.einsum("td,tc->dc", full_in, grad_vals, preferred_element_type=jnp.float32)
    grad_bquery = jnp.sum(grad_queries.astype(jnp.float32), axis=0)
    grad_bvalue = jnp.sum(grad_vals.astype(jnp.float32), axis=0)

    def input_term(start, count):
        total = jnp.einsum("tc,dc->td", grad_queries, w_query, preferred_element_type=jnp.float32)
        total = total + jnp.einsum(
            "tc,dc->td", grad_keys, w_key, preferred_element_type=jnp.float32
        )
        return total + jnp.einsum(
            "tc,dc->td", grad_vals, w_value, preferred_element_type=jnp.float32
        )

    grad_input = grad_h1 + back_sum(input_term, share)
    matrices = (
        grad_wquery[None],
        grad_wkey[None],
        grad_wvalue[None],
        grad_wout[None],
        grad_wup[None],
        grad_wdown[None],
    )
    vectors = (
        spread(grad_bquery, D)[None],
        spread(grad_bvalue, D)[None],
        spread(grad_ckey, D)[None],
        spread(grad_cval, D)[None],
        grad_bout[None],
        grad_again[None],
        grad_ashift[None],
        spread(grad_bup, FF)[None],
        grad_bdown[None],
        grad_fgain[None],
        grad_fshift[None],
    )
    return (grad_input, matrices, vectors)


def on_device(
    tokens,
    lengths,
    w_query,
    w_key,
    w_value,
    b_query,
    b_value,
    conv_key,
    conv_value,
    w_out,
    b_out,
    attn_gain,
    attn_shift,
    w_up,
    b_up,
    w_down,
    b_down,
    ffn_gain,
    ffn_shift,
    cotangent,
):
    stacks = (
        w_query,
        w_key,
        w_value,
        b_query,
        b_value,
        conv_key,
        conv_value,
        w_out,
        b_out,
        attn_gain,
        attn_shift,
        w_up,
        b_up,
        w_down,
        b_down,
        ffn_gain,
        ffn_shift,
    )
    total_rows = tokens.shape[0]
    share = total_rows // lax.axis_size("mp")
    place = lax.axis_index("mp") * share
    resid = lax.dynamic_slice_in_dim(tokens, place, share, 0).astype(jnp.float32)
    layer = 0
    params = tuple((stack[layer] for stack in stacks))
    result, kept = layer_forward(tokens, resid, lengths, params, share)
    kept_all = [kept]
    activations = result.astype(jnp.bfloat16)
    grad_out = cotangent.astype(jnp.float32)
    matrix_list = [None] * LAYERS
    vector_list = [None] * LAYERS
    for layer in reversed(range(LAYERS)):
        params = tuple((stack[layer] for stack in stacks))
        grad_out, matrices, vectors = layer_backward(
            grad_out, kept_all[layer], params, lengths, share
        )
        matrix_list[layer] = matrices
        vector_list[layer] = vectors
    grad_wquery, grad_wkey, grad_wvalue, grad_wout, grad_wup, grad_wdown = tuple(
        (jnp.concatenate([entry[index] for entry in matrix_list], axis=0) for index in range(6))
    )
    (
        grad_bquery,
        grad_bvalue,
        grad_ckey,
        grad_cval,
        grad_bout,
        grad_again,
        grad_ashift,
        grad_bup,
        grad_bdown,
        grad_fgain,
        grad_fshift,
    ) = tuple(
        (jnp.concatenate([entry[index] for entry in vector_list], axis=0) for index in range(11))
    )
    grad_wquery, grad_wkey, grad_wvalue, grad_wout, grad_wup, grad_wdown = (
        lax.psum_scatter(grad_wquery, "dp", scatter_dimension=1, tiled=True),
        lax.psum_scatter(grad_wkey, "dp", scatter_dimension=1, tiled=True),
        lax.psum_scatter(grad_wvalue, "dp", scatter_dimension=1, tiled=True),
        lax.psum_scatter(grad_wout, "dp", scatter_dimension=2, tiled=True),
        lax.psum_scatter(grad_wup, "dp", scatter_dimension=1, tiled=True),
        lax.psum_scatter(grad_wdown, "dp", scatter_dimension=2, tiled=True),
    )
    (
        grad_bquery,
        grad_bvalue,
        grad_ckey,
        grad_cval,
        grad_bout,
        grad_again,
        grad_ashift,
        grad_bup,
        grad_bdown,
        grad_fgain,
        grad_fshift,
    ) = lax.psum(
        (
            grad_bquery,
            grad_bvalue,
            grad_ckey,
            grad_cval,
            grad_bout,
            grad_again,
            grad_ashift,
            grad_bup,
            grad_bdown,
            grad_fgain,
            grad_fshift,
        ),
        ("dp", "mp"),
    )
    return (
        activations,
        grad_out,
        grad_wquery,
        grad_wkey,
        grad_wvalue,
        grad_bquery,
        grad_bvalue,
        grad_ckey,
        grad_cval,
        grad_wout,
        grad_bout,
        grad_again,
        grad_ashift,
        grad_wup,
        grad_bup,
        grad_wdown,
        grad_bdown,
        grad_fgain,
        grad_fshift,
    )


BF = jnp.bfloat16
F32 = jnp.float32
MESH = pl.DeviceIdType.MESH
ROWS = 256
QUARTERS = 4
CHANS = D // QUARTERS
QHEADS = CHANS // HEAD_DIM
SEQ = QUARTERS * ROWS
REACH = WINDOW // 2
PREACH = POOL_WINDOW // 2 // STRIDE
OWNP = ROWS // STRIDE
KW = ROWS + 2 * REACH
KP = OWNP + 2 * PREACH
KEYS = KW + KP
QB = 128
NEAR = QB + 2 * REACH
FAR = QB // STRIDE + 2 * PREACH
COMP = 800
HALFC = COMP // 2
FRONT = 256
KVROWS = 1408
BASE = 288
PIECE = D // 8
BIG_NEG = -1e30
SCALE = HEAD_DIM ** -0.5
VROWS = 64
TILES = 2 * CHANS // 128


def nn(a, b):
    return jnp.dot(a, b, preferred_element_type=F32)


def nt(a, b):
    return lax.dot_general(a, b, (((1,), (1,)), ((), ())), preferred_element_type=F32)


def tn(a, b):
    return lax.dot_general(a, b, (((0,), (0,)), ((), ())), preferred_element_type=F32)


def rows_iota(rows, cols):
    return lax.broadcasted_iota(jnp.int32, (rows, cols), 0)


def cols_iota(rows, cols):
    return lax.broadcasted_iota(jnp.int32, (rows, cols), 1)


def mean_row(v):
    return jnp.mean(v, axis=-1, keepdims=True)


def sum_col(v):
    return jnp.sum(v, axis=0, keepdims=True)


def kernel(
    len_hbm, tok_hbm, wk, wv, wq, wo, wup, wdown, bq_h, bv_h, ck_h, cv_h, bup_h, bo_h, ag_h, ash_h, bd_h, fg_h, fs_h, cot_hbm,
    act_hbm, gtok_hbm, gmats_hbm, gvec_hbm,
    W, VEC, kvf, KV, KVS, Q, CTX, P, maskn, maskf, n1, r1, y1, y1b, dg, av,
    yT, fT, gab, GKV, pt, GQ, VG,
    CR, S1, S2, ZR, ZF, HL, HR, HLL, SL, SR, GVR, GVZ, VO, tok, cot,
    len_ref, bq, bv, ck, cv, bup, bo, ag, ash, bd, fg, fs, act_out, gtok, gmats,
    ssem, osem, lsem, asend, arecv, zsend, zrecv, lsend, hsend, hrecv, rsend, rrecv, zsum, zfsum, gsend, grecv,
):
    acc, n2, xT, gub = gtok, y1, yT, y1b
    dp = lax.axis_index("dp")
    z = lax.axis_index("mp")
    c = lax.rem(dp, 2)
    x = lax.rem(lax.div(dp, 2), 2)
    y = lax.div(dp, 4)
    core = (dp + 1 - 2 * c, z)
    xdev = (dp + 2 - 4 * x, z)
    ydev = (dp + 4 - 8 * y, z)
    yx = 2 * y + x

    def zdev(step):
        return (dp, lax.rem(z + step, QUARTERS))

    def rcopy(src, dst, ssem, rsem, dev):
        return pltpu.make_async_remote_copy(
            src_ref=src, dst_ref=dst, send_sem=ssem, recv_sem=rsem,
            device_id=dev, device_id_type=MESH,
        )

    barrier = pltpu.get_barrier_semaphore()
    for dev in (core, xdev, ydev, zdev(1), zdev(2), zdev(3)):
        pl.semaphore_signal(barrier, inc=1, device_id=dev, device_id_type=MESH)

    def loads():
        parts = [(wk, 0), (wv, CHANS), (wq, 2 * CHANS), (wo, 3 * CHANS)]
        copies = [
            pltpu.make_async_copy(src, W.at[0, z, at : at + CHANS, :], lsem.at[0])
            for src, at in parts
        ]
        copies.append(pltpu.make_async_copy(wup, W.at[1, z], lsem.at[1]))
        copies.append(pltpu.make_async_copy(wdown, W.at[2, z], lsem.at[2]))
        return copies

    small = [
        pltpu.make_async_copy(src, dst, ssem.at[i])
        for i, (src, dst) in enumerate(
            (
                (bup_h, bup), (bv_h, bv), (bq_h, bq), (ck_h, ck), (cv_h, cv), (len_hbm, len_ref),
                (bo_h, bo), (ag_h, ag), (ash_h, ash), (bd_h, bd), (fg_h, fg), (fs_h, fs),
            )
        )
    ]
    outs = [
        pltpu.make_async_copy(src, dst, osem.at[i])
        for i, (src, dst) in enumerate(
            (
                (act_out, act_hbm), (gtok, gtok_hbm), (gmats.at[0], gmats_hbm.at[0]),
                (gmats.at[1], gmats_hbm.at[1]), (gmats.at[2], gmats_hbm.at[2]), (VO, gvec_hbm),
            )
        )
    ]
    for cp in small[:6]:
        cp.start()
    own = loads()
    tok_in = pltpu.make_async_copy(tok_hbm, tok, lsem.at[3])
    cot_in = pltpu.make_async_copy(cot_hbm, cot, lsem.at[4])
    for cp in own:
        cp.start()
    tok_in.start()
    for cp in small[6:]:
        cp.start()
    cot_in.start()
    for cp in small[:6]:
        cp.wait()
    length = len_ref[0]
    vpack = VG.at[0:8, :]
    vpack[...] = jnp.zeros_like(vpack)
    vpack[0:1, :] = bup[...]
    vpack[1:2, CHANS : 2 * CHANS] = bv[...]
    vpack[1:2, 2 * CHANS : 3 * CHANS] = bq[...]
    for t in range(5):
        vpack[2 + t : 3 + t, 0:CHANS] = ck[t]
        vpack[2 + t : 3 + t, CHANS : 2 * CHANS] = cv[t]
    VEC[z] = vpack[...]
    pl.semaphore_wait(barrier, 6)

    def block(j):
        return pl.ds(pl.multiple_of(j * PIECE, PIECE), PIECE)

    piece_me = c * 4 + yx
    piece_x = c * 4 + 2 * y + 1 - x
    piece_y = c * 4 + 2 * (1 - y) + x
    piece_d = c * 4 + 2 * (1 - y) + 1 - x
    LO, HI = pl.ds(0, D // 2), pl.ds(D // 2, D // 2)
    ALL = pl.ds(0, D)
    CHUNKS = 9
    ends = [(0, 1), (1, 1), (0, 2), (1, 2), (0, 3), (2, 1), (2, 2), (1, 3), (2, 3)]
    inner = [(0, 1), (0, 2), (1, 1), (1, 2), (0, 3), (2, 1), (2, 2), (1, 3), (2, 3)]
    sources = [(1, 2, 3), (2, 0, 3), (1, 3, 0), (2, 1, 0)]
    targets = [(3, 2, 1, 0), (3, 0, 2, 1), (0, 3, 1, 2), (0, 1, 2, 3)]
    DOWN = 2
    FAR_STEPS = 2
    at_end = (z == 0) | (z == QUARTERS - 1)

    def table(values, bits=2):
        word = sum(v << (bits * i) for i, v in enumerate(values))
        return jnp.int32(word - (1 << 32) if word >> 31 else word)

    def lookup(word, i, bits=2):
        return lax.bitwise_and(lax.shift_right_logical(word, bits * i), (1 << bits) - 1)

    def by_place(a, b):
        return lax.select(at_end, a, b)

    mats_of = by_place(table(m for m, d in ends), table(m for m, d in inner))
    dist_of = by_place(table(d for m, d in ends), table(d for m, d in inner))
    looks_of = by_place(table((1, 2, 4, 5, 6, 7, 8, 9), 4), table((2, 4, 5, 7, 8, 9, 9, 9), 4))
    sends_of = by_place(table((1, 2, 4, 5, 6, 7, 8, 9), 4), table((2, 3, 4, 5, 6, 7, 8, 9), 4))

    def source(d):
        return lookup(table(v for row in sources for v in row), 3 * z + d - 1)

    def target(t):
        return lookup(table(v for row in targets for v in row), 4 * z + t)

    def chunk(k):
        return lookup(mats_of, k), source(lookup(dist_of, k))

    def is_far(k):
        return (lookup(mats_of, k) == DOWN) & (lookup(dist_of, k) < FAR_STEPS)

    def own_block(m, up, piece, sem):
        src = W.at[m, z, block(piece), :]
        return rcopy(src, src, zsend.at[0, up], zrecv.at[sem, z], (dp, z + 2 * up - 1))

    def own_z(m, up):
        return own_block(m, up, piece_me, m)

    def far_z(up):
        return own_block(DOWN, up, piece_d, 4)

    def wants_far(up):
        to = z + 2 * up - 1
        inner_to = (to == 1) | (to == 2)
        return jnp.logical_not(inner_to) | (z == 3 - to)

    def relay(m, src, dev):
        ref = W.at[m, src, block(piece_me), :]
        return rcopy(ref, ref, lsend.at[0], zrecv.at[m, src], dev)

    def relay_far(src, dev):
        ref = W.at[DOWN, src, block(piece_d), :]
        return rcopy(ref, ref, lsend.at[0], zrecv.at[4, src], dev)

    def own_vec(up):
        src = VEC.at[z]
        return rcopy(src, src, zsend.at[1, up], zrecv.at[3, z], (dp, z + 2 * up - 1))

    def relay_vec(src, dev):
        ref = VEC.at[src]
        return rcopy(ref, ref, lsend.at[1], zrecv.at[3, src], dev)

    def onward(src):
        return jnp.where(src > z, z > 0, z < QUARTERS - 1)

    def next_dev(src):
        return (dp, jnp.where(src > z, z - 1, z + 1))

    def plane(k, which, piece, cols, dev):
        m, src = chunk(k)
        ref = W.at[m, src, block(piece), cols]
        return rcopy(ref, ref, asend.at[k], arecv.at[k, (which - 1) // 2], dev)

    def look(k):
        m, src = chunk(k)

        @pl.when(m == 0)
        def _():
            relay_vec(src, core).wait_recv()
            pl.when(onward(src))(lambda: relay_vec(src, next_dev(src)).start())

        relay(m, src, core).wait_recv()
        pl.when(onward(src))(lambda: relay(m, src, next_dev(src)).start())

        @pl.when(is_far(k))
        def _():
            relay_far(src, core).wait_recv()

        pl.when(at_end)(lambda: first(k))

    LAST_CHUNK = CHUNKS - 1

    def cross_piece(k, piece):
        m, src = chunk(k)
        ref = W.at[m, src, block(piece), :]
        return rcopy(ref, ref, asend.at[k], arecv.at[k, 2], core)

    def first(k):
        plane(k, 1, piece_me, ALL, xdev).start()
        plane(k, 2, piece_me, ALL, ydev).start()
        pl.when(k == LAST_CHUNK)(lambda: cross_piece(k, piece_me).start())

    def rows_of(count):
        return W.at[0, 0, 0:count, :]

    def wait_rows(sem, count):
        pltpu.make_async_copy(rows_of(count), rows_of(count), sem).wait()

    def second(k):
        wait_rows(arecv.at[k, 0], 2 * PIECE)

        @pl.when(jnp.logical_not(is_far(k)))
        def _():
            plane(k, 3, piece_x, LO, ydev).start()
            plane(k, 4, piece_y, HI, xdev).start()

        @pl.when(k == LAST_CHUNK)
        def _():
            cross_piece(k, piece_x).start()
            cross_piece(k, piece_y).start()

    def half(j):
        return pl.ds(pl.multiple_of(j * (D // 2), D // 2), D // 2)

    def cross(k, j):
        m, src = chunk(k)
        ref = W.at[m, src, half(j), :]
        return rcopy(ref, ref, asend.at[k], arecv.at[k, 2], core)

    def third(k):
        pl.when(jnp.logical_not(is_far(k)))(lambda: wait_rows(arecv.at[k, 1], PIECE))
        pl.when(k < LAST_CHUNK)(lambda: cross(k, c).start())
        pl.when(k == LAST_CHUNK)(lambda: cross_piece(k, piece_d).start())

    def fourth(k):
        cross(k, 1 - c).wait_recv()

    def looks(i):
        return jnp.where(i < 0, 0, lookup(looks_of, lax.clamp(0, i, 7), 4))

    def sends(i):
        return jnp.where(i < 0, 0, lookup(sends_of, lax.clamp(0, i, 7), 4))

    def each(fn):
        def body(k, carry):
            fn(k)
            return carry

        return body

    def gather_slot(i, carry):
        lax.fori_loop(looks(i - 1), looks(i), each(look), 0)
        pl.when((i == 2) & jnp.logical_not(at_end))(lambda: both(own_down))
        lo = jnp.where(at_end, sends(i), sends(i - 1))
        lax.fori_loop(lo, sends(i), each(first), 0)
        for lag, stage in ((1, second), (2, third), (3, fourth)):
            k = i - lag
            pl.when((k >= 0) & (k < CHUNKS))(lambda stage=stage, k=k: stage(k))
        return carry

    def gather_done(k, carry):
        m, src = chunk(k)

        far = is_far(k)
        pl.when(far)(lambda: wait_rows(asend.at[k], 6 * PIECE))
        pl.when(jnp.logical_not(far))(lambda: wait_rows(asend.at[k], 7 * PIECE))
        return carry

    def got(s):
        return lax.rem(z + QUARTERS - s, QUARTERS)

    def both(fn):
        pl.when(z > 0)(lambda: fn(0))
        pl.when(z < QUARTERS - 1)(lambda: fn(1))

    both(lambda up: own_vec(up).start())
    for m in range(3):
        pltpu.make_async_copy(W.at[m, z], W.at[m, z], lsem.at[m]).wait()
        if m != DOWN:
            both(lambda up: own_z(m, up).start())

    def own_down(up):
        own_z(DOWN, up).start()
        pl.when(wants_far(up))(lambda: far_z(up).start())

    pl.when(at_end)(lambda: both(own_down))

    def own_sent(up):
        own_vec(up).wait_send()
        far = wants_far(up)
        pl.when(far)(lambda: wait_rows(zsend.at[0, up], 4 * PIECE))
        pl.when(jnp.logical_not(far))(lambda: wait_rows(zsend.at[0, up], 3 * PIECE))

    base = z * ROWS
    start = lax.select(z < 2, jnp.int32(0), jnp.int32(SEQ - COMP))
    place = pl.multiple_of(start - base + BASE + FRONT, 32)
    start = pl.multiple_of(start, 32)
    kvf[...] = jnp.zeros_like(kvf)
    for b in range(2):
        i = base + b * QB + cols_iota(1, QB)
        j = base - REACH + b * QB + rows_iota(NEAR, 1)
        ok = (jnp.abs(i - j) <= REACH) & (j >= 0) & (j < length)
        maskn[b] = jnp.where(ok, 0.0, BIG_NEG)
        j = (OWNP * z - PREACH + b * (QB // STRIDE) + rows_iota(FAR, 1)) * STRIDE
        ok = (jnp.abs(i - j) <= POOL_WINDOW // 2) & (j >= 0) & (j < length)
        maskf[b] = jnp.where(ok, 0.0, BIG_NEG)
    own_rows = pl.ds(pl.multiple_of(base, ROWS), ROWS)
    tok_in.wait()
    cot_in.wait()
    for cp in small[6:]:
        cp.wait()
    xb = tok[own_rows, :]
    acc[...] = jnp.zeros_like(acc)

    def taps(zq, t):
        return VEC[zq, 2 + t : 3 + t, 0 : 2 * CHANS]

    def strided(t):
        at = pl.ds(FRONT + BASE - POOL_WINDOW // 2 - 2 + t, KP, stride=STRIDE)
        return jnp.concatenate([kvf[i, at, :] for i in range(TILES)], axis=1)

    def tile(i):
        return slice(i * 128, (i + 1) * 128)

    def window(lo, rows):
        return jnp.concatenate([kvf[i, lo : lo + rows, :] for i in range(TILES)], axis=1)

    def quarter(s):
        return lax.select(s == 0, z, source(lax.max(s, 1)))

    def attend(s, carry):
        zq = quarter(s)
        for blk in range(2):
            xr = tok[pl.ds(pl.multiple_of(start + blk * HALFC, 16), HALFC), :]
            kv = nt(xr, W[0, zq, 0 : 2 * CHANS, :]) + VEC[zq, 1:2, 0 : 2 * CHANS]
            pos = start + blk * HALFC + rows_iota(HALFC, 1)
            kvb = jnp.where(pos < length, kv.astype(BF).astype(F32), 0.0)
            for i in range(TILES):
                kvf[i, pl.ds(pl.multiple_of(place + blk * HALFC, 8), HALFC), :] = kvb[:, tile(i)]
        KVS[zq] = window(FRONT, COMP).astype(BF)
        KV[zq, 0:KW, :] = window(FRONT + BASE - REACH, KW).astype(BF)
        pooled = jnp.zeros((KP, 2 * CHANS), F32)
        for t in range(5):
            pooled = pooled + taps(zq, t) * strided(t)
        KV[zq, KW:KEYS, :] = pooled.astype(BF)
        qz = nt(xb, W[0, zq, 2 * CHANS : 3 * CHANS, :]) + VEC[zq, 1:2, 2 * CHANS : 3 * CHANS]
        Q[zq] = qz.astype(BF)
        for b in range(2):
            live = base + b * QB + cols_iota(1, QB) < length
            n0, f0 = b * QB, KW + b * (QB // STRIDE)
            for h in range(QHEADS):
                kl = slice(h * HEAD_DIM, (h + 1) * HEAD_DIM)
                vl = slice(CHANS + h * HEAD_DIM, CHANS + (h + 1) * HEAD_DIM)
                qh = Q[zq, b * QB : (b + 1) * QB, kl]
                sn = nt(KV[zq, n0 : n0 + NEAR, kl], qh) * SCALE + maskn[b]
                sf = nt(KV[zq, f0 : f0 + FAR, kl], qh) * SCALE + maskf[b]
                peak = jnp.maximum(
                    jnp.max(sn, axis=0, keepdims=True), jnp.max(sf, axis=0, keepdims=True)
                )
                en, ef = jnp.exp(sn - peak), jnp.exp(sf - peak)
                inv = 1.0 / (sum_col(en) + sum_col(ef))
                pn, pf = en * inv, ef * inv
                P[zq, h, b, 0:NEAR, :] = pn
                P[zq, h, b, NEAR : NEAR + FAR, :] = pf
                ct = tn(KV[zq, n0 : n0 + NEAR, vl], pn.astype(BF))
                ct = ct + tn(KV[zq, f0 : f0 + FAR, vl], pf.astype(BF))
                ct = jnp.where(live, ct, 0.0)
                CTX[zq, b * QB : (b + 1) * QB, kl] = ct.T.astype(BF)
        acc[...] += nn(CTX[zq], W[0, zq, 3 * CHANS : D, :])
        lax.fori_loop(lookup_slots(s), lookup_slots(s + 1), gather_slot, 0)
        return carry

    def lookup_slots(s):
        return jnp.where(s == 0, 0, jnp.where(s < 3, 2 + 2 * s, 8))

    lax.fori_loop(0, QUARTERS, attend, 0)

    def store_T(dst, v, cols):
        vt = v.T.astype(BF)
        for j in range(8):
            to = (j % 2) * 4 + j // 2
            dst[to * PIECE : (to + 1) * PIECE, cols] = vt[j * PIECE : (j + 1) * PIECE]

    def span(i, size):
        if isinstance(i, int):
            return pl.ds(i * size, size)
        return pl.ds(pl.multiple_of(i * size, size), size)

    def norm_one(i, carry):
        rows = span(i, QB)
        res = tok[pl.ds(pl.multiple_of(base + i * QB, QB), QB), :].astype(F32)
        hid = res + (acc[rows, :] + bo[...])
        cen = hid - mean_row(hid)
        r = lax.rsqrt(mean_row(cen * cen) + epsilon)
        n = cen * r
        n1[rows, :] = n
        r1[rows, :] = r
        out = n * ag[...] + ash[...]
        y1[rows, :] = out
        y1b[rows, :] = out.astype(BF)
        store_T(yT, out, rows)
        acc[rows, :] = jnp.zeros_like(out)
        return carry

    lax.fori_loop(0, ROWS // QB, norm_one, 0)

    def most_gathered():
        lax.fori_loop(0, CHUNKS - 1, gather_done, 0)

    def feed(s, carry):
        zq = quarter(s)

        def up(i, carry):
            cols = span(i, ROWS)
            u = nn(y1b[...], W[1, zq, :, cols]) + VEC[zq, 0:1, cols]
            cdf = 0.5 * (1.0 + lax.erf(u * (0.5 ** 0.5)))
            dg[zq, :, cols] = cdf + u * jnp.exp(-0.5 * u * u) * ((2.0 * 3.141592653589793) ** -0.5)
            av[zq, :, cols] = (u * cdf).astype(BF)
            return carry

        for i in range(D // ROWS):
            up(i, 0)
        pl.when(s == QUARTERS - 1)(most_gathered)
        lax.fori_loop(8 + s, 9 + s, gather_slot, 0)
        acc[...] += nn(av[zq], W[2, zq])
        return carry

    lax.fori_loop(0, QUARTERS, feed, 0)
    VG[...] = jnp.zeros_like(VG)
    GEN = 8 * QUARTERS

    def add_row(row, v):
        VG[row : row + 1, :] += sum_col(v)

    def norm_two(i, carry):
        rows = span(i, QB)
        hid = y1[rows, :] + (acc[rows, :] + bd[...])
        cen = hid - mean_row(hid)
        r = lax.rsqrt(mean_row(cen * cen) + epsilon)
        n = cen * r
        act_out[rows, :] = (n * fg[...] + fs[...]).astype(BF)
        g = cot[rows, :].astype(F32)
        add_row(GEN + 4, g * n)
        add_row(GEN + 5, g)
        e = g * fg[...]
        gh2 = r * (e - mean_row(e) - n * mean_row(e * n))
        acc[rows, :] = gh2
        gf = gh2.astype(BF)
        gab[rows, :] = gf
        gff = gf.astype(F32)
        add_row(GEN + 3, gff)
        store_T(fT, gff, rows)
        return carry

    lax.fori_loop(0, ROWS // QB, norm_two, 0)
    outs[0].start()

    PARTS = 12

    def part(r):
        m = lax.select(r < 8, 2 - lax.rem(r, 2), 0)
        t = lax.select(r < 8, lax.div(r, 2), r - 8)
        return m, t

    def r_core(r):
        m, t = part(r)
        src = W.at[m, target(t), half(1 - c), :]
        return rcopy(src, CR.at[r], rsend.at[r], rrecv.at[r, 0], core)

    def blk4(r, yy, xx, cols):
        return CR.at[r, block(2 * yy + xx), cols]

    THIRD = D // 3
    wide = (LO, HI, D // 2, ALL)
    thin = (pl.ds(0, THIRD), pl.ds(THIRD, THIRD), THIRD, pl.ds(0, 2 * THIRD))
    LAST = pl.ds(2 * THIRD, THIRD)
    OWN_DOWN = 6

    def narrow(r):
        m, t = part(r)
        return (m == DOWN) & (t < QUARTERS - 1)

    def by_width(r, fn):
        pl.when(narrow(r))(lambda: fn(thin))
        pl.when(jnp.logical_not(narrow(r)))(lambda: fn(wide))

    def r_stage1(r, i, cut):
        if i < 2:
            src, dev = blk4(r, i, 1 - x, cut[0]), xdev
        else:
            src, dev = blk4(r, 1 - y, i - 2, cut[1]), ydev
        return rcopy(src, S1.at[r, i, :, 0 : cut[2]], rsend.at[r], rrecv.at[r, 1], dev)

    def r_stage2(r, i, cut):
        if i == 0:
            src, dev = blk4(r, 1 - y, x, cut[0]), ydev
        else:
            src, dev = blk4(r, y, 1 - x, cut[1]), xdev
        return rcopy(src, S2.at[r, i, :, 0 : cut[2]], rsend.at[r], rrecv.at[r, 2], dev)

    def onto(r):
        dst = target(part(r)[1])
        left = dst < z
        slot = jnp.where(left & (dst == z - 1), QUARTERS, dst)
        return slot, (dp, jnp.where(left, z - 1, z + 1))

    def r_z(r, cut):
        slot, dev = onto(r)
        m = part(r)[0]
        src = CR.at[r, block(yx), cut[3]]
        return rcopy(src, ZR.at[m, slot, :, cut[3]], rsend.at[r], zsum.at[m, slot], dev)

    def z_wait(m, slot, cut):
        ref = ZR.at[m, slot, :, cut[3]]
        pltpu.make_async_copy(ref, ref, zsum.at[m, slot]).wait()

    def r_zf(r):
        slot, dev = onto(r)
        return rcopy(CR.at[r, :, LAST], ZF.at[slot], rsend.at[r], zfsum.at[slot], dev)

    def take_zf(r, slot):
        ref = ZF.at[slot]
        pltpu.make_async_copy(ref, ref, zfsum.at[slot]).wait()
        CR[r, :, LAST] = CR[r, :, LAST] + ZF[slot]

    def upstream(dst):
        return jnp.where(dst < z, z < QUARTERS - 1, z > 0)

    def reduce1(r):
        m, t = part(r)
        r_core(r).wait_recv()
        zq = target(t)

        def add(i, carry):
            CR[r, block(i), :] = CR[r, block(i), :] + W[m, zq, block(4 * c + i), :]
            return carry

        lax.fori_loop(0, 4, add, 0)

        @pl.when(r == OWN_DOWN)
        def _():
            pl.when(z > 0)(lambda: take_zf(r, z))
            pl.when(z < QUARTERS - 1)(lambda: take_zf(r, jnp.int32(QUARTERS)))

        def go(cut):
            for i in range(4):
                r_stage1(r, i, cut).start()

        by_width(r, go)
        pl.when(narrow(r) & jnp.logical_not(upstream(zq)))(lambda: r_zf(r).start())

    def reduce_f(r):
        dst = target(part(r)[1])

        @pl.when(upstream(dst))
        def _():
            take_zf(r, dst)
            r_zf(r).start()

    def reduce2(r):
        def go(cut):
            ref = S1.at[r, :, :, 0 : cut[2]]
            pltpu.make_async_copy(ref, ref, rrecv.at[r, 1]).wait()
            for i in range(2):
                a = blk4(r, i, x, cut[0])
                a[...] = a[...] + S1[r, i, :, 0 : cut[2]]
                a = blk4(r, y, i, cut[1])
                a[...] = a[...] + S1[r, 2 + i, :, 0 : cut[2]]
            for i in range(2):
                r_stage2(r, i, cut).start()

        by_width(r, go)

    def reduce3(r):
        dst = target(part(r)[1])

        def go(cut):
            ref = S2.at[r, :, :, 0 : cut[2]]
            pltpu.make_async_copy(ref, ref, rrecv.at[r, 2]).wait()
            for i in range(2):
                a = blk4(r, y, x, cut[i])
                a[...] = a[...] + S2[r, i, :, 0 : cut[2]]
            pl.when((dst != z) & jnp.logical_not(upstream(dst)))(lambda: r_z(r, cut).start())

        by_width(r, go)

    def reduce4(r):
        m, t = part(r)
        dst = target(t)

        def go(cut):
            @pl.when((dst != z) & upstream(dst))
            def _():
                z_wait(m, dst, cut)
                a = CR.at[r, block(yx), cut[3]]
                a[...] = a[...] + ZR[m, dst, :, cut[3]]
                r_z(r, cut).start()

        by_width(r, go)

    def stage(fn, ok, r):
        pl.when(ok)(lambda: fn(r))

    def weight_grad(left, right, dst, width):
        dst[:, 0:width] = nn(left[...], right).astype(BF)

    def feed_back(s, carry):
        zq = target(s)
        vrow = pl.multiple_of(8 * zq, 8)

        def hidden(i, carry):
            cols = span(i, ROWS)
            gact = nt(gab[...], W[2, zq, cols, :])
            gu = (gact * dg[zq, :, cols]).astype(BF)
            gub[:, cols] = gu
            VG[pl.ds(vrow, 1), cols] = sum_col(gu.astype(F32))
            return carry

        for i in range(D // ROWS):
            hidden(i, 0)
        weight_grad(fT, av[zq], W.at[2, zq], D)
        r_core(2 * s).start()
        acc[...] += nt(gub[...], W[1, zq])
        weight_grad(yT, gub[...], W.at[1, zq], D)
        r_core(2 * s + 1).start()
        reduce1(jnp.where(s < 2, s, s + 1))
        stage(reduce1, s == 1, jnp.int32(2))
        stage(reduce2, s == 3, jnp.int32(0))
        return carry

    gather_done(jnp.int32(LAST_CHUNK), 0)
    both(own_sent)

    @pl.when(jnp.logical_not(at_end))
    def _():
        pieces = W.at[:, 0, 0 : 3 * PIECE, :]
        pltpu.make_async_copy(pieces, pieces, lsend.at[0]).wait()
        vecs = VEC.at[0 : QUARTERS - 1]
        pltpu.make_async_copy(vecs, vecs, lsend.at[1]).wait()

    lax.fori_loop(0, QUARTERS, feed_back, 0)

    def norm_back(i, carry):
        rows = span(i, QB)
        gy = acc[rows, :]
        n = n1[rows, :]
        add_row(GEN + 1, gy * n)
        add_row(GEN + 2, gy)
        e = gy * ag[...]
        gh1 = r1[rows, :] * (e - mean_row(e) - n * mean_row(e * n))
        acc[rows, :] = gh1
        ga = gh1.astype(BF)
        gab[rows, :] = ga
        gaf = ga.astype(F32)
        add_row(GEN, gaf)
        store_T(fT, gaf, rows)
        store_T(xT, tok[pl.ds(pl.multiple_of(base + i * QB, QB), QB), :].astype(F32), rows)
        return carry

    lax.fori_loop(0, ROWS // QB, norm_back, 0)

    def hl(zq):
        return rcopy(SL.at[zq], HL.at[zq], hsend.at[0], hrecv.at[0, zq], zdev(3))

    def hr(zq):
        return rcopy(SR.at[zq], HR.at[zq], hsend.at[1], hrecv.at[1, zq], zdev(1))

    def hll(zq):
        return rcopy(
            SL.at[zq, REACH : REACH + 16, :], HLL.at[zq], hsend.at[2], hrecv.at[2, zq], zdev(2)
        )

    def attend_back(s, carry):
        zq = lookup(table((3, 0, 2, 1)), s)
        gc = nt(gab[...], W[0, zq, 3 * CHANS : D, :])
        alive = base + rows_iota(ROWS, 1) < length
        gcb = jnp.where(alive, gc, 0.0).astype(BF)
        GKV[zq] = jnp.zeros((KEYS, 2 * CHANS), F32)
        for b in range(2):
            n0, f0 = b * QB, KW + b * (QB // STRIDE)
            for h in range(QHEADS):
                kl = slice(h * HEAD_DIM, (h + 1) * HEAD_DIM)
                vl = slice(CHANS + h * HEAD_DIM, CHANS + (h + 1) * HEAD_DIM)
                gch = gcb[b * QB : (b + 1) * QB, kl]
                qh = Q[zq, b * QB : (b + 1) * QB, kl]
                pn = P[zq, h, b, 0:NEAR, :]
                pf = P[zq, h, b, NEAR : NEAR + FAR, :]
                gpn = nt(KV[zq, n0 : n0 + NEAR, vl], gch)
                gpf = nt(KV[zq, f0 : f0 + FAR, vl], gch)
                delta = sum_col(pn * gpn) + sum_col(pf * gpf)
                gsn = (pn * (gpn - delta)).astype(BF)
                gsf = (pf * (gpf - delta)).astype(BF)
                qt = tn(KV[zq, n0 : n0 + NEAR, kl], gsn) + tn(KV[zq, f0 : f0 + FAR, kl], gsf)
                GQ[zq, b * QB : (b + 1) * QB, 2 * CHANS + h * HEAD_DIM : 2 * CHANS + (h + 1) * HEAD_DIM] = (
                    (qt * SCALE).T.astype(BF)
                )
                GKV[zq, n0 : n0 + NEAR, kl] += nn(gsn, qh) * SCALE
                GKV[zq, f0 : f0 + FAR, kl] += nn(gsf, qh) * SCALE
                GKV[zq, n0 : n0 + NEAR, vl] += nn(pn.astype(BF), gch)
                GKV[zq, f0 : f0 + FAR, vl] += nn(pf.astype(BF), gch)
        vrow = pl.multiple_of(8 * zq, 8)
        for i in range(TILES):
            kvf[i, FRONT : FRONT + COMP, :] = KVS[zq, :, tile(i)].astype(F32)
        gp = GKV[zq, KW:KEYS, :]
        sums = jnp.concatenate(
            [jnp.zeros((1, CHANS), F32), sum_col(GKV[zq, 0:KW, CHANS : 2 * CHANS])], axis=1
        )
        far_at = (OWNP * z - PREACH + rows_iota(KP, 1)) * STRIDE
        for t in range(5):
            VG[pl.ds(vrow + 2 + t, 1), 0 : 2 * CHANS] = sum_col(gp * strided(t))
            to = far_at + (t - 2)
            inside = (to >= 0) & (to < length)
            sums = sums + taps(zq, t) * sum_col(jnp.where(inside, gp, 0.0))
        VG[pl.ds(vrow + 1, 1), CHANS : 2 * CHANS] = sums[:, CHANS : 2 * CHANS]
        VG[pl.ds(vrow + 1, 1), 2 * CHANS : 3 * CHANS] = sum_col(
            GQ[zq, :, 2 * CHANS : 3 * CHANS].astype(F32)
        )
        SL[zq, 0:REACH, :] = GKV[zq, 0:REACH, :].astype(BF)
        SL[zq, REACH : REACH + 80, :] = GKV[zq, KW : KW + 80, :].astype(BF)
        SR[zq, 0:REACH, :] = GKV[zq, KW - REACH : KW, :].astype(BF)
        SR[zq, REACH : REACH + OWNP, :] = GKV[zq, KEYS - OWNP : KEYS, :].astype(BF)
        pl.when(z > 0)(lambda: hl(zq).start())
        pl.when(z < QUARTERS - 1)(lambda: hr(zq).start())
        pl.when(z > 1)(lambda: hll(zq).start())
        stage(reduce1, s == 0, jnp.int32(5))
        reduce2(s + 1)
        stage(reduce3, s == 3, jnp.int32(0))
        stage(reduce_f, s > 0, jnp.where(s == 1, 0, jnp.where(s == 2, 4, 2)))
        return carry

    lax.fori_loop(0, QUARTERS, attend_back, 0)

    half_row = pl.multiple_of(32 * c, 32)
    row_x = pl.multiple_of(half_row + 16 * x, 16)
    row_y = pl.multiple_of(row_x + 8 * y, 8)

    def vrows(at, size):
        return pl.ds(pl.multiple_of(at, 8), size)

    folds = [
        (core, VG.at[vrows(32 - half_row, 32), :], GVR.at[0:32], vrows(half_row, 32)),
        (xdev, VG.at[vrows(half_row + 16 - 16 * x, 16), :], GVR.at[32:48], vrows(row_x, 16)),
        (ydev, VG.at[vrows(row_x + 8 - 8 * y, 8), :], GVR.at[48:56], vrows(row_y, 8)),
    ]

    def fold(i):
        dev, src, dst, keep = folds[i]
        return rcopy(src, dst, gsend.at[i], grecv.at[i], dev)

    def fold_done(i):
        fold(i).wait()
        keep = folds[i][3]
        VG[keep, :] = VG[keep, :] + folds[i][2][...]

    def g_z(s):
        src = VG.at[vrows(row_y, 8), :]
        return rcopy(src, GVZ.at[z], gsend.at[2 + s], grecv.at[2 + s], zdev(s))

    def g_z_in(s):
        dst = GVZ.at[got(s)]
        return rcopy(dst, dst, gsend.at[2 + s], grecv.at[2 + s], core)

    opens = [
        (ydev, vrows(row_y, 8), vrows(row_x + 8 - 8 * y, 8)),
        (xdev, vrows(row_x, 16), vrows(half_row + 16 - 16 * x, 16)),
        (core, vrows(half_row, 32), vrows(32 - half_row, 32)),
    ]

    def unfold(i):
        dev, mine, other = opens[i]
        ref = VO.at[mine, :]
        return rcopy(ref, ref, gsend.at[6 + i], grecv.at[6 + i], dev)

    def unfold_done(i):
        ref = VO.at[opens[i][2], :]
        rcopy(ref, ref, gsend.at[6 + i], grecv.at[6 + i], core).wait_recv()

    def vector_two():
        fold_done(0)
        fold(1).start()

    def vector_three():
        fold_done(1)
        fold(2).start()

    def vector_z():
        fold_done(2)
        for step in (1, 2, 3):
            g_z(step).start()
        GVZ[z] = VG[vrows(row_y, 8), :]

    def vector_back():
        for step in (1, 2, 3):
            g_z_in(step).wait_recv()
        VO[vrows(row_y, 8), :] = GVZ[0] + GVZ[1] + GVZ[2] + GVZ[3]
        unfold(0).start()

    fold(0).start()

    def project_back(s, carry):
        zq = target(s)
        pl.when(z < QUARTERS - 1)(lambda: hl(zq).wait_recv())
        pl.when(z > 0)(lambda: hr(zq).wait_recv())
        pl.when(z < QUARTERS - 2)(lambda: hll(zq).wait_recv())
        near = GKV.at[zq]

        def when(ok, v):
            return jnp.where(ok, v.astype(F32), 0.0)

        has_l, has_r, has_rr = z > 0, z < QUARTERS - 1, z < QUARTERS - 2
        near[REACH : 2 * REACH, :] += when(has_l, HR[zq, 0:REACH, :])
        near[ROWS : ROWS + REACH, :] += when(has_r, HL[zq, 0:REACH, :])
        gp = GKV[zq, KW + OWNP : KW + 2 * OWNP, :] + when(has_l, HR[zq, REACH : REACH + OWNP, :])
        gp = gp + when(has_r, HL[zq, REACH : REACH + OWNP, :])
        nxt = GKV[zq, KW + 2 * OWNP : KW + 2 * OWNP + 1, :]
        nxt = nxt + when(has_r, HL[zq, REACH + OWNP : REACH + OWNP + 16, :])[0:1, :]
        nxt = nxt + when(has_rr, HLL[zq])[0:1, :]
        gp1 = jnp.concatenate([gp[1:, :], nxt], axis=0)
        fills = (
            taps(zq, 2) * gp,
            taps(zq, 3) * gp,
            taps(zq, 4) * gp + taps(zq, 0) * gp1,
            taps(zq, 1) * gp1,
        )
        for k, fill in enumerate(fills):
            for i in range(TILES):
                pt[i, pl.ds(k, OWNP, stride=STRIDE), :] = fill[:, tile(i)]
        back = jnp.concatenate([pt[i, 0:ROWS, :] for i in range(TILES)], axis=1)
        alive = base + rows_iota(ROWS, 1) < length
        gkv = GKV[zq, REACH : REACH + ROWS, :] + jnp.where(alive, back, 0.0)
        GQ[zq, :, 0 : 2 * CHANS] = gkv.astype(BF)

        acc[...] += nn(GQ[zq], W[0, zq, 0 : 3 * CHANS, :])
        weight_grad(xT, GQ[zq], W.at[0, zq], 3 * CHANS)

        W[0, zq, :, 3 * CHANS : D] = nn(fT[...], CTX[zq]).astype(BF)
        r_core(8 + s).start()
        stage(reduce2, s == 0, jnp.int32(5))
        stage(reduce3, s > 0, s)
        stage(reduce4, s > 1, s - 2)
        pl.when(s == 0)(vector_two)
        stage(reduce1, s < 3, 8 + s)
        stage(reduce1, s == 1, jnp.int32(7))
        pl.when(s == 2)(vector_three)
        return carry

    lax.fori_loop(0, QUARTERS, project_back, 0)
    outs[1].start()

    def wait_all(ref, sem):
        pltpu.make_async_copy(ref, ref, sem).wait()

    pl.when(z > 0)(lambda: wait_all(SL, hsend.at[0]))
    pl.when(z < QUARTERS - 1)(lambda: wait_all(SR, hsend.at[1]))
    pl.when(z > 1)(lambda: wait_all(HLL, hsend.at[2]))

    def final(m):
        own_part = (11, 7, 6)[m]
        gmats[m] = CR[own_part, block(yx), :].astype(F32)

        def more(slot):
            cut = thin if m == DOWN else wide
            z_wait(m, slot, cut)
            at = gmats.at[m, :, cut[3]]
            at[...] += ZR[m, slot, :, cut[3]].astype(F32)

        pl.when(z > 0)(lambda: more(z))
        pl.when(z < QUARTERS - 1)(lambda: more(QUARTERS))
        outs[2 + m].start()

    def at(r):
        return jnp.int32(r)

    reduce2(at(8))
    reduce1(at(6))
    reduce3(at(4))
    vector_z()
    reduce4(at(2))
    reduce2(at(9))
    reduce1(at(11))
    reduce3(at(5))
    reduce4(at(3))
    reduce2(at(10))
    reduce2(at(7))
    reduce4(at(4))
    reduce3(at(8))
    vector_back()
    reduce4(at(5))
    reduce3(at(9))
    reduce4(at(8))
    reduce2(at(6))
    unfold_done(0)
    unfold(1).start()
    reduce3(at(10))
    reduce4(at(9))
    reduce2(at(11))
    reduce4(at(10))
    unfold_done(1)
    unfold(2).start()
    reduce3(at(7))
    final(1)
    reduce3(at(6))
    final(2)
    unfold_done(2)
    outs[5].start()
    reduce3(at(11))
    final(0)
    for i in range(3):
        unfold(i).wait_send()
    for s in (1, 2, 3):
        g_z(s).wait_send()

    def sent(r, carry):
        own_part = part(r)[1] == QUARTERS - 1
        pl.when(own_part)(lambda: wait_rows(rsend.at[r], 7 * PIECE))
        pl.when(jnp.logical_not(own_part))(lambda: wait_rows(rsend.at[r], 8 * PIECE))
        return carry

    lax.fori_loop(0, PARTS, sent, 0)
    for cp in outs:
        cp.wait()


def unpack(
    act, gtok, gmats, gvec,
    act_out, gtok_out, gq, gk, gv, gbq, gbv, gck, gcv, go, gbo, gag, gas, gup, gbu, gdown, gbd, gfg, gfs,
):
    act_out[...] = act[...]
    gtok_out[...] = gtok[...]
    gk[...] = gmats[0, :, 0:CHANS]
    gv[...] = gmats[0, :, CHANS : 2 * CHANS]
    gq[...] = gmats[0, :, 2 * CHANS : 3 * CHANS]
    go[...] = gmats[0, :, 3 * CHANS : D].T
    gup[...] = gmats[1]
    gdown[...] = gmats[2]
    for j in range(QUARTERS):
        at = slice(j * CHANS, (j + 1) * CHANS)
        row = 8 * j
        gbu[:, j * D : (j + 1) * D] = gvec[row : row + 1, :]
        gbv[:, at] = gvec[row + 1 : row + 2, CHANS : 2 * CHANS]
        gbq[:, at] = gvec[row + 1 : row + 2, 2 * CHANS : 3 * CHANS]
        for t in range(5):
            gck[t, :, at] = gvec[row + 2 + t : row + 3 + t, 0:CHANS]
            gcv[t, :, at] = gvec[row + 2 + t : row + 3 + t, CHANS : 2 * CHANS]
    for j, out in enumerate((gbo, gag, gas, gbd, gfg, gfs)):
        out[...] = gvec[8 * QUARTERS + j : 8 * QUARTERS + j + 1, :]


def fused_layer(
    tokens, lengths, w_query, w_key, w_value, b_query, b_value, conv_key, conv_value, w_out,
    b_out, attn_gain, attn_shift, w_up, b_up, w_down, b_down, ffn_gain, ffn_shift, cotangent,
):
    Q4 = QUARTERS
    vm = pltpu.VMEM
    dma = pltpu.SemaphoreType.DMA
    scratch = [
        vm((3, Q4, D, D), BF),
        vm((Q4, 8, D), F32),
        vm((TILES, KVROWS, 128), F32),
        vm((Q4, KEYS, 2 * CHANS), BF),
        vm((Q4, COMP, 2 * CHANS), BF),
        vm((Q4, ROWS, CHANS), BF),
        vm((Q4, ROWS, CHANS), BF),
        vm((Q4, QHEADS, 2, NEAR + FAR, QB), F32),
        vm((2, NEAR, QB), F32),
        vm((2, FAR, QB), F32),
        vm((ROWS, D), F32),
        vm((ROWS, 1), F32),
        vm((ROWS, D), F32),
        vm((ROWS, D), BF),
        vm((Q4, ROWS, D), F32),
        vm((Q4, ROWS, D), BF),
        vm((D, ROWS), BF),
        vm((D, ROWS), BF),
        vm((ROWS, D), BF),
        vm((Q4, KEYS, 2 * CHANS), F32),
        vm((TILES, ROWS + 8, 128), F32),
        vm((Q4, ROWS, 3 * CHANS), BF),
        vm((VROWS, D), F32),
        vm((12, D // 2, D), BF),
        vm((12, 4, PIECE, D // 2), BF),
        vm((12, 2, PIECE, D // 2), BF),
        vm((3, Q4 + 1, PIECE, D), BF),
        vm((Q4 + 1, D // 2, D // 3), BF),
        vm((Q4, REACH + 80, 2 * CHANS), BF),
        vm((Q4, REACH + OWNP, 2 * CHANS), BF),
        vm((Q4, 16, 2 * CHANS), BF),
        vm((Q4, REACH + 80, 2 * CHANS), BF),
        vm((Q4, REACH + OWNP, 2 * CHANS), BF),
        vm((VROWS, D), F32),
        vm((Q4, 8, D), F32),
        vm((VROWS, D), F32),
        vm((SEQ, D), BF),
        vm((ROWS, D), BF),
        pltpu.SMEM((1,), jnp.int32),
        vm((1, CHANS), F32),
        vm((1, CHANS), F32),
        vm((5, 1, CHANS), F32),
        vm((5, 1, CHANS), F32),
        vm((1, D), F32),
        vm((1, D), F32),
        vm((1, D), F32),
        vm((1, D), F32),
        vm((1, D), F32),
        vm((1, D), F32),
        vm((1, D), F32),
        vm((ROWS, D), BF),
        vm((ROWS, D), F32),
        vm((3, PIECE, D), F32),
        dma((12,)),
        dma((6,)),
        dma((5,)),
        dma((9,)),
        dma((9, 3)),
        dma((2, 2)),
        dma((5, Q4)),
        dma((2,)),
        dma((3,)),
        dma((3, Q4)),
        dma((12,)),
        dma((12, 3)),
        dma((3, Q4 + 1)),
        dma((Q4 + 1,)),
        dma((9,)),
        dma((9,)),
    ]
    vspec = pl.BlockSpec(memory_space=pltpu.VMEM)
    hspec = pl.BlockSpec(memory_space=pl.ANY)
    packed = pl.pallas_call(
        kernel,
        out_shape=(
            jax.ShapeDtypeStruct((ROWS, D), BF),
            jax.ShapeDtypeStruct((ROWS, D), F32),
            jax.ShapeDtypeStruct((3, PIECE, D), F32),
            jax.ShapeDtypeStruct((VROWS, D), F32),
        ),
        in_specs=[hspec] * 20,
        out_specs=(hspec,) * 4,
        scratch_shapes=scratch,
        compiler_params=pltpu.CompilerParams(
            collective_id=0, has_side_effects=True, vmem_limit_bytes=67043328
        ),
        name="layer",
    )(
        lengths, tokens, w_key[0].T, w_value[0].T, w_query[0].T, w_out[0], w_up[0], w_down[0],
        b_query, b_value, conv_key.transpose(1, 0, 2), conv_value.transpose(1, 0, 2), b_up, b_out, attn_gain, attn_shift, b_down,
        ffn_gain, ffn_shift, cotangent,
    )
    row = (1, D)
    shapes = [
        (ROWS, D), (PIECE, CHANS), (PIECE, CHANS), (PIECE, CHANS), row, row, (5, 1, D), (5, 1, D), (CHANS, PIECE),
        row, row, row, (PIECE, D), (1, FF), (PIECE, D), row, row, row,
    ]
    outs = pl.pallas_call(
        unpack,
        out_shape=[jax.ShapeDtypeStruct((ROWS, D), BF)] + [jax.ShapeDtypeStruct(v, F32) for v in shapes],
        in_specs=[vspec] * 4,
        out_specs=[vspec] * 19,
        name="unpack",
    )(*packed)
    act, gtok, gq, gk, gv, gbq, gbv, gck, gcv, go, gbo, gag, gas, gup, gbu, gdown, gbd, gfg, gfs = outs
    return (
        act, gtok, gq[None], gk[None], gv[None], gbq, gbv, gck.transpose(1, 0, 2), gcv.transpose(1, 0, 2), go[None], gbo, gag, gas,
        gup[None], gbu, gdown.T[None], gbd, gfg, gfs,
    )


def solution(mesh):
    small = mesh.shape["dp"] == 8 and mesh.shape["mp"] == QUARTERS
    return jax.shard_map(
        fused_layer if small else on_device,
        mesh=mesh,
        in_specs=(
            P("dp", None),
            P("dp"),
            P(None, None, "mp"),
            P(None, None, "mp"),
            P(None, None, "mp"),
            P(None, "mp"),
            P(None, "mp"),
            P(None, None, "mp"),
            P(None, None, "mp"),
            P(None, "mp", None),
            P(),
            P(),
            P(),
            P(None, None, "mp"),
            P(None, "mp"),
            P(None, "mp", None),
            P(),
            P(),
            P(),
            P(("dp", "mp"), None),
        ),
        out_specs=(
            P(("dp", "mp"), None),
            P(("dp", "mp"), None),
            P(None, "dp", "mp"),
            P(None, "dp", "mp"),
            P(None, "dp", "mp"),
            P(),
            P(),
            P(),
            P(),
            P(None, "mp", "dp"),
            P(),
            P(),
            P(),
            P(None, "dp", "mp"),
            P(),
            P(None, "mp", "dp"),
            P(),
            P(),
            P(),
        ),
        check_vma=False,
    )
```

```python
import jax
import jax.numpy as jnp
from jax import lax
from jax.experimental import pallas as pl
from jax.experimental.pallas import tpu as pltpu
from jax.sharding import PartitionSpec as P

D = 768
HEAD_DIM = 64
FF = 3072
WINDOW = 128
POOL_WINDOW = 512
STRIDE = 4
LAYERS = 1


block_rows = 512
mask_fill = -1000000000.0
epsilon = 1e-05


def norm_rows(hidden, gain, shift):
    center = hidden - jnp.mean(hidden, axis=-1, keepdims=True)
    spread = jnp.mean(center * center, axis=-1, keepdims=True)
    return center * lax.rsqrt(spread + epsilon) * gain + shift


def gelu_exact(values):
    return jax.nn.gelu(values, approximate=False)


def pool_rows(values, kernel):
    seqs, length, chans = values.shape
    width = kernel.shape[0]
    half = width // 2
    pooled_len = length // STRIDE
    padded = jnp.pad(values, ((0, 0), (half, width), (0, 0)))
    total = jnp.zeros((seqs, pooled_len, chans), jnp.float32)
    for offset in range(width):
        total = total + kernel[offset] * padded[:, offset : offset + STRIDE * pooled_len : STRIDE]
    return total


def block_mask(start, lengths):
    reach = WINDOW // 2
    pool_reach = POOL_WINDOW // 2 // STRIDE
    span = block_rows // STRIDE + 2 * pool_reach
    rows = start + jnp.arange(block_rows, dtype=jnp.int32)
    near_pos = start - reach + jnp.arange(block_rows + 2 * reach, dtype=jnp.int32)
    far_pos = (start // STRIDE - pool_reach + jnp.arange(span, dtype=jnp.int32)) * STRIDE
    limit = lengths[:, None, None]
    near_ok = (
        (jnp.abs(rows[:, None] - near_pos[None, :]) <= reach)[None]
        & (near_pos >= 0)[None, None]
        & (near_pos[None, None] < limit)
    )
    far_ok = (
        (jnp.abs(rows[:, None] - far_pos[None, :]) <= POOL_WINDOW // 2)[None]
        & (far_pos >= 0)[None, None]
        & (far_pos[None, None] < limit)
    )
    return jnp.concatenate([near_ok, far_ok], axis=-1)


def padded_keys(keys_loc, vals_loc, far_keys, far_vals):
    reach = WINDOW // 2
    pool_reach = POOL_WINDOW // 2 // STRIDE
    pad_near = ((0, 0), (reach, reach), (0, 0), (0, 0))
    pad_far = ((0, 0), (pool_reach, pool_reach), (0, 0), (0, 0))
    return (
        jnp.pad(keys_loc, pad_near),
        jnp.pad(vals_loc, pad_near),
        jnp.pad(far_keys, pad_far),
        jnp.pad(far_vals, pad_far),
    )


def block_inputs(start, queries, padded):
    near_k, near_v, far_k, far_v = padded
    near_len = block_rows + 2 * (WINDOW // 2)
    span = block_rows // STRIDE + 2 * (POOL_WINDOW // 2 // STRIDE)
    pool_start = start // STRIDE
    q_rows = queries[:, start : start + block_rows]
    keys_b = jnp.concatenate(
        [near_k[:, start : start + near_len], far_k[:, pool_start : pool_start + span]], axis=1
    )
    vals_b = jnp.concatenate(
        [near_v[:, start : start + near_len], far_v[:, pool_start : pool_start + span]], axis=1
    )
    return (q_rows, keys_b, vals_b)


def forward_block(q_rows, keys_b, vals_b, mask, live):
    scale = q_rows.shape[-1] ** (-0.5)
    scores = (
        jnp.einsum("sqhe,skhe->shqk", q_rows, keys_b, preferred_element_type=jnp.float32) * scale
    )
    scores = jnp.where(mask[:, None], scores, mask_fill)
    peak = jnp.max(scores, axis=-1, keepdims=True)
    expo = jnp.exp(scores - peak)
    total = jnp.sum(expo, axis=-1, keepdims=True)
    weights = (expo / total).astype(jnp.bfloat16)
    result = jnp.einsum("shqk,skhe->sqhe", weights, vals_b, preferred_element_type=jnp.float32)
    result = jnp.where(live[:, :, None, None], result, 0.0)
    return (result, peak + jnp.log(total))


def forward_skip(q_rows, keys_b, vals_b, mask, live):
    seqs, rows, heads, size = q_rows.shape
    return (
        jnp.zeros((seqs, rows, heads, size), jnp.float32),
        jnp.zeros((seqs, heads, rows, 1), jnp.float32),
    )


def backward_block(q_rows, keys_b, vals_b, mask, logsum, grad_rows):
    scale = q_rows.shape[-1] ** (-0.5)
    scores = (
        jnp.einsum("sqhe,skhe->shqk", q_rows, keys_b, preferred_element_type=jnp.float32) * scale
    )
    scores = jnp.where(mask[:, None], scores, mask_fill)
    probs = jnp.exp(scores - logsum)
    grad_probs = jnp.einsum(
        "sqhe,skhe->shqk", grad_rows, vals_b, preferred_element_type=jnp.float32
    )
    delta = jnp.sum(probs * grad_probs, axis=-1, keepdims=True)
    grad_scores = (probs * (grad_probs - delta)).astype(jnp.bfloat16)
    grad_q = (
        jnp.einsum("shqk,skhe->sqhe", grad_scores, keys_b, preferred_element_type=jnp.float32)
        * scale
    )
    grad_keys = (
        jnp.einsum("shqk,sqhe->skhe", grad_scores, q_rows, preferred_element_type=jnp.float32)
        * scale
    )
    grad_vals = jnp.einsum(
        "shqk,sqhe->skhe", probs.astype(jnp.bfloat16), grad_rows, preferred_element_type=jnp.float32
    )
    return (grad_q, grad_keys, grad_vals)


def backward_skip(q_rows, keys_b, vals_b, mask, logsum, grad_rows):
    return (
        jnp.zeros(q_rows.shape, jnp.float32),
        jnp.zeros(keys_b.shape, jnp.float32),
        jnp.zeros(vals_b.shape, jnp.float32),
    )


def attend_forward(queries, keys_loc, vals_loc, far_keys, far_vals, lengths):
    length = queries.shape[1]
    padded = padded_keys(keys_loc, vals_loc, far_keys, far_vals)
    longest = jnp.max(lengths)
    results, logsums = ([], [])
    for block in range(length // block_rows):
        start = block * block_rows
        q_rows, keys_b, vals_b = block_inputs(start, queries, padded)
        mask = block_mask(start, lengths)
        live = start + jnp.arange(block_rows, dtype=jnp.int32)[None, :] < lengths[:, None]
        result, logsum = lax.cond(
            start < longest, forward_block, forward_skip, q_rows, keys_b, vals_b, mask, live
        )
        results.append(result)
        logsums.append(logsum)
    return (jnp.concatenate(results, axis=1), logsums)


def attend_backward(
    queries, keys_loc, vals_loc, far_keys, far_vals, lengths, logsums, grad_context
):
    seqs, length, heads, size = queries.shape
    pooled_len = far_keys.shape[1]
    reach = WINDOW // 2
    pool_reach = POOL_WINDOW // 2 // STRIDE
    near_len = block_rows + 2 * reach
    span = block_rows // STRIDE + 2 * pool_reach
    padded = padded_keys(keys_loc, vals_loc, far_keys, far_vals)
    longest = jnp.max(lengths)
    grad_near_k = jnp.zeros((seqs, length + 2 * reach, heads, size), jnp.float32)
    grad_near_v = jnp.zeros((seqs, length + 2 * reach, heads, size), jnp.float32)
    grad_far_k = jnp.zeros((seqs, pooled_len + 2 * pool_reach, heads, size), jnp.float32)
    grad_far_v = jnp.zeros((seqs, pooled_len + 2 * pool_reach, heads, size), jnp.float32)
    grad_queries = []
    for block in range(length // block_rows):
        start = block * block_rows
        pool_start = start // STRIDE
        q_rows, keys_b, vals_b = block_inputs(start, queries, padded)
        mask = block_mask(start, lengths)
        grad_rows = grad_context[:, start : start + block_rows]
        grad_q, grad_keys, grad_vals = lax.cond(
            start < longest,
            backward_block,
            backward_skip,
            q_rows,
            keys_b,
            vals_b,
            mask,
            logsums[block],
            grad_rows,
        )
        grad_queries.append(grad_q)
        grad_near_k = grad_near_k.at[:, start : start + near_len].add(grad_keys[:, :near_len])
        grad_near_v = grad_near_v.at[:, start : start + near_len].add(grad_vals[:, :near_len])
        grad_far_k = grad_far_k.at[:, pool_start : pool_start + span].add(grad_keys[:, near_len:])
        grad_far_v = grad_far_v.at[:, pool_start : pool_start + span].add(grad_vals[:, near_len:])
    return (
        jnp.concatenate(grad_queries, axis=1),
        grad_near_k[:, reach : reach + length],
        grad_near_v[:, reach : reach + length],
        grad_far_k[:, pool_reach : pool_reach + pooled_len],
        grad_far_v[:, pool_reach : pool_reach + pooled_len],
    )


def row_sum(left, right, share):

    def term(start, count):
        return jnp.dot(left, right, preferred_element_type=jnp.float32)

    return lax.psum_scatter(
        term(jnp.int32(0), share * lax.axis_size("mp")), "mp", scatter_dimension=0, tiled=True
    )


def share_rows(values):
    return lax.all_gather(values, "mp", axis=0, tiled=True)


def share_back(values):
    return lax.all_gather(values, "mp", axis=0, tiled=True)


def back_sum(term, share):
    return lax.psum_scatter(
        term(jnp.int32(0), share * lax.axis_size("mp")), "mp", scatter_dimension=0, tiled=True
    )


def spread(values, width):
    whole = jnp.zeros(values.shape[:-1] + (width,), jnp.float32)
    start = lax.axis_index("mp") * values.shape[-1]
    return lax.dynamic_update_slice_in_dim(whole, values, start, values.ndim - 1)


def layer_forward(full_in, resid, lengths, params, share):
    (
        w_query,
        w_key,
        w_value,
        b_query,
        b_value,
        conv_key,
        conv_value,
        w_out,
        b_out,
        attn_gain,
        attn_shift,
        w_up,
        b_up,
        w_down,
        b_down,
        ffn_gain,
        ffn_shift,
    ) = params
    seqs = lengths.shape[0]
    total_rows = full_in.shape[0]
    length = total_rows // seqs
    chans = w_query.shape[1]
    heads = chans // HEAD_DIM
    pooled_len = length // STRIDE
    queries = (jnp.dot(full_in, w_query, preferred_element_type=jnp.float32) + b_query).astype(
        jnp.bfloat16
    )
    keys_loc = jnp.dot(full_in, w_key, preferred_element_type=jnp.float32).astype(jnp.bfloat16)
    vals_loc = (jnp.dot(full_in, w_value, preferred_element_type=jnp.float32) + b_value).astype(
        jnp.bfloat16
    )
    valid = (jnp.arange(length, dtype=jnp.int32)[None, :] < lengths[:, None]).astype(jnp.float32)[
        :, :, None
    ]
    far_keys = pool_rows(
        keys_loc.reshape(seqs, length, chans).astype(jnp.float32) * valid, conv_key
    ).astype(jnp.bfloat16)
    far_vals = pool_rows(
        vals_loc.reshape(seqs, length, chans).astype(jnp.float32) * valid, conv_value
    ).astype(jnp.bfloat16)
    context, logsums = attend_forward(
        queries.reshape(seqs, length, heads, HEAD_DIM),
        keys_loc.reshape(seqs, length, heads, HEAD_DIM),
        vals_loc.reshape(seqs, length, heads, HEAD_DIM),
        far_keys.reshape(seqs, pooled_len, heads, HEAD_DIM),
        far_vals.reshape(seqs, pooled_len, heads, HEAD_DIM),
        lengths,
    )
    context = context.reshape(total_rows, chans).astype(jnp.bfloat16)
    hidden_one = resid + (row_sum(context, w_out, share) + b_out)
    normed = norm_rows(hidden_one, attn_gain, attn_shift)
    full_normed = share_rows(normed.astype(jnp.bfloat16))
    upper = jnp.dot(full_normed, w_up, preferred_element_type=jnp.float32) + b_up
    active = gelu_exact(upper).astype(jnp.bfloat16)
    hidden_two = normed + (row_sum(active, w_down, share) + b_down)
    result = norm_rows(hidden_two, ffn_gain, ffn_shift)
    kept = (
        full_in,
        queries,
        keys_loc,
        vals_loc,
        far_keys,
        far_vals,
        logsums,
        context,
        hidden_one,
        full_normed,
        upper,
        active,
        hidden_two,
    )
    return (result, kept)


def layer_backward(grad_out, kept, params, lengths, share):
    (
        w_query,
        w_key,
        w_value,
        b_query,
        b_value,
        conv_key,
        conv_value,
        w_out,
        b_out,
        attn_gain,
        attn_shift,
        w_up,
        b_up,
        w_down,
        b_down,
        ffn_gain,
        ffn_shift,
    ) = params
    (
        full_in,
        queries,
        keys_loc,
        vals_loc,
        far_keys,
        far_vals,
        logsums,
        context,
        hidden_one,
        full_normed,
        saved_upper,
        active,
        hidden_two,
    ) = kept
    seqs = lengths.shape[0]
    total_rows = full_in.shape[0]
    length = total_rows // seqs
    chans = w_query.shape[1]
    heads = chans // HEAD_DIM
    pooled_len = length // STRIDE
    unused_two, pull_two = jax.vjp(norm_rows, hidden_two, ffn_gain, ffn_shift)
    grad_h2, grad_fgain, grad_fshift = pull_two(grad_out)
    grad_ffn = grad_h2.astype(jnp.bfloat16)
    grad_bdown = jnp.sum(grad_ffn.astype(jnp.float32), axis=0)
    full_gffn = share_back(grad_ffn)
    grad_wdown = jnp.einsum("tf,td->fd", active, full_gffn, preferred_element_type=jnp.float32)
    grad_active = jnp.einsum("td,fd->tf", full_gffn, w_down, preferred_element_type=jnp.float32)
    unused_gelu, pull_gelu = jax.vjp(gelu_exact, saved_upper)
    grad_upper = pull_gelu(grad_active)[0].astype(jnp.bfloat16)
    grad_bup = jnp.sum(grad_upper.astype(jnp.float32), axis=0)
    grad_wup = jnp.einsum("td,tf->df", full_normed, grad_upper, preferred_element_type=jnp.float32)

    def up_term(start, count):
        return jnp.einsum("tf,df->td", grad_upper, w_up, preferred_element_type=jnp.float32)

    grad_y1 = grad_h2 + back_sum(up_term, share)
    unused_one, pull_one = jax.vjp(norm_rows, hidden_one, attn_gain, attn_shift)
    grad_h1, grad_again, grad_ashift = pull_one(grad_y1)
    grad_attn = grad_h1.astype(jnp.bfloat16)
    grad_bout = jnp.sum(grad_attn.astype(jnp.float32), axis=0)
    full_gattn = share_back(grad_attn)
    grad_wout = jnp.einsum("tc,td->cd", context, full_gattn, preferred_element_type=jnp.float32)
    grad_context = jnp.einsum("td,cd->tc", full_gattn, w_out, preferred_element_type=jnp.float32)
    valid = (jnp.arange(length, dtype=jnp.int32)[None, :] < lengths[:, None]).astype(jnp.float32)[
        :, :, None
    ]
    grad_context = (grad_context.reshape(seqs, length, chans) * valid).astype(jnp.bfloat16)
    grad_q, grad_near_k, grad_near_v, grad_far_k, grad_far_v = attend_backward(
        queries.reshape(seqs, length, heads, HEAD_DIM),
        keys_loc.reshape(seqs, length, heads, HEAD_DIM),
        vals_loc.reshape(seqs, length, heads, HEAD_DIM),
        far_keys.reshape(seqs, pooled_len, heads, HEAD_DIM),
        far_vals.reshape(seqs, pooled_len, heads, HEAD_DIM),
        lengths,
        logsums,
        grad_context.reshape(seqs, length, heads, HEAD_DIM),
    )
    masked_keys = keys_loc.reshape(seqs, length, chans).astype(jnp.float32) * valid
    masked_vals = vals_loc.reshape(seqs, length, chans).astype(jnp.float32) * valid
    unused_pk, pull_key = jax.vjp(pool_rows, masked_keys, conv_key)
    grad_kpool, grad_ckey = pull_key(grad_far_k.reshape(seqs, pooled_len, chans))
    unused_pv, pull_val = jax.vjp(pool_rows, masked_vals, conv_value)
    grad_vpool, grad_cval = pull_val(grad_far_v.reshape(seqs, pooled_len, chans))
    grad_queries = grad_q.reshape(total_rows, chans).astype(jnp.bfloat16)
    grad_keys = (
        (grad_near_k.reshape(seqs, length, chans) + grad_kpool * valid)
        .reshape(total_rows, chans)
        .astype(jnp.bfloat16)
    )
    grad_vals = (
        (grad_near_v.reshape(seqs, length, chans) + grad_vpool * valid)
        .reshape(total_rows, chans)
        .astype(jnp.bfloat16)
    )
    grad_wquery = jnp.einsum("td,tc->dc", full_in, grad_queries, preferred_element_type=jnp.float32)
    grad_wkey = jnp.einsum("td,tc->dc", full_in, grad_keys, preferred_element_type=jnp.float32)
    grad_wvalue = jnp.einsum("td,tc->dc", full_in, grad_vals, preferred_element_type=jnp.float32)
    grad_bquery = jnp.sum(grad_queries.astype(jnp.float32), axis=0)
    grad_bvalue = jnp.sum(grad_vals.astype(jnp.float32), axis=0)

    def input_term(start, count):
        total = jnp.einsum("tc,dc->td", grad_queries, w_query, preferred_element_type=jnp.float32)
        total = total + jnp.einsum(
            "tc,dc->td", grad_keys, w_key, preferred_element_type=jnp.float32
        )
        return total + jnp.einsum(
            "tc,dc->td", grad_vals, w_value, preferred_element_type=jnp.float32
        )

    grad_input = grad_h1 + back_sum(input_term, share)
    matrices = (
        grad_wquery[None],
        grad_wkey[None],
        grad_wvalue[None],
        grad_wout[None],
        grad_wup[None],
        grad_wdown[None],
    )
    vectors = (
        spread(grad_bquery, D)[None],
        spread(grad_bvalue, D)[None],
        spread(grad_ckey, D)[None],
        spread(grad_cval, D)[None],
        grad_bout[None],
        grad_again[None],
        grad_ashift[None],
        spread(grad_bup, FF)[None],
        grad_bdown[None],
        grad_fgain[None],
        grad_fshift[None],
    )
    return (grad_input, matrices, vectors)


def on_device(
    tokens,
    lengths,
    w_query,
    w_key,
    w_value,
    b_query,
    b_value,
    conv_key,
    conv_value,
    w_out,
    b_out,
    attn_gain,
    attn_shift,
    w_up,
    b_up,
    w_down,
    b_down,
    ffn_gain,
    ffn_shift,
    cotangent,
):
    stacks = (
        w_query,
        w_key,
        w_value,
        b_query,
        b_value,
        conv_key,
        conv_value,
        w_out,
        b_out,
        attn_gain,
        attn_shift,
        w_up,
        b_up,
        w_down,
        b_down,
        ffn_gain,
        ffn_shift,
    )
    total_rows = tokens.shape[0]
    share = total_rows // lax.axis_size("mp")
    place = lax.axis_index("mp") * share
    resid = lax.dynamic_slice_in_dim(tokens, place, share, 0).astype(jnp.float32)
    layer = 0
    params = tuple((stack[layer] for stack in stacks))
    result, kept = layer_forward(tokens, resid, lengths, params, share)
    kept_all = [kept]
    activations = result.astype(jnp.bfloat16)
    grad_out = cotangent.astype(jnp.float32)
    matrix_list = [None] * LAYERS
    vector_list = [None] * LAYERS
    for layer in reversed(range(LAYERS)):
        params = tuple((stack[layer] for stack in stacks))
        grad_out, matrices, vectors = layer_backward(
            grad_out, kept_all[layer], params, lengths, share
        )
        matrix_list[layer] = matrices
        vector_list[layer] = vectors
    grad_wquery, grad_wkey, grad_wvalue, grad_wout, grad_wup, grad_wdown = tuple(
        (jnp.concatenate([entry[index] for entry in matrix_list], axis=0) for index in range(6))
    )
    (
        grad_bquery,
        grad_bvalue,
        grad_ckey,
        grad_cval,
        grad_bout,
        grad_again,
        grad_ashift,
        grad_bup,
        grad_bdown,
        grad_fgain,
        grad_fshift,
    ) = tuple(
        (jnp.concatenate([entry[index] for entry in vector_list], axis=0) for index in range(11))
    )
    grad_wquery, grad_wkey, grad_wvalue, grad_wout, grad_wup, grad_wdown = (
        lax.psum_scatter(grad_wquery, "dp", scatter_dimension=1, tiled=True),
        lax.psum_scatter(grad_wkey, "dp", scatter_dimension=1, tiled=True),
        lax.psum_scatter(grad_wvalue, "dp", scatter_dimension=1, tiled=True),
        lax.psum_scatter(grad_wout, "dp", scatter_dimension=2, tiled=True),
        lax.psum_scatter(grad_wup, "dp", scatter_dimension=1, tiled=True),
        lax.psum_scatter(grad_wdown, "dp", scatter_dimension=2, tiled=True),
    )
    (
        grad_bquery,
        grad_bvalue,
        grad_ckey,
        grad_cval,
        grad_bout,
        grad_again,
        grad_ashift,
        grad_bup,
        grad_bdown,
        grad_fgain,
        grad_fshift,
    ) = lax.psum(
        (
            grad_bquery,
            grad_bvalue,
            grad_ckey,
            grad_cval,
            grad_bout,
            grad_again,
            grad_ashift,
            grad_bup,
            grad_bdown,
            grad_fgain,
            grad_fshift,
        ),
        ("dp", "mp"),
    )
    return (
        activations,
        grad_out,
        grad_wquery,
        grad_wkey,
        grad_wvalue,
        grad_bquery,
        grad_bvalue,
        grad_ckey,
        grad_cval,
        grad_wout,
        grad_bout,
        grad_again,
        grad_ashift,
        grad_wup,
        grad_bup,
        grad_wdown,
        grad_bdown,
        grad_fgain,
        grad_fshift,
    )


BF = jnp.bfloat16
F32 = jnp.float32
MESH = pl.DeviceIdType.MESH
ROWS = 256
QUARTERS = 4
CHANS = D // QUARTERS
QHEADS = CHANS // HEAD_DIM
SEQ = QUARTERS * ROWS
REACH = WINDOW // 2
PREACH = POOL_WINDOW // 2 // STRIDE
OWNP = ROWS // STRIDE
KW = ROWS + 2 * REACH
KP = OWNP + 2 * PREACH
KEYS = KW + KP
QB = 128
NEAR = QB + 2 * REACH
FAR = QB // STRIDE + 2 * PREACH
COMP = 800
HALFC = COMP // 2
FRONT = 256
KVROWS = 1408
BASE = 288
PIECE = D // 8
BIG_NEG = -1e30
SCALE = HEAD_DIM ** -0.5
VROWS = 64
TILES = 2 * CHANS // 128


def nn(a, b):
    return jnp.dot(a, b, preferred_element_type=F32)


def nt(a, b):
    return lax.dot_general(a, b, (((1,), (1,)), ((), ())), preferred_element_type=F32)


def tn(a, b):
    return lax.dot_general(a, b, (((0,), (0,)), ((), ())), preferred_element_type=F32)


def rows_iota(rows, cols):
    return lax.broadcasted_iota(jnp.int32, (rows, cols), 0)


def cols_iota(rows, cols):
    return lax.broadcasted_iota(jnp.int32, (rows, cols), 1)


def mean_row(v):
    return jnp.mean(v, axis=-1, keepdims=True)


def sum_col(v):
    return jnp.sum(v, axis=0, keepdims=True)


def kernel(
    len_hbm, tok_hbm, wk, wv, wq, wo, wup, wdown, bq_h, bv_h, ck_h, cv_h, bup_h, bo_h, ag_h, ash_h, bd_h, fg_h, fs_h, cot_hbm,
    act_hbm, gtok_hbm, gmats_hbm, gvec_hbm,
    W, VEC, kvf, KV, KVS, Q, CTX, P, maskn, maskf, n1, r1, y1, y1b, dg, av,
    yT, fT, gab, GKV, pt, GQ, VG,
    CR, S1, S2, ZR, ZF, HL, HR, HLL, SL, SR, GVR, GVZ, VO, tok, cot,
    len_ref, bq, bv, ck, cv, bup, bo, ag, ash, bd, fg, fs, act_out, gtok, gmats,
    ssem, osem, lsem, asend, arecv, zsend, zrecv, lsend, hsend, hrecv, rsend, rrecv, zsum, zfsum, gsend, grecv,
):
    acc, n2, xT, gub = gtok, y1, yT, y1b
    dp = lax.axis_index("dp")
    z = lax.axis_index("mp")
    c = lax.rem(dp, 2)
    x = lax.rem(lax.div(dp, 2), 2)
    y = lax.div(dp, 4)
    core = (dp + 1 - 2 * c, z)
    xdev = (dp + 2 - 4 * x, z)
    ydev = (dp + 4 - 8 * y, z)
    yx = 2 * y + x

    def zdev(step):
        return (dp, lax.rem(z + step, QUARTERS))

    def rcopy(src, dst, ssem, rsem, dev):
        return pltpu.make_async_remote_copy(
            src_ref=src, dst_ref=dst, send_sem=ssem, recv_sem=rsem,
            device_id=dev, device_id_type=MESH,
        )

    barrier = pltpu.get_barrier_semaphore()
    for dev in (core, xdev, ydev, zdev(1), zdev(2), zdev(3)):
        pl.semaphore_signal(barrier, inc=1, device_id=dev, device_id_type=MESH)

    def loads():
        parts = [(wk, 0), (wv, CHANS), (wq, 2 * CHANS), (wo, 3 * CHANS)]
        copies = [
            pltpu.make_async_copy(src, W.at[0, z, at : at + CHANS, :], lsem.at[0])
            for src, at in parts
        ]
        copies.append(pltpu.make_async_copy(wup, W.at[1, z], lsem.at[1]))
        copies.append(pltpu.make_async_copy(wdown, W.at[2, z], lsem.at[2]))
        return copies

    small = [
        pltpu.make_async_copy(src, dst, ssem.at[i])
        for i, (src, dst) in enumerate(
            (
                (bup_h, bup), (bv_h, bv), (bq_h, bq), (ck_h, ck), (cv_h, cv), (len_hbm, len_ref),
                (bo_h, bo), (ag_h, ag), (ash_h, ash), (bd_h, bd), (fg_h, fg), (fs_h, fs),
            )
        )
    ]
    outs = [
        pltpu.make_async_copy(src, dst, osem.at[i])
        for i, (src, dst) in enumerate(
            (
                (act_out, act_hbm), (gtok, gtok_hbm), (gmats.at[0], gmats_hbm.at[0]),
                (gmats.at[1], gmats_hbm.at[1]), (gmats.at[2], gmats_hbm.at[2]), (VO, gvec_hbm),
            )
        )
    ]
    for cp in small[:6]:
        cp.start()
    own = loads()
    tok_in = pltpu.make_async_copy(tok_hbm, tok, lsem.at[3])
    cot_in = pltpu.make_async_copy(cot_hbm, cot, lsem.at[4])
    for cp in own:
        cp.start()
    tok_in.start()
    for cp in small[6:]:
        cp.start()
    cot_in.start()
    for cp in small[:6]:
        cp.wait()
    length = len_ref[0]
    vpack = VG.at[0:8, :]
    vpack[...] = jnp.zeros_like(vpack)
    vpack[0:1, :] = bup[...]
    vpack[1:2, CHANS : 2 * CHANS] = bv[...]
    vpack[1:2, 2 * CHANS : 3 * CHANS] = bq[...]
    for t in range(5):
        vpack[2 + t : 3 + t, 0:CHANS] = ck[t]
        vpack[2 + t : 3 + t, CHANS : 2 * CHANS] = cv[t]
    VEC[z] = vpack[...]
    pl.semaphore_wait(barrier, 6)

    def block(j):
        return pl.ds(pl.multiple_of(j * PIECE, PIECE), PIECE)

    piece_me = c * 4 + yx
    piece_x = c * 4 + 2 * y + 1 - x
    piece_y = c * 4 + 2 * (1 - y) + x
    piece_d = c * 4 + 2 * (1 - y) + 1 - x
    LO, HI = pl.ds(0, D // 2), pl.ds(D // 2, D // 2)
    ALL = pl.ds(0, D)
    CHUNKS = 9
    ends = [(0, 1), (1, 1), (0, 2), (1, 2), (0, 3), (2, 1), (2, 2), (1, 3), (2, 3)]
    inner = [(0, 1), (0, 2), (1, 1), (1, 2), (0, 3), (2, 1), (2, 2), (1, 3), (2, 3)]
    sources = [(1, 2, 3), (2, 0, 3), (1, 3, 0), (2, 1, 0)]
    targets = [(3, 2, 1, 0), (3, 0, 2, 1), (0, 3, 1, 2), (0, 1, 2, 3)]
    DOWN = 2
    FAR_STEPS = 2
    at_end = (z == 0) | (z == QUARTERS - 1)

    def table(values, bits=2):
        word = sum(v << (bits * i) for i, v in enumerate(values))
        return jnp.int32(word - (1 << 32) if word >> 31 else word)

    def lookup(word, i, bits=2):
        return lax.bitwise_and(lax.shift_right_logical(word, bits * i), (1 << bits) - 1)

    def by_place(a, b):
        return lax.select(at_end, a, b)

    mats_of = by_place(table(m for m, d in ends), table(m for m, d in inner))
    dist_of = by_place(table(d for m, d in ends), table(d for m, d in inner))
    looks_of = by_place(table((1, 2, 4, 5, 6, 7, 8, 9), 4), table((2, 4, 5, 7, 8, 9, 9, 9), 4))
    sends_of = by_place(table((1, 2, 4, 5, 6, 7, 8, 9), 4), table((2, 3, 4, 5, 6, 7, 8, 9), 4))

    def source(d):
        return lookup(table(v for row in sources for v in row), 3 * z + d - 1)

    def target(t):
        return lookup(table(v for row in targets for v in row), 4 * z + t)

    def chunk(k):
        return lookup(mats_of, k), source(lookup(dist_of, k))

    def is_far(k):
        return (lookup(mats_of, k) == DOWN) & (lookup(dist_of, k) < FAR_STEPS)

    def own_block(m, up, piece, sem):
        src = W.at[m, z, block(piece), :]
        return rcopy(src, src, zsend.at[0, up], zrecv.at[sem, z], (dp, z + 2 * up - 1))

    def own_z(m, up):
        return own_block(m, up, piece_me, m)

    def far_z(up):
        return own_block(DOWN, up, piece_d, 4)

    def wants_far(up):
        to = z + 2 * up - 1
        inner_to = (to == 1) | (to == 2)
        return jnp.logical_not(inner_to) | (z == 3 - to)

    def relay(m, src, dev):
        ref = W.at[m, src, block(piece_me), :]
        return rcopy(ref, ref, lsend.at[0], zrecv.at[m, src], dev)

    def relay_far(src, dev):
        ref = W.at[DOWN, src, block(piece_d), :]
        return rcopy(ref, ref, lsend.at[0], zrecv.at[4, src], dev)

    def own_vec(up):
        src = VEC.at[z]
        return rcopy(src, src, zsend.at[1, up], zrecv.at[3, z], (dp, z + 2 * up - 1))

    def relay_vec(src, dev):
        ref = VEC.at[src]
        return rcopy(ref, ref, lsend.at[1], zrecv.at[3, src], dev)

    def onward(src):
        return jnp.where(src > z, z > 0, z < QUARTERS - 1)

    def next_dev(src):
        return (dp, jnp.where(src > z, z - 1, z + 1))

    def plane(k, which, piece, cols, dev):
        m, src = chunk(k)
        ref = W.at[m, src, block(piece), cols]
        return rcopy(ref, ref, asend.at[k], arecv.at[k, (which - 1) // 2], dev)

    def look(k):
        m, src = chunk(k)

        @pl.when(m == 0)
        def _():
            relay_vec(src, core).wait_recv()
            pl.when(onward(src))(lambda: relay_vec(src, next_dev(src)).start())

        relay(m, src, core).wait_recv()
        pl.when(onward(src))(lambda: relay(m, src, next_dev(src)).start())

        @pl.when(is_far(k))
        def _():
            relay_far(src, core).wait_recv()

        pl.when(at_end)(lambda: first(k))

    LAST_CHUNK = CHUNKS - 1

    def cross_piece(k, piece):
        m, src = chunk(k)
        ref = W.at[m, src, block(piece), :]
        return rcopy(ref, ref, asend.at[k], arecv.at[k, 2], core)

    def first(k):
        plane(k, 1, piece_me, ALL, xdev).start()
        plane(k, 2, piece_me, ALL, ydev).start()
        pl.when(k == LAST_CHUNK)(lambda: cross_piece(k, piece_me).start())

    def rows_of(count):
        return W.at[0, 0, 0:count, :]

    def wait_rows(sem, count):
        pltpu.make_async_copy(rows_of(count), rows_of(count), sem).wait()

    def second(k):
        wait_rows(arecv.at[k, 0], 2 * PIECE)

        @pl.when(jnp.logical_not(is_far(k)))
        def _():
            plane(k, 3, piece_x, LO, ydev).start()
            plane(k, 4, piece_y, HI, xdev).start()

        @pl.when(k == LAST_CHUNK)
        def _():
            cross_piece(k, piece_x).start()
            cross_piece(k, piece_y).start()

    def half(j):
        return pl.ds(pl.multiple_of(j * (D // 2), D // 2), D // 2)

    def cross(k, j):
        m, src = chunk(k)
        ref = W.at[m, src, half(j), :]
        return rcopy(ref, ref, asend.at[k], arecv.at[k, 2], core)

    def third(k):
        pl.when(jnp.logical_not(is_far(k)))(lambda: wait_rows(arecv.at[k, 1], PIECE))
        pl.when(k < LAST_CHUNK)(lambda: cross(k, c).start())
        pl.when(k == LAST_CHUNK)(lambda: cross_piece(k, piece_d).start())

    def fourth(k):
        cross(k, 1 - c).wait_recv()

    def looks(i):
        return jnp.where(i < 0, 0, lookup(looks_of, lax.clamp(0, i, 7), 4))

    def sends(i):
        return jnp.where(i < 0, 0, lookup(sends_of, lax.clamp(0, i, 7), 4))

    def each(fn):
        def body(k, carry):
            fn(k)
            return carry

        return body

    def gather_slot(i, carry):
        lax.fori_loop(looks(i - 1), looks(i), each(look), 0)
        pl.when((i == 2) & jnp.logical_not(at_end))(lambda: both(own_down))
        lo = jnp.where(at_end, sends(i), sends(i - 1))
        lax.fori_loop(lo, sends(i), each(first), 0)
        for lag, stage in ((1, second), (2, third), (3, fourth)):
            k = i - lag
            pl.when((k >= 0) & (k < CHUNKS))(lambda stage=stage, k=k: stage(k))
        return carry

    def gather_done(k, carry):
        m, src = chunk(k)

        far = is_far(k)
        pl.when(far)(lambda: wait_rows(asend.at[k], 6 * PIECE))
        pl.when(jnp.logical_not(far))(lambda: wait_rows(asend.at[k], 7 * PIECE))
        return carry

    def got(s):
        return lax.rem(z + QUARTERS - s, QUARTERS)

    def both(fn):
        pl.when(z > 0)(lambda: fn(0))
        pl.when(z < QUARTERS - 1)(lambda: fn(1))

    both(lambda up: own_vec(up).start())
    for m in range(3):
        pltpu.make_async_copy(W.at[m, z], W.at[m, z], lsem.at[m]).wait()
        if m != DOWN:
            both(lambda up: own_z(m, up).start())

    def own_down(up):
        own_z(DOWN, up).start()
        pl.when(wants_far(up))(lambda: far_z(up).start())

    pl.when(at_end)(lambda: both(own_down))

    def own_sent(up):
        own_vec(up).wait_send()
        far = wants_far(up)
        pl.when(far)(lambda: wait_rows(zsend.at[0, up], 4 * PIECE))
        pl.when(jnp.logical_not(far))(lambda: wait_rows(zsend.at[0, up], 3 * PIECE))

    base = z * ROWS
    start = lax.select(z < 2, jnp.int32(0), jnp.int32(SEQ - COMP))
    place = pl.multiple_of(start - base + BASE + FRONT, 32)
    start = pl.multiple_of(start, 32)
    kvf[...] = jnp.zeros_like(kvf)
    for b in range(2):
        i = base + b * QB + cols_iota(1, QB)
        j = base - REACH + b * QB + rows_iota(NEAR, 1)
        ok = (jnp.abs(i - j) <= REACH) & (j >= 0) & (j < length)
        maskn[b] = jnp.where(ok, 0.0, BIG_NEG)
        j = (OWNP * z - PREACH + b * (QB // STRIDE) + rows_iota(FAR, 1)) * STRIDE
        ok = (jnp.abs(i - j) <= POOL_WINDOW // 2) & (j >= 0) & (j < length)
        maskf[b] = jnp.where(ok, 0.0, BIG_NEG)
    own_rows = pl.ds(pl.multiple_of(base, ROWS), ROWS)
    tok_in.wait()
    cot_in.wait()
    for cp in small[6:]:
        cp.wait()
    xb = tok[own_rows, :]
    acc[...] = jnp.zeros_like(acc)

    def taps(zq, t):
        return VEC[zq, 2 + t : 3 + t, 0 : 2 * CHANS]

    def strided(t):
        at = pl.ds(FRONT + BASE - POOL_WINDOW // 2 - 2 + t, KP, stride=STRIDE)
        return jnp.concatenate([kvf[i, at, :] for i in range(TILES)], axis=1)

    def tile(i):
        return slice(i * 128, (i + 1) * 128)

    def window(lo, rows):
        return jnp.concatenate([kvf[i, lo : lo + rows, :] for i in range(TILES)], axis=1)

    def quarter(s):
        return lax.select(s == 0, z, source(lax.max(s, 1)))

    def attend(s, carry):
        zq = quarter(s)
        for blk in range(2):
            xr = tok[pl.ds(pl.multiple_of(start + blk * HALFC, 16), HALFC), :]
            kv = nt(xr, W[0, zq, 0 : 2 * CHANS, :]) + VEC[zq, 1:2, 0 : 2 * CHANS]
            pos = start + blk * HALFC + rows_iota(HALFC, 1)
            kvb = jnp.where(pos < length, kv.astype(BF).astype(F32), 0.0)
            for i in range(TILES):
                kvf[i, pl.ds(pl.multiple_of(place + blk * HALFC, 8), HALFC), :] = kvb[:, tile(i)]
        KVS[zq] = window(FRONT, COMP).astype(BF)
        KV[zq, 0:KW, :] = window(FRONT + BASE - REACH, KW).astype(BF)
        pooled = jnp.zeros((KP, 2 * CHANS), F32)
        for t in range(5):
            pooled = pooled + taps(zq, t) * strided(t)
        KV[zq, KW:KEYS, :] = pooled.astype(BF)
        qz = nt(xb, W[0, zq, 2 * CHANS : 3 * CHANS, :]) + VEC[zq, 1:2, 2 * CHANS : 3 * CHANS]
        Q[zq] = qz.astype(BF)
        for b in range(2):
            live = base + b * QB + cols_iota(1, QB) < length
            n0, f0 = b * QB, KW + b * (QB // STRIDE)
            for h in range(QHEADS):
                kl = slice(h * HEAD_DIM, (h + 1) * HEAD_DIM)
                vl = slice(CHANS + h * HEAD_DIM, CHANS + (h + 1) * HEAD_DIM)
                qh = Q[zq, b * QB : (b + 1) * QB, kl]
                sn = nt(KV[zq, n0 : n0 + NEAR, kl], qh) * SCALE + maskn[b]
                sf = nt(KV[zq, f0 : f0 + FAR, kl], qh) * SCALE + maskf[b]
                peak = jnp.maximum(
                    jnp.max(sn, axis=0, keepdims=True), jnp.max(sf, axis=0, keepdims=True)
                )
                en, ef = jnp.exp(sn - peak), jnp.exp(sf - peak)
                inv = 1.0 / (sum_col(en) + sum_col(ef))
                pn, pf = en * inv, ef * inv
                P[zq, h, b, 0:NEAR, :] = pn
                P[zq, h, b, NEAR : NEAR + FAR, :] = pf
                ct = tn(KV[zq, n0 : n0 + NEAR, vl], pn.astype(BF))
                ct = ct + tn(KV[zq, f0 : f0 + FAR, vl], pf.astype(BF))
                ct = jnp.where(live, ct, 0.0)
                CTX[zq, b * QB : (b + 1) * QB, kl] = ct.T.astype(BF)
        acc[...] += nn(CTX[zq], W[0, zq, 3 * CHANS : D, :])
        lax.fori_loop(lookup_slots(s), lookup_slots(s + 1), gather_slot, 0)
        return carry

    def lookup_slots(s):
        return jnp.where(s == 0, 0, jnp.where(s < 3, 2 + 2 * s, 8))

    lax.fori_loop(0, QUARTERS, attend, 0)

    def store_T(dst, v, cols):
        vt = v.T.astype(BF)
        for j in range(8):
            to = (j % 2) * 4 + j // 2
            dst[to * PIECE : (to + 1) * PIECE, cols] = vt[j * PIECE : (j + 1) * PIECE]

    def span(i, size):
        if isinstance(i, int):
            return pl.ds(i * size, size)
        return pl.ds(pl.multiple_of(i * size, size), size)

    def norm_one(i, carry):
        rows = span(i, QB)
        res = tok[pl.ds(pl.multiple_of(base + i * QB, QB), QB), :].astype(F32)
        hid = res + (acc[rows, :] + bo[...])
        cen = hid - mean_row(hid)
        r = lax.rsqrt(mean_row(cen * cen) + epsilon)
        n = cen * r
        n1[rows, :] = n
        r1[rows, :] = r
        out = n * ag[...] + ash[...]
        y1[rows, :] = out
        y1b[rows, :] = out.astype(BF)
        store_T(yT, out, rows)
        acc[rows, :] = jnp.zeros_like(out)
        return carry

    lax.fori_loop(0, ROWS // QB, norm_one, 0)

    def most_gathered():
        lax.fori_loop(0, CHUNKS - 1, gather_done, 0)

    def feed(s, carry):
        zq = quarter(s)

        def up(i, carry):
            cols = span(i, ROWS)
            u = nn(y1b[...], W[1, zq, :, cols]) + VEC[zq, 0:1, cols]
            cdf = 0.5 * (1.0 + lax.erf(u * (0.5 ** 0.5)))
            dg[zq, :, cols] = cdf + u * jnp.exp(-0.5 * u * u) * ((2.0 * 3.141592653589793) ** -0.5)
            av[zq, :, cols] = (u * cdf).astype(BF)
            return carry

        for i in range(D // ROWS):
            up(i, 0)
        pl.when(s == QUARTERS - 1)(most_gathered)
        lax.fori_loop(8 + s, 9 + s, gather_slot, 0)
        acc[...] += nn(av[zq], W[2, zq])
        return carry

    lax.fori_loop(0, QUARTERS, feed, 0)
    VG[...] = jnp.zeros_like(VG)
    GEN = 8 * QUARTERS

    def add_row(row, v):
        VG[row : row + 1, :] += sum_col(v)

    def norm_two(i, carry):
        rows = span(i, QB)
        hid = y1[rows, :] + (acc[rows, :] + bd[...])
        cen = hid - mean_row(hid)
        r = lax.rsqrt(mean_row(cen * cen) + epsilon)
        n = cen * r
        act_out[rows, :] = (n * fg[...] + fs[...]).astype(BF)
        g = cot[rows, :].astype(F32)
        add_row(GEN + 4, g * n)
        add_row(GEN + 5, g)
        e = g * fg[...]
        gh2 = r * (e - mean_row(e) - n * mean_row(e * n))
        acc[rows, :] = gh2
        gf = gh2.astype(BF)
        gab[rows, :] = gf
        gff = gf.astype(F32)
        add_row(GEN + 3, gff)
        store_T(fT, gff, rows)
        return carry

    lax.fori_loop(0, ROWS // QB, norm_two, 0, unroll=True)
    outs[0].start()

    PARTS = 12

    def part(r):
        m = lax.select(r < 8, 2 - lax.rem(r, 2), 0)
        t = lax.select(r < 8, lax.div(r, 2), r - 8)
        return m, t

    def r_core(r):
        m, t = part(r)
        src = W.at[m, target(t), half(1 - c), :]
        return rcopy(src, CR.at[r], rsend.at[r], rrecv.at[r, 0], core)

    def blk4(r, yy, xx, cols):
        return CR.at[r, block(2 * yy + xx), cols]

    THIRD = D // 3
    wide = (LO, HI, D // 2, ALL)
    thin = (pl.ds(0, THIRD), pl.ds(THIRD, THIRD), THIRD, pl.ds(0, 2 * THIRD))
    LAST = pl.ds(2 * THIRD, THIRD)
    OWN_DOWN = 6

    def narrow(r):
        m, t = part(r)
        return (m == DOWN) & (t < QUARTERS - 1)

    def by_width(r, fn):
        pl.when(narrow(r))(lambda: fn(thin))
        pl.when(jnp.logical_not(narrow(r)))(lambda: fn(wide))

    def r_stage1(r, i, cut):
        if i < 2:
            src, dev = blk4(r, i, 1 - x, cut[0]), xdev
        else:
            src, dev = blk4(r, 1 - y, i - 2, cut[1]), ydev
        return rcopy(src, S1.at[r, i, :, 0 : cut[2]], rsend.at[r], rrecv.at[r, 1], dev)

    def r_stage2(r, i, cut):
        if i == 0:
            src, dev = blk4(r, 1 - y, x, cut[0]), ydev
        else:
            src, dev = blk4(r, y, 1 - x, cut[1]), xdev
        return rcopy(src, S2.at[r, i, :, 0 : cut[2]], rsend.at[r], rrecv.at[r, 2], dev)

    def onto(r):
        dst = target(part(r)[1])
        left = dst < z
        slot = jnp.where(left & (dst == z - 1), QUARTERS, dst)
        return slot, (dp, jnp.where(left, z - 1, z + 1))

    def r_z(r, cut):
        slot, dev = onto(r)
        m = part(r)[0]
        src = CR.at[r, block(yx), cut[3]]
        return rcopy(src, ZR.at[m, slot, :, cut[3]], rsend.at[r], zsum.at[m, slot], dev)

    def z_wait(m, slot, cut):
        ref = ZR.at[m, slot, :, cut[3]]
        pltpu.make_async_copy(ref, ref, zsum.at[m, slot]).wait()

    def r_zf(r):
        slot, dev = onto(r)
        return rcopy(CR.at[r, :, LAST], ZF.at[slot], rsend.at[r], zfsum.at[slot], dev)

    def take_zf(r, slot):
        ref = ZF.at[slot]
        pltpu.make_async_copy(ref, ref, zfsum.at[slot]).wait()
        CR[r, :, LAST] = CR[r, :, LAST] + ZF[slot]

    def upstream(dst):
        return jnp.where(dst < z, z < QUARTERS - 1, z > 0)

    def reduce1(r):
        m, t = part(r)
        r_core(r).wait_recv()
        zq = target(t)

        def add(i, carry):
            CR[r, block(i), :] = CR[r, block(i), :] + W[m, zq, block(4 * c + i), :]
            return carry

        lax.fori_loop(0, 4, add, 0)

        @pl.when(r == OWN_DOWN)
        def _():
            pl.when(z > 0)(lambda: take_zf(r, z))
            pl.when(z < QUARTERS - 1)(lambda: take_zf(r, jnp.int32(QUARTERS)))

        def go(cut):
            for i in range(4):
                r_stage1(r, i, cut).start()

        by_width(r, go)
        pl.when(narrow(r) & jnp.logical_not(upstream(zq)))(lambda: r_zf(r).start())

    def reduce_f(r):
        dst = target(part(r)[1])

        @pl.when(upstream(dst))
        def _():
            take_zf(r, dst)
            r_zf(r).start()

    def reduce2(r):
        def go(cut):
            ref = S1.at[r, :, :, 0 : cut[2]]
            pltpu.make_async_copy(ref, ref, rrecv.at[r, 1]).wait()
            for i in range(2):
                a = blk4(r, i, x, cut[0])
                a[...] = a[...] + S1[r, i, :, 0 : cut[2]]
                a = blk4(r, y, i, cut[1])
                a[...] = a[...] + S1[r, 2 + i, :, 0 : cut[2]]
            for i in range(2):
                r_stage2(r, i, cut).start()

        by_width(r, go)

    def reduce3(r):
        dst = target(part(r)[1])

        def go(cut):
            ref = S2.at[r, :, :, 0 : cut[2]]
            pltpu.make_async_copy(ref, ref, rrecv.at[r, 2]).wait()
            for i in range(2):
                a = blk4(r, y, x, cut[i])
                a[...] = a[...] + S2[r, i, :, 0 : cut[2]]
            pl.when((dst != z) & jnp.logical_not(upstream(dst)))(lambda: r_z(r, cut).start())

        by_width(r, go)

    def reduce4(r):
        m, t = part(r)
        dst = target(t)

        def go(cut):
            @pl.when((dst != z) & upstream(dst))
            def _():
                z_wait(m, dst, cut)
                a = CR.at[r, block(yx), cut[3]]
                a[...] = a[...] + ZR[m, dst, :, cut[3]]
                r_z(r, cut).start()

        by_width(r, go)

    def stage(fn, ok, r):
        pl.when(ok)(lambda: fn(r))

    def weight_grad(left, right, dst, width):
        dst[:, 0:width] = nn(left[...], right).astype(BF)

    def feed_back(s, carry):
        zq = target(s)
        vrow = pl.multiple_of(8 * zq, 8)

        def hidden(i, carry):
            cols = span(i, ROWS)
            gact = nt(gab[...], W[2, zq, cols, :])
            gu = (gact * dg[zq, :, cols]).astype(BF)
            gub[:, cols] = gu
            VG[pl.ds(vrow, 1), cols] = sum_col(gu.astype(F32))
            return carry

        for i in range(D // ROWS):
            hidden(i, 0)
        weight_grad(fT, av[zq], W.at[2, zq], D)
        r_core(2 * s).start()
        acc[...] += nt(gub[...], W[1, zq])
        weight_grad(yT, gub[...], W.at[1, zq], D)
        r_core(2 * s + 1).start()
        reduce1(jnp.where(s < 2, s, s + 1))
        stage(reduce1, s == 1, jnp.int32(2))
        stage(reduce2, s == 3, jnp.int32(0))
        return carry

    gather_done(jnp.int32(LAST_CHUNK), 0)
    both(own_sent)

    @pl.when(jnp.logical_not(at_end))
    def _():
        pieces = W.at[:, 0, 0 : 3 * PIECE, :]
        pltpu.make_async_copy(pieces, pieces, lsend.at[0]).wait()
        vecs = VEC.at[0 : QUARTERS - 1]
        pltpu.make_async_copy(vecs, vecs, lsend.at[1]).wait()

    lax.fori_loop(0, QUARTERS, feed_back, 0)

    def norm_back(i, carry):
        rows = span(i, QB)
        gy = acc[rows, :]
        n = n1[rows, :]
        add_row(GEN + 1, gy * n)
        add_row(GEN + 2, gy)
        e = gy * ag[...]
        gh1 = r1[rows, :] * (e - mean_row(e) - n * mean_row(e * n))
        acc[rows, :] = gh1
        ga = gh1.astype(BF)
        gab[rows, :] = ga
        gaf = ga.astype(F32)
        add_row(GEN, gaf)
        store_T(fT, gaf, rows)
        store_T(xT, tok[pl.ds(pl.multiple_of(base + i * QB, QB), QB), :].astype(F32), rows)
        return carry

    lax.fori_loop(0, ROWS // QB, norm_back, 0)

    def hl(zq):
        return rcopy(SL.at[zq], HL.at[zq], hsend.at[0], hrecv.at[0, zq], zdev(3))

    def hr(zq):
        return rcopy(SR.at[zq], HR.at[zq], hsend.at[1], hrecv.at[1, zq], zdev(1))

    def hll(zq):
        return rcopy(
            SL.at[zq, REACH : REACH + 16, :], HLL.at[zq], hsend.at[2], hrecv.at[2, zq], zdev(2)
        )

    def attend_back(s, carry):
        zq = lookup(table((3, 0, 2, 1)), s)
        gc = nt(gab[...], W[0, zq, 3 * CHANS : D, :])
        alive = base + rows_iota(ROWS, 1) < length
        gcb = jnp.where(alive, gc, 0.0).astype(BF)
        GKV[zq] = jnp.zeros((KEYS, 2 * CHANS), F32)
        for b in range(2):
            n0, f0 = b * QB, KW + b * (QB // STRIDE)
            for h in range(QHEADS):
                kl = slice(h * HEAD_DIM, (h + 1) * HEAD_DIM)
                vl = slice(CHANS + h * HEAD_DIM, CHANS + (h + 1) * HEAD_DIM)
                gch = gcb[b * QB : (b + 1) * QB, kl]
                qh = Q[zq, b * QB : (b + 1) * QB, kl]
                pn = P[zq, h, b, 0:NEAR, :]
                pf = P[zq, h, b, NEAR : NEAR + FAR, :]
                gpn = nt(KV[zq, n0 : n0 + NEAR, vl], gch)
                gpf = nt(KV[zq, f0 : f0 + FAR, vl], gch)
                delta = sum_col(pn * gpn) + sum_col(pf * gpf)
                gsn = (pn * (gpn - delta)).astype(BF)
                gsf = (pf * (gpf - delta)).astype(BF)
                qt = tn(KV[zq, n0 : n0 + NEAR, kl], gsn) + tn(KV[zq, f0 : f0 + FAR, kl], gsf)
                GQ[zq, b * QB : (b + 1) * QB, 2 * CHANS + h * HEAD_DIM : 2 * CHANS + (h + 1) * HEAD_DIM] = (
                    (qt * SCALE).T.astype(BF)
                )
                GKV[zq, n0 : n0 + NEAR, kl] += nn(gsn, qh) * SCALE
                GKV[zq, f0 : f0 + FAR, kl] += nn(gsf, qh) * SCALE
                GKV[zq, n0 : n0 + NEAR, vl] += nn(pn.astype(BF), gch)
                GKV[zq, f0 : f0 + FAR, vl] += nn(pf.astype(BF), gch)
        vrow = pl.multiple_of(8 * zq, 8)
        for i in range(TILES):
            kvf[i, FRONT : FRONT + COMP, :] = KVS[zq, :, tile(i)].astype(F32)
        gp = GKV[zq, KW:KEYS, :]
        sums = jnp.concatenate(
            [jnp.zeros((1, CHANS), F32), sum_col(GKV[zq, 0:KW, CHANS : 2 * CHANS])], axis=1
        )
        far_at = (OWNP * z - PREACH + rows_iota(KP, 1)) * STRIDE
        for t in range(5):
            VG[pl.ds(vrow + 2 + t, 1), 0 : 2 * CHANS] = sum_col(gp * strided(t))
            to = far_at + (t - 2)
            inside = (to >= 0) & (to < length)
            sums = sums + taps(zq, t) * sum_col(jnp.where(inside, gp, 0.0))
        VG[pl.ds(vrow + 1, 1), CHANS : 2 * CHANS] = sums[:, CHANS : 2 * CHANS]
        VG[pl.ds(vrow + 1, 1), 2 * CHANS : 3 * CHANS] = sum_col(
            GQ[zq, :, 2 * CHANS : 3 * CHANS].astype(F32)
        )
        SL[zq, 0:REACH, :] = GKV[zq, 0:REACH, :].astype(BF)
        SL[zq, REACH : REACH + 80, :] = GKV[zq, KW : KW + 80, :].astype(BF)
        SR[zq, 0:REACH, :] = GKV[zq, KW - REACH : KW, :].astype(BF)
        SR[zq, REACH : REACH + OWNP, :] = GKV[zq, KEYS - OWNP : KEYS, :].astype(BF)
        pl.when(z > 0)(lambda: hl(zq).start())
        pl.when(z < QUARTERS - 1)(lambda: hr(zq).start())
        pl.when(z > 1)(lambda: hll(zq).start())
        stage(reduce1, s == 0, jnp.int32(5))
        reduce2(s + 1)
        stage(reduce3, s == 3, jnp.int32(0))
        stage(reduce_f, s > 0, jnp.where(s == 1, 0, jnp.where(s == 2, 4, 2)))
        return carry

    lax.fori_loop(0, QUARTERS, attend_back, 0)

    half_row = pl.multiple_of(32 * c, 32)
    row_x = pl.multiple_of(half_row + 16 * x, 16)
    row_y = pl.multiple_of(row_x + 8 * y, 8)

    def vrows(at, size):
        return pl.ds(pl.multiple_of(at, 8), size)

    folds = [
        (core, VG.at[vrows(32 - half_row, 32), :], GVR.at[0:32], vrows(half_row, 32)),
        (xdev, VG.at[vrows(half_row + 16 - 16 * x, 16), :], GVR.at[32:48], vrows(row_x, 16)),
        (ydev, VG.at[vrows(row_x + 8 - 8 * y, 8), :], GVR.at[48:56], vrows(row_y, 8)),
    ]

    def fold(i):
        dev, src, dst, keep = folds[i]
        return rcopy(src, dst, gsend.at[i], grecv.at[i], dev)

    def fold_done(i):
        fold(i).wait()
        keep = folds[i][3]
        VG[keep, :] = VG[keep, :] + folds[i][2][...]

    def g_z(s):
        src = VG.at[vrows(row_y, 8), :]
        return rcopy(src, GVZ.at[z], gsend.at[2 + s], grecv.at[2 + s], zdev(s))

    def g_z_in(s):
        dst = GVZ.at[got(s)]
        return rcopy(dst, dst, gsend.at[2 + s], grecv.at[2 + s], core)

    opens = [
        (ydev, vrows(row_y, 8), vrows(row_x + 8 - 8 * y, 8)),
        (xdev, vrows(row_x, 16), vrows(half_row + 16 - 16 * x, 16)),
        (core, vrows(half_row, 32), vrows(32 - half_row, 32)),
    ]

    def unfold(i):
        dev, mine, other = opens[i]
        ref = VO.at[mine, :]
        return rcopy(ref, ref, gsend.at[6 + i], grecv.at[6 + i], dev)

    def unfold_done(i):
        ref = VO.at[opens[i][2], :]
        rcopy(ref, ref, gsend.at[6 + i], grecv.at[6 + i], core).wait_recv()

    def vector_two():
        fold_done(0)
        fold(1).start()

    def vector_three():
        fold_done(1)
        fold(2).start()

    def vector_z():
        fold_done(2)
        for step in (1, 2, 3):
            g_z(step).start()
        GVZ[z] = VG[vrows(row_y, 8), :]

    def vector_back():
        for step in (1, 2, 3):
            g_z_in(step).wait_recv()
        VO[vrows(row_y, 8), :] = GVZ[0] + GVZ[1] + GVZ[2] + GVZ[3]
        unfold(0).start()

    fold(0).start()

    def project_back(s, carry):
        zq = target(s)
        pl.when(z < QUARTERS - 1)(lambda: hl(zq).wait_recv())
        pl.when(z > 0)(lambda: hr(zq).wait_recv())
        pl.when(z < QUARTERS - 2)(lambda: hll(zq).wait_recv())
        near = GKV.at[zq]

        def when(ok, v):
            return jnp.where(ok, v.astype(F32), 0.0)

        has_l, has_r, has_rr = z > 0, z < QUARTERS - 1, z < QUARTERS - 2
        near[REACH : 2 * REACH, :] += when(has_l, HR[zq, 0:REACH, :])
        near[ROWS : ROWS + REACH, :] += when(has_r, HL[zq, 0:REACH, :])
        gp = GKV[zq, KW + OWNP : KW + 2 * OWNP, :] + when(has_l, HR[zq, REACH : REACH + OWNP, :])
        gp = gp + when(has_r, HL[zq, REACH : REACH + OWNP, :])
        nxt = GKV[zq, KW + 2 * OWNP : KW + 2 * OWNP + 1, :]
        nxt = nxt + when(has_r, HL[zq, REACH + OWNP : REACH + OWNP + 16, :])[0:1, :]
        nxt = nxt + when(has_rr, HLL[zq])[0:1, :]
        gp1 = jnp.concatenate([gp[1:, :], nxt], axis=0)
        fills = (
            taps(zq, 2) * gp,
            taps(zq, 3) * gp,
            taps(zq, 4) * gp + taps(zq, 0) * gp1,
            taps(zq, 1) * gp1,
        )
        for k, fill in enumerate(fills):
            for i in range(TILES):
                pt[i, pl.ds(k, OWNP, stride=STRIDE), :] = fill[:, tile(i)]
        back = jnp.concatenate([pt[i, 0:ROWS, :] for i in range(TILES)], axis=1)
        alive = base + rows_iota(ROWS, 1) < length
        gkv = GKV[zq, REACH : REACH + ROWS, :] + jnp.where(alive, back, 0.0)
        GQ[zq, :, 0 : 2 * CHANS] = gkv.astype(BF)

        acc[...] += nn(GQ[zq], W[0, zq, 0 : 3 * CHANS, :])
        weight_grad(xT, GQ[zq], W.at[0, zq], 3 * CHANS)

        W[0, zq, :, 3 * CHANS : D] = nn(fT[...], CTX[zq]).astype(BF)
        r_core(8 + s).start()
        stage(reduce2, s == 0, jnp.int32(5))
        stage(reduce3, s > 0, s)
        stage(reduce4, s > 1, s - 2)
        pl.when(s == 0)(vector_two)
        stage(reduce1, s < 3, 8 + s)
        stage(reduce1, s == 1, jnp.int32(7))
        pl.when(s == 2)(vector_three)
        return carry

    lax.fori_loop(0, QUARTERS, project_back, 0)
    outs[1].start()

    def wait_all(ref, sem):
        pltpu.make_async_copy(ref, ref, sem).wait()

    pl.when(z > 0)(lambda: wait_all(SL, hsend.at[0]))
    pl.when(z < QUARTERS - 1)(lambda: wait_all(SR, hsend.at[1]))
    pl.when(z > 1)(lambda: wait_all(HLL, hsend.at[2]))

    def final(m):
        own_part = (11, 7, 6)[m]
        gmats[m] = CR[own_part, block(yx), :].astype(F32)

        def more(slot):
            cut = thin if m == DOWN else wide
            z_wait(m, slot, cut)
            at = gmats.at[m, :, cut[3]]
            at[...] += ZR[m, slot, :, cut[3]].astype(F32)

        pl.when(z > 0)(lambda: more(z))
        pl.when(z < QUARTERS - 1)(lambda: more(QUARTERS))
        outs[2 + m].start()

    def at(r):
        return jnp.int32(r)

    reduce2(at(8))
    reduce1(at(6))
    reduce3(at(4))
    vector_z()
    reduce4(at(2))
    reduce2(at(9))
    reduce1(at(11))
    reduce3(at(5))
    reduce4(at(3))
    reduce2(at(10))
    reduce2(at(7))
    reduce4(at(4))
    reduce3(at(8))
    vector_back()
    reduce4(at(5))
    reduce3(at(9))
    reduce4(at(8))
    reduce2(at(6))
    unfold_done(0)
    unfold(1).start()
    reduce3(at(10))
    reduce4(at(9))
    reduce2(at(11))
    reduce4(at(10))
    unfold_done(1)
    unfold(2).start()
    reduce3(at(7))
    final(1)
    reduce3(at(6))
    final(2)
    unfold_done(2)
    outs[5].start()
    reduce3(at(11))
    final(0)
    for i in range(3):
        unfold(i).wait_send()
    for s in (1, 2, 3):
        g_z(s).wait_send()

    def sent(r, carry):
        own_part = part(r)[1] == QUARTERS - 1
        pl.when(own_part)(lambda: wait_rows(rsend.at[r], 7 * PIECE))
        pl.when(jnp.logical_not(own_part))(lambda: wait_rows(rsend.at[r], 8 * PIECE))
        return carry

    lax.fori_loop(0, PARTS, sent, 0)
    for cp in outs:
        cp.wait()


def unpack(
    act, gtok, gmats, gvec,
    act_out, gtok_out, gq, gk, gv, gbq, gbv, gck, gcv, go, gbo, gag, gas, gup, gbu, gdown, gbd, gfg, gfs,
):
    act_out[...] = act[...]
    gtok_out[...] = gtok[...]
    gk[...] = gmats[0, :, 0:CHANS]
    gv[...] = gmats[0, :, CHANS : 2 * CHANS]
    gq[...] = gmats[0, :, 2 * CHANS : 3 * CHANS]
    go[...] = gmats[0, :, 3 * CHANS : D].T
    gup[...] = gmats[1]
    gdown[...] = gmats[2]
    for j in range(QUARTERS):
        at = slice(j * CHANS, (j + 1) * CHANS)
        row = 8 * j
        gbu[:, j * D : (j + 1) * D] = gvec[row : row + 1, :]
        gbv[:, at] = gvec[row + 1 : row + 2, CHANS : 2 * CHANS]
        gbq[:, at] = gvec[row + 1 : row + 2, 2 * CHANS : 3 * CHANS]
        for t in range(5):
            gck[t, :, at] = gvec[row + 2 + t : row + 3 + t, 0:CHANS]
            gcv[t, :, at] = gvec[row + 2 + t : row + 3 + t, CHANS : 2 * CHANS]
    for j, out in enumerate((gbo, gag, gas, gbd, gfg, gfs)):
        out[...] = gvec[8 * QUARTERS + j : 8 * QUARTERS + j + 1, :]


def fused_layer(
    tokens, lengths, w_query, w_key, w_value, b_query, b_value, conv_key, conv_value, w_out,
    b_out, attn_gain, attn_shift, w_up, b_up, w_down, b_down, ffn_gain, ffn_shift, cotangent,
):
    Q4 = QUARTERS
    vm = pltpu.VMEM
    dma = pltpu.SemaphoreType.DMA
    scratch = [
        vm((3, Q4, D, D), BF),
        vm((Q4, 8, D), F32),
        vm((TILES, KVROWS, 128), F32),
        vm((Q4, KEYS, 2 * CHANS), BF),
        vm((Q4, COMP, 2 * CHANS), BF),
        vm((Q4, ROWS, CHANS), BF),
        vm((Q4, ROWS, CHANS), BF),
        vm((Q4, QHEADS, 2, NEAR + FAR, QB), F32),
        vm((2, NEAR, QB), F32),
        vm((2, FAR, QB), F32),
        vm((ROWS, D), F32),
        vm((ROWS, 1), F32),
        vm((ROWS, D), F32),
        vm((ROWS, D), BF),
        vm((Q4, ROWS, D), F32),
        vm((Q4, ROWS, D), BF),
        vm((D, ROWS), BF),
        vm((D, ROWS), BF),
        vm((ROWS, D), BF),
        vm((Q4, KEYS, 2 * CHANS), F32),
        vm((TILES, ROWS + 8, 128), F32),
        vm((Q4, ROWS, 3 * CHANS), BF),
        vm((VROWS, D), F32),
        vm((12, D // 2, D), BF),
        vm((12, 4, PIECE, D // 2), BF),
        vm((12, 2, PIECE, D // 2), BF),
        vm((3, Q4 + 1, PIECE, D), BF),
        vm((Q4 + 1, D // 2, D // 3), BF),
        vm((Q4, REACH + 80, 2 * CHANS), BF),
        vm((Q4, REACH + OWNP, 2 * CHANS), BF),
        vm((Q4, 16, 2 * CHANS), BF),
        vm((Q4, REACH + 80, 2 * CHANS), BF),
        vm((Q4, REACH + OWNP, 2 * CHANS), BF),
        vm((VROWS, D), F32),
        vm((Q4, 8, D), F32),
        vm((VROWS, D), F32),
        vm((SEQ, D), BF),
        vm((ROWS, D), BF),
        pltpu.SMEM((1,), jnp.int32),
        vm((1, CHANS), F32),
        vm((1, CHANS), F32),
        vm((5, 1, CHANS), F32),
        vm((5, 1, CHANS), F32),
        vm((1, D), F32),
        vm((1, D), F32),
        vm((1, D), F32),
        vm((1, D), F32),
        vm((1, D), F32),
        vm((1, D), F32),
        vm((1, D), F32),
        vm((ROWS, D), BF),
        vm((ROWS, D), F32),
        vm((3, PIECE, D), F32),
        dma((12,)),
        dma((6,)),
        dma((5,)),
        dma((9,)),
        dma((9, 3)),
        dma((2, 2)),
        dma((5, Q4)),
        dma((2,)),
        dma((3,)),
        dma((3, Q4)),
        dma((12,)),
        dma((12, 3)),
        dma((3, Q4 + 1)),
        dma((Q4 + 1,)),
        dma((9,)),
        dma((9,)),
    ]
    vspec = pl.BlockSpec(memory_space=pltpu.VMEM)
    hspec = pl.BlockSpec(memory_space=pl.ANY)
    packed = pl.pallas_call(
        kernel,
        out_shape=(
            jax.ShapeDtypeStruct((ROWS, D), BF),
            jax.ShapeDtypeStruct((ROWS, D), F32),
            jax.ShapeDtypeStruct((3, PIECE, D), F32),
            jax.ShapeDtypeStruct((VROWS, D), F32),
        ),
        in_specs=[hspec] * 20,
        out_specs=(hspec,) * 4,
        scratch_shapes=scratch,
        compiler_params=pltpu.CompilerParams(
            collective_id=0, has_side_effects=True, vmem_limit_bytes=67043328
        ),
        name="layer",
    )(
        lengths, tokens, w_key[0].T, w_value[0].T, w_query[0].T, w_out[0], w_up[0], w_down[0],
        b_query, b_value, conv_key.transpose(1, 0, 2), conv_value.transpose(1, 0, 2), b_up, b_out, attn_gain, attn_shift, b_down,
        ffn_gain, ffn_shift, cotangent,
    )
    row = (1, D)
    shapes = [
        (ROWS, D), (PIECE, CHANS), (PIECE, CHANS), (PIECE, CHANS), row, row, (5, 1, D), (5, 1, D), (CHANS, PIECE),
        row, row, row, (PIECE, D), (1, FF), (PIECE, D), row, row, row,
    ]
    outs = pl.pallas_call(
        unpack,
        out_shape=[jax.ShapeDtypeStruct((ROWS, D), BF)] + [jax.ShapeDtypeStruct(v, F32) for v in shapes],
        in_specs=[vspec] * 4,
        out_specs=[vspec] * 19,
        name="unpack",
    )(*packed)
    act, gtok, gq, gk, gv, gbq, gbv, gck, gcv, go, gbo, gag, gas, gup, gbu, gdown, gbd, gfg, gfs = outs
    return (
        act, gtok, gq[None], gk[None], gv[None], gbq, gbv, gck.transpose(1, 0, 2), gcv.transpose(1, 0, 2), go[None], gbo, gag, gas,
        gup[None], gbu, gdown.T[None], gbd, gfg, gfs,
    )


def solution(mesh):
    small = mesh.shape["dp"] == 8 and mesh.shape["mp"] == QUARTERS
    return jax.shard_map(
        fused_layer if small else on_device,
        mesh=mesh,
        in_specs=(
            P("dp", None),
            P("dp"),
            P(None, None, "mp"),
            P(None, None, "mp"),
            P(None, None, "mp"),
            P(None, "mp"),
            P(None, "mp"),
            P(None, None, "mp"),
            P(None, None, "mp"),
            P(None, "mp", None),
            P(),
            P(),
            P(),
            P(None, None, "mp"),
            P(None, "mp"),
            P(None, "mp", None),
            P(),
            P(),
            P(),
            P(("dp", "mp"), None),
        ),
        out_specs=(
            P(("dp", "mp"), None),
            P(("dp", "mp"), None),
            P(None, "dp", "mp"),
            P(None, "dp", "mp"),
            P(None, "dp", "mp"),
            P(),
            P(),
            P(),
            P(),
            P(None, "mp", "dp"),
            P(),
            P(),
            P(),
            P(None, "dp", "mp"),
            P(),
            P(None, "mp", "dp"),
            P(),
            P(),
            P(),
        ),
        check_vma=False,
    )
```
